256 devices in a mesh: vel: 4 (over x_lo, core), space: 64 (over x_hi, y, z).
Axes of the slice: x: 4 (x_hi: 2, x_lo: 2; x = x_hi * 2 + x_lo), y: 4, z: 8, core: 2. Of those that a mesh axis runs over, the one named last changes fastest.
Arguments:
- distribution: float32 [256, 8, 64, 512], P('space', None, None, 'vel'), may hold values from -8 to 8
- forcing: float32 [3, 256, 8, 64], P(None, 'space'), may hold values from -6 to 6
Outputs:
- updated: float32 [256, 8, 64, 512], P('space', None, None, 'vel')
- macro_fields: float32 [5, 256, 8, 64], P(None, 'space')
The draws below stay inside these ranges and needn't reach their ends.
All inputs are finite; a program needn't handle non-finite values.
Results may differ from the reference program's by a relative error of at most 0.0001.
Values sent between devices are 32-bit elements; how exact they have to be, the bound alone decides.
No kernel may reach another device: no remote copies, remote signals or barrier semaphores. Data moves between devices by JAX's collectives and lax.ppermute only.
A program may use at most 128 MiB of HBM per device.

```python
import math
import jax
import jax.numpy as jnp
from jax import lax

V_DEV = 128
STEPS = 2
PASSES = 3
NX = 256
NY = 8
NZ = 64
VELS = 512
N_VEL = 4


def velocity_set_drawn(global_ids, per_device):
    half_count = per_device // 2
    device_rank = global_ids // per_device
    local_rank = global_ids % per_device
    upper_part = local_rank // half_count
    mixed = ((device_rank * half_count + local_rank % half_count) * 5179 + 7) % 16384
    index_x = upper_part * 16 + mixed // 1024
    index_y = mixed // 32 % 32
    index_z = mixed % 32
    grid_points = jnp.stack([index_x, index_y, index_z]).astype(jnp.float32)
    speeds = (grid_points + 0.5) * 0.25 - 4.0
    return speeds


def equilibrium_drawn(fields, speeds):
    speed_x, speed_y, speed_z = (speeds[0], speeds[1], speeds[2])
    squared = speed_x * speed_x + speed_y * speed_y + speed_z * speed_z
    maxwell = math.pi ** (-1.5) * jnp.exp(-squared)
    expanded = fields[..., None]
    return maxwell * (expanded[0] + 2.0 * (expanded[1] * speed_x + expanded[2] * speed_y + expanded[3] * speed_z) + expanded[4] * (squared - 1.5))


def draw_distribution(key, part):
    key_fields = jax.random.fold_in(key, 11)
    key_noise = jax.random.fold_in(key, 12)
    fields = jnp.clip(jax.random.normal(key_fields, (5, NX, NY, NZ), jnp.float32), -4.0, 4.0)
    noise = jnp.clip(jax.random.normal(key_noise, (NX, NY, NZ, VELS), jnp.float32), -4.0, 4.0)
    global_ids = jnp.arange(VELS, dtype=jnp.int32)
    speeds = velocity_set_drawn(global_ids, V_DEV)
    value = equilibrium_drawn(fields, speeds) + 0.05 * noise
    return jnp.clip(value, -8.0, 8.0).astype(jnp.float32)


def steps_of(stream_key, dims, split, least, largest):
    gain, own = 1.0, jax.random.fold_in(stream_key, 6)
    for position, shards_of in split:
        heights = jnp.exp(jax.random.uniform(jax.random.fold_in(own, position), (shards_of,), jnp.float32, least / len(split), largest / len(split)))
        gain = gain * jnp.repeat(heights, dims[position] // shards_of).reshape([-1 if axis == position else 1 for axis in range(len(dims))])
    return gain


def normal_values(rng, extent, spread, reach, shards=(), kind=jnp.bfloat16):
    values = jax.random.normal(rng, extent, jnp.float32) * spread
    if len(shards) > 0:
        values = steps_of(rng, extent, shards, -0.22, 0.18) * values
    return jnp.clip(values, min=-reach, max=reach).astype(kind)


def setup_inputs(seed: int = 0) -> dict:
    key_of = jax.random.split(jax.random.key(seed), 3)
    distribution = draw_distribution(jax.random.fold_in(key_of[2], 71), 0)
    forcing = normal_values(key_of[1], (3, NX, NY, NZ), 1.0, 6.0, ((1, 64),), jnp.float32)
    return dict(distribution=distribution, forcing=forcing)


root_fifth = 0.4472135954999579
fine_points = [-1.0, -root_fifth, root_fifth, 1.0]
fine_weights = [1.0 / 6.0, 5.0 / 6.0, 5.0 / 6.0, 1.0 / 6.0]
coarse_points = [-1.0, 1.0]
coarse_weights = [1.0, 1.0]
metric_scale = 0.5
time_step = 0.02
collision_rate = 10.0
relax_time = 0.5
coupling = 1.0
epsilon = 1e-6


def lagrange_table(points):
    point_count = len(points)
    barycentric = []
    for row_rank in range(point_count):
        product = 1.0
        for col_rank in range(point_count):
            if col_rank != row_rank:
                product = product * (points[row_rank] - points[col_rank])
        barycentric.append(1.0 / product)
    matrix_rows = [[0.0] * point_count for row_rank in range(point_count)]
    for row_rank in range(point_count):
        diagonal_sum = 0.0
        for col_rank in range(point_count):
            if col_rank != row_rank:
                entry = barycentric[col_rank] / barycentric[row_rank] / (points[row_rank] - points[col_rank])
                matrix_rows[row_rank][col_rank] = entry
                diagonal_sum = diagonal_sum + entry
        matrix_rows[row_rank][row_rank] = -diagonal_sum
    return matrix_rows


def fine_rows():
    return lagrange_table(fine_points)


def coarse_rows():
    return lagrange_table(coarse_points)


def prolong_rows():
    return [[(1.0 - point_value) / 2.0, (1.0 + point_value) / 2.0] for point_value in fine_points]


def restrict_rows():
    prolong_table = prolong_rows()
    return [[fine_weights[node_rank] * prolong_table[node_rank][coarse_rank] for node_rank in range(4)] for coarse_rank in range(2)]


def velocity_set(global_ids, per_device, total_count):
    half_count = per_device // 2
    device_rank = global_ids // per_device
    local_rank = global_ids % per_device
    upper_part = local_rank // half_count
    mixed = ((device_rank * half_count + local_rank % half_count) * 5179 + 7) % 16384
    index_x = upper_part * 16 + mixed // 1024
    index_y = (mixed // 32) % 32
    index_z = mixed % 32
    grid_points = jnp.stack([index_x, index_y, index_z]).astype(jnp.float32)
    speeds = (grid_points + 0.5) * 0.25 - 4.0
    return speeds, 512.0 / total_count


def moment_rows(speeds, weight):
    speed_x, speed_y, speed_z = speeds[0], speeds[1], speeds[2]
    squared = speed_x * speed_x + speed_y * speed_y + speed_z * speed_z
    rows_list = [jnp.ones_like(speed_x), speed_x, speed_y, speed_z, 2.0 * squared / 3.0 - 1.0,
                 2.0 * (speed_x * speed_x - squared / 3.0), 2.0 * (speed_y * speed_y - squared / 3.0),
                 2.0 * speed_x * speed_y, 2.0 * speed_x * speed_z, 2.0 * speed_y * speed_z,
                 speed_x * (squared - 2.5), speed_y * (squared - 2.5), speed_z * (squared - 2.5)]
    return (jnp.stack(rows_list) * weight).astype(jnp.float32)


def equilibrium(fields, speeds):
    speed_x, speed_y, speed_z = speeds[0], speeds[1], speeds[2]
    squared = speed_x * speed_x + speed_y * speed_y + speed_z * speed_z
    maxwell = (math.pi ** -1.5) * jnp.exp(-squared)
    expanded = fields[..., None]
    return maxwell * (expanded[0] + 2.0 * (expanded[1] * speed_x + expanded[2] * speed_y + expanded[3] * speed_z)
                      + expanded[4] * (squared - 1.5))


def project_moments(moment_table, current):
    return lax.dot_general(moment_table, current, (((1,), (3,)), ((), ())),
                           precision=lax.Precision.HIGHEST, preferred_element_type=jnp.float32)


def element_rows(values, axis_dim, matrix_rows):
    rows_in = len(matrix_rows[0])
    full_shape = values.shape
    elements = full_shape[axis_dim] // rows_in
    viewed = values.reshape(full_shape[:axis_dim] + (elements, rows_in) + full_shape[axis_dim + 1:])
    pieces = [lax.index_in_dim(viewed, col_rank, axis_dim + 1, keepdims=False) for col_rank in range(rows_in)]
    outputs = []
    for row_list in matrix_rows:
        running = pieces[0] * row_list[0]
        for col_rank in range(1, rows_in):
            running = running + pieces[col_rank] * row_list[col_rank]
        outputs.append(running)
    return outputs, pieces, elements


def assemble(outputs, axis_dim, full_shape, elements):
    stacked = jnp.stack(outputs, axis_dim + 1)
    return stacked.reshape(full_shape[:axis_dim] + (elements * len(outputs),) + full_shape[axis_dim + 1:])


def nodal_apply(values, axis_dim, matrix_rows):
    outputs, pieces, elements = element_rows(values, axis_dim, matrix_rows)
    return assemble(outputs, axis_dim, values.shape, elements)


def derivative_plus(values, axis_dim, lower_rim, matrix_rows, end_weight):
    outputs, pieces, elements = element_rows(values, axis_dim, matrix_rows)
    previous = jnp.concatenate([lower_rim, lax.slice_in_dim(pieces[-1], 0, elements - 1, axis=axis_dim)], axis_dim)
    outputs[0] = outputs[0] - (previous - pieces[0]) / end_weight
    return assemble(outputs, axis_dim, values.shape, elements) * metric_scale


def derivative_minus(values, axis_dim, upper_rim, matrix_rows, end_weight):
    outputs, pieces, elements = element_rows(values, axis_dim, matrix_rows)
    following = jnp.concatenate([lax.slice_in_dim(pieces[0], 1, elements, axis=axis_dim), upper_rim], axis_dim)
    outputs[-1] = outputs[-1] + (following - pieces[-1]) / end_weight
    return assemble(outputs, axis_dim, values.shape, elements) * metric_scale


def wrap_rims(values, axis_dim):
    length = values.shape[axis_dim]
    return lax.slice_in_dim(values, length - 1, length, axis=axis_dim), lax.slice_in_dim(values, 0, 1, axis=axis_dim)


def upwind_terms(current, speeds, axis_dim, lower_rim, upper_rim):
    positive = jnp.maximum(speeds[axis_dim], 0.0)
    negative = jnp.minimum(speeds[axis_dim], 0.0)
    return (positive * derivative_plus(current, axis_dim, lower_rim, fine_rows(), fine_weights[0])
            + negative * derivative_minus(current, axis_dim, upper_rim, fine_rows(), fine_weights[-1]))


def transport_update(current, speeds, moments_five, x_term):
    flux = x_term
    for axis_dim in (1, 2):
        lower_rim, upper_rim = wrap_rims(current, axis_dim)
        flux = flux + upwind_terms(current, speeds, axis_dim, lower_rim, upper_rim)
    source = collision_rate * (equilibrium(moments_five, speeds) - current)
    return current + time_step * (source - flux)


def central_gradient(padded_field, spatial_axis, matrix_rows, end_weight):
    interior = padded_field[1:-1, :, 1:-1]
    if spatial_axis == 0:
        lower_rim = padded_field[0:1, :, 1:-1]
        upper_rim = padded_field[-1:, :, 1:-1]
    elif spatial_axis == 1:
        lower_rim, upper_rim = wrap_rims(interior, 1)
    else:
        lower_rim = padded_field[1:-1, :, 0:1]
        upper_rim = padded_field[1:-1, :, -1:]
    return 0.5 * (derivative_plus(interior, spatial_axis, lower_rim, matrix_rows, end_weight)
                  + derivative_minus(interior, spatial_axis, upper_rim, matrix_rows, end_weight))


def apply_operator(padded, matrix_rows, end_weight):
    def gradient(padded_field, spatial_axis):
        return central_gradient(padded_field, spatial_axis, matrix_rows, end_weight)

    divergence = gradient(padded[1], 0) + gradient(padded[2], 1) + gradient(padded[3], 2)
    pressure = padded[0] + padded[4]
    coupled = jnp.stack([divergence, gradient(pressure, 0), gradient(pressure, 1), gradient(pressure, 2), divergence])
    return padded[:, 1:-1, :, 1:-1] / relax_time + coupling * coupled


def level_dot(leading, second, level_weights):
    def weights_for(length):
        return jnp.tile(jnp.array(level_weights, jnp.float32), length // len(level_weights))

    along_x = weights_for(leading.shape[1])
    along_y = weights_for(leading.shape[2])
    along_z = weights_for(leading.shape[3])
    return jnp.sum(leading * second * along_x[:, None, None] * along_y[None, :, None] * along_z[None, None, :])


def restrict_fields(values):
    for axis_dim in (1, 2, 3):
        values = nodal_apply(values, axis_dim, restrict_rows())
    return values


def prolong_fields(values):
    for axis_dim in (1, 2, 3):
        values = nodal_apply(values, axis_dim, prolong_rows())
    return values


def smooth(moments, forcing, with_rims, global_sums):
    leading_five = moments[:5]
    padded_flux = with_rims(moments[5:])

    def gradient(padded_field, spatial_axis):
        return central_gradient(padded_field, spatial_axis, fine_rows(), fine_weights[0])

    stress_xx, stress_yy, stress_xy = padded_flux[0], padded_flux[1], padded_flux[2]
    stress_xz, stress_yz = padded_flux[3], padded_flux[4]
    stress_zz = -(padded_flux[0] + padded_flux[1])
    heat_x, heat_y, heat_z = padded_flux[5], padded_flux[6], padded_flux[7]
    target = jnp.stack([
        leading_five[0] / relax_time,
        leading_five[1] / relax_time - coupling * (gradient(stress_xx, 0) + gradient(stress_xy, 1) + gradient(stress_xz, 2)) + forcing[0],
        leading_five[2] / relax_time - coupling * (gradient(stress_xy, 0) + gradient(stress_yy, 1) + gradient(stress_yz, 2)) + forcing[1],
        leading_five[3] / relax_time - coupling * (gradient(stress_xz, 0) + gradient(stress_yz, 1) + gradient(stress_zz, 2)) + forcing[2],
        leading_five[4] / relax_time - coupling * (gradient(heat_x, 0) + gradient(heat_y, 1) + gradient(heat_z, 2))])
    fields = leading_five
    for pass_number in range(PASSES):
        residual = target - apply_operator(with_rims(fields), fine_rows(), fine_weights[0])
        coarse_residual = restrict_fields(residual)
        coarse_applied = apply_operator(with_rims(coarse_residual), coarse_rows(), coarse_weights[0])
        upper_sum, lower_sum = global_sums(level_dot(coarse_residual, coarse_applied, coarse_weights),
                                           level_dot(coarse_applied, coarse_applied, coarse_weights))
        fields = fields + prolong_fields(coarse_residual * (upper_sum / (lower_sum + epsilon)))
        residual = target - apply_operator(with_rims(fields), fine_rows(), fine_weights[0])
        applied = apply_operator(with_rims(residual), fine_rows(), fine_weights[0])
        upper_sum, lower_sum = global_sums(level_dot(residual, applied, fine_weights),
                                           level_dot(applied, applied, fine_weights))
        fields = fields + (upper_sum / (lower_sum + epsilon)) * residual
    return fields


def wrap_pad(values):
    lower_rim, upper_rim = wrap_rims(values, 1)
    padded_x = jnp.concatenate([lower_rim, values, upper_rim], 1)
    lower_rim, upper_rim = wrap_rims(padded_x, 3)
    return jnp.concatenate([lower_rim, padded_x, upper_rim], 3)


def plain_sums(leading, second):
    return leading, second


def reference(distribution, forcing):
    total_count = V_DEV * N_VEL
    blocks = []
    speed_list = []
    table_list = []
    for block_rank in range(N_VEL):
        global_ids = jnp.arange(block_rank * V_DEV, (block_rank + 1) * V_DEV, dtype=jnp.int32)
        speeds, weight = velocity_set(global_ids, V_DEV, total_count)
        speed_list.append(speeds)
        table_list.append(moment_rows(speeds, weight))
        blocks.append(distribution[:, :, :, block_rank * V_DEV:(block_rank + 1) * V_DEV])
    for step_number in range(STEPS):
        moments_five = project_moments(table_list[0][:5], blocks[0])
        for block_rank in range(1, N_VEL):
            moments_five = moments_five + project_moments(table_list[block_rank][:5], blocks[block_rank])
        updated_blocks = []
        for block_rank in range(N_VEL):
            current = blocks[block_rank]
            x_term = upwind_terms(current, speed_list[block_rank], 0, current[-1:], current[:1])
            updated_blocks.append(transport_update(current, speed_list[block_rank], moments_five, x_term))
        blocks = updated_blocks
    moments = project_moments(table_list[0], blocks[0])
    for block_rank in range(1, N_VEL):
        moments = moments + project_moments(table_list[block_rank], blocks[block_rank])
    fields = smooth(moments, forcing, wrap_pad, plain_sums)
    correction = fields - moments[:5]
    result = jnp.concatenate([blocks[block_rank] + equilibrium(correction, speed_list[block_rank])
                              for block_rank in range(N_VEL)], 3)
    return result, fields
```

```python
import math

import jax
import jax.numpy as jnp
import numpy as np
from jax import lax
from jax.experimental import pallas as pl
from jax.experimental.pallas import tpu as pltpu
from jax.sharding import PartitionSpec as P

INTERPRET = False
DT = 0.02
RF = 0.4472135954999579
POINTS = [-1.0, -RF, RF, 1.0]
WEIGHTS = [1.0 / 6.0, 5.0 / 6.0, 5.0 / 6.0, 1.0 / 6.0]
EPS = 1e-6
HI = lax.Precision.HIGHEST


def lagrange_table(points):
    n = len(points)
    bary = []
    for i in range(n):
        product = 1.0
        for j in range(n):
            if j != i:
                product *= points[i] - points[j]
        bary.append(1.0 / product)
    rows = [[0.0] * n for _ in range(n)]
    for i in range(n):
        for j in range(n):
            if j != i:
                rows[i][j] = bary[j] / bary[i] / (points[i] - points[j])
        rows[i][i] = -sum(rows[i])
    return rows


D4 = lagrange_table(POINTS)
for _i in (1, 2):
    D4[_i][_i] = 0.0
PR = [[(1.0 - x) / 2.0, (1.0 + x) / 2.0] for x in POINTS]
RT = [[WEIGHTS[i] * PR[i][a] for i in range(4)] for a in range(2)]


def constant_tables():
    k = np.arange(512)
    b, j = k // 128, k % 128
    s = j // 64
    m = ((b * 64 + j % 64) * 5179 + 7) % 16384
    xi = np.stack([16 * s + m // 1024, (m // 32) % 32, m % 32]).astype(np.float64)
    xi = -4.0 + 0.25 * (xi + 0.5)
    sq = (xi * xi).sum(0)
    e = math.pi ** (-1.5) * np.exp(-sq)
    x, y, z = xi
    phi = np.stack(
        [np.ones(512), x, y, z, 2 * sq / 3 - 1, 2 * (x * x - sq / 3), 2 * (y * y - sq / 3),
         2 * x * y, 2 * x * z, 2 * y * z, x * (sq - 2.5), y * (sq - 2.5), z * (sq - 2.5)]
    )
    p = phi[0] + phi[4]
    zero = np.zeros(512)

    def eight(rows):
        return np.stack(list(rows) + [zero] * (8 - len(rows)))

    low = eight(phi[:5])
    along_x = eight([phi[1], p + phi[5], phi[7], phi[8], phi[1] + phi[10]])
    along_y = eight([phi[2], phi[7], p + phi[6], phi[9], phi[2] + phi[11]])
    along_z = eight([phi[3], phi[8], phi[9], p - phi[5] - phi[6], phi[3] + phi[12]])
    rows32 = np.concatenate([low, along_x, along_y, along_z])
    ec = eight([e, 2 * x * e, 2 * y * e, 2 * z * e, e * (sq - 1.5)])
    pos, neg = np.maximum(xi, 0.0), np.minimum(xi, 0.0)

    def per_rank(rows):
        return np.stack([rows[:, r * 128:(r + 1) * 128] for r in range(4)]).astype(np.float32)

    ispos = (x > 0).astype(np.float64)
    ax = np.abs(x)
    d4 = np.array(D4)
    vec = [-DT * 0.5 * x, -DT * 0.5 * y, -DT * 0.5 * z,
           -3 * DT * pos[1], -3 * DT * neg[1], -3 * DT * pos[2], -3 * DT * neg[2],
           -3 * DT * pos[0], 3 * DT * neg[0], 3 * DT * ax]
    for i in range(4):
        kap = -DT * 0.5 * x * np.where(ispos > 0, d4[i][0], d4[i][3])
        if i == 0:
            kap = kap + ispos * (0.8 - 3 * DT * ax)
        if i == 3:
            kap = kap + (1 - ispos) * (0.8 - 3 * DT * ax)
        vec.append(kap)
    vec.append(ispos)
    for jj in range(4):
        vec.append(-DT * 0.5 * x * np.where(ispos > 0, d4[3][jj], d4[0][jj]))
    while len(vec) < 24:
        vec.append(zero)
    vec = per_rank(np.stack(vec))

    def moment_columns(start, rows):
        out = np.zeros((4, 128, 128))
        for r in range(4):
            out[r, :, start:start + len(rows)] = rows[:, r * 128:(r + 1) * 128].T
        return out.astype(np.float32)

    tab2 = moment_columns(0, rows32)
    tab1 = moment_columns(40, low)
    tab0 = moment_columns(32, low)
    tabr = moment_columns(0, low)
    g = rows32 @ ec.T
    g5 = g[:8]
    mix = np.zeros((40, 64))
    mix[:32, 0:8] = 0.16 * g + 0.04 * g @ g5
    mix[:32, 8:16] = 0.2 * g
    mix[32:, 0:8] = 0.2 * g5
    mix[32:, 8:16] = np.eye(8)
    final = [ec]
    for d in range(3):
        for i, part in enumerate((pos[d], neg[d])):
            c0 = 16 + 16 * d + 8 * i
            mix[:32, c0:c0 + 8] = -0.2 * DT * (rows32 * part) @ ec.T
            final.append(-0.2 * DT * ec * part)
    final = per_rank(np.concatenate(final))
    lane = np.arange(128)
    yi, ze = (lane // 16) % 4, lane % 16
    rows = []
    shifts = (-3, -2, -1, 1, 2, 3)

    def entry(table, sft):
        return np.array([table(i, i + sft) if 0 <= i + sft < 4 else 0.0 for i in yi])

    for sft in shifts:
        c = entry(lambda i, q: 0.5 * D4[i][q], sft)
        if sft == -1:
            c = c - 1.5 * (yi == 0)
        if sft == 1:
            c = c + 1.5 * (yi == 3)
        rows.append(c)
    for a in range(2):
        for sft in range(-3, 4):
            rows.append(entry(lambda i, q: RT[a][q], sft))
    rows += [np.array([PR[i][0] for i in yi]), np.array([PR[i][1] for i in yi])]
    rows += [np.array([WEIGHTS[i] for i in yi]), (yi == 0) * 1.0, (ze == 0) * 1.0, (ze == 15) * 1.0]
    for sft in shifts:
        rows.append(entry(lambda i, q: 0.5 * D4[i][q], sft))
    rows += [entry(lambda i, q: 0.5 * D4[i][q], 0), 3.0 * (yi == 0), 3.0 * (yi == 3)]
    while len(rows) < 40:
        rows.append(np.zeros(128))
    lanes = np.stack(rows).astype(np.float32)
    return dict(vec=vec, tab2=tab2, tab1=tab1, tab0=tab0, tabr=tabr, mix=mix.astype(np.float32),
                final=final, lanes=lanes, ec=per_rank(ec))


def call(kernel, name, idx, full, ranked, outs, scratch=()):
    in_specs = [pl.BlockSpec(a.shape, lambda i, s, n=a.ndim: (0,) * n) for a in full]
    in_specs += [pl.BlockSpec((1,) + a.shape[1:], lambda i, s, n=a.ndim: (s[0],) + (0,) * (n - 1))
                 for a in ranked]
    res = pl.pallas_call(
        kernel,
        name=name,
        out_shape=[jax.ShapeDtypeStruct(s, jnp.float32) for s in outs],
        grid_spec=pltpu.PrefetchScalarGridSpec(
            num_scalar_prefetch=1, grid=(1,), in_specs=in_specs,
            out_specs=[pl.BlockSpec(s, lambda i, t, n=len(s): (0,) * n) for s in outs],
            scratch_shapes=[pltpu.VMEM(s, jnp.float32) for s in scratch]),
        compiler_params=pltpu.CompilerParams(vmem_limit_bytes=56 << 20),
        interpret=INTERPRET,
    )(idx, *full, *ranked)
    return res


def combine(row, values):
    total = None
    for c, v in zip(row, values):
        if c != 0.0:
            total = c * v if total is None else total + c * v
    return total


def layer_yz(src, dst, vec):
    def over_y(y, _):
        q = [src[zi, y] for zi in range(4)]
        for zi in range(4):
            v = vec[0, 2:3] * combine(D4[zi], q)
            if zi == 0:
                v = v + vec[0, 5:6] * (q[0] - pltpu.roll(q[3], 1, 0))
            if zi == 3:
                v = v + vec[0, 6:7] * (pltpu.roll(q[0], 15, 0) - q[3])
            dst[zi, y] = v
        return 0
    lax.fori_loop(0, 8, over_y, 0)

    def over_z(zi, _):
        q = [src[zi, y] for y in range(8)]
        for y in range(8):
            e, yi = 4 * (y // 4), y % 4
            v = vec[0, 1:2] * combine(D4[yi], q[e:e + 4])
            if yi == 0:
                v = v + vec[0, 3:4] * (q[y] - q[(y + 7) % 8])
            if yi == 3:
                v = v + vec[0, 4:5] * (q[(y + 1) % 8] - q[y])
            dst[zi, y] = dst[zi, y] + v
        return 0
    lax.fori_loop(0, 4, over_z, 0)


def every_fourth(h, xi, y, zi):
    if INTERPRET:
        return h[xi, y][zi::4]
    return h[xi, y, pl.ds(zi, 16, stride=4), :]


def rim_kernel(idx, h, vec, tabr, up, down, q, t, r0, r3):
    pos = vec[0, 14:15] > 0.5
    for zi in range(4):
        def over_y(y, _):
            x = [every_fourth(h, xi, y, zi) for xi in range(4)]
            ql = jnp.where(pos, x[3], x[0])
            q[zi, y] = ql
            r0[zi, y] = x[0]
            r3[zi, y] = x[3]
            v = 0.8 * ql
            for j in range(4):
                v = v + vec[0, 15 + j:16 + j] * x[j]
            up[pl.ds(pl.multiple_of((zi * 8 + y) * 16, 16), 16)] = v
            return 0
        lax.fori_loop(0, 8, over_y, 0)
    layer_yz(q, t, vec)
    right = lax.broadcasted_iota(jnp.int32, (16, 128), 1) >= 64

    def pack(n, _):
        zi, y = n // 8, n % 8
        at = pl.ds(pl.multiple_of(n * 16, 16), 16)
        tl = pltpu.roll(t[zi, y] + up[at], 64, 1)
        ql = q[zi, y]
        up[at] = jnp.where(right, ql, tl)
        down[at] = jnp.where(right, tl, ql)
        return 0
    lax.fori_loop(0, 32, pack, 0)
    for zi in range(4):
        for out, layer in ((up, r3), (down, r0)):
            m = jnp.dot(layer[zi].reshape(128, 128), tabr[0], precision=HI,
                        preferred_element_type=jnp.float32)
            out[512 + 8 * zi:520 + 8 * zi] = m.T[0:8]


def local_update(src, dst, vec):
    def over_y(y, _):
        q = [src[c, y] for c in range(16)]
        for xi in range(4):
            for zi in range(4):
                own = q[xi * 4 + zi]
                v = 0.8 * own + vec[0, 0:1] * combine(D4[xi], [q[j * 4 + zi] for j in range(4)])
                v = v + vec[0, 2:3] * combine(D4[zi], q[xi * 4:xi * 4 + 4])
                if zi == 0:
                    v = v + vec[0, 5:6] * (own - pltpu.roll(q[xi * 4 + 3], 1, 0))
                if zi == 3:
                    v = v + vec[0, 6:7] * (pltpu.roll(q[xi * 4], 15, 0) - own)
                if xi == 0:
                    v = v + vec[0, 7:8] * own
                if xi == 3:
                    v = v + vec[0, 8:9] * own
                dst[xi * 4 + zi, y] = v
        return 0
    lax.fori_loop(0, 8, over_y, 0)

    def over_c(c, _):
        q = [src[c, y] for y in range(8)]
        for y in range(8):
            e, yi = 4 * (y // 4), y % 4
            v = vec[0, 1:2] * combine(D4[yi], q[e:e + 4])
            if yi == 0:
                v = v + vec[0, 3:4] * (q[y] - q[(y + 7) % 8])
            if yi == 3:
                v = v + vec[0, 4:5] * (q[(y + 1) % 8] - q[y])
            dst[c, y] = dst[c, y] + v
        return 0
    lax.fori_loop(0, 16, over_c, 0)


def local_kernel(idx, h, vec, tab0, tab1, twice, mom, first, once):
    for c in range(16):
        xi, zi = c // 4, c % 4

        def over_y(y, _):
            first[c, y] = every_fourth(h, xi, y, zi)
            return 0
        lax.fori_loop(0, 8, over_y, 0)
    local_update(first, once, vec)
    local_update(once, twice, vec)

    def moments(c, _):
        m = jnp.dot(first[c].reshape(128, 128), tab0[0], precision=HI,
                    preferred_element_type=jnp.float32)
        m = m + jnp.dot(once[c].reshape(128, 128), tab1[0], precision=HI,
                        preferred_element_type=jnp.float32)
        mom[c] = m.T[32:48]
        return 0
    lax.fori_loop(0, 16, moments, 0)


def z_before(q, lt):
    return jnp.where(lt[24:25] > 0.5, pltpu.roll(q, 113, 1), pltpu.roll(q, 1, 1))


def z_after(q, lt):
    return jnp.where(lt[25:26] > 0.5, pltpu.roll(q, 15, 1), pltpu.roll(q, 127, 1))


SHIFTS = (-3, -2, -1, 1, 2, 3)


def central_y(q, lt):
    total = None
    for n, s in enumerate(SHIFTS):
        term = lt[n:n + 1] * pltpu.roll(q, (-16 * s) % 128, 1)
        total = term if total is None else total + term
    return total


def one_sided(load, low, high, c, lt):
    xi, zi = c // 4, c % 4
    q = load(c)
    cx = combine([0.5 * v for v in D4[xi]], [load(j * 4 + zi) for j in range(4)])
    px = cx + 3.0 * (q - low(zi)) if xi == 0 else cx
    mx = cx + 3.0 * (high(zi) - q) if xi == 3 else cx
    cy = lt[32:33] * q
    for n, s in enumerate(SHIFTS):
        r = pltpu.roll(q, (-16 * s) % 128, 1)
        cy = cy + lt[26 + n:27 + n] * r
        if s == -1:
            py = lt[33:34] * (q - r)
        if s == 1:
            my = lt[34:35] * (r - q)
    cz = combine([0.5 * v for v in D4[zi]], [load(xi * 4 + j) for j in range(4)])
    pz = cz + 3.0 * (q - z_before(load(xi * 4 + 3), lt)) if zi == 0 else cz
    mz = cz + 3.0 * (z_after(load(xi * 4), lt) - q) if zi == 3 else cz
    return [px, mx, cy + py, cy + my, pz, mz]


CENTRAL = [[0.0 if i == j else 0.5 * D4[i][j] for j in range(4)] for i in range(4)]


def moment_kernel(idx, up, down, twice, moma, mix, lt, vec, tab2, tab1, pay, t2,
                  delta, yz, extra, mom, full):
    right = lax.broadcasted_iota(jnp.int32, (16, 128), 1) >= 64
    pos = vec[0, 14:15]

    def unpack(n, _):
        at = pl.ds(pl.multiple_of(n * 16, 16), 16)
        u, d = up[at], down[at]
        zi, y = n // 8, n % 8
        delta[zi, y] = vec[0, 9:10] * jnp.where(right, u, d)
        extra[zi, y] = vec[0, 9:10] * pltpu.roll(jnp.where(right, d, u), 64, 1)
        return 0
    lax.fori_loop(0, 32, unpack, 0)
    layer_yz(delta, yz, vec)
    for xi in range(4):
        def over_n(n, _):
            zi, y = n // 8, n % 8
            v = twice[xi * 4 + zi, y] + vec[0, 10 + xi:11 + xi] * delta[zi, y]
            if xi in (0, 3):
                w = pos if xi == 0 else 1.0 - pos
                v = v + w * (yz[zi, y] + extra[zi, y])
            t2[xi * 4 + zi, y] = v
            return 0
        lax.fori_loop(0, 32, over_n, 0)

        def over_z(zi, _):
            c = xi * 4 + zi
            m = jnp.dot(t2[c].reshape(128, 128), tab2[0], precision=HI,
                        preferred_element_type=jnp.float32)
            if xi in (0, 3):
                w = pos if xi == 0 else 1.0 - pos
                m = m + jnp.dot(delta[zi].reshape(128, 128) * w, tab1[0], precision=HI,
                                preferred_element_type=jnp.float32)
            m = m.T
            mom[c, 0:32] = m[0:32]
            mom[c, 32:48] = m[32:48] + moma[c]
            return 0
        lax.fori_loop(0, 4, over_z, 0)

    def load0(c):
        return mom[c, 32:40]

    for c in range(16):
        six = one_sided(load0, lambda zi: up[512 + 8 * zi:520 + 8 * zi],
                        lambda zi: down[512 + 8 * zi:520 + 8 * zi], c, lt)
        stack = jnp.concatenate([mom[c, 32:40], mom[c, 40:48]] + six, axis=0)
        add = jnp.dot(mix[...], stack, precision=HI, preferred_element_type=jnp.float32)
        full[c, 0:32] = mom[c, 0:32] + add[0:32]
        full[c, 32:40] = add[32:40]
    for c in range(16):
        xi, zi = c // 4, c % 4
        r = combine(CENTRAL[xi], [full[j * 4 + zi, 8:16] for j in range(4)])
        r = r + central_y(full[c, 16:24], lt)
        r = r + combine(CENTRAL[zi], [full[xi * 4 + j, 24:32] for j in range(4)])
        if zi == 0:
            r = r - 1.5 * z_before(full[xi * 4 + 3, 24:32], lt)
        if zi == 3:
            r = r + 1.5 * z_after(full[xi * 4, 24:32], lt)
        pay[5 * c:5 * c + 5] = -r[0:5]
        pay[120 + 5 * c:125 + 5 * c] = full[c, 0:5]
        pay[200 + 5 * c:205 + 5 * c] = mom[c, 32:37]
        pay[280 + 5 * c:285 + 5 * c] = full[c, 32:37]
    for zi in range(4):
        pay[80 + 5 * zi:85 + 5 * zi] = full[zi, 8:13]
        pay[100 + 5 * zi:105 + 5 * zi] = full[12 + zi, 8:13]
        pay[360 + 5 * zi:365 + 5 * zi] = up[512 + 8 * zi:517 + 8 * zi]
        pay[380 + 5 * zi:385 + 5 * zi] = down[512 + 8 * zi:517 + 8 * zi]


def residual_kernel(idx, got, force, out, peers):
    t = got[0, 0:120] + got[1, 0:120] + got[2, 0:120] + got[3, 0:120]
    v = t[0:80] + force[...]
    for n in range(peers):
        out[n, 0:80] = v
        out[n, 80:120] = t[80:120]


def feq_kernel(idx, got, t2, lt, final, h2, low, s0, lo, hi):
    def total(a, n):
        return got[0, a:a + n] + got[1, a:a + n] + got[2, a:a + n] + got[3, a:a + n]

    s0[...] = jnp.zeros_like(s0)
    lo[...] = jnp.zeros_like(lo)
    hi[...] = jnp.zeros_like(hi)
    for c in range(16):
        s0[c, 0:5] = total(200 + 5 * c, 5)
    for zi in range(4):
        lo[zi, 0:5] = total(360 + 5 * zi, 5)
        hi[zi, 0:5] = total(380 + 5 * zi, 5)
    low[...] = total(120, 80)
    pad = jnp.zeros((3, 128), jnp.float32)
    for c in range(16):
        z = jnp.concatenate([0.2 * total(280 + 5 * c, 5), pad], axis=0) + 0.16 * s0[c]
        six = one_sided(lambda k: s0[k], lambda zi: lo[zi], lambda zi: hi[zi], c, lt)
        stack = jnp.concatenate([z] + six, axis=0)
        add = lax.dot_general(stack, final[0], (((0,), (0,)), ((), ())), precision=HI,
                              preferred_element_type=jnp.float32)
        h2[c] = t2[c] + add.reshape(8, 16, 128)


def apply_operator(src, dst, lt):
    def along_x(zi, _):
        u = [src[16 + j * 4 + zi] for j in range(4)]
        p = [src[j * 4 + zi] + src[64 + j * 4 + zi] for j in range(4)]
        for xi in range(4):
            du = combine(CENTRAL[xi], u)
            dp = combine(CENTRAL[xi], p)
            if xi == 0:
                du = du - 1.5 * pltpu.roll(u[3], 1, 0)
                dp = dp - 1.5 * pltpu.roll(p[3], 1, 0)
            if xi == 3:
                du = du + 1.5 * pltpu.roll(u[0], 23, 0)
                dp = dp + 1.5 * pltpu.roll(p[0], 23, 0)
            dst[xi * 4 + zi] = du
            dst[16 + xi * 4 + zi] = 2.0 * u[xi] + dp
        return 0
    lax.fori_loop(0, 4, along_x, 0)

    def along_z(xi, _):
        u = [src[48 + xi * 4 + j] for j in range(4)]
        p = [src[xi * 4 + j] + src[64 + xi * 4 + j] for j in range(4)]
        for zi in range(4):
            du = combine(CENTRAL[zi], u)
            dp = combine(CENTRAL[zi], p)
            if zi == 0:
                du = du - 1.5 * z_before(u[3], lt)
                dp = dp - 1.5 * z_before(p[3], lt)
            if zi == 3:
                du = du + 1.5 * z_after(u[0], lt)
                dp = dp + 1.5 * z_after(p[0], lt)
            dst[xi * 4 + zi] = dst[xi * 4 + zi] + du
            dst[48 + xi * 4 + zi] = 2.0 * u[zi] + dp
        return 0
    lax.fori_loop(0, 4, along_z, 0)

    def along_y(c, _):
        rho, u, t = src[c], src[32 + c], src[64 + c]
        div = dst[c] + central_y(u, lt)
        dst[32 + c] = 2.0 * u + central_y(rho + t, lt)
        dst[c] = 2.0 * rho + div
        dst[64 + c] = 2.0 * t + div
        return 0
    lax.fori_loop(0, 16, along_y, 0)


def two_level(r, pe, co, lt):
    def over_f(f, _):
        tz = [[None, None] for _ in range(4)]
        for xi in range(4):
            q = [r[f * 16 + xi * 4 + zi] for zi in range(4)]
            for za in range(2):
                tz[xi][za] = combine(RT[za], q)
        for za in range(2):
            py = []
            for xa in range(2):
                t = combine(RT[xa], [tz[xi][za] for xi in range(4)])
                e0, e1 = lt[9:10] * t, lt[16:17] * t
                for s in SHIFTS:
                    rolled = pltpu.roll(t, (-16 * s) % 128, 1)
                    e0 = e0 + lt[9 + s:10 + s] * rolled
                    e1 = e1 + lt[16 + s:17 + s] * rolled
                co[f * 8 + xa * 4 + za * 2] = e0
                co[f * 8 + xa * 4 + za * 2 + 1] = e1
                py.append(lt[20:21] * e0 + lt[21:22] * e1)
            for xi in range(4):
                v = combine(PR[xi], py)
                for zi in range(4):
                    if PR[zi][za] == 0.0:
                        continue
                    at = f * 16 + xi * 4 + zi
                    if za == 0 or PR[zi][0] == 0.0:
                        pe[at] = PR[zi][za] * v
                    else:
                        pe[at] = pe[at] + PR[zi][za] * v
        return 0
    lax.fori_loop(0, 5, over_f, 0)


def coarse_products(co, lt):
    def at(f, xa, za, ya):
        return co[f * 8 + xa * 4 + za * 2 + ya]

    def own(q):
        return q[8:16]

    def dx(q, xa, za, ya):
        if xa == 0:
            v = q(1, za, ya)
            return 0.25 * (own(v) - own(pltpu.roll(v, 1, 0)))
        v = q(0, za, ya)
        return 0.25 * (own(pltpu.roll(v, 23, 0)) - own(v))

    def dz(q, xa, za, ya):
        v = own(q(xa, 1 - za, ya))
        if za == 0:
            return 0.25 * (v - z_before(v, lt))
        return 0.25 * (z_after(v, lt) - v)

    def dy(q, xa, za, ya):
        v = own(q(xa, za, 1 - ya))
        w = pltpu.roll(v, 64, 1)
        return 0.25 * (v - w) if ya == 0 else 0.25 * (w - v)

    up = jnp.zeros((8, 128), jnp.float32)
    low = jnp.zeros((8, 128), jnp.float32)
    for xa in range(2):
        for za in range(2):
            for ya in range(2):
                def field(f):
                    return lambda a, b, c: at(f, a, b, c)

                def pressure(a, b, c):
                    return at(0, a, b, c) + at(4, a, b, c)
                e = [own(at(f, xa, za, ya)) for f in range(5)]
                div = (dx(field(1), xa, za, ya) + dy(field(2), xa, za, ya)
                       + dz(field(3), xa, za, ya))
                g = [2.0 * e[0] + div, 2.0 * e[1] + dx(pressure, xa, za, ya),
                     2.0 * e[2] + dy(pressure, xa, za, ya),
                     2.0 * e[3] + dz(pressure, xa, za, ya), 2.0 * e[4] + div]
                for f in range(5):
                    up = up + e[f] * g[f]
                    low = low + g[f] * g[f]
    return up * lt[23:24], low * lt[23:24]


def fine_products(r, m, ar, am, lt):
    total = [jnp.zeros((8, 128), jnp.float32) for _ in range(6)]
    for xi in range(4):
        for zi in range(4):
            def over_f(f, acc):
                k = f * 16 + xi * 4 + zi
                a, b, c, d = r[k, 8:16], m[k, 8:16], ar[k, 8:16], am[k, 8:16]
                return (acc[0] + a * c, acc[1] + a * d + b * c, acc[2] + b * d,
                        acc[3] + c * c, acc[4] + c * d, acc[5] + d * d)
            zero = jnp.zeros((8, 128), jnp.float32)
            acc = lax.fori_loop(0, 5, over_f, (zero,) * 6, unroll=True)
            w = WEIGHTS[xi] * WEIGHTS[zi]
            total = [t + w * a for t, a in zip(total, acc)]
    return [t * lt[22:23] for t in total]


def pass_words(r, m, ar, am, pe, co, gram, lt, peers):
    two_level(r, pe, co, lt)
    apply_operator(pe, m, lt)
    apply_operator(r, ar, lt)
    apply_operator(m, am, lt)
    products = list(coarse_products(co, lt)) + fine_products(r, m, ar, am, lt)
    rows = jnp.concatenate([jnp.sum(p, axis=0, keepdims=True) for p in products], axis=0)
    for n in range(peers):
        gram[n] = rows


def first_pass_kernel(idx, lower, mine, upper, lt, r, m, ar, am, pe, gram, co, lox, hix):
    for f in range(5):
        for zi in range(4):
            for n, src in enumerate((lower, mine, upper)):
                lox[f * 4 + zi, 8 * n:8 * n + 8] = src[pl.ds(80 + 5 * zi + f, 8, stride=120), :]
                hix[f * 4 + zi, 8 * n:8 * n + 8] = src[pl.ds(100 + 5 * zi + f, 8, stride=120), :]
        for c in range(16):
            xi, zi = c // 4, c % 4
            for n, src in enumerate((lower, mine, upper)):
                r[f * 16 + c, 8 * n:8 * n + 8] = src[pl.ds(5 * c + f, 8, stride=120), :]
            if xi == 0:
                r[f * 16 + c] = r[f * 16 + c] + 1.5 * pltpu.roll(hix[f * 4 + zi], 1, 0)
            if xi == 3:
                r[f * 16 + c] = r[f * 16 + c] - 1.5 * pltpu.roll(lox[f * 4 + zi], 23, 0)
    pass_words(r, m, ar, am, pe, co, gram, lt, gram.shape[0])


def step_sizes(sums, peers):
    s = sums[0]
    for n in range(1, peers):
        s = s + sums[n]
    s = jnp.broadcast_to(jnp.sum(s, axis=1, keepdims=True), (8, 128))
    a1 = s[0:1] / (s[1:2] + EPS)
    up = s[2:3] - a1 * s[3:4] + a1 * a1 * s[4:5]
    low = s[5:6] - 2.0 * a1 * s[6:7] + a1 * a1 * s[7:8]
    return a1, up / (low + EPS)


def next_pass_kernel(first, idx, sums, r, m, ar, am, pe, *rest):
    if first:
        lt, r2, m2, ar2, am2, pe2, acc2, gram, co = rest
    else:
        acc, lt, r2, m2, ar2, am2, pe2, acc2, gram, co = rest
    a1, a2 = step_sizes(sums, gram.shape[0])

    def over_k(k, _):
        q = r[k] - a1 * m[k]
        v = a1 * pe[k, 8:16] + a2 * q[8:16]
        acc2[k] = v if first else acc[k] + v
        r2[k] = q - a2 * (ar[k] - a1 * am[k])
        return 0
    lax.fori_loop(0, 80, over_k, 0, unroll=4)
    pass_words(r2, m2, ar2, am2, pe2, co, gram, lt, gram.shape[0])


def last_kernel(idx, sums, r, m, pe, acc, low, h2, ec, out, fields, change):
    a1, a2 = step_sizes(sums, sums.shape[0])

    def over_k(k, _):
        q = r[k, 8:16] - a1 * m[k, 8:16]
        change[pl.ds(pl.multiple_of(k * 8, 8), 8)] = acc[k] + a1 * pe[k, 8:16] + a2 * q
        return 0
    lax.fori_loop(0, 80, over_k, 0, unroll=4)
    z = idx[1]
    zero = jnp.zeros((3, 128), jnp.float32)
    for c in range(16):
        xi, zi = c // 4, c % 4
        d = jnp.concatenate([change[pl.ds((f * 16 + c) * 8 + z, 1)] for f in range(5)] + [zero], axis=0)
        new = low[5 * c:5 * c + 5] + d[0:5]
        for f in range(5):
            fields[16 * f + c:16 * f + c + 1] = new[f:f + 1]
        add = lax.dot_general(d, ec[0], (((0,), (0,)), ((), ())), precision=HI,
                              preferred_element_type=jnp.float32)
        v = h2[c] + add.reshape(8, 16, 128)
        for y in range(8):
            out[xi, y, pl.ds(zi, 16, stride=4), :] = v[y]


def on_device(distribution, forcing):
    import functools
    tables = {k: jnp.asarray(v) for k, v in constant_tables().items()}
    spaces = lax.axis_size("space")
    blocks = spaces // 8
    idx = jnp.stack([lax.axis_index("vel"), lax.axis_index("space") % 8]).astype(jnp.int32)
    vec, lt = tables["vec"], tables["lanes"]
    wide = (16, 8, 16, 128)
    layer = (4, 8, 16, 128)

    def shifted(x, by):
        return lax.ppermute(x, "space", [(i, (i + by) % spaces) for i in range(spaces)])

    up, down = call(rim_kernel, "rims", idx, [distribution], [vec, tables["tabr"]],
                    [(544, 128)] * 2, [layer] * 4)
    up, down = shifted(up, 1), shifted(down, -1)
    twice, moma = call(local_kernel, "local", idx, [distribution],
                       [vec, tables["tab0"], tables["tab1"]],
                       [wide, (16, 16, 128)], [wide, wide])
    force = jnp.pad(forcing, ((1, 1), (0, 0), (0, 0), (0, 0)))
    force = force.reshape(5, 4, 8, 16, 4).transpose(1, 4, 0, 2, 3).reshape(80, 128)
    pay, t2 = call(moment_kernel, "moments", idx, [up, down, twice, moma, tables["mix"], lt],
                   [vec, tables["tab2"], tables["tab1"]], [(400, 128), wide],
                   [layer, layer, layer, (16, 48, 128), (16, 40, 128)])
    got = lax.all_gather(pay, "vel")
    (res,) = call(lambda i, g, fo, o: residual_kernel(i, g, fo, o, 8), "residual", idx,
                  [got, force], [], [(8, 120, 128)])
    near = [[a * 8 + b for b in range(8)] for a in range(blocks)]
    far = [[a * 8 + b for a in range(blocks)] for b in range(8)]
    mine = lax.all_to_all(res, "space", 0, 0, axis_index_groups=near, tiled=True).reshape(960, 128)
    lower, upper = shifted(mine, 8), shifted(mine, -8)
    h2, low = call(feq_kernel, "feq", idx, [got, t2, lt], [tables["final"]],
                   [wide, (80, 128)], [(16, 8, 128), (4, 8, 128), (4, 8, 128)])

    def summed(gram):
        return lax.all_to_all(gram, "space", 0, 0, axis_index_groups=far, tiled=True)

    win, own, part = (80, 24, 128), (80, 8, 128), (blocks, 8, 128)
    co = (40, 24, 128)
    r, m, ar, am, pe, gram = call(first_pass_kernel, "pass1", idx, [lower, mine, upper, lt], [],
                                  [win] * 5 + [part], [co, (20, 24, 128), (20, 24, 128)])
    r, m, ar, am, pe, acc, gram = call(functools.partial(next_pass_kernel, True), "pass2", idx,
                                       [summed(gram), r, m, ar, am, pe, lt], [],
                                       [win] * 5 + [own, part], [co])
    r, m, ar, am, pe, acc, gram = call(functools.partial(next_pass_kernel, False), "pass3", idx,
                                       [summed(gram), r, m, ar, am, pe, acc, lt], [],
                                       [win] * 5 + [own, part], [co])
    out, fields = call(last_kernel, "last", idx, [summed(gram), r, m, pe, acc, low, h2],
                       [tables["ec"]], [(4, 8, 64, 128), (80, 128)], [(640, 128)])
    fields = fields.reshape(5, 4, 4, 8, 16).transpose(0, 1, 3, 4, 2).reshape(5, 4, 8, 64)
    return out, fields


def solution(mesh):
    return jax.shard_map(
        on_device,
        mesh=mesh,
        in_specs=(P("space", None, None, "vel"), P(None, "space", None, None)),
        out_specs=(P("space", None, None, "vel"), P(None, "space", None, None)),
        check_vma=False,
    )
```

```python
import math

import jax
import jax.numpy as jnp
import numpy as np
from jax import lax
from jax.experimental import pallas as pl
from jax.experimental.pallas import tpu as pltpu
from jax.sharding import PartitionSpec as P

INTERPRET = False
DT = 0.02
RF = 0.4472135954999579
POINTS = [-1.0, -RF, RF, 1.0]
WEIGHTS = [1.0 / 6.0, 5.0 / 6.0, 5.0 / 6.0, 1.0 / 6.0]
EPS = 1e-6
HI = lax.Precision.HIGHEST


def lagrange_table(points):
    n = len(points)
    bary = []
    for i in range(n):
        product = 1.0
        for j in range(n):
            if j != i:
                product *= points[i] - points[j]
        bary.append(1.0 / product)
    rows = [[0.0] * n for _ in range(n)]
    for i in range(n):
        for j in range(n):
            if j != i:
                rows[i][j] = bary[j] / bary[i] / (points[i] - points[j])
        rows[i][i] = -sum(rows[i])
    return rows


D4 = lagrange_table(POINTS)
for _i in (1, 2):
    D4[_i][_i] = 0.0
PR = [[(1.0 - x) / 2.0, (1.0 + x) / 2.0] for x in POINTS]
RT = [[WEIGHTS[i] * PR[i][a] for i in range(4)] for a in range(2)]


def constant_tables():
    k = np.arange(512)
    b, j = k // 128, k % 128
    s = j // 64
    m = ((b * 64 + j % 64) * 5179 + 7) % 16384
    xi = np.stack([16 * s + m // 1024, (m // 32) % 32, m % 32]).astype(np.float64)
    xi = -4.0 + 0.25 * (xi + 0.5)
    sq = (xi * xi).sum(0)
    e = math.pi ** (-1.5) * np.exp(-sq)
    x, y, z = xi
    phi = np.stack(
        [np.ones(512), x, y, z, 2 * sq / 3 - 1, 2 * (x * x - sq / 3), 2 * (y * y - sq / 3),
         2 * x * y, 2 * x * z, 2 * y * z, x * (sq - 2.5), y * (sq - 2.5), z * (sq - 2.5)]
    )
    p = phi[0] + phi[4]
    zero = np.zeros(512)

    def eight(rows):
        return np.stack(list(rows) + [zero] * (8 - len(rows)))

    low = eight(phi[:5])
    along_x = eight([phi[1], p + phi[5], phi[7], phi[8], phi[1] + phi[10]])
    along_y = eight([phi[2], phi[7], p + phi[6], phi[9], phi[2] + phi[11]])
    along_z = eight([phi[3], phi[8], phi[9], p - phi[5] - phi[6], phi[3] + phi[12]])
    rows32 = np.concatenate([low, along_x, along_y, along_z])
    ec = eight([e, 2 * x * e, 2 * y * e, 2 * z * e, e * (sq - 1.5)])
    pos, neg = np.maximum(xi, 0.0), np.minimum(xi, 0.0)

    def per_rank(rows):
        return np.stack([rows[:, r * 128:(r + 1) * 128] for r in range(4)]).astype(np.float32)

    ispos = (x > 0).astype(np.float64)
    ax = np.abs(x)
    d4 = np.array(D4)
    vec = [-DT * 0.5 * x, -DT * 0.5 * y, -DT * 0.5 * z,
           -3 * DT * pos[1], -3 * DT * neg[1], -3 * DT * pos[2], -3 * DT * neg[2],
           -3 * DT * pos[0], 3 * DT * neg[0], 3 * DT * ax]
    for i in range(4):
        kap = -DT * 0.5 * x * np.where(ispos > 0, d4[i][0], d4[i][3])
        if i == 0:
            kap = kap + ispos * (0.8 - 3 * DT * ax)
        if i == 3:
            kap = kap + (1 - ispos) * (0.8 - 3 * DT * ax)
        vec.append(kap)
    vec.append(ispos)
    for jj in range(4):
        vec.append(-DT * 0.5 * x * np.where(ispos > 0, d4[3][jj], d4[0][jj]))
    while len(vec) < 24:
        vec.append(zero)
    vec = per_rank(np.stack(vec))

    def moment_columns(start, rows):
        out = np.zeros((4, 128, 128))
        for r in range(4):
            out[r, :, start:start + len(rows)] = rows[:, r * 128:(r + 1) * 128].T
        return out.astype(np.float32)

    tab2 = moment_columns(0, rows32)
    tab1 = moment_columns(40, low)
    tab0 = moment_columns(32, low)
    tabr = moment_columns(0, low)
    g = rows32 @ ec.T
    g5 = g[:8]
    mix = np.zeros((40, 64))
    mix[:32, 0:8] = 0.16 * g + 0.04 * g @ g5
    mix[:32, 8:16] = 0.2 * g
    mix[32:, 0:8] = 0.2 * g5
    mix[32:, 8:16] = np.eye(8)
    final = [ec]
    for d in range(3):
        for i, part in enumerate((pos[d], neg[d])):
            c0 = 16 + 16 * d + 8 * i
            mix[:32, c0:c0 + 8] = -0.2 * DT * (rows32 * part) @ ec.T
            final.append(-0.2 * DT * ec * part)
    final = per_rank(np.concatenate(final))
    lane = np.arange(128)
    yi, ze = (lane // 16) % 4, lane % 16
    rows = []
    shifts = (-3, -2, -1, 1, 2, 3)

    def entry(table, sft):
        return np.array([table(i, i + sft) if 0 <= i + sft < 4 else 0.0 for i in yi])

    for sft in shifts:
        c = entry(lambda i, q: 0.5 * D4[i][q], sft)
        if sft == -1:
            c = c - 1.5 * (yi == 0)
        if sft == 1:
            c = c + 1.5 * (yi == 3)
        rows.append(c)
    for a in range(2):
        for sft in range(-3, 4):
            rows.append(entry(lambda i, q: RT[a][q], sft))
    rows += [np.array([PR[i][0] for i in yi]), np.array([PR[i][1] for i in yi])]
    rows += [np.array([WEIGHTS[i] for i in yi]), (yi == 0) * 1.0, (ze == 0) * 1.0, (ze == 15) * 1.0]
    for sft in shifts:
        rows.append(entry(lambda i, q: 0.5 * D4[i][q], sft))
    rows += [entry(lambda i, q: 0.5 * D4[i][q], 0), 3.0 * (yi == 0), 3.0 * (yi == 3)]
    while len(rows) < 40:
        rows.append(np.zeros(128))
    lanes = np.stack(rows).astype(np.float32)
    return dict(vec=vec, tab2=tab2, tab1=tab1, tab0=tab0, tabr=tabr, mix=mix.astype(np.float32),
                final=final, lanes=lanes, ec=per_rank(ec))


def call(kernel, name, idx, full, ranked, outs, scratch=(), limit=24):
    n = len(full)

    def body(idx, *refs):
        rank = [r.at[pl.ds(idx[0], 1)] for r in refs[n:n + len(ranked)]]
        kernel(idx, *refs[:n], *rank, *refs[n + len(ranked):])

    vmem = pl.BlockSpec(memory_space=pltpu.VMEM)
    return pl.pallas_call(
        body,
        name=name,
        out_shape=[jax.ShapeDtypeStruct(s, jnp.float32) for s in outs],
        in_specs=[pl.BlockSpec(memory_space=pltpu.SMEM)] + [vmem] * (n + len(ranked)),
        out_specs=[vmem] * len(outs),
        scratch_shapes=[pltpu.VMEM(s, jnp.float32) for s in scratch],
        compiler_params=pltpu.CompilerParams(vmem_limit_bytes=limit << 20),
        interpret=INTERPRET,
    )(idx, *full, *ranked)


def exact_dot(a, b):
    return jnp.dot(a, b, precision=HI, preferred_element_type=jnp.float32)


def combine(row, values):
    total = None
    for c, v in zip(row, values):
        if c != 0.0:
            total = c * v if total is None else total + c * v
    return total


def layer_yz(src, dst, vec):
    def over_y(y, _):
        q = [src[zi, y] for zi in range(4)]
        for zi in range(4):
            v = vec[0, 2:3] * combine(D4[zi], q)
            if zi == 0:
                v = v + vec[0, 5:6] * (q[0] - pltpu.roll(q[3], 1, 0))
            if zi == 3:
                v = v + vec[0, 6:7] * (pltpu.roll(q[0], 15, 0) - q[3])
            dst[zi, y] = v
        return 0
    lax.fori_loop(0, 8, over_y, 0)

    def over_z(zi, _):
        q = [src[zi, y] for y in range(8)]
        for y in range(8):
            e, yi = 4 * (y // 4), y % 4
            v = vec[0, 1:2] * combine(D4[yi], q[e:e + 4])
            if yi == 0:
                v = v + vec[0, 3:4] * (q[y] - q[(y + 7) % 8])
            if yi == 3:
                v = v + vec[0, 4:5] * (q[(y + 1) % 8] - q[y])
            dst[zi, y] = dst[zi, y] + v
        return 0
    lax.fori_loop(0, 4, over_z, 0)


def every_fourth(h, xi, y, zi):
    if INTERPRET:
        return h[xi, y][zi::4]
    return h[xi, y, pl.ds(zi, 16, stride=4), :]


def rim_kernel(idx, h, vec, tabr, up, down, q, t, ends, m):
    pos = vec[0, 14:15] > 0.5
    for zi in range(4):
        def over_y(y, _):
            x = [every_fourth(h, xi, y, zi) for xi in range(4)]
            ql = jnp.where(pos, x[3], x[0])
            q[zi, y] = ql
            ends[zi, y] = x[0]
            ends[4 + zi, y] = x[3]
            v = 0.8 * ql
            for j in range(4):
                v = v + vec[0, 15 + j:16 + j] * x[j]
            up[pl.ds(pl.multiple_of((zi * 8 + y) * 16, 16), 16)] = v
            return 0
        lax.fori_loop(0, 8, over_y, 0)
    layer_yz(q, t, vec)
    right = lax.broadcasted_iota(jnp.int32, (16, 128), 1) >= 64

    def pack(n, _):
        zi, y = n // 8, n % 8
        at = pl.ds(pl.multiple_of(n * 16, 16), 16)
        tl = pltpu.roll(t[zi, y] + up[at], 64, 1)
        ql = q[zi, y]
        up[at] = jnp.where(right, ql, tl)
        down[at] = jnp.where(right, tl, ql)
        return 0
    lax.fori_loop(0, 32, pack, 0)
    m[...] = exact_dot(ends[...].reshape(1024, 128), tabr[0])
    for n in range(8):
        zi, out = n % 4, (down, up)[n // 4]
        out[512 + 8 * zi:520 + 8 * zi] = m[128 * n:128 * n + 128].T[0:8]


def local_update(src, dst, vec):
    def over_y(y, _):
        q = [src[c, y] for c in range(16)]
        for xi in range(4):
            for zi in range(4):
                own = q[xi * 4 + zi]
                v = 0.8 * own + vec[0, 0:1] * combine(D4[xi], [q[j * 4 + zi] for j in range(4)])
                v = v + vec[0, 2:3] * combine(D4[zi], q[xi * 4:xi * 4 + 4])
                if zi == 0:
                    v = v + vec[0, 5:6] * (own - pltpu.roll(q[xi * 4 + 3], 1, 0))
                if zi == 3:
                    v = v + vec[0, 6:7] * (pltpu.roll(q[xi * 4], 15, 0) - own)
                if xi == 0:
                    v = v + vec[0, 7:8] * own
                if xi == 3:
                    v = v + vec[0, 8:9] * own
                dst[xi * 4 + zi, y] = v
        return 0
    lax.fori_loop(0, 8, over_y, 0)

    def over_c(c, _):
        q = [src[c, y] for y in range(8)]
        for y in range(8):
            e, yi = 4 * (y // 4), y % 4
            v = vec[0, 1:2] * combine(D4[yi], q[e:e + 4])
            if yi == 0:
                v = v + vec[0, 3:4] * (q[y] - q[(y + 7) % 8])
            if yi == 3:
                v = v + vec[0, 4:5] * (q[(y + 1) % 8] - q[y])
            dst[c, y] = dst[c, y] + v
        return 0
    lax.fori_loop(0, 16, over_c, 0)


def local_kernel(idx, h, vec, tab0, tab1, twice, mom, first, once, m):
    for c in range(16):
        xi, zi = c // 4, c % 4

        def over_y(y, _):
            first[c, y] = every_fourth(h, xi, y, zi)
            return 0
        lax.fori_loop(0, 8, over_y, 0)
    local_update(first, once, vec)
    local_update(once, twice, vec)

    m[...] = exact_dot(first[...].reshape(2048, 128), tab0[0])
    m[...] = m[...] + exact_dot(once[...].reshape(2048, 128), tab1[0])
    for c in range(16):
        mom[c] = m[128 * c:128 * c + 128].T[32:48]


def z_before(q, lt):
    return jnp.where(lt[24:25] > 0.5, pltpu.roll(q, 113, 1), pltpu.roll(q, 1, 1))


def z_after(q, lt):
    return jnp.where(lt[25:26] > 0.5, pltpu.roll(q, 15, 1), pltpu.roll(q, 127, 1))


SHIFTS = (-3, -2, -1, 1, 2, 3)


def central_y(q, lt):
    total = None
    for n, s in enumerate(SHIFTS):
        term = lt[n:n + 1] * pltpu.roll(q, (-16 * s) % 128, 1)
        total = term if total is None else total + term
    return total


def one_sided(load, low, high, c, lt):
    xi, zi = c // 4, c % 4
    q = load(c)
    cx = combine([0.5 * v for v in D4[xi]], [load(j * 4 + zi) for j in range(4)])
    px = cx + 3.0 * (q - low(zi)) if xi == 0 else cx
    mx = cx + 3.0 * (high(zi) - q) if xi == 3 else cx
    cy = lt[32:33] * q
    for n, s in enumerate(SHIFTS):
        r = pltpu.roll(q, (-16 * s) % 128, 1)
        cy = cy + lt[26 + n:27 + n] * r
        if s == -1:
            py = lt[33:34] * (q - r)
        if s == 1:
            my = lt[34:35] * (r - q)
    cz = combine([0.5 * v for v in D4[zi]], [load(xi * 4 + j) for j in range(4)])
    pz = cz + 3.0 * (q - z_before(load(xi * 4 + 3), lt)) if zi == 0 else cz
    mz = cz + 3.0 * (z_after(load(xi * 4), lt) - q) if zi == 3 else cz
    return [px, mx, cy + py, cy + my, pz, mz]


CENTRAL = [[0.0 if i == j else 0.5 * D4[i][j] for j in range(4)] for i in range(4)]


def moment_kernel(idx, up, down, twice, moma, mix, lt, vec, tab2, tab1, pay, t2,
                  delta, yz, extra, mom, full, m, stack):
    right = lax.broadcasted_iota(jnp.int32, (16, 128), 1) >= 64
    pos = vec[0, 14:15]

    def unpack(n, _):
        at = pl.ds(pl.multiple_of(n * 16, 16), 16)
        u, d = up[at], down[at]
        zi, y = n // 8, n % 8
        delta[zi, y] = vec[0, 9:10] * jnp.where(right, u, d)
        extra[zi, y] = vec[0, 9:10] * pltpu.roll(jnp.where(right, d, u), 64, 1)
        return 0
    lax.fori_loop(0, 32, unpack, 0)
    layer_yz(delta, yz, vec)
    for xi in range(4):
        def over_n(n, _):
            zi, y = n // 8, n % 8
            v = twice[xi * 4 + zi, y] + vec[0, 10 + xi:11 + xi] * delta[zi, y]
            if xi in (0, 3):
                w = pos if xi == 0 else 1.0 - pos
                v = v + w * (yz[zi, y] + extra[zi, y])
            t2[xi * 4 + zi, y] = v
            return 0
        lax.fori_loop(0, 32, over_n, 0)

    m[...] = exact_dot(t2[...].reshape(2048, 128), tab2[0])
    d = delta[...].reshape(512, 128)
    m[0:512] = m[0:512] + exact_dot(d * pos, tab1[0])
    m[1536:2048] = m[1536:2048] + exact_dot(d * (1.0 - pos), tab1[0])
    for c in range(16):
        t = m[128 * c:128 * c + 128].T
        mom[c, 0:32] = t[0:32]
        mom[c, 32:48] = t[32:48] + moma[c]

    def load0(c):
        return mom[c, 32:40]

    for c in range(16):
        six = one_sided(load0, lambda zi: up[512 + 8 * zi:520 + 8 * zi],
                        lambda zi: down[512 + 8 * zi:520 + 8 * zi], c, lt)
        at = slice(128 * c, 128 * c + 128)
        stack[0:16, at] = mom[c, 32:48]
        for n in range(6):
            stack[16 + 8 * n:24 + 8 * n, at] = six[n]
    add = exact_dot(mix[...], stack[...])
    for c in range(16):
        at = slice(128 * c, 128 * c + 128)
        full[c, 0:32] = mom[c, 0:32] + add[0:32, at]
        full[c, 32:40] = add[32:40, at]
    for c in range(16):
        xi, zi = c // 4, c % 4
        r = combine(CENTRAL[xi], [full[j * 4 + zi, 8:16] for j in range(4)])
        r = r + central_y(full[c, 16:24], lt)
        r = r + combine(CENTRAL[zi], [full[xi * 4 + j, 24:32] for j in range(4)])
        if zi == 0:
            r = r - 1.5 * z_before(full[xi * 4 + 3, 24:32], lt)
        if zi == 3:
            r = r + 1.5 * z_after(full[xi * 4, 24:32], lt)
        pay[5 * c:5 * c + 5] = -r[0:5]
        pay[120 + 5 * c:125 + 5 * c] = full[c, 0:5]
        pay[200 + 5 * c:205 + 5 * c] = mom[c, 32:37]
        pay[280 + 5 * c:285 + 5 * c] = full[c, 32:37]
    for zi in range(4):
        pay[80 + 5 * zi:85 + 5 * zi] = full[zi, 8:13]
        pay[100 + 5 * zi:105 + 5 * zi] = full[12 + zi, 8:13]
        pay[360 + 5 * zi:365 + 5 * zi] = up[512 + 8 * zi:517 + 8 * zi]
        pay[380 + 5 * zi:385 + 5 * zi] = down[512 + 8 * zi:517 + 8 * zi]


def residual_kernel(idx, got, force, out, peers):
    t = got[0, 0:120] + got[1, 0:120] + got[2, 0:120] + got[3, 0:120]
    v = t[0:80] + force[...]
    for n in range(peers):
        out[n, 0:80] = v
        out[n, 80:120] = t[80:120]


def feq_kernel(idx, got, t2, lt, final, h2, low, s0, lo, hi, stack):
    def total(a, n):
        return got[0, a:a + n] + got[1, a:a + n] + got[2, a:a + n] + got[3, a:a + n]

    s0[...] = jnp.zeros_like(s0)
    lo[...] = jnp.zeros_like(lo)
    hi[...] = jnp.zeros_like(hi)
    for c in range(16):
        s0[c, 0:5] = total(200 + 5 * c, 5)
    for zi in range(4):
        lo[zi, 0:5] = total(360 + 5 * zi, 5)
        hi[zi, 0:5] = total(380 + 5 * zi, 5)
    low[...] = total(120, 80)
    pad = jnp.zeros((3, 128), jnp.float32)
    for c in range(16):
        z = jnp.concatenate([0.2 * total(280 + 5 * c, 5), pad], axis=0) + 0.16 * s0[c]
        six = one_sided(lambda k: s0[k], lambda zi: lo[zi], lambda zi: hi[zi], c, lt)
        for n, v in enumerate([z] + six):
            stack[8 * n:8 * n + 8, 128 * c:128 * c + 128] = v
    add = lax.dot_general(stack[...], final[0], (((0,), (0,)), ((), ())), precision=HI,
                          preferred_element_type=jnp.float32)
    h2[...] = t2[...] + add.reshape(16, 8, 16, 128)


def apply_operator(src, dst, lt):
    def along_x(zi, _):
        u = [src[16 + j * 4 + zi] for j in range(4)]
        p = [src[j * 4 + zi] + src[64 + j * 4 + zi] for j in range(4)]
        for xi in range(4):
            du = combine(CENTRAL[xi], u)
            dp = combine(CENTRAL[xi], p)
            if xi == 0:
                du = du - 1.5 * pltpu.roll(u[3], 1, 0)
                dp = dp - 1.5 * pltpu.roll(p[3], 1, 0)
            if xi == 3:
                du = du + 1.5 * pltpu.roll(u[0], 23, 0)
                dp = dp + 1.5 * pltpu.roll(p[0], 23, 0)
            dst[xi * 4 + zi] = du
            dst[16 + xi * 4 + zi] = 2.0 * u[xi] + dp
        return 0
    lax.fori_loop(0, 4, along_x, 0, unroll=True)

    def along_z(xi, _):
        u = [src[48 + xi * 4 + j] for j in range(4)]
        p = [src[xi * 4 + j] + src[64 + xi * 4 + j] for j in range(4)]
        for zi in range(4):
            du = combine(CENTRAL[zi], u)
            dp = combine(CENTRAL[zi], p)
            if zi == 0:
                du = du - 1.5 * z_before(u[3], lt)
                dp = dp - 1.5 * z_before(p[3], lt)
            if zi == 3:
                du = du + 1.5 * z_after(u[0], lt)
                dp = dp + 1.5 * z_after(p[0], lt)
            dst[xi * 4 + zi] = dst[xi * 4 + zi] + du
            dst[48 + xi * 4 + zi] = 2.0 * u[zi] + dp
        return 0
    lax.fori_loop(0, 4, along_z, 0, unroll=True)

    def along_y(c, _):
        rho, u, t = src[c], src[32 + c], src[64 + c]
        div = dst[c] + central_y(u, lt)
        dst[32 + c] = 2.0 * u + central_y(rho + t, lt)
        dst[c] = 2.0 * rho + div
        dst[64 + c] = 2.0 * t + div
        return 0
    lax.fori_loop(0, 16, along_y, 0, unroll=4)


def two_level(r, pe, co, lt):
    def over_f(f, _):
        tz = [[None, None] for _ in range(4)]
        for xi in range(4):
            q = [r[f * 16 + xi * 4 + zi] for zi in range(4)]
            for za in range(2):
                tz[xi][za] = combine(RT[za], q)
        for za in range(2):
            py = []
            for xa in range(2):
                t = combine(RT[xa], [tz[xi][za] for xi in range(4)])
                e0, e1 = lt[9:10] * t, lt[16:17] * t
                for s in SHIFTS:
                    rolled = pltpu.roll(t, (-16 * s) % 128, 1)
                    e0 = e0 + lt[9 + s:10 + s] * rolled
                    e1 = e1 + lt[16 + s:17 + s] * rolled
                co[f * 8 + xa * 4 + za * 2] = e0
                co[f * 8 + xa * 4 + za * 2 + 1] = e1
                py.append(lt[20:21] * e0 + lt[21:22] * e1)
            for xi in range(4):
                v = combine(PR[xi], py)
                for zi in range(4):
                    if PR[zi][za] == 0.0:
                        continue
                    at = f * 16 + xi * 4 + zi
                    if za == 0 or PR[zi][0] == 0.0:
                        pe[at] = PR[zi][za] * v
                    else:
                        pe[at] = pe[at] + PR[zi][za] * v
        return 0
    lax.fori_loop(0, 5, over_f, 0)


def coarse_products(co, lt):
    def at(f, xa, za, ya):
        return co[f * 8 + xa * 4 + za * 2 + ya]

    def own(q):
        return q[8:16]

    def dx(q, xa, za, ya):
        if xa == 0:
            v = q(1, za, ya)
            return 0.25 * (own(v) - own(pltpu.roll(v, 1, 0)))
        v = q(0, za, ya)
        return 0.25 * (own(pltpu.roll(v, 23, 0)) - own(v))

    def dz(q, xa, za, ya):
        v = own(q(xa, 1 - za, ya))
        if za == 0:
            return 0.25 * (v - z_before(v, lt))
        return 0.25 * (z_after(v, lt) - v)

    def dy(q, xa, za, ya):
        v = own(q(xa, za, 1 - ya))
        w = pltpu.roll(v, 64, 1)
        return 0.25 * (v - w) if ya == 0 else 0.25 * (w - v)

    up = jnp.zeros((8, 128), jnp.float32)
    low = jnp.zeros((8, 128), jnp.float32)
    for xa in range(2):
        for za in range(2):
            for ya in range(2):
                def field(f):
                    return lambda a, b, c: at(f, a, b, c)

                def pressure(a, b, c):
                    return at(0, a, b, c) + at(4, a, b, c)
                e = [own(at(f, xa, za, ya)) for f in range(5)]
                div = (dx(field(1), xa, za, ya) + dy(field(2), xa, za, ya)
                       + dz(field(3), xa, za, ya))
                g = [2.0 * e[0] + div, 2.0 * e[1] + dx(pressure, xa, za, ya),
                     2.0 * e[2] + dy(pressure, xa, za, ya),
                     2.0 * e[3] + dz(pressure, xa, za, ya), 2.0 * e[4] + div]
                for f in range(5):
                    up = up + e[f] * g[f]
                    low = low + g[f] * g[f]
    return up * lt[23:24], low * lt[23:24]


def fine_products(r, m, ar, am, lt):
    total = [jnp.zeros((8, 128), jnp.float32) for _ in range(6)]
    for xi in range(4):
        for zi in range(4):
            def over_f(f, acc):
                k = f * 16 + xi * 4 + zi
                a, b, c, d = r[k, 8:16], m[k, 8:16], ar[k, 8:16], am[k, 8:16]
                return (acc[0] + a * c, acc[1] + a * d + b * c, acc[2] + b * d,
                        acc[3] + c * c, acc[4] + c * d, acc[5] + d * d)
            zero = jnp.zeros((8, 128), jnp.float32)
            acc = lax.fori_loop(0, 5, over_f, (zero,) * 6, unroll=True)
            w = WEIGHTS[xi] * WEIGHTS[zi]
            total = [t + w * a for t, a in zip(total, acc)]
    return [t * lt[22:23] for t in total]


def pass_words(r, m, ar, am, pe, co, gram, lt, peers):
    two_level(r, pe, co, lt)
    apply_operator(pe, m, lt)
    apply_operator(r, ar, lt)
    apply_operator(m, am, lt)
    products = list(coarse_products(co, lt)) + fine_products(r, m, ar, am, lt)
    rows = jnp.concatenate([jnp.sum(p, axis=0, keepdims=True) for p in products], axis=0)
    for n in range(peers):
        gram[n] = rows


def pack_kernel(idx, mine, own, to_upper, to_lower):
    first = lax.broadcasted_iota(jnp.int32, (8, 128), 0) == 0
    last = lax.broadcasted_iota(jnp.int32, (8, 128), 0) == 7
    for f in range(5):
        for zi in range(4):
            high = mine[pl.ds(100 + 5 * zi + f, 8, stride=120), :]
            low = mine[pl.ds(80 + 5 * zi + f, 8, stride=120), :]
            for xi in range(4):
                c = xi * 4 + zi
                k = f * 16 + c
                v = mine[pl.ds(5 * c + f, 8, stride=120), :]
                if xi == 0:
                    v = v + 1.5 * jnp.where(first, 0.0, pltpu.roll(high, 1, 0))
                if xi == 3:
                    v = v - 1.5 * jnp.where(last, 0.0, pltpu.roll(low, 7, 0))
                own[k] = v
                to_upper[pl.ds(k, 6, stride=80), :] = v[2:8]
                to_lower[pl.ds(k, 6, stride=80), :] = v[0:6]
            to_upper[480 + f * 4 + zi:481 + f * 4 + zi] = high[7:8]
            to_lower[480 + f * 4 + zi:481 + f * 4 + zi] = low[0:1]


def first_pass_kernel(idx, lower, own, upper, edge_low, edge_high, lt, r, m, ar, am, pe, gram, co):
    zero = jnp.zeros((2, 128), jnp.float32)
    for f in range(5):
        for c in range(16):
            xi, zi = c // 4, c % 4
            k, e = f * 16 + c, f * 4 + zi
            r[k, 0:8] = jnp.concatenate([zero, lower[pl.ds(k, 6, stride=80), :]], axis=0)
            r[k, 8:16] = own[k]
            r[k, 16:24] = jnp.concatenate([upper[pl.ds(k, 6, stride=80), :], zero], axis=0)
            if xi == 0:
                r[k, 8:9] = r[k, 8:9] + 1.5 * lower[480 + e:481 + e]
                r[k, 16:17] = r[k, 16:17] + 1.5 * edge_high[480 + e:481 + e]
            if xi == 3:
                r[k, 15:16] = r[k, 15:16] - 1.5 * upper[480 + e:481 + e]
                r[k, 7:8] = r[k, 7:8] - 1.5 * edge_low[480 + e:481 + e]
    pass_words(r, m, ar, am, pe, co, gram, lt, gram.shape[0])


def step_sizes(sums, peers):
    s = sums[0]
    for n in range(1, peers):
        s = s + sums[n]
    s = jnp.broadcast_to(jnp.sum(s, axis=1, keepdims=True), (8, 128))
    a1 = s[0:1] / (s[1:2] + EPS)
    up = s[2:3] - a1 * s[3:4] + a1 * a1 * s[4:5]
    low = s[5:6] - 2.0 * a1 * s[6:7] + a1 * a1 * s[7:8]
    return a1, up / (low + EPS)


def next_pass_kernel(first, idx, sums, r, m, ar, am, pe, *rest):
    if first:
        lt, r2, m2, ar2, am2, pe2, acc2, gram, co = rest
    else:
        acc, lt, r2, m2, ar2, am2, pe2, acc2, gram, co = rest
    a1, a2 = step_sizes(sums, gram.shape[0])

    def over_k(k, _):
        q = r[k] - a1 * m[k]
        v = a1 * pe[k, 8:16] + a2 * q[8:16]
        acc2[k] = v if first else acc[k] + v
        r2[k] = q - a2 * (ar[k] - a1 * am[k])
        return 0
    lax.fori_loop(0, 80, over_k, 0, unroll=4)
    pass_words(r2, m2, ar2, am2, pe2, co, gram, lt, gram.shape[0])


def third_pass_kernel(idx, sums, r, m, ar, am, pe, acc, lt, ro, mo, po, acc2, gram,
                      r2, m2, ar2, am2, pe2, co):
    next_pass_kernel(False, idx, sums, r, m, ar, am, pe, acc, lt, r2, m2, ar2, am2, pe2, acc2, gram, co)
    ro[...] = r2[:, 8:16]
    mo[...] = m2[:, 8:16]
    po[...] = pe2[:, 8:16]


def last_kernel(idx, sums, r, m, pe, acc, low, h2, ec, out, fields, change, stack):
    a1, a2 = step_sizes(sums, sums.shape[0])

    def over_k(k, _):
        q = r[k] - a1 * m[k]
        change[pl.ds(pl.multiple_of(k * 8, 8), 8)] = acc[k] + a1 * pe[k] + a2 * q
        return 0
    lax.fori_loop(0, 80, over_k, 0, unroll=4)
    z = idx[1]
    stack[...] = jnp.zeros_like(stack)
    for c in range(16):
        for f in range(5):
            k = f * 16 + c
            d = change[pl.ds(k * 8 + z, 1)]
            stack[f:f + 1, 128 * c:128 * c + 128] = d
            fields[k:k + 1] = low[5 * c + f:5 * c + f + 1] + d
    add = lax.dot_general(stack[...], ec[0], (((0,), (0,)), ((), ())), precision=HI,
                          preferred_element_type=jnp.float32).reshape(16, 8, 16, 128)
    for c in range(16):
        xi, zi = c // 4, c % 4
        v = h2[c] + add[c]
        for y in range(8):
            out[xi, y, pl.ds(zi, 16, stride=4), :] = v[y]


def on_device(distribution, forcing):
    import functools
    tables = {k: jnp.asarray(v) for k, v in constant_tables().items()}
    spaces = lax.axis_size("space")
    blocks = spaces // 8
    idx = jnp.stack([lax.axis_index("vel"), lax.axis_index("space") % 8]).astype(jnp.int32)
    vec, lt = tables["vec"], tables["lanes"]
    wide = (16, 8, 16, 128)
    layer = (4, 8, 16, 128)

    def shifted(x, by):
        return lax.ppermute(x, "space", [(i, (i + by) % spaces) for i in range(spaces)])

    up, down = call(rim_kernel, "rims", idx, [distribution], [vec, tables["tabr"]],
                    [(544, 128)] * 2, [layer, layer, (8, 8, 16, 128), (1024, 128)])
    up, down = shifted(up, 1), shifted(down, -1)
    twice, moma = call(local_kernel, "local", idx, [distribution],
                       [vec, tables["tab0"], tables["tab1"]],
                       [wide, (16, 16, 128)], [wide, wide, (2048, 128)])
    force = jnp.pad(forcing, ((1, 1), (0, 0), (0, 0), (0, 0)))
    force = force.reshape(5, 4, 8, 16, 4).transpose(1, 4, 0, 2, 3).reshape(80, 128)
    pay, t2 = call(moment_kernel, "moments", idx, [up, down, twice, moma, tables["mix"], lt],
                   [vec, tables["tab2"], tables["tab1"]], [(400, 128), wide],
                   [layer, layer, layer, (16, 48, 128), (16, 40, 128), (2048, 128), (64, 2048)])
    got = lax.all_gather(pay, "vel")
    (res,) = call(lambda i, g, fo, o: residual_kernel(i, g, fo, o, 8), "residual", idx,
                  [got, force], [], [(8, 120, 128)])
    near = [[a * 8 + b for b in range(8)] for a in range(blocks)]
    far = [[a * 8 + b for a in range(blocks)] for b in range(8)]
    mine = lax.all_to_all(res, "space", 0, 0, axis_index_groups=near, tiled=True).reshape(960, 128)
    own_r, to_upper, to_lower = call(pack_kernel, "pack", idx, [mine], [],
                                     [(80, 8, 128), (500, 128), (500, 128)])
    lower, upper = shifted(to_upper, 8), shifted(to_lower, -8)
    h2, low = call(feq_kernel, "feq", idx, [got, t2, lt], [tables["final"]],
                   [wide, (80, 128)], [(16, 8, 128), (4, 8, 128), (4, 8, 128), (56, 2048)])

    def summed(gram):
        return lax.all_to_all(gram, "space", 0, 0, axis_index_groups=far, tiled=True)

    win, own, part = (80, 24, 128), (80, 8, 128), (blocks, 8, 128)
    co = (40, 24, 128)
    r, m, ar, am, pe, gram = call(first_pass_kernel, "pass1", idx,
                                  [lower, own_r, upper, to_lower, to_upper, lt], [],
                                  [win] * 5 + [part], [co])
    r, m, ar, am, pe, acc, gram = call(functools.partial(next_pass_kernel, True), "pass2", idx,
                                       [summed(gram), r, m, ar, am, pe, lt], [],
                                       [win] * 5 + [own, part], [co])
    r, m, pe, acc, gram = call(third_pass_kernel, "pass3", idx,
                               [summed(gram), r, m, ar, am, pe, acc, lt], [],
                               [own] * 4 + [part], [win] * 5 + [co])
    out, fields = call(last_kernel, "last", idx, [summed(gram), r, m, pe, acc, low, h2],
                       [tables["ec"]], [(4, 8, 64, 128), (80, 128)], [(640, 128), (8, 2048)])
    fields = fields.reshape(5, 4, 4, 8, 16).transpose(0, 1, 3, 4, 2).reshape(5, 4, 8, 64)
    return out, fields


def solution(mesh):
    return jax.shard_map(
        on_device,
        mesh=mesh,
        in_specs=(P("space", None, None, "vel"), P(None, "space", None, None)),
        out_specs=(P("space", None, None, "vel"), P(None, "space", None, None)),
        check_vma=False,
    )
```

```python
import math

import jax
import jax.numpy as jnp
import numpy as np
from jax import lax
from jax.experimental import pallas as pl
from jax.experimental.pallas import tpu as pltpu
from jax.sharding import PartitionSpec as P

INTERPRET = False
DT = 0.02
RF = 0.4472135954999579
POINTS = [-1.0, -RF, RF, 1.0]
WEIGHTS = [1.0 / 6.0, 5.0 / 6.0, 5.0 / 6.0, 1.0 / 6.0]
EPS = 1e-6
HI = lax.Precision.HIGHEST


def lagrange_table(points):
    n = len(points)
    bary = []
    for i in range(n):
        product = 1.0
        for j in range(n):
            if j != i:
                product *= points[i] - points[j]
        bary.append(1.0 / product)
    rows = [[0.0] * n for _ in range(n)]
    for i in range(n):
        for j in range(n):
            if j != i:
                rows[i][j] = bary[j] / bary[i] / (points[i] - points[j])
        rows[i][i] = -sum(rows[i])
    return rows


D4 = lagrange_table(POINTS)
for _i in (1, 2):
    D4[_i][_i] = 0.0
PR = [[(1.0 - x) / 2.0, (1.0 + x) / 2.0] for x in POINTS]
RT = [[WEIGHTS[i] * PR[i][a] for i in range(4)] for a in range(2)]


def constant_tables():
    k = np.arange(512)
    b, j = k // 128, k % 128
    s = j // 64
    m = ((b * 64 + j % 64) * 5179 + 7) % 16384
    xi = np.stack([16 * s + m // 1024, (m // 32) % 32, m % 32]).astype(np.float64)
    xi = -4.0 + 0.25 * (xi + 0.5)
    sq = (xi * xi).sum(0)
    e = math.pi ** (-1.5) * np.exp(-sq)
    x, y, z = xi
    phi = np.stack(
        [np.ones(512), x, y, z, 2 * sq / 3 - 1, 2 * (x * x - sq / 3), 2 * (y * y - sq / 3),
         2 * x * y, 2 * x * z, 2 * y * z, x * (sq - 2.5), y * (sq - 2.5), z * (sq - 2.5)]
    )
    p = phi[0] + phi[4]
    zero = np.zeros(512)

    def eight(rows):
        return np.stack(list(rows) + [zero] * (8 - len(rows)))

    low = eight(phi[:5])
    along_x = eight([phi[1], p + phi[5], phi[7], phi[8], phi[1] + phi[10]])
    along_y = eight([phi[2], phi[7], p + phi[6], phi[9], phi[2] + phi[11]])
    along_z = eight([phi[3], phi[8], phi[9], p - phi[5] - phi[6], phi[3] + phi[12]])
    rows32 = np.concatenate([low, along_x, along_y, along_z])
    ec = eight([e, 2 * x * e, 2 * y * e, 2 * z * e, e * (sq - 1.5)])
    pos, neg = np.maximum(xi, 0.0), np.minimum(xi, 0.0)

    def per_rank(rows):
        return np.stack([rows[:, r * 128:(r + 1) * 128] for r in range(4)]).astype(np.float32)

    ispos = (x > 0).astype(np.float64)
    ax = np.abs(x)
    d4 = np.array(D4)
    vec = [-DT * 0.5 * x, -DT * 0.5 * y, -DT * 0.5 * z,
           -3 * DT * pos[1], -3 * DT * neg[1], -3 * DT * pos[2], -3 * DT * neg[2],
           -3 * DT * pos[0], 3 * DT * neg[0], 3 * DT * ax]
    for i in range(4):
        kap = -DT * 0.5 * x * np.where(ispos > 0, d4[i][0], d4[i][3])
        if i == 0:
            kap = kap + ispos * (0.8 - 3 * DT * ax)
        if i == 3:
            kap = kap + (1 - ispos) * (0.8 - 3 * DT * ax)
        vec.append(kap)
    vec.append(ispos)
    for jj in range(4):
        vec.append(-DT * 0.5 * x * np.where(ispos > 0, d4[3][jj], d4[0][jj]))
    while len(vec) < 24:
        vec.append(zero)
    vec = per_rank(np.stack(vec))

    def moment_rows(start, rows, height):
        out = np.zeros((height, 512))
        out[start:start + len(rows)] = rows
        return per_rank(out)

    tab2 = moment_rows(0, rows32, 48)
    tab1 = moment_rows(40, low, 48)
    tab0 = moment_rows(32, low, 48)
    tabr = moment_rows(0, low, 8)
    select = np.zeros((64, 512))
    for n in range(4):
        for la in range(128):
            select[4 * (la % 16) + n, 128 * n + la] = 1.0
    g = rows32 @ ec.T
    g5 = g[:8]
    mix = np.zeros((40, 64))
    mix[:32, 0:8] = 0.16 * g + 0.04 * g @ g5
    mix[:32, 8:16] = 0.2 * g
    mix[32:, 0:8] = 0.2 * g5
    mix[32:, 8:16] = np.eye(8)
    final = [ec]
    for d in range(3):
        for i, part in enumerate((pos[d], neg[d])):
            c0 = 16 + 16 * d + 8 * i
            mix[:32, c0:c0 + 8] = -0.2 * DT * (rows32 * part) @ ec.T
            final.append(-0.2 * DT * ec * part)
    final = per_rank(np.concatenate(final))
    lane = np.arange(128)
    yi, ze = (lane // 16) % 4, lane % 16
    rows = []
    shifts = (-3, -2, -1, 1, 2, 3)

    def entry(table, sft):
        return np.array([table(i, i + sft) if 0 <= i + sft < 4 else 0.0 for i in yi])

    for sft in shifts:
        c = entry(lambda i, q: 0.5 * D4[i][q], sft)
        if sft == -1:
            c = c - 1.5 * (yi == 0)
        if sft == 1:
            c = c + 1.5 * (yi == 3)
        rows.append(c)
    for a in range(2):
        for sft in range(-3, 4):
            rows.append(entry(lambda i, q: RT[a][q], sft))
    rows += [np.array([PR[i][0] for i in yi]), np.array([PR[i][1] for i in yi])]
    rows += [np.array([WEIGHTS[i] for i in yi]), (yi == 0) * 1.0, (ze == 0) * 1.0, (ze == 15) * 1.0]
    for sft in shifts:
        rows.append(entry(lambda i, q: 0.5 * D4[i][q], sft))
    rows += [entry(lambda i, q: 0.5 * D4[i][q], 0), 3.0 * (yi == 0), 3.0 * (yi == 3)]
    while len(rows) < 40:
        rows.append(np.zeros(128))
    lanes = np.stack(rows).astype(np.float32)
    return dict(vec=vec, tab2=tab2, tab1=tab1, tab0=tab0, tabr=tabr, mix=mix.astype(np.float32),
                final=final, lanes=lanes, ec=per_rank(ec), select=select.astype(np.float32))


def call(kernel, name, idx, full, ranked, outs, scratch=(), limit=24):
    n = len(full)

    def body(idx, *refs):
        rank = [r.at[pl.ds(idx[0], 1)] for r in refs[n:n + len(ranked)]]
        kernel(idx, *refs[:n], *rank, *refs[n + len(ranked):])

    vmem = pl.BlockSpec(memory_space=pltpu.VMEM)
    return pl.pallas_call(
        body,
        name=name,
        out_shape=[jax.ShapeDtypeStruct(s, jnp.float32) for s in outs],
        in_specs=[pl.BlockSpec(memory_space=pltpu.SMEM)] + [vmem] * (n + len(ranked)),
        out_specs=[vmem] * len(outs),
        scratch_shapes=[pltpu.VMEM(s, jnp.float32) for s in scratch],
        compiler_params=pltpu.CompilerParams(vmem_limit_bytes=limit << 20),
        interpret=INTERPRET,
    )(idx, *full, *ranked)


def exact_dot(a, b):
    return jnp.dot(a, b, precision=HI, preferred_element_type=jnp.float32)


def project(x, rows):
    return lax.dot_general(x, rows, (((1,), (1,)), ((), ())), precision=HI,
                           preferred_element_type=jnp.float32)


def combine(row, values):
    total = None
    for c, v in zip(row, values):
        if c != 0.0:
            total = c * v if total is None else total + c * v
    return total


def layer_yz(src, dst, vec):
    def over_y(y, _):
        q = [src[zi, y] for zi in range(4)]
        for zi in range(4):
            v = vec[0, 2:3] * combine(D4[zi], q)
            if zi == 0:
                v = v + vec[0, 5:6] * (q[0] - pltpu.roll(q[3], 1, 0))
            if zi == 3:
                v = v + vec[0, 6:7] * (pltpu.roll(q[0], 15, 0) - q[3])
            dst[zi, y] = v
        return 0
    lax.fori_loop(0, 8, over_y, 0)

    def over_z(zi, _):
        q = [src[zi, y] for y in range(8)]
        for y in range(8):
            e, yi = 4 * (y // 4), y % 4
            v = vec[0, 1:2] * combine(D4[yi], q[e:e + 4])
            if yi == 0:
                v = v + vec[0, 3:4] * (q[y] - q[(y + 7) % 8])
            if yi == 3:
                v = v + vec[0, 4:5] * (q[(y + 1) % 8] - q[y])
            dst[zi, y] = dst[zi, y] + v
        return 0
    lax.fori_loop(0, 4, over_z, 0)


def every_fourth(h, xi, y, zi):
    if INTERPRET:
        return h[xi, y][zi::4]
    return h[xi, y, pl.ds(zi, 16, stride=4), :]


def rim_kernel(idx, h, vec, tabr, up, down, q, t, ends, m):
    pos = vec[0, 14:15] > 0.5
    for zi in range(4):
        def over_y(y, _):
            x = [every_fourth(h, xi, y, zi) for xi in range(4)]
            ql = jnp.where(pos, x[3], x[0])
            q[zi, y] = ql
            ends[zi, y] = x[0]
            ends[4 + zi, y] = x[3]
            v = 0.8 * ql
            for j in range(4):
                v = v + vec[0, 15 + j:16 + j] * x[j]
            up[pl.ds(pl.multiple_of((zi * 8 + y) * 16, 16), 16)] = v
            return 0
        lax.fori_loop(0, 8, over_y, 0)
    layer_yz(q, t, vec)
    right = lax.broadcasted_iota(jnp.int32, (16, 128), 1) >= 64

    def pack(n, _):
        zi, y = n // 8, n % 8
        at = pl.ds(pl.multiple_of(n * 16, 16), 16)
        tl = pltpu.roll(t[zi, y] + up[at], 64, 1)
        ql = q[zi, y]
        up[at] = jnp.where(right, ql, tl)
        down[at] = jnp.where(right, tl, ql)
        return 0
    lax.fori_loop(0, 32, pack, 0)
    m[...] = project(ends[...].reshape(1024, 128), tabr[0])
    for n in range(8):
        zi, out = n % 4, (down, up)[n // 4]
        out[512 + 8 * zi:520 + 8 * zi] = m[128 * n:128 * n + 128].T


def local_update(src, dst, vec):
    def over_y(y, _):
        q = [src[c, y] for c in range(16)]
        for xi in range(4):
            for zi in range(4):
                own = q[xi * 4 + zi]
                v = 0.8 * own + vec[0, 0:1] * combine(D4[xi], [q[j * 4 + zi] for j in range(4)])
                v = v + vec[0, 2:3] * combine(D4[zi], q[xi * 4:xi * 4 + 4])
                if zi == 0:
                    v = v + vec[0, 5:6] * (own - pltpu.roll(q[xi * 4 + 3], 1, 0))
                if zi == 3:
                    v = v + vec[0, 6:7] * (pltpu.roll(q[xi * 4], 15, 0) - own)
                if xi == 0:
                    v = v + vec[0, 7:8] * own
                if xi == 3:
                    v = v + vec[0, 8:9] * own
                dst[xi * 4 + zi, y] = v
        return 0
    lax.fori_loop(0, 8, over_y, 0)

    def over_c(c, _):
        q = [src[c, y] for y in range(8)]
        for y in range(8):
            e, yi = 4 * (y // 4), y % 4
            v = vec[0, 1:2] * combine(D4[yi], q[e:e + 4])
            if yi == 0:
                v = v + vec[0, 3:4] * (q[y] - q[(y + 7) % 8])
            if yi == 3:
                v = v + vec[0, 4:5] * (q[(y + 1) % 8] - q[y])
            dst[c, y] = dst[c, y] + v
        return 0
    lax.fori_loop(0, 16, over_c, 0)


def row_of_y():
    y = lax.broadcasted_iota(jnp.int32, (8, 128), 0)
    return (lax.broadcasted_iota(jnp.int32, (8, 128), 1) // 16 == y).astype(jnp.float32)


def local_kernel(idx, h, forcing, select, vec, tab0, tab1, twice, mom, force, first, once, m):
    spread = exact_dot(forcing[...].reshape(96, 64), select[...])
    here = row_of_y()
    force[...] = jnp.zeros_like(force)
    for f in range(3):
        for c in range(16):
            n = 8 * (f * 4 + c // 4)
            v = spread[n:n + 8, 128 * (c % 4):128 * (c % 4) + 128] * here
            force[5 * c + f + 1:5 * c + f + 2] = jnp.sum(v, axis=0, keepdims=True)
    for c in range(16):
        xi, zi = c // 4, c % 4

        def over_y(y, _):
            first[c, y] = every_fourth(h, xi, y, zi)
            return 0
        lax.fori_loop(0, 8, over_y, 0)
    local_update(first, once, vec)
    local_update(once, twice, vec)

    m[...] = project(first[...].reshape(2048, 128), tab0[0])
    m[...] = m[...] + project(once[...].reshape(2048, 128), tab1[0])
    for c in range(16):
        mom[c] = m[128 * c:128 * c + 128].T[32:48]


def z_before(q, lt):
    return jnp.where(lt[24:25] > 0.5, pltpu.roll(q, 113, 1), pltpu.roll(q, 1, 1))


def z_after(q, lt):
    return jnp.where(lt[25:26] > 0.5, pltpu.roll(q, 15, 1), pltpu.roll(q, 127, 1))


SHIFTS = (-3, -2, -1, 1, 2, 3)


def central_y(q, lt):
    total = None
    for n, s in enumerate(SHIFTS):
        term = lt[n:n + 1] * pltpu.roll(q, (-16 * s) % 128, 1)
        total = term if total is None else total + term
    return total


def one_sided(load, low, high, c, lt):
    xi, zi = c // 4, c % 4
    q = load(c)
    cx = combine([0.5 * v for v in D4[xi]], [load(j * 4 + zi) for j in range(4)])
    px = cx + 3.0 * (q - low(zi)) if xi == 0 else cx
    mx = cx + 3.0 * (high(zi) - q) if xi == 3 else cx
    cy = lt[32:33] * q
    for n, s in enumerate(SHIFTS):
        r = pltpu.roll(q, (-16 * s) % 128, 1)
        cy = cy + lt[26 + n:27 + n] * r
        if s == -1:
            py = lt[33:34] * (q - r)
        if s == 1:
            my = lt[34:35] * (r - q)
    cz = combine([0.5 * v for v in D4[zi]], [load(xi * 4 + j) for j in range(4)])
    pz = cz + 3.0 * (q - z_before(load(xi * 4 + 3), lt)) if zi == 0 else cz
    mz = cz + 3.0 * (z_after(load(xi * 4), lt) - q) if zi == 3 else cz
    return [px, mx, cy + py, cy + my, pz, mz]


CENTRAL = [[0.0 if i == j else 0.5 * D4[i][j] for j in range(4)] for i in range(4)]


def moment_kernel(idx, up, down, twice, moma, mix, lt, vec, tab2, tab1, pay, t2,
                  delta, yz, extra, mom, full, m, stack):
    right = lax.broadcasted_iota(jnp.int32, (16, 128), 1) >= 64
    pos = vec[0, 14:15]

    def unpack(n, _):
        at = pl.ds(pl.multiple_of(n * 16, 16), 16)
        u, d = up[at], down[at]
        zi, y = n // 8, n % 8
        delta[zi, y] = vec[0, 9:10] * jnp.where(right, u, d)
        extra[zi, y] = vec[0, 9:10] * pltpu.roll(jnp.where(right, d, u), 64, 1)
        return 0
    lax.fori_loop(0, 32, unpack, 0)
    layer_yz(delta, yz, vec)
    for xi in range(4):
        def over_n(n, _):
            zi, y = n // 8, n % 8
            v = twice[xi * 4 + zi, y] + vec[0, 10 + xi:11 + xi] * delta[zi, y]
            if xi in (0, 3):
                w = pos if xi == 0 else 1.0 - pos
                v = v + w * (yz[zi, y] + extra[zi, y])
            t2[xi * 4 + zi, y] = v
            return 0
        lax.fori_loop(0, 32, over_n, 0)

    m[...] = project(t2[...].reshape(2048, 128), tab2[0])
    d = delta[...].reshape(512, 128)
    m[0:512] = m[0:512] + project(d * pos, tab1[0])
    m[1536:2048] = m[1536:2048] + project(d * (1.0 - pos), tab1[0])
    for c in range(16):
        t = m[128 * c:128 * c + 128].T
        mom[c, 0:32] = t[0:32]
        mom[c, 32:48] = t[32:48] + moma[c]

    def load0(c):
        return mom[c, 32:40]

    for c in range(16):
        six = one_sided(load0, lambda zi: up[512 + 8 * zi:520 + 8 * zi],
                        lambda zi: down[512 + 8 * zi:520 + 8 * zi], c, lt)
        at = slice(128 * c, 128 * c + 128)
        stack[0:16, at] = mom[c, 32:48]
        for n in range(6):
            stack[16 + 8 * n:24 + 8 * n, at] = six[n]
    add = exact_dot(mix[...], stack[...])
    for c in range(16):
        at = slice(128 * c, 128 * c + 128)
        full[c, 0:32] = mom[c, 0:32] + add[0:32, at]
        full[c, 32:40] = add[32:40, at]
    for c in range(16):
        xi, zi = c // 4, c % 4
        r = combine(CENTRAL[xi], [full[j * 4 + zi, 8:16] for j in range(4)])
        r = r + central_y(full[c, 16:24], lt)
        r = r + combine(CENTRAL[zi], [full[xi * 4 + j, 24:32] for j in range(4)])
        if zi == 0:
            r = r - 1.5 * z_before(full[xi * 4 + 3, 24:32], lt)
        if zi == 3:
            r = r + 1.5 * z_after(full[xi * 4, 24:32], lt)
        pay[5 * c:5 * c + 5] = -r[0:5]
        pay[120 + 5 * c:125 + 5 * c] = full[c, 0:5]
        pay[200 + 5 * c:205 + 5 * c] = mom[c, 32:37]
        pay[280 + 5 * c:285 + 5 * c] = full[c, 32:37]
    for zi in range(4):
        pay[80 + 5 * zi:85 + 5 * zi] = full[zi, 8:13]
        pay[100 + 5 * zi:105 + 5 * zi] = full[12 + zi, 8:13]
        pay[360 + 5 * zi:365 + 5 * zi] = up[512 + 8 * zi:517 + 8 * zi]
        pay[380 + 5 * zi:385 + 5 * zi] = down[512 + 8 * zi:517 + 8 * zi]


def residual_kernel(idx, got, force, out, peers):
    t = got[0, 0:120] + got[1, 0:120] + got[2, 0:120] + got[3, 0:120]
    v = t[0:80] + force[...]
    for n in range(peers):
        out[n, 0:80] = v
        out[n, 80:120] = t[80:120]


def feq_kernel(idx, got, t2, lt, final, h2, low, s0, lo, hi, stack):
    def total(a, n):
        return got[0, a:a + n] + got[1, a:a + n] + got[2, a:a + n] + got[3, a:a + n]

    s0[...] = jnp.zeros_like(s0)
    lo[...] = jnp.zeros_like(lo)
    hi[...] = jnp.zeros_like(hi)
    for c in range(16):
        s0[c, 0:5] = total(200 + 5 * c, 5)
    for zi in range(4):
        lo[zi, 0:5] = total(360 + 5 * zi, 5)
        hi[zi, 0:5] = total(380 + 5 * zi, 5)
    low[...] = total(120, 80)
    pad = jnp.zeros((3, 128), jnp.float32)
    for c in range(16):
        z = jnp.concatenate([0.2 * total(280 + 5 * c, 5), pad], axis=0) + 0.16 * s0[c]
        six = one_sided(lambda k: s0[k], lambda zi: lo[zi], lambda zi: hi[zi], c, lt)
        for n, v in enumerate([z] + six):
            stack[8 * n:8 * n + 8, 128 * c:128 * c + 128] = v
    add = lax.dot_general(stack[...], final[0], (((0,), (0,)), ((), ())), precision=HI,
                          preferred_element_type=jnp.float32)
    h2[...] = t2[...] + add.reshape(16, 8, 16, 128)


def apply_operator(src, dst, lt):
    def along_x(zi, _):
        u = [src[16 + j * 4 + zi] for j in range(4)]
        p = [src[j * 4 + zi] + src[64 + j * 4 + zi] for j in range(4)]
        for xi in range(4):
            du = combine(CENTRAL[xi], u)
            dp = combine(CENTRAL[xi], p)
            if xi == 0:
                du = du - 1.5 * pltpu.roll(u[3], 1, 0)
                dp = dp - 1.5 * pltpu.roll(p[3], 1, 0)
            if xi == 3:
                du = du + 1.5 * pltpu.roll(u[0], 23, 0)
                dp = dp + 1.5 * pltpu.roll(p[0], 23, 0)
            dst[xi * 4 + zi] = du
            dst[16 + xi * 4 + zi] = 2.0 * u[xi] + dp
        return 0
    lax.fori_loop(0, 4, along_x, 0, unroll=True)

    def along_z(xi, _):
        u = [src[48 + xi * 4 + j] for j in range(4)]
        p = [src[xi * 4 + j] + src[64 + xi * 4 + j] for j in range(4)]
        for zi in range(4):
            du = combine(CENTRAL[zi], u)
            dp = combine(CENTRAL[zi], p)
            if zi == 0:
                du = du - 1.5 * z_before(u[3], lt)
                dp = dp - 1.5 * z_before(p[3], lt)
            if zi == 3:
                du = du + 1.5 * z_after(u[0], lt)
                dp = dp + 1.5 * z_after(p[0], lt)
            dst[xi * 4 + zi] = dst[xi * 4 + zi] + du
            dst[48 + xi * 4 + zi] = 2.0 * u[zi] + dp
        return 0
    lax.fori_loop(0, 4, along_z, 0, unroll=True)

    def along_y(c, _):
        rho, u, t = src[c], src[32 + c], src[64 + c]
        div = dst[c] + central_y(u, lt)
        dst[32 + c] = 2.0 * u + central_y(rho + t, lt)
        dst[c] = 2.0 * rho + div
        dst[64 + c] = 2.0 * t + div
        return 0
    lax.fori_loop(0, 16, along_y, 0, unroll=4)


def two_level(r, pe, co, lt):
    def over_f(f, _):
        tz = [[None, None] for _ in range(4)]
        for xi in range(4):
            q = [r[f * 16 + xi * 4 + zi] for zi in range(4)]
            for za in range(2):
                tz[xi][za] = combine(RT[za], q)
        for za in range(2):
            py = []
            for xa in range(2):
                t = combine(RT[xa], [tz[xi][za] for xi in range(4)])
                e0, e1 = lt[9:10] * t, lt[16:17] * t
                for s in SHIFTS:
                    rolled = pltpu.roll(t, (-16 * s) % 128, 1)
                    e0 = e0 + lt[9 + s:10 + s] * rolled
                    e1 = e1 + lt[16 + s:17 + s] * rolled
                co[f * 8 + xa * 4 + za * 2] = e0
                co[f * 8 + xa * 4 + za * 2 + 1] = e1
                py.append(lt[20:21] * e0 + lt[21:22] * e1)
            for xi in range(4):
                v = combine(PR[xi], py)
                for zi in range(4):
                    if PR[zi][za] == 0.0:
                        continue
                    at = f * 16 + xi * 4 + zi
                    if za == 0 or PR[zi][0] == 0.0:
                        pe[at] = PR[zi][za] * v
                    else:
                        pe[at] = pe[at] + PR[zi][za] * v
        return 0
    lax.fori_loop(0, 5, over_f, 0)


def coarse_products(co, lt):
    def at(f, xa, za, ya):
        return co[f * 8 + xa * 4 + za * 2 + ya]

    def own(q):
        return q[8:16]

    def dx(q, xa, za, ya):
        if xa == 0:
            v = q(1, za, ya)
            return 0.25 * (own(v) - own(pltpu.roll(v, 1, 0)))
        v = q(0, za, ya)
        return 0.25 * (own(pltpu.roll(v, 23, 0)) - own(v))

    def dz(q, xa, za, ya):
        v = own(q(xa, 1 - za, ya))
        if za == 0:
            return 0.25 * (v - z_before(v, lt))
        return 0.25 * (z_after(v, lt) - v)

    def dy(q, xa, za, ya):
        v = own(q(xa, za, 1 - ya))
        w = pltpu.roll(v, 64, 1)
        return 0.25 * (v - w) if ya == 0 else 0.25 * (w - v)

    up = jnp.zeros((8, 128), jnp.float32)
    low = jnp.zeros((8, 128), jnp.float32)
    for xa in range(2):
        for za in range(2):
            for ya in range(2):
                def field(f):
                    return lambda a, b, c: at(f, a, b, c)

                def pressure(a, b, c):
                    return at(0, a, b, c) + at(4, a, b, c)
                e = [own(at(f, xa, za, ya)) for f in range(5)]
                div = (dx(field(1), xa, za, ya) + dy(field(2), xa, za, ya)
                       + dz(field(3), xa, za, ya))
                g = [2.0 * e[0] + div, 2.0 * e[1] + dx(pressure, xa, za, ya),
                     2.0 * e[2] + dy(pressure, xa, za, ya),
                     2.0 * e[3] + dz(pressure, xa, za, ya), 2.0 * e[4] + div]
                for f in range(5):
                    up = up + e[f] * g[f]
                    low = low + g[f] * g[f]
    return up * lt[23:24], low * lt[23:24]


def fine_products(r, m, ar, am, lt):
    total = [jnp.zeros((8, 128), jnp.float32) for _ in range(6)]
    for xi in range(4):
        for zi in range(4):
            def over_f(f, acc):
                k = f * 16 + xi * 4 + zi
                a, b, c, d = r[k, 8:16], m[k, 8:16], ar[k, 8:16], am[k, 8:16]
                return (acc[0] + a * c, acc[1] + a * d + b * c, acc[2] + b * d,
                        acc[3] + c * c, acc[4] + c * d, acc[5] + d * d)
            zero = jnp.zeros((8, 128), jnp.float32)
            acc = lax.fori_loop(0, 5, over_f, (zero,) * 6, unroll=True)
            w = WEIGHTS[xi] * WEIGHTS[zi]
            total = [t + w * a for t, a in zip(total, acc)]
    return [t * lt[22:23] for t in total]


def pass_words(r, m, ar, am, pe, co, gram, lt, peers):
    two_level(r, pe, co, lt)
    apply_operator(pe, m, lt)
    apply_operator(r, ar, lt)
    apply_operator(m, am, lt)
    products = list(coarse_products(co, lt)) + fine_products(r, m, ar, am, lt)
    rows = jnp.concatenate([jnp.sum(p, axis=0, keepdims=True) for p in products], axis=0)
    for n in range(peers):
        gram[n] = rows


def pack_kernel(idx, mine, own, to_upper, to_lower):
    first = lax.broadcasted_iota(jnp.int32, (8, 128), 0) == 0
    last = lax.broadcasted_iota(jnp.int32, (8, 128), 0) == 7
    for f in range(5):
        for zi in range(4):
            high = mine[pl.ds(100 + 5 * zi + f, 8, stride=120), :]
            low = mine[pl.ds(80 + 5 * zi + f, 8, stride=120), :]
            for xi in range(4):
                c = xi * 4 + zi
                k = f * 16 + c
                v = mine[pl.ds(5 * c + f, 8, stride=120), :]
                if xi == 0:
                    v = v + 1.5 * jnp.where(first, 0.0, pltpu.roll(high, 1, 0))
                if xi == 3:
                    v = v - 1.5 * jnp.where(last, 0.0, pltpu.roll(low, 7, 0))
                own[k] = v
                to_upper[pl.ds(k, 6, stride=80), :] = v[2:8]
                to_lower[pl.ds(k, 6, stride=80), :] = v[0:6]
            to_upper[480 + f * 4 + zi:481 + f * 4 + zi] = high[7:8]
            to_lower[480 + f * 4 + zi:481 + f * 4 + zi] = low[0:1]


def first_pass_kernel(idx, lower, own, upper, edge_low, edge_high, after, lt, r, m, ar, am, pe, gram, co):
    zero = jnp.zeros((2, 128), jnp.float32)
    for f in range(5):
        for c in range(16):
            xi, zi = c // 4, c % 4
            k, e = f * 16 + c, f * 4 + zi
            r[k, 0:8] = jnp.concatenate([zero, lower[pl.ds(k, 6, stride=80), :]], axis=0)
            r[k, 8:16] = own[k]
            r[k, 16:24] = jnp.concatenate([upper[pl.ds(k, 6, stride=80), :], zero], axis=0)
            if xi == 0:
                r[k, 8:9] = r[k, 8:9] + 1.5 * lower[480 + e:481 + e]
                r[k, 16:17] = r[k, 16:17] + 1.5 * edge_high[480 + e:481 + e]
            if xi == 3:
                r[k, 15:16] = r[k, 15:16] - 1.5 * upper[480 + e:481 + e]
                r[k, 7:8] = r[k, 7:8] - 1.5 * edge_low[480 + e:481 + e]
    pass_words(r, m, ar, am, pe, co, gram, lt, gram.shape[0])


def step_sizes(sums, peers):
    s = sums[0]
    for n in range(1, peers):
        s = s + sums[n]
    s = jnp.broadcast_to(jnp.sum(s, axis=1, keepdims=True), (8, 128))
    a1 = s[0:1] / (s[1:2] + EPS)
    up = s[2:3] - a1 * s[3:4] + a1 * a1 * s[4:5]
    low = s[5:6] - 2.0 * a1 * s[6:7] + a1 * a1 * s[7:8]
    return a1, up / (low + EPS)


def next_pass_kernel(first, idx, sums, r, m, ar, am, pe, *rest):
    if first:
        lt, r2, m2, ar2, am2, pe2, acc2, gram, co = rest
    else:
        acc, lt, r2, m2, ar2, am2, pe2, acc2, gram, co = rest
    a1, a2 = step_sizes(sums, gram.shape[0])

    def over_k(k, _):
        q = r[k] - a1 * m[k]
        v = a1 * pe[k, 8:16] + a2 * q[8:16]
        acc2[k] = v if first else acc[k] + v
        r2[k] = q - a2 * (ar[k] - a1 * am[k])
        return 0
    lax.fori_loop(0, 80, over_k, 0, unroll=4)
    pass_words(r2, m2, ar2, am2, pe2, co, gram, lt, gram.shape[0])


def third_pass_kernel(idx, sums, r, m, ar, am, pe, acc, lt, ro, mo, po, acc2, gram,
                      r2, m2, ar2, am2, pe2, co):
    next_pass_kernel(False, idx, sums, r, m, ar, am, pe, acc, lt, r2, m2, ar2, am2, pe2, acc2, gram, co)
    ro[...] = r2[:, 8:16]
    mo[...] = m2[:, 8:16]
    po[...] = pe2[:, 8:16]


def last_kernel(idx, sums, r, m, pe, acc, low, h2, select, ec, out, fields, change, stack, rows):
    a1, a2 = step_sizes(sums, sums.shape[0])

    def over_k(k, _):
        q = r[k] - a1 * m[k]
        change[pl.ds(pl.multiple_of(k * 8, 8), 8)] = acc[k] + a1 * pe[k] + a2 * q
        return 0
    lax.fori_loop(0, 80, over_k, 0, unroll=4)
    z = idx[1]
    stack[...] = jnp.zeros_like(stack)
    here = row_of_y()
    for c in range(16):
        for f in range(5):
            k = f * 16 + c
            d = change[pl.ds(k * 8 + z, 1)]
            stack[f:f + 1, 128 * c:128 * c + 128] = d
            n = 8 * (k // 4)
            rows[n:n + 8, 128 * (c % 4):128 * (c % 4) + 128] = (low[5 * c + f:5 * c + f + 1] + d) * here
    fields[...] = project(rows[...], select[...]).reshape(5, 4, 8, 64)
    add = lax.dot_general(stack[...], ec[0], (((0,), (0,)), ((), ())), precision=HI,
                          preferred_element_type=jnp.float32).reshape(16, 8, 16, 128)
    for c in range(16):
        xi, zi = c // 4, c % 4
        v = h2[c] + add[c]
        for y in range(8):
            out[xi, y, pl.ds(zi, 16, stride=4), :] = v[y]


def on_device(distribution, forcing):
    import functools
    tables = {k: jnp.asarray(v) for k, v in constant_tables().items()}
    spaces = lax.axis_size("space")
    blocks = spaces // 8
    idx = jnp.stack([lax.axis_index("vel"), lax.axis_index("space") % 8]).astype(jnp.int32)
    vec, lt = tables["vec"], tables["lanes"]
    wide = (16, 8, 16, 128)
    layer = (4, 8, 16, 128)

    def shifted(x, by):
        return lax.ppermute(x, "space", [(i, (i + by) % spaces) for i in range(spaces)])

    up, down = call(rim_kernel, "rims", idx, [distribution], [vec, tables["tabr"]],
                    [(544, 128)] * 2, [layer, layer, (8, 8, 16, 128), (1024, 8)])
    up, down = shifted(up, 1), shifted(down, -1)
    twice, moma, force = call(local_kernel, "local", idx, [distribution, forcing, tables["select"]],
                              [vec, tables["tab0"], tables["tab1"]],
                              [wide, (16, 16, 128), (80, 128)], [wide, wide, (2048, 48)])
    pay, t2 = call(moment_kernel, "moments", idx, [up, down, twice, moma, tables["mix"], lt],
                   [vec, tables["tab2"], tables["tab1"]], [(400, 128), wide],
                   [layer, layer, layer, (16, 48, 128), (16, 40, 128), (2048, 48), (64, 2048)])
    got = lax.all_gather(pay, "vel")
    (res,) = call(lambda i, g, fo, o: residual_kernel(i, g, fo, o, 8), "residual", idx,
                  [got, force], [], [(8, 120, 128)])
    near = [[a * 8 + b for b in range(8)] for a in range(blocks)]
    far = [[a * 8 + b for a in range(blocks)] for b in range(8)]
    mine = lax.all_to_all(res, "space", 0, 0, axis_index_groups=near, tiled=True).reshape(960, 128)
    own_r, to_upper, to_lower = call(pack_kernel, "pack", idx, [mine], [],
                                     [(80, 8, 128), (500, 128), (500, 128)])
    lower, upper = shifted(to_upper, 8), shifted(to_lower, -8)
    h2, low = call(feq_kernel, "feq", idx, [got, t2, lt], [tables["final"]],
                   [wide, (80, 128)], [(16, 8, 128), (4, 8, 128), (4, 8, 128), (56, 2048)])

    def summed(gram):
        return lax.all_to_all(gram, "space", 0, 0, axis_index_groups=far, tiled=True)

    win, own, part = (80, 24, 128), (80, 8, 128), (blocks, 8, 128)
    co = (40, 24, 128)
    r, m, ar, am, pe, gram = call(first_pass_kernel, "pass1", idx,
                                  [lower, own_r, upper, to_lower, to_upper, low, lt], [],
                                  [win] * 5 + [part], [co])
    r, m, ar, am, pe, acc, gram = call(functools.partial(next_pass_kernel, True), "pass2", idx,
                                       [summed(gram), r, m, ar, am, pe, lt], [],
                                       [win] * 5 + [own, part], [co])
    r, m, pe, acc, gram = call(third_pass_kernel, "pass3", idx,
                               [summed(gram), r, m, ar, am, pe, acc, lt], [],
                               [own] * 4 + [part], [win] * 5 + [co])
    out, fields = call(last_kernel, "last", idx,
                       [summed(gram), r, m, pe, acc, low, h2, tables["select"]], [tables["ec"]],
                       [(4, 8, 64, 128), (5, 4, 8, 64)], [(640, 128), (8, 2048), (160, 512)])
    return out, fields


def solution(mesh):
    return jax.shard_map(
        on_device,
        mesh=mesh,
        in_specs=(P("space", None, None, "vel"), P(None, "space", None, None)),
        out_specs=(P("space", None, None, "vel"), P(None, "space", None, None)),
        check_vma=False,
    )
```

```python
import math

import jax
import jax.numpy as jnp
import numpy as np
from jax import lax
from jax.experimental import pallas as pl
from jax.experimental.pallas import tpu as pltpu
from jax.sharding import PartitionSpec as P

INTERPRET = False
DT = 0.02
RF = 0.4472135954999579
POINTS = [-1.0, -RF, RF, 1.0]
WEIGHTS = [1.0 / 6.0, 5.0 / 6.0, 5.0 / 6.0, 1.0 / 6.0]
EPS = 1e-6
HI = lax.Precision.HIGHEST


def lagrange_table(points):
    n = len(points)
    bary = []
    for i in range(n):
        product = 1.0
        for j in range(n):
            if j != i:
                product *= points[i] - points[j]
        bary.append(1.0 / product)
    rows = [[0.0] * n for _ in range(n)]
    for i in range(n):
        for j in range(n):
            if j != i:
                rows[i][j] = bary[j] / bary[i] / (points[i] - points[j])
        rows[i][i] = -sum(rows[i])
    return rows


D4 = lagrange_table(POINTS)
for _i in (1, 2):
    D4[_i][_i] = 0.0
PR = [[(1.0 - x) / 2.0, (1.0 + x) / 2.0] for x in POINTS]
RT = [[WEIGHTS[i] * PR[i][a] for i in range(4)] for a in range(2)]


def constant_tables():
    k = np.arange(512)
    b, j = k // 128, k % 128
    s = j // 64
    m = ((b * 64 + j % 64) * 5179 + 7) % 16384
    xi = np.stack([16 * s + m // 1024, (m // 32) % 32, m % 32]).astype(np.float64)
    xi = -4.0 + 0.25 * (xi + 0.5)
    sq = (xi * xi).sum(0)
    e = math.pi ** (-1.5) * np.exp(-sq)
    x, y, z = xi
    phi = np.stack(
        [np.ones(512), x, y, z, 2 * sq / 3 - 1, 2 * (x * x - sq / 3), 2 * (y * y - sq / 3),
         2 * x * y, 2 * x * z, 2 * y * z, x * (sq - 2.5), y * (sq - 2.5), z * (sq - 2.5)]
    )
    p = phi[0] + phi[4]
    zero = np.zeros(512)

    def eight(rows):
        return np.stack(list(rows) + [zero] * (8 - len(rows)))

    low = eight(phi[:5])
    along_x = eight([phi[1], p + phi[5], phi[7], phi[8], phi[1] + phi[10]])
    along_y = eight([phi[2], phi[7], p + phi[6], phi[9], phi[2] + phi[11]])
    along_z = eight([phi[3], phi[8], phi[9], p - phi[5] - phi[6], phi[3] + phi[12]])
    rows32 = np.concatenate([low, along_x, along_y, along_z])
    ec = eight([e, 2 * x * e, 2 * y * e, 2 * z * e, e * (sq - 1.5)])
    pos, neg = np.maximum(xi, 0.0), np.minimum(xi, 0.0)

    def per_rank(rows):
        return np.stack([rows[:, r * 128:(r + 1) * 128] for r in range(4)]).astype(np.float32)

    ispos = (x > 0).astype(np.float64)
    ax = np.abs(x)
    d4 = np.array(D4)
    vec = [-DT * 0.5 * x, -DT * 0.5 * y, -DT * 0.5 * z,
           -3 * DT * pos[1], -3 * DT * neg[1], -3 * DT * pos[2], -3 * DT * neg[2],
           -3 * DT * pos[0], 3 * DT * neg[0], 3 * DT * ax]
    for i in range(4):
        kap = -DT * 0.5 * x * np.where(ispos > 0, d4[i][0], d4[i][3])
        if i == 0:
            kap = kap + ispos * (0.8 - 3 * DT * ax)
        if i == 3:
            kap = kap + (1 - ispos) * (0.8 - 3 * DT * ax)
        vec.append(kap)
    vec.append(ispos)
    for jj in range(4):
        vec.append(-DT * 0.5 * x * np.where(ispos > 0, d4[3][jj], d4[0][jj]))
    while len(vec) < 24:
        vec.append(zero)
    vec = per_rank(np.concatenate([np.stack(vec), low]))

    def moment_rows(start, rows, height):
        out = np.zeros((height, 512))
        out[start:start + len(rows)] = rows
        return per_rank(out)

    tab2 = moment_rows(0, rows32, 48)
    tab1 = moment_rows(40, low, 48)
    tab0 = moment_rows(32, low, 48)
    select = np.zeros((64, 512))
    for n in range(4):
        for la in range(128):
            select[4 * (la % 16) + n, 128 * n + la] = 1.0
    g = rows32 @ ec.T
    g5 = g[:8]
    mix = np.zeros((40, 64))
    mix[:32, 0:8] = 0.16 * g + 0.04 * g @ g5
    mix[:32, 8:16] = 0.2 * g
    mix[32:, 0:8] = 0.2 * g5
    mix[32:, 8:16] = np.eye(8)
    final = [ec]
    for d in range(3):
        for i, part in enumerate((pos[d], neg[d])):
            c0 = 16 + 16 * d + 8 * i
            mix[:32, c0:c0 + 8] = -0.2 * DT * (rows32 * part) @ ec.T
            final.append(-0.2 * DT * ec * part)
    final = per_rank(np.concatenate(final))
    lane = np.arange(128)
    yi, ze = (lane // 16) % 4, lane % 16
    rows = []
    shifts = (-3, -2, -1, 1, 2, 3)

    def entry(table, sft):
        return np.array([table(i, i + sft) if 0 <= i + sft < 4 else 0.0 for i in yi])

    for sft in shifts:
        c = entry(lambda i, q: 0.5 * D4[i][q], sft)
        if sft == -1:
            c = c - 1.5 * (yi == 0)
        if sft == 1:
            c = c + 1.5 * (yi == 3)
        rows.append(c)
    for a in range(2):
        for sft in range(-3, 4):
            rows.append(entry(lambda i, q: RT[a][q], sft))
    rows += [np.array([PR[i][0] for i in yi]), np.array([PR[i][1] for i in yi])]
    rows += [np.array([WEIGHTS[i] for i in yi]), (yi == 0) * 1.0, (ze == 0) * 1.0, (ze == 15) * 1.0]
    for sft in shifts:
        rows.append(entry(lambda i, q: 0.5 * D4[i][q], sft))
    rows += [entry(lambda i, q: 0.5 * D4[i][q], 0), 3.0 * (yi == 0), 3.0 * (yi == 3)]
    while len(rows) < 40:
        rows.append(np.zeros(128))
    lanes = np.stack(rows).astype(np.float32)
    return dict(vec=vec, tab2=tab2, tab1=tab1, tab0=tab0, mix=mix.astype(np.float32),
                final=final, lanes=lanes, ec=per_rank(ec), select=select.astype(np.float32))


def call(kernel, name, idx, full, ranked, outs, scratch=(), limit=24):
    n = len(full)

    def body(idx, *refs):
        rank = [r.at[pl.ds(idx[0], 1)] for r in refs[n:n + len(ranked)]]
        kernel(idx, *refs[:n], *rank, *refs[n + len(ranked):])

    vmem = pl.BlockSpec(memory_space=pltpu.VMEM)
    return pl.pallas_call(
        body,
        name=name,
        out_shape=[jax.ShapeDtypeStruct(s, jnp.float32) for s in outs],
        in_specs=[pl.BlockSpec(memory_space=pltpu.SMEM)] + [vmem] * (n + len(ranked)),
        out_specs=[vmem] * len(outs),
        scratch_shapes=[pltpu.VMEM(s, jnp.float32) for s in scratch],
        compiler_params=pltpu.CompilerParams(vmem_limit_bytes=limit << 20),
        interpret=INTERPRET,
    )(idx, *full, *ranked)


def exact_dot(a, b):
    return jnp.dot(a, b, precision=HI, preferred_element_type=jnp.float32)


def project(x, rows):
    return lax.dot_general(x, rows, (((1,), (1,)), ((), ())), precision=HI,
                           preferred_element_type=jnp.float32)


def combine(row, values):
    total = None
    for c, v in zip(row, values):
        if c != 0.0:
            total = c * v if total is None else total + c * v
    return total


def layer_yz(src, dst, vec):
    def over_y(y, _):
        q = [src[zi, y] for zi in range(4)]
        for zi in range(4):
            v = vec[0, 2:3] * combine(D4[zi], q)
            if zi == 0:
                v = v + vec[0, 5:6] * (q[0] - pltpu.roll(q[3], 1, 0))
            if zi == 3:
                v = v + vec[0, 6:7] * (pltpu.roll(q[0], 15, 0) - q[3])
            dst[zi, y] = v
        return 0
    lax.fori_loop(0, 8, over_y, 0, unroll=True)

    def over_z(zi, _):
        q = [src[zi, y] for y in range(8)]
        for y in range(8):
            e, yi = 4 * (y // 4), y % 4
            v = vec[0, 1:2] * combine(D4[yi], q[e:e + 4])
            if yi == 0:
                v = v + vec[0, 3:4] * (q[y] - q[(y + 7) % 8])
            if yi == 3:
                v = v + vec[0, 4:5] * (q[(y + 1) % 8] - q[y])
            dst[zi, y] = dst[zi, y] + v
        return 0
    lax.fori_loop(0, 4, over_z, 0, unroll=True)


def every_fourth(h, xi, y, zi):
    if INTERPRET:
        return h[xi, y][zi::4]
    return h[xi, y, pl.ds(zi, 16, stride=4), :]


def rim_kernel(idx, h, vec, up, down, q, t, ends, m):
    pos = vec[0, 14:15] > 0.5
    for zi in range(4):
        def over_y(y, _):
            x = [every_fourth(h, xi, y, zi) for xi in range(4)]
            ql = jnp.where(pos, x[3], x[0])
            q[zi, y] = ql
            ends[zi, y] = x[0]
            ends[4 + zi, y] = x[3]
            v = 0.8 * ql
            for j in range(4):
                v = v + vec[0, 15 + j:16 + j] * x[j]
            up[pl.ds(pl.multiple_of((zi * 8 + y) * 16, 16), 16)] = v
            return 0
        lax.fori_loop(0, 8, over_y, 0, unroll=True)
    layer_yz(q, t, vec)
    right = lax.broadcasted_iota(jnp.int32, (16, 128), 1) >= 64

    def pack(n, _):
        zi, y = n // 8, n % 8
        at = pl.ds(pl.multiple_of(n * 16, 16), 16)
        tl = pltpu.roll(t[zi, y] + up[at], 64, 1)
        ql = q[zi, y]
        up[at] = jnp.where(right, ql, tl)
        down[at] = jnp.where(right, tl, ql)
        return 0
    lax.fori_loop(0, 32, pack, 0, unroll=8)
    m[...] = project(ends[...].reshape(1024, 128), vec[0, 24:32])
    for n in range(8):
        zi, out = n % 4, (down, up)[n // 4]
        out[512 + 8 * zi:520 + 8 * zi] = m[128 * n:128 * n + 128].T


def local_update(src, dst, vec):
    def over_y(y, _):
        q = [src[c, y] for c in range(16)]
        for xi in range(4):
            for zi in range(4):
                own = q[xi * 4 + zi]
                v = 0.8 * own + vec[0, 0:1] * combine(D4[xi], [q[j * 4 + zi] for j in range(4)])
                v = v + vec[0, 2:3] * combine(D4[zi], q[xi * 4:xi * 4 + 4])
                if zi == 0:
                    v = v + vec[0, 5:6] * (own - pltpu.roll(q[xi * 4 + 3], 1, 0))
                if zi == 3:
                    v = v + vec[0, 6:7] * (pltpu.roll(q[xi * 4], 15, 0) - own)
                if xi == 0:
                    v = v + vec[0, 7:8] * own
                if xi == 3:
                    v = v + vec[0, 8:9] * own
                dst[xi * 4 + zi, y] = v
        return 0
    lax.fori_loop(0, 8, over_y, 0, unroll=2)

    def over_c(c, _):
        q = [src[c, y] for y in range(8)]
        for y in range(8):
            e, yi = 4 * (y // 4), y % 4
            v = vec[0, 1:2] * combine(D4[yi], q[e:e + 4])
            if yi == 0:
                v = v + vec[0, 3:4] * (q[y] - q[(y + 7) % 8])
            if yi == 3:
                v = v + vec[0, 4:5] * (q[(y + 1) % 8] - q[y])
            dst[c, y] = dst[c, y] + v
        return 0
    lax.fori_loop(0, 16, over_c, 0, unroll=4)


def row_of_y():
    y = lax.broadcasted_iota(jnp.int32, (8, 128), 0)
    return (lax.broadcasted_iota(jnp.int32, (8, 128), 1) // 16 == y).astype(jnp.float32)


def local_kernel(idx, h, forcing, select, vec, tab0, tab1, twice, mom, force, first, once, m):
    spread = exact_dot(forcing[...].reshape(96, 64), select[...])
    here = row_of_y()
    force[...] = jnp.zeros_like(force)
    for f in range(3):
        for c in range(16):
            n = 8 * (f * 4 + c // 4)
            v = spread[n:n + 8, 128 * (c % 4):128 * (c % 4) + 128] * here
            force[5 * c + f + 1:5 * c + f + 2] = jnp.sum(v, axis=0, keepdims=True)
    for c in range(16):
        xi, zi = c // 4, c % 4

        def over_y(y, _):
            first[c, y] = every_fourth(h, xi, y, zi)
            return 0
        lax.fori_loop(0, 8, over_y, 0, unroll=True)
    local_update(first, once, vec)
    local_update(once, twice, vec)

    m[...] = project(first[...].reshape(2048, 128), tab0[0])
    m[...] = m[...] + project(once[...].reshape(2048, 128), tab1[0])
    for c in range(16):
        mom[c] = m[128 * c:128 * c + 128].T[32:48]


def z_before(q, lt):
    return jnp.where(lt[24:25] > 0.5, pltpu.roll(q, 113, 1), pltpu.roll(q, 1, 1))


def z_after(q, lt):
    return jnp.where(lt[25:26] > 0.5, pltpu.roll(q, 15, 1), pltpu.roll(q, 127, 1))


SHIFTS = (-3, -2, -1, 1, 2, 3)


def central_y(q, lt):
    total = None
    for n, s in enumerate(SHIFTS):
        term = lt[n:n + 1] * pltpu.roll(q, (-16 * s) % 128, 1)
        total = term if total is None else total + term
    return total


def one_sided(load, low, high, c, lt):
    xi, zi = c // 4, c % 4
    q = load(c)
    cx = combine([0.5 * v for v in D4[xi]], [load(j * 4 + zi) for j in range(4)])
    px = cx + 3.0 * (q - low(zi)) if xi == 0 else cx
    mx = cx + 3.0 * (high(zi) - q) if xi == 3 else cx
    cy = lt[32:33] * q
    for n, s in enumerate(SHIFTS):
        r = pltpu.roll(q, (-16 * s) % 128, 1)
        cy = cy + lt[26 + n:27 + n] * r
        if s == -1:
            py = lt[33:34] * (q - r)
        if s == 1:
            my = lt[34:35] * (r - q)
    cz = combine([0.5 * v for v in D4[zi]], [load(xi * 4 + j) for j in range(4)])
    pz = cz + 3.0 * (q - z_before(load(xi * 4 + 3), lt)) if zi == 0 else cz
    mz = cz + 3.0 * (z_after(load(xi * 4), lt) - q) if zi == 3 else cz
    return [px, mx, cy + py, cy + my, pz, mz]


CENTRAL = [[0.0 if i == j else 0.5 * D4[i][j] for j in range(4)] for i in range(4)]


def moment_kernel(idx, up, down, twice, moma, mix, lt, vec, tab2, tab1, pay, t2,
                  delta, yz, extra, mom, full, m, stack):
    right = lax.broadcasted_iota(jnp.int32, (16, 128), 1) >= 64
    pos = vec[0, 14:15]

    def unpack(n, _):
        at = pl.ds(pl.multiple_of(n * 16, 16), 16)
        u, d = up[at], down[at]
        zi, y = n // 8, n % 8
        delta[zi, y] = vec[0, 9:10] * jnp.where(right, u, d)
        extra[zi, y] = vec[0, 9:10] * pltpu.roll(jnp.where(right, d, u), 64, 1)
        return 0
    lax.fori_loop(0, 32, unpack, 0, unroll=8)
    layer_yz(delta, yz, vec)
    for xi in range(4):
        def over_n(n, _):
            zi, y = n // 8, n % 8
            v = twice[xi * 4 + zi, y] + vec[0, 10 + xi:11 + xi] * delta[zi, y]
            if xi in (0, 3):
                w = pos if xi == 0 else 1.0 - pos
                v = v + w * (yz[zi, y] + extra[zi, y])
            t2[xi * 4 + zi, y] = v
            return 0
        lax.fori_loop(0, 32, over_n, 0, unroll=8)

    m[...] = project(t2[...].reshape(2048, 128), tab2[0])
    d = delta[...].reshape(512, 128)
    m[0:512] = m[0:512] + project(d * pos, tab1[0])
    m[1536:2048] = m[1536:2048] + project(d * (1.0 - pos), tab1[0])
    for c in range(16):
        t = m[128 * c:128 * c + 128].T
        mom[c, 0:32] = t[0:32]
        mom[c, 32:48] = t[32:48] + moma[c]

    def load0(c):
        return mom[c, 32:40]

    for c in range(16):
        six = one_sided(load0, lambda zi: up[512 + 8 * zi:520 + 8 * zi],
                        lambda zi: down[512 + 8 * zi:520 + 8 * zi], c, lt)
        at = slice(128 * c, 128 * c + 128)
        stack[0:16, at] = mom[c, 32:48]
        for n in range(6):
            stack[16 + 8 * n:24 + 8 * n, at] = six[n]
    add = exact_dot(mix[...], stack[...])
    for c in range(16):
        at = slice(128 * c, 128 * c + 128)
        full[c, 0:32] = mom[c, 0:32] + add[0:32, at]
        full[c, 32:40] = add[32:40, at]
    for c in range(16):
        xi, zi = c // 4, c % 4
        r = combine(CENTRAL[xi], [full[j * 4 + zi, 8:16] for j in range(4)])
        r = r + central_y(full[c, 16:24], lt)
        r = r + combine(CENTRAL[zi], [full[xi * 4 + j, 24:32] for j in range(4)])
        if zi == 0:
            r = r - 1.5 * z_before(full[xi * 4 + 3, 24:32], lt)
        if zi == 3:
            r = r + 1.5 * z_after(full[xi * 4, 24:32], lt)
        pay[5 * c:5 * c + 5] = -r[0:5]
        pay[120 + 5 * c:125 + 5 * c] = full[c, 0:5]
        pay[200 + 5 * c:205 + 5 * c] = mom[c, 32:37]
        pay[280 + 5 * c:285 + 5 * c] = full[c, 32:37]
    for zi in range(4):
        pay[80 + 5 * zi:85 + 5 * zi] = full[zi, 8:13]
        pay[100 + 5 * zi:105 + 5 * zi] = full[12 + zi, 8:13]
        pay[360 + 5 * zi:365 + 5 * zi] = up[512 + 8 * zi:517 + 8 * zi]
        pay[380 + 5 * zi:385 + 5 * zi] = down[512 + 8 * zi:517 + 8 * zi]


def residual_kernel(idx, got, force, out, peers):
    t = got[0, 0:120] + got[1, 0:120] + got[2, 0:120] + got[3, 0:120]
    v = t[0:80] + force[...]
    for n in range(peers):
        out[n, 0:80] = v
        out[n, 80:120] = t[80:120]


def feq_kernel(idx, got, t2, lt, final, h2, low, s0, lo, hi, stack):
    def total(a, n):
        return got[0, a:a + n] + got[1, a:a + n] + got[2, a:a + n] + got[3, a:a + n]

    s0[...] = jnp.zeros_like(s0)
    lo[...] = jnp.zeros_like(lo)
    hi[...] = jnp.zeros_like(hi)
    for c in range(16):
        s0[c, 0:5] = total(200 + 5 * c, 5)
    for zi in range(4):
        lo[zi, 0:5] = total(360 + 5 * zi, 5)
        hi[zi, 0:5] = total(380 + 5 * zi, 5)
    low[...] = total(120, 80)
    pad = jnp.zeros((3, 128), jnp.float32)
    for c in range(16):
        z = jnp.concatenate([0.2 * total(280 + 5 * c, 5), pad], axis=0) + 0.16 * s0[c]
        six = one_sided(lambda k: s0[k], lambda zi: lo[zi], lambda zi: hi[zi], c, lt)
        for n, v in enumerate([z] + six):
            stack[8 * n:8 * n + 8, 128 * c:128 * c + 128] = v
    add = lax.dot_general(stack[...], final[0], (((0,), (0,)), ((), ())), precision=HI,
                          preferred_element_type=jnp.float32)
    h2[...] = t2[...] + add.reshape(16, 8, 16, 128)


def apply_operator(src, dst, lt, own=False):
    rows = slice(8, 16) if own else slice(0, 24)

    def before(k, add):
        if own:
            return src[k, 7:15] + src[k + add, 7:15] if add else src[k, 7:15]
        return pltpu.roll(src[k] + src[k + add] if add else src[k], 1, 0)

    def after(k, add):
        if own:
            return src[k, 9:17] + src[k + add, 9:17] if add else src[k, 9:17]
        return pltpu.roll(src[k] + src[k + add] if add else src[k], 23, 0)

    for zi in range(4):
        u = [src[16 + j * 4 + zi, rows] for j in range(4)]
        p = [src[j * 4 + zi, rows] + src[64 + j * 4 + zi, rows] for j in range(4)]
        for xi in range(4):
            du = combine(CENTRAL[xi], u)
            dp = combine(CENTRAL[xi], p)
            if xi == 0:
                du = du - 1.5 * before(28 + zi, 0)
                dp = dp - 1.5 * before(12 + zi, 64)
            if xi == 3:
                du = du + 1.5 * after(16 + zi, 0)
                dp = dp + 1.5 * after(zi, 64)
            dst[xi * 4 + zi] = du
            dst[16 + xi * 4 + zi] = 2.0 * u[xi] + dp
    for xi in range(4):
        u = [src[48 + xi * 4 + j, rows] for j in range(4)]
        p = [src[xi * 4 + j, rows] + src[64 + xi * 4 + j, rows] for j in range(4)]
        for zi in range(4):
            du = combine(CENTRAL[zi], u)
            dp = combine(CENTRAL[zi], p)
            if zi == 0:
                du = du - 1.5 * z_before(u[3], lt)
                dp = dp - 1.5 * z_before(p[3], lt)
            if zi == 3:
                du = du + 1.5 * z_after(u[0], lt)
                dp = dp + 1.5 * z_after(p[0], lt)
            dst[xi * 4 + zi] = dst[xi * 4 + zi] + du
            dst[48 + xi * 4 + zi] = 2.0 * u[zi] + dp

    def along_y(c, _):
        rho, u, t = src[c, rows], src[32 + c, rows], src[64 + c, rows]
        div = dst[c] + central_y(u, lt)
        dst[32 + c] = 2.0 * u + central_y(rho + t, lt)
        dst[c] = 2.0 * rho + div
        dst[64 + c] = 2.0 * t + div
        return 0
    lax.fori_loop(0, 16, along_y, 0, unroll=8)


def two_level(r, pe, co, lt):
    def over_f(f, _):
        tz = [[None, None] for _ in range(4)]
        for xi in range(4):
            q = [r[f * 16 + xi * 4 + zi] for zi in range(4)]
            for za in range(2):
                tz[xi][za] = combine(RT[za], q)
        for za in range(2):
            py = []
            for xa in range(2):
                t = combine(RT[xa], [tz[xi][za] for xi in range(4)])
                e0, e1 = lt[9:10] * t, lt[16:17] * t
                for s in SHIFTS:
                    rolled = pltpu.roll(t, (-16 * s) % 128, 1)
                    e0 = e0 + lt[9 + s:10 + s] * rolled
                    e1 = e1 + lt[16 + s:17 + s] * rolled
                co[f * 8 + xa * 4 + za * 2] = e0
                co[f * 8 + xa * 4 + za * 2 + 1] = e1
                py.append(lt[20:21] * e0 + lt[21:22] * e1)
            for xi in range(4):
                v = combine(PR[xi], py)
                for zi in range(4):
                    if PR[zi][za] == 0.0:
                        continue
                    at = f * 16 + xi * 4 + zi
                    if za == 0 or PR[zi][0] == 0.0:
                        pe[at] = PR[zi][za] * v
                    else:
                        pe[at] = pe[at] + PR[zi][za] * v
        return 0
    lax.fori_loop(0, 5, over_f, 0)


def coarse_products(co, lt):
    def at(f, xa, za, ya):
        return co[f * 8 + xa * 4 + za * 2 + ya]

    def own(q):
        return q[8:16]

    def dx(q, xa, za, ya):
        if xa == 0:
            v = q(1, za, ya)
            return 0.25 * (own(v) - own(pltpu.roll(v, 1, 0)))
        v = q(0, za, ya)
        return 0.25 * (own(pltpu.roll(v, 23, 0)) - own(v))

    def dz(q, xa, za, ya):
        v = own(q(xa, 1 - za, ya))
        if za == 0:
            return 0.25 * (v - z_before(v, lt))
        return 0.25 * (z_after(v, lt) - v)

    def dy(q, xa, za, ya):
        v = own(q(xa, za, 1 - ya))
        w = pltpu.roll(v, 64, 1)
        return 0.25 * (v - w) if ya == 0 else 0.25 * (w - v)

    up = jnp.zeros((8, 128), jnp.float32)
    low = jnp.zeros((8, 128), jnp.float32)
    for xa in range(2):
        for za in range(2):
            for ya in range(2):
                def field(f):
                    return lambda a, b, c: at(f, a, b, c)

                def pressure(a, b, c):
                    return at(0, a, b, c) + at(4, a, b, c)
                e = [own(at(f, xa, za, ya)) for f in range(5)]
                div = (dx(field(1), xa, za, ya) + dy(field(2), xa, za, ya)
                       + dz(field(3), xa, za, ya))
                g = [2.0 * e[0] + div, 2.0 * e[1] + dx(pressure, xa, za, ya),
                     2.0 * e[2] + dy(pressure, xa, za, ya),
                     2.0 * e[3] + dz(pressure, xa, za, ya), 2.0 * e[4] + div]
                for f in range(5):
                    up = up + e[f] * g[f]
                    low = low + g[f] * g[f]
    return up * lt[23:24], low * lt[23:24]


def fine_products(r, m, ar, am, lt, own):
    rows = slice(0, 8) if own else slice(8, 16)
    total = [jnp.zeros((8, 128), jnp.float32) for _ in range(6)]
    for xi in range(4):
        for zi in range(4):
            def over_f(f, acc):
                k = f * 16 + xi * 4 + zi
                a, b, c, d = r[k, 8:16], m[k, 8:16], ar[k, rows], am[k, rows]
                return (acc[0] + a * c, acc[1] + a * d + b * c, acc[2] + b * d,
                        acc[3] + c * c, acc[4] + c * d, acc[5] + d * d)
            zero = jnp.zeros((8, 128), jnp.float32)
            acc = lax.fori_loop(0, 5, over_f, (zero,) * 6, unroll=True)
            w = WEIGHTS[xi] * WEIGHTS[zi]
            total = [t + w * a for t, a in zip(total, acc)]
    return [t * lt[22:23] for t in total]


def pass_words(r, m, ar, am, pe, co, gram, lt, peers, own=False):
    two_level(r, pe, co, lt)
    apply_operator(pe, m, lt)
    apply_operator(r, ar, lt, own)
    apply_operator(m, am, lt, own)
    products = list(coarse_products(co, lt)) + fine_products(r, m, ar, am, lt, own)
    rows = jnp.concatenate([jnp.sum(p, axis=0, keepdims=True) for p in products], axis=0)
    for n in range(peers):
        gram[n] = rows


def pack_kernel(idx, mine, own, to_upper, to_lower):
    first = lax.broadcasted_iota(jnp.int32, (8, 128), 0) == 0
    last = lax.broadcasted_iota(jnp.int32, (8, 128), 0) == 7
    for f in range(5):
        for zi in range(4):
            high = mine[pl.ds(100 + 5 * zi + f, 8, stride=120), :]
            low = mine[pl.ds(80 + 5 * zi + f, 8, stride=120), :]
            for xi in range(4):
                c = xi * 4 + zi
                k = f * 16 + c
                v = mine[pl.ds(5 * c + f, 8, stride=120), :]
                if xi == 0:
                    v = v + 1.5 * jnp.where(first, 0.0, pltpu.roll(high, 1, 0))
                if xi == 3:
                    v = v - 1.5 * jnp.where(last, 0.0, pltpu.roll(low, 7, 0))
                own[k] = v
                to_upper[pl.ds(k, 6, stride=80), :] = v[2:8]
                to_lower[pl.ds(k, 6, stride=80), :] = v[0:6]
            to_upper[480 + f * 4 + zi:481 + f * 4 + zi] = high[7:8]
            to_lower[480 + f * 4 + zi:481 + f * 4 + zi] = low[0:1]


def first_pass_kernel(idx, lower, own, upper, edge_low, edge_high, after, lt, r, m, ar, am, pe, gram, co):
    zero = jnp.zeros((2, 128), jnp.float32)
    for f in range(5):
        for c in range(16):
            xi, zi = c // 4, c % 4
            k, e = f * 16 + c, f * 4 + zi
            r[k, 0:8] = jnp.concatenate([zero, lower[pl.ds(k, 6, stride=80), :]], axis=0)
            r[k, 8:16] = own[k]
            r[k, 16:24] = jnp.concatenate([upper[pl.ds(k, 6, stride=80), :], zero], axis=0)
            if xi == 0:
                r[k, 8:9] = r[k, 8:9] + 1.5 * lower[480 + e:481 + e]
                r[k, 16:17] = r[k, 16:17] + 1.5 * edge_high[480 + e:481 + e]
            if xi == 3:
                r[k, 15:16] = r[k, 15:16] - 1.5 * upper[480 + e:481 + e]
                r[k, 7:8] = r[k, 7:8] - 1.5 * edge_low[480 + e:481 + e]
    pass_words(r, m, ar, am, pe, co, gram, lt, gram.shape[0])


def step_sizes(sums, peers):
    s = sums[0]
    for n in range(1, peers):
        s = s + sums[n]
    s = jnp.broadcast_to(jnp.sum(s, axis=1, keepdims=True), (8, 128))
    a1 = s[0:1] / (s[1:2] + EPS)
    up = s[2:3] - a1 * s[3:4] + a1 * a1 * s[4:5]
    low = s[5:6] - 2.0 * a1 * s[6:7] + a1 * a1 * s[7:8]
    return a1, up / (low + EPS)


def next_pass_kernel(first, idx, sums, r, m, ar, am, pe, *rest):
    if first:
        lt, r2, m2, ar2, am2, pe2, acc2, gram, co = rest
    else:
        acc, lt, r2, m2, ar2, am2, pe2, acc2, gram, co = rest
    a1, a2 = step_sizes(sums, gram.shape[0])

    def over_k(k, _):
        q = r[k] - a1 * m[k]
        v = a1 * pe[k, 8:16] + a2 * q[8:16]
        acc2[k] = v if first else acc[k] + v
        r2[k] = q - a2 * (ar[k] - a1 * am[k])
        return 0
    lax.fori_loop(0, 80, over_k, 0, unroll=4)
    pass_words(r2, m2, ar2, am2, pe2, co, gram, lt, gram.shape[0], own=not first)


def third_pass_kernel(idx, sums, r, m, ar, am, pe, acc, lt, ro, mo, po, acc2, gram,
                      r2, m2, ar2, am2, pe2, co):
    next_pass_kernel(False, idx, sums, r, m, ar, am, pe, acc, lt, r2, m2, ar2, am2, pe2, acc2, gram, co)
    ro[...] = r2[:, 8:16]
    mo[...] = m2[:, 8:16]
    po[...] = pe2[:, 8:16]


def last_kernel(idx, sums, r, m, pe, acc, low, h2, select, ec, out, fields, change, stack, rows):
    a1, a2 = step_sizes(sums, sums.shape[0])

    def over_k(k, _):
        q = r[k] - a1 * m[k]
        change[pl.ds(pl.multiple_of(k * 8, 8), 8)] = acc[k] + a1 * pe[k] + a2 * q
        return 0
    lax.fori_loop(0, 80, over_k, 0, unroll=4)
    z = idx[1]
    stack[...] = jnp.zeros_like(stack)
    here = row_of_y()
    for c in range(16):
        for f in range(5):
            k = f * 16 + c
            d = change[pl.ds(k * 8 + z, 1)]
            stack[f:f + 1, 128 * c:128 * c + 128] = d
            n = 8 * (k // 4)
            rows[n:n + 8, 128 * (c % 4):128 * (c % 4) + 128] = (low[5 * c + f:5 * c + f + 1] + d) * here
    fields[...] = project(rows[...], select[...]).reshape(5, 4, 8, 64)
    add = lax.dot_general(stack[...], ec[0], (((0,), (0,)), ((), ())), precision=HI,
                          preferred_element_type=jnp.float32).reshape(16, 8, 16, 128)
    for c in range(16):
        xi, zi = c // 4, c % 4
        v = h2[c] + add[c]
        for y in range(8):
            out[xi, y, pl.ds(zi, 16, stride=4), :] = v[y]


def on_device(distribution, forcing):
    import functools
    tables = {k: jnp.asarray(v) for k, v in constant_tables().items()}
    spaces = lax.axis_size("space")
    blocks = spaces // 8
    idx = jnp.stack([lax.axis_index("vel"), lax.axis_index("space") % 8]).astype(jnp.int32)
    vec, lt = tables["vec"], tables["lanes"]
    wide = (16, 8, 16, 128)
    layer = (4, 8, 16, 128)

    def shifted(x, by):
        return lax.ppermute(x, "space", [(i, (i + by) % spaces) for i in range(spaces)])

    up, down = call(rim_kernel, "rims", idx, [distribution], [vec],
                    [(544, 128)] * 2, [layer, layer, (8, 8, 16, 128), (1024, 8)])
    up, down = shifted(up, 1), shifted(down, -1)
    twice, moma, force = call(local_kernel, "local", idx, [distribution, forcing, tables["select"]],
                              [vec, tables["tab0"], tables["tab1"]],
                              [wide, (16, 16, 128), (80, 128)], [wide, wide, (2048, 48)])
    pay, t2 = call(moment_kernel, "moments", idx, [up, down, twice, moma, tables["mix"], lt],
                   [vec, tables["tab2"], tables["tab1"]], [(400, 128), wide],
                   [layer, layer, layer, (16, 48, 128), (16, 40, 128), (2048, 48), (64, 2048)])
    got = lax.all_gather(pay, "vel")
    (res,) = call(lambda i, g, fo, o: residual_kernel(i, g, fo, o, 8), "residual", idx,
                  [got, force], [], [(8, 120, 128)])
    near = [[a * 8 + b for b in range(8)] for a in range(blocks)]
    far = [[a * 8 + b for a in range(blocks)] for b in range(8)]
    mine = lax.all_to_all(res, "space", 0, 0, axis_index_groups=near, tiled=True).reshape(960, 128)
    own_r, to_upper, to_lower = call(pack_kernel, "pack", idx, [mine], [],
                                     [(80, 8, 128), (500, 128), (500, 128)])
    lower, upper = shifted(to_upper, 8), shifted(to_lower, -8)
    h2, low = call(feq_kernel, "feq", idx, [got, t2, lt], [tables["final"]],
                   [wide, (80, 128)], [(16, 8, 128), (4, 8, 128), (4, 8, 128), (56, 2048)])

    def summed(gram):
        return lax.all_to_all(gram, "space", 0, 0, axis_index_groups=far, tiled=True)

    win, own, part = (80, 24, 128), (80, 8, 128), (blocks, 8, 128)
    co = (40, 24, 128)
    r, m, ar, am, pe, gram = call(first_pass_kernel, "pass1", idx,
                                  [lower, own_r, upper, to_lower, to_upper, low, lt], [],
                                  [win] * 5 + [part], [co])
    r, m, ar, am, pe, acc, gram = call(functools.partial(next_pass_kernel, True), "pass2", idx,
                                       [summed(gram), r, m, ar, am, pe, lt], [],
                                       [win] * 5 + [own, part], [co])
    r, m, pe, acc, gram = call(third_pass_kernel, "pass3", idx,
                               [summed(gram), r, m, ar, am, pe, acc, lt], [],
                               [own] * 4 + [part], [win, win, own, own, win, co])
    out, fields = call(last_kernel, "last", idx,
                       [summed(gram), r, m, pe, acc, low, h2, tables["select"]], [tables["ec"]],
                       [(4, 8, 64, 128), (5, 4, 8, 64)], [(640, 128), (8, 2048), (160, 512)])
    return out, fields


def solution(mesh):
    return jax.shard_map(
        on_device,
        mesh=mesh,
        in_specs=(P("space", None, None, "vel"), P(None, "space", None, None)),
        out_specs=(P("space", None, None, "vel"), P(None, "space", None, None)),
        check_vma=False,
    )
```

```python
import math

import jax
import jax.numpy as jnp
import numpy as np
from jax import lax
from jax.experimental import pallas as pl
from jax.experimental.pallas import tpu as pltpu
from jax.sharding import PartitionSpec as P

INTERPRET = False
DT = 0.02
RF = 0.4472135954999579
POINTS = [-1.0, -RF, RF, 1.0]
WEIGHTS = [1.0 / 6.0, 5.0 / 6.0, 5.0 / 6.0, 1.0 / 6.0]
EPS = 1e-6
HI = lax.Precision.HIGHEST


def lagrange_table(points):
    n = len(points)
    bary = []
    for i in range(n):
        product = 1.0
        for j in range(n):
            if j != i:
                product *= points[i] - points[j]
        bary.append(1.0 / product)
    rows = [[0.0] * n for _ in range(n)]
    for i in range(n):
        for j in range(n):
            if j != i:
                rows[i][j] = bary[j] / bary[i] / (points[i] - points[j])
        rows[i][i] = -sum(rows[i])
    return rows


D4 = lagrange_table(POINTS)
for _i in (1, 2):
    D4[_i][_i] = 0.0
PR = [[(1.0 - x) / 2.0, (1.0 + x) / 2.0] for x in POINTS]
RT = [[WEIGHTS[i] * PR[i][a] for i in range(4)] for a in range(2)]


def constant_tables():
    k = np.arange(512)
    b, j = k // 128, k % 128
    s = j // 64
    m = ((b * 64 + j % 64) * 5179 + 7) % 16384
    xi = np.stack([16 * s + m // 1024, (m // 32) % 32, m % 32]).astype(np.float64)
    xi = -4.0 + 0.25 * (xi + 0.5)
    sq = (xi * xi).sum(0)
    e = math.pi ** (-1.5) * np.exp(-sq)
    x, y, z = xi
    phi = np.stack(
        [np.ones(512), x, y, z, 2 * sq / 3 - 1, 2 * (x * x - sq / 3), 2 * (y * y - sq / 3),
         2 * x * y, 2 * x * z, 2 * y * z, x * (sq - 2.5), y * (sq - 2.5), z * (sq - 2.5)]
    )
    p = phi[0] + phi[4]
    zero = np.zeros(512)

    def eight(rows):
        return np.stack(list(rows) + [zero] * (8 - len(rows)))

    low = eight(phi[:5])
    along_x = eight([phi[1], p + phi[5], phi[7], phi[8], phi[1] + phi[10]])
    along_y = eight([phi[2], phi[7], p + phi[6], phi[9], phi[2] + phi[11]])
    along_z = eight([phi[3], phi[8], phi[9], p - phi[5] - phi[6], phi[3] + phi[12]])
    rows32 = np.concatenate([low, along_x, along_y, along_z])
    ec = eight([e, 2 * x * e, 2 * y * e, 2 * z * e, e * (sq - 1.5)])
    pos, neg = np.maximum(xi, 0.0), np.minimum(xi, 0.0)

    def per_rank(rows):
        return np.stack([rows[:, r * 128:(r + 1) * 128] for r in range(4)]).astype(np.float32)

    ispos = (x > 0).astype(np.float64)
    ax = np.abs(x)
    d4 = np.array(D4)
    vec = [-DT * 0.5 * x, -DT * 0.5 * y, -DT * 0.5 * z,
           -3 * DT * pos[1], -3 * DT * neg[1], -3 * DT * pos[2], -3 * DT * neg[2],
           -3 * DT * pos[0], 3 * DT * neg[0], 3 * DT * ax]
    for i in range(4):
        kap = -DT * 0.5 * x * np.where(ispos > 0, d4[i][0], d4[i][3])
        if i == 0:
            kap = kap + ispos * (0.8 - 3 * DT * ax)
        if i == 3:
            kap = kap + (1 - ispos) * (0.8 - 3 * DT * ax)
        vec.append(kap)
    vec.append(ispos)
    for jj in range(4):
        vec.append(-DT * 0.5 * x * np.where(ispos > 0, d4[3][jj], d4[0][jj]))
    while len(vec) < 24:
        vec.append(zero)
    vec = per_rank(np.concatenate([np.stack(vec), low]))

    def moment_rows(start, rows, height):
        out = np.zeros((height, 512))
        out[start:start + len(rows)] = rows
        return per_rank(out)

    tab2 = moment_rows(0, rows32, 48)
    tab1 = moment_rows(40, low, 48)
    tab0 = moment_rows(32, low, 48)
    select = np.zeros((64, 512))
    for n in range(4):
        for la in range(128):
            select[4 * (la % 16) + n, 128 * n + la] = 1.0
    g = rows32 @ ec.T
    g5 = g[:8]
    mix = np.zeros((40, 64))
    mix[:32, 0:8] = 0.16 * g + 0.04 * g @ g5
    mix[:32, 8:16] = 0.2 * g
    mix[32:, 0:8] = 0.2 * g5
    mix[32:, 8:16] = np.eye(8)
    final = [ec]
    for d in range(3):
        for i, part in enumerate((pos[d], neg[d])):
            c0 = 16 + 16 * d + 8 * i
            mix[:32, c0:c0 + 8] = -0.2 * DT * (rows32 * part) @ ec.T
            final.append(-0.2 * DT * ec * part)
    final = per_rank(np.concatenate(final))
    lane = np.arange(128)
    yi, ze = (lane // 16) % 4, lane % 16
    rows = []
    shifts = (-3, -2, -1, 1, 2, 3)

    def entry(table, sft):
        return np.array([table(i, i + sft) if 0 <= i + sft < 4 else 0.0 for i in yi])

    for sft in shifts:
        c = entry(lambda i, q: 0.5 * D4[i][q], sft)
        if sft == -1:
            c = c - 1.5 * (yi == 0)
        if sft == 1:
            c = c + 1.5 * (yi == 3)
        rows.append(c)
    for a in range(2):
        for sft in range(-3, 4):
            rows.append(entry(lambda i, q: RT[a][q], sft))
    rows += [np.array([PR[i][0] for i in yi]), np.array([PR[i][1] for i in yi])]
    rows += [np.array([WEIGHTS[i] for i in yi]), (yi == 0) * 1.0, (ze == 0) * 1.0, (ze == 15) * 1.0]
    for sft in shifts:
        rows.append(entry(lambda i, q: 0.5 * D4[i][q], sft))
    rows += [entry(lambda i, q: 0.5 * D4[i][q], 0), 3.0 * (yi == 0), 3.0 * (yi == 3)]
    while len(rows) < 40:
        rows.append(np.zeros(128))
    lanes = np.stack(rows).astype(np.float32)
    return dict(vec=vec, tab2=tab2, tab1=tab1, tab0=tab0, mix=mix.astype(np.float32),
                final=final, lanes=lanes, ec=per_rank(ec), select=select.astype(np.float32))


def call(kernel, name, idx, full, ranked, outs, scratch=(), limit=24):
    n = len(full)

    def body(idx, *refs):
        rank = [r.at[pl.ds(idx[0], 1)] for r in refs[n:n + len(ranked)]]
        kernel(idx, *refs[:n], *rank, *refs[n + len(ranked):])

    vmem = pl.BlockSpec(memory_space=pltpu.VMEM)
    return pl.pallas_call(
        body,
        name=name,
        out_shape=[jax.ShapeDtypeStruct(s, jnp.float32) for s in outs],
        in_specs=[pl.BlockSpec(memory_space=pltpu.SMEM)] + [vmem] * (n + len(ranked)),
        out_specs=[vmem] * len(outs),
        scratch_shapes=[pltpu.VMEM(s, jnp.float32) for s in scratch],
        compiler_params=pltpu.CompilerParams(vmem_limit_bytes=limit << 20),
        interpret=INTERPRET,
    )(idx, *full, *ranked)


def exact_dot(a, b):
    return jnp.dot(a, b, precision=HI, preferred_element_type=jnp.float32)


def project(x, rows):
    return lax.dot_general(x, rows, (((1,), (1,)), ((), ())), precision=HI,
                           preferred_element_type=jnp.float32)


def combine(row, values):
    total = None
    for c, v in zip(row, values):
        if c != 0.0:
            total = c * v if total is None else total + c * v
    return total


def layer_yz(src, dst, vec):
    def over_y(y, _):
        q = [src[zi, y] for zi in range(4)]
        for zi in range(4):
            v = vec[0, 2:3] * combine(D4[zi], q)
            if zi == 0:
                v = v + vec[0, 5:6] * (q[0] - pltpu.roll(q[3], 1, 0))
            if zi == 3:
                v = v + vec[0, 6:7] * (pltpu.roll(q[0], 15, 0) - q[3])
            dst[zi, y] = v
        return 0
    lax.fori_loop(0, 8, over_y, 0, unroll=True)

    def over_z(zi, _):
        q = [src[zi, y] for y in range(8)]
        for y in range(8):
            e, yi = 4 * (y // 4), y % 4
            v = vec[0, 1:2] * combine(D4[yi], q[e:e + 4])
            if yi == 0:
                v = v + vec[0, 3:4] * (q[y] - q[(y + 7) % 8])
            if yi == 3:
                v = v + vec[0, 4:5] * (q[(y + 1) % 8] - q[y])
            dst[zi, y] = dst[zi, y] + v
        return 0
    lax.fori_loop(0, 4, over_z, 0, unroll=True)


def every_fourth(h, xi, y, zi):
    if INTERPRET:
        return h[xi, y][zi::4]
    return h[xi, y, pl.ds(zi, 16, stride=4), :]


def rim_kernel(idx, h, vec, up, down, q, t, ends, m):
    pos = vec[0, 14:15] > 0.5
    for zi in range(4):
        def over_y(y, _):
            x = [every_fourth(h, xi, y, zi) for xi in range(4)]
            ql = jnp.where(pos, x[3], x[0])
            q[zi, y] = ql
            ends[zi, y] = x[0]
            ends[4 + zi, y] = x[3]
            v = 0.8 * ql
            for j in range(4):
                v = v + vec[0, 15 + j:16 + j] * x[j]
            up[pl.ds(pl.multiple_of((zi * 8 + y) * 16, 16), 16)] = v
            return 0
        lax.fori_loop(0, 8, over_y, 0, unroll=True)
    layer_yz(q, t, vec)
    right = lax.broadcasted_iota(jnp.int32, (16, 128), 1) >= 64

    def pack(n, _):
        zi, y = n // 8, n % 8
        at = pl.ds(pl.multiple_of(n * 16, 16), 16)
        tl = pltpu.roll(t[zi, y] + up[at], 64, 1)
        ql = q[zi, y]
        up[at] = jnp.where(right, ql, tl)
        down[at] = jnp.where(right, tl, ql)
        return 0
    lax.fori_loop(0, 32, pack, 0, unroll=8)
    m[...] = project(ends[...].reshape(1024, 128), vec[0, 24:32])
    for n in range(8):
        zi, out = n % 4, (down, up)[n // 4]
        out[512 + 8 * zi:520 + 8 * zi] = m[128 * n:128 * n + 128].T


def local_update(src, dst, vec):
    def over_y(y, _):
        q = [src[c, y] for c in range(16)]
        for xi in range(4):
            for zi in range(4):
                own = q[xi * 4 + zi]
                v = 0.8 * own + vec[0, 0:1] * combine(D4[xi], [q[j * 4 + zi] for j in range(4)])
                v = v + vec[0, 2:3] * combine(D4[zi], q[xi * 4:xi * 4 + 4])
                if zi == 0:
                    v = v + vec[0, 5:6] * (own - pltpu.roll(q[xi * 4 + 3], 1, 0))
                if zi == 3:
                    v = v + vec[0, 6:7] * (pltpu.roll(q[xi * 4], 15, 0) - own)
                if xi == 0:
                    v = v + vec[0, 7:8] * own
                if xi == 3:
                    v = v + vec[0, 8:9] * own
                dst[xi * 4 + zi, y] = v
        return 0
    lax.fori_loop(0, 8, over_y, 0, unroll=2)

    def over_c(c, _):
        q = [src[c, y] for y in range(8)]
        for y in range(8):
            e, yi = 4 * (y // 4), y % 4
            v = vec[0, 1:2] * combine(D4[yi], q[e:e + 4])
            if yi == 0:
                v = v + vec[0, 3:4] * (q[y] - q[(y + 7) % 8])
            if yi == 3:
                v = v + vec[0, 4:5] * (q[(y + 1) % 8] - q[y])
            dst[c, y] = dst[c, y] + v
        return 0
    lax.fori_loop(0, 16, over_c, 0, unroll=4)


def row_of_y():
    y = lax.broadcasted_iota(jnp.int32, (8, 128), 0)
    return (lax.broadcasted_iota(jnp.int32, (8, 128), 1) // 16 == y).astype(jnp.float32)


def local_kernel(idx, h, forcing, select, vec, tab0, tab1, twice, mom, force, first, once, m):
    spread = exact_dot(forcing[...].reshape(96, 64), select[...])
    here = row_of_y()
    force[...] = jnp.zeros_like(force)
    for f in range(3):
        for c in range(16):
            n = 8 * (f * 4 + c // 4)
            v = spread[n:n + 8, 128 * (c % 4):128 * (c % 4) + 128] * here
            at = 5 * (c // 4) + f + 1
            force[c % 4, at:at + 1] = jnp.sum(v, axis=0, keepdims=True)
    for c in range(16):
        xi, zi = c // 4, c % 4

        def over_y(y, _):
            first[c, y] = every_fourth(h, xi, y, zi)
            return 0
        lax.fori_loop(0, 8, over_y, 0, unroll=True)
    local_update(first, once, vec)
    local_update(once, twice, vec)

    m[...] = project(first[...].reshape(2048, 128), tab0[0])
    m[...] = m[...] + project(once[...].reshape(2048, 128), tab1[0])
    for c in range(16):
        mom[c] = m[128 * c:128 * c + 128].T[32:48]


def z_before(q, lt):
    return jnp.where(lt[24:25] > 0.5, pltpu.roll(q, 113, 1), pltpu.roll(q, 1, 1))


def z_after(q, lt):
    return jnp.where(lt[25:26] > 0.5, pltpu.roll(q, 15, 1), pltpu.roll(q, 127, 1))


SHIFTS = (-3, -2, -1, 1, 2, 3)


def central_y(q, lt):
    total = None
    for n, s in enumerate(SHIFTS):
        term = lt[n:n + 1] * pltpu.roll(q, (-16 * s) % 128, 1)
        total = term if total is None else total + term
    return total


def one_sided(load, low, high, c, lt):
    xi, zi = c // 4, c % 4
    q = load(c)
    cx = combine([0.5 * v for v in D4[xi]], [load(j * 4 + zi) for j in range(4)])
    px = cx + 3.0 * (q - low(zi)) if xi == 0 else cx
    mx = cx + 3.0 * (high(zi) - q) if xi == 3 else cx
    cy = lt[32:33] * q
    for n, s in enumerate(SHIFTS):
        r = pltpu.roll(q, (-16 * s) % 128, 1)
        cy = cy + lt[26 + n:27 + n] * r
        if s == -1:
            py = lt[33:34] * (q - r)
        if s == 1:
            my = lt[34:35] * (r - q)
    cz = combine([0.5 * v for v in D4[zi]], [load(xi * 4 + j) for j in range(4)])
    pz = cz + 3.0 * (q - z_before(load(xi * 4 + 3), lt)) if zi == 0 else cz
    mz = cz + 3.0 * (z_after(load(xi * 4), lt) - q) if zi == 3 else cz
    return [px, mx, cy + py, cy + my, pz, mz]


CENTRAL = [[0.0 if i == j else 0.5 * D4[i][j] for j in range(4)] for i in range(4)]


def moment_kernel(idx, up, down, twice, moma, mix, lt, vec, tab2, tab1, pay, rest, t2,
                  delta, yz, extra, mom, full, m, stack):
    right = lax.broadcasted_iota(jnp.int32, (16, 128), 1) >= 64
    pos = vec[0, 14:15]

    def unpack(n, _):
        at = pl.ds(pl.multiple_of(n * 16, 16), 16)
        u, d = up[at], down[at]
        zi, y = n // 8, n % 8
        delta[zi, y] = vec[0, 9:10] * jnp.where(right, u, d)
        extra[zi, y] = vec[0, 9:10] * pltpu.roll(jnp.where(right, d, u), 64, 1)
        return 0
    lax.fori_loop(0, 32, unpack, 0, unroll=8)
    layer_yz(delta, yz, vec)
    for xi in range(4):
        def over_n(n, _):
            zi, y = n // 8, n % 8
            v = twice[xi * 4 + zi, y] + vec[0, 10 + xi:11 + xi] * delta[zi, y]
            if xi in (0, 3):
                w = pos if xi == 0 else 1.0 - pos
                v = v + w * (yz[zi, y] + extra[zi, y])
            t2[xi * 4 + zi, y] = v
            return 0
        lax.fori_loop(0, 32, over_n, 0, unroll=8)

    m[...] = project(t2[...].reshape(2048, 128), tab2[0])
    d = delta[...].reshape(512, 128)
    m[0:512] = m[0:512] + project(d * pos, tab1[0])
    m[1536:2048] = m[1536:2048] + project(d * (1.0 - pos), tab1[0])
    for c in range(16):
        t = m[128 * c:128 * c + 128].T
        mom[c, 0:32] = t[0:32]
        mom[c, 32:48] = t[32:48] + moma[c]

    def load0(c):
        return mom[c, 32:40]

    for c in range(16):
        six = one_sided(load0, lambda zi: up[512 + 8 * zi:520 + 8 * zi],
                        lambda zi: down[512 + 8 * zi:520 + 8 * zi], c, lt)
        at = slice(128 * c, 128 * c + 128)
        stack[0:16, at] = mom[c, 32:48]
        for n in range(6):
            stack[16 + 8 * n:24 + 8 * n, at] = six[n]
    add = exact_dot(mix[...], stack[...])
    for c in range(16):
        at = slice(128 * c, 128 * c + 128)
        full[c, 0:32] = mom[c, 0:32] + add[0:32, at]
        full[c, 32:40] = add[32:40, at]
    for c in range(16):
        xi, zi = c // 4, c % 4
        r = combine(CENTRAL[xi], [full[j * 4 + zi, 8:16] for j in range(4)])
        r = r + central_y(full[c, 16:24], lt)
        r = r + combine(CENTRAL[zi], [full[xi * 4 + j, 24:32] for j in range(4)])
        if zi == 0:
            r = r - 1.5 * z_before(full[xi * 4 + 3, 24:32], lt)
        if zi == 3:
            r = r + 1.5 * z_after(full[xi * 4, 24:32], lt)
        pay[zi, 5 * xi:5 * xi + 5] = -r[0:5]
        rest[5 * c:5 * c + 5] = full[c, 0:5]
        rest[80 + 5 * c:85 + 5 * c] = mom[c, 32:37]
        rest[160 + 5 * c:165 + 5 * c] = full[c, 32:37]
    for zi in range(4):
        pay[zi, 20:25] = full[zi, 8:13]
        pay[zi, 25:30] = full[12 + zi, 8:13]
        rest[240 + 5 * zi:245 + 5 * zi] = up[512 + 8 * zi:517 + 8 * zi]
        rest[260 + 5 * zi:265 + 5 * zi] = down[512 + 8 * zi:517 + 8 * zi]


def residual_kernel(idx, got, force, out):
    t = got[0] + got[1] + got[2] + got[3]
    v = t[0:20] + force[idx[0]]
    for n in range(8):
        out[n, 0:20] = v
        out[n, 20:30] = t[20:30]


def feq_kernel(idx, got, t2, lt, final, h2, low, s0, lo, hi, stack):
    def total(a, n):
        return got[0, a:a + n] + got[1, a:a + n] + got[2, a:a + n] + got[3, a:a + n]

    s0[...] = jnp.zeros_like(s0)
    lo[...] = jnp.zeros_like(lo)
    hi[...] = jnp.zeros_like(hi)
    for c in range(16):
        s0[c, 0:5] = total(80 + 5 * c, 5)
    for zi in range(4):
        lo[zi, 0:5] = total(240 + 5 * zi, 5)
        hi[zi, 0:5] = total(260 + 5 * zi, 5)
    low[...] = total(0, 80)
    pad = jnp.zeros((3, 128), jnp.float32)
    for c in range(16):
        z = jnp.concatenate([0.2 * total(160 + 5 * c, 5), pad], axis=0) + 0.16 * s0[c]
        six = one_sided(lambda k: s0[k], lambda zi: lo[zi], lambda zi: hi[zi], c, lt)
        for n, v in enumerate([z] + six):
            stack[8 * n:8 * n + 8, 128 * c:128 * c + 128] = v
    add = lax.dot_general(stack[...], final[0], (((0,), (0,)), ((), ())), precision=HI,
                          preferred_element_type=jnp.float32)
    h2[...] = t2[...] + add.reshape(16, 8, 16, 128)


def apply_operator(src, dst, lt, own=False):
    rows = slice(8, 16) if own else slice(0, 24)

    def before(k, add):
        if own:
            return src[k, 7:15] + src[k + add, 7:15] if add else src[k, 7:15]
        return pltpu.roll(src[k] + src[k + add] if add else src[k], 1, 0)

    def after(k, add):
        if own:
            return src[k, 9:17] + src[k + add, 9:17] if add else src[k, 9:17]
        return pltpu.roll(src[k] + src[k + add] if add else src[k], 23, 0)

    for zi in range(4):
        u = [src[16 + j * 4 + zi, rows] for j in range(4)]
        p = [src[j * 4 + zi, rows] + src[64 + j * 4 + zi, rows] for j in range(4)]
        for xi in range(4):
            du = combine(CENTRAL[xi], u)
            dp = combine(CENTRAL[xi], p)
            if xi == 0:
                du = du - 1.5 * before(28 + zi, 0)
                dp = dp - 1.5 * before(12 + zi, 64)
            if xi == 3:
                du = du + 1.5 * after(16 + zi, 0)
                dp = dp + 1.5 * after(zi, 64)
            dst[xi * 4 + zi] = du
            dst[16 + xi * 4 + zi] = 2.0 * u[xi] + dp
    for xi in range(4):
        u = [src[48 + xi * 4 + j, rows] for j in range(4)]
        p = [src[xi * 4 + j, rows] + src[64 + xi * 4 + j, rows] for j in range(4)]
        for zi in range(4):
            du = combine(CENTRAL[zi], u)
            dp = combine(CENTRAL[zi], p)
            if zi == 0:
                du = du - 1.5 * z_before(u[3], lt)
                dp = dp - 1.5 * z_before(p[3], lt)
            if zi == 3:
                du = du + 1.5 * z_after(u[0], lt)
                dp = dp + 1.5 * z_after(p[0], lt)
            dst[xi * 4 + zi] = dst[xi * 4 + zi] + du
            dst[48 + xi * 4 + zi] = 2.0 * u[zi] + dp

    def along_y(c, _):
        rho, u, t = src[c, rows], src[32 + c, rows], src[64 + c, rows]
        div = dst[c] + central_y(u, lt)
        dst[32 + c] = 2.0 * u + central_y(rho + t, lt)
        dst[c] = 2.0 * rho + div
        dst[64 + c] = 2.0 * t + div
        return 0
    lax.fori_loop(0, 16, along_y, 0, unroll=8)


def two_level(r, pe, co, lt):
    def over_f(f, _):
        tz = [[None, None] for _ in range(4)]
        for xi in range(4):
            q = [r[f * 16 + xi * 4 + zi] for zi in range(4)]
            for za in range(2):
                tz[xi][za] = combine(RT[za], q)
        for za in range(2):
            py = []
            for xa in range(2):
                t = combine(RT[xa], [tz[xi][za] for xi in range(4)])
                e0, e1 = lt[9:10] * t, lt[16:17] * t
                for s in SHIFTS:
                    rolled = pltpu.roll(t, (-16 * s) % 128, 1)
                    e0 = e0 + lt[9 + s:10 + s] * rolled
                    e1 = e1 + lt[16 + s:17 + s] * rolled
                co[f * 8 + xa * 4 + za * 2] = e0
                co[f * 8 + xa * 4 + za * 2 + 1] = e1
                py.append(lt[20:21] * e0 + lt[21:22] * e1)
            for xi in range(4):
                v = combine(PR[xi], py)
                for zi in range(4):
                    if PR[zi][za] == 0.0:
                        continue
                    at = f * 16 + xi * 4 + zi
                    if za == 0 or PR[zi][0] == 0.0:
                        pe[at] = PR[zi][za] * v
                    else:
                        pe[at] = pe[at] + PR[zi][za] * v
        return 0
    lax.fori_loop(0, 5, over_f, 0)


def coarse_products(co, lt):
    def at(f, xa, za, ya):
        return co[f * 8 + xa * 4 + za * 2 + ya]

    def own(q):
        return q[8:16]

    def dx(q, xa, za, ya):
        if xa == 0:
            v = q(1, za, ya)
            return 0.25 * (own(v) - own(pltpu.roll(v, 1, 0)))
        v = q(0, za, ya)
        return 0.25 * (own(pltpu.roll(v, 23, 0)) - own(v))

    def dz(q, xa, za, ya):
        v = own(q(xa, 1 - za, ya))
        if za == 0:
            return 0.25 * (v - z_before(v, lt))
        return 0.25 * (z_after(v, lt) - v)

    def dy(q, xa, za, ya):
        v = own(q(xa, za, 1 - ya))
        w = pltpu.roll(v, 64, 1)
        return 0.25 * (v - w) if ya == 0 else 0.25 * (w - v)

    up = jnp.zeros((8, 128), jnp.float32)
    low = jnp.zeros((8, 128), jnp.float32)
    for xa in range(2):
        for za in range(2):
            for ya in range(2):
                def field(f):
                    return lambda a, b, c: at(f, a, b, c)

                def pressure(a, b, c):
                    return at(0, a, b, c) + at(4, a, b, c)
                e = [own(at(f, xa, za, ya)) for f in range(5)]
                div = (dx(field(1), xa, za, ya) + dy(field(2), xa, za, ya)
                       + dz(field(3), xa, za, ya))
                g = [2.0 * e[0] + div, 2.0 * e[1] + dx(pressure, xa, za, ya),
                     2.0 * e[2] + dy(pressure, xa, za, ya),
                     2.0 * e[3] + dz(pressure, xa, za, ya), 2.0 * e[4] + div]
                for f in range(5):
                    up = up + e[f] * g[f]
                    low = low + g[f] * g[f]
    return up * lt[23:24], low * lt[23:24]


def fine_products(r, m, ar, am, lt, own):
    rows = slice(0, 8) if own else slice(8, 16)
    total = [jnp.zeros((8, 128), jnp.float32) for _ in range(6)]
    for xi in range(4):
        for zi in range(4):
            def over_f(f, acc):
                k = f * 16 + xi * 4 + zi
                a, b, c, d = r[k, 8:16], m[k, 8:16], ar[k, rows], am[k, rows]
                return (acc[0] + a * c, acc[1] + a * d + b * c, acc[2] + b * d,
                        acc[3] + c * c, acc[4] + c * d, acc[5] + d * d)
            zero = jnp.zeros((8, 128), jnp.float32)
            acc = lax.fori_loop(0, 5, over_f, (zero,) * 6, unroll=True)
            w = WEIGHTS[xi] * WEIGHTS[zi]
            total = [t + w * a for t, a in zip(total, acc)]
    return [t * lt[22:23] for t in total]


def pass_words(r, m, ar, am, pe, co, gram, lt, peers, own=False):
    two_level(r, pe, co, lt)
    apply_operator(pe, m, lt)
    apply_operator(r, ar, lt, own)
    apply_operator(m, am, lt, own)
    products = list(coarse_products(co, lt)) + fine_products(r, m, ar, am, lt, own)
    rows = jnp.concatenate([jnp.sum(p, axis=0, keepdims=True) for p in products], axis=0)
    for n in range(peers):
        gram[n] = rows


def pack_kernel(idx, mine, own, to_upper, to_lower):
    first = lax.broadcasted_iota(jnp.int32, (8, 128), 0) == 0
    last = lax.broadcasted_iota(jnp.int32, (8, 128), 0) == 7
    for f in range(5):
        low = mine[pl.ds(20 + f, 8, stride=30), :]
        high = mine[pl.ds(25 + f, 8, stride=30), :]
        for xi in range(4):
            k = f * 4 + xi
            v = mine[pl.ds(5 * xi + f, 8, stride=30), :]
            if xi == 0:
                v = v + 1.5 * jnp.where(first, 0.0, pltpu.roll(high, 1, 0))
            if xi == 3:
                v = v - 1.5 * jnp.where(last, 0.0, pltpu.roll(low, 7, 0))
            own[k] = v
            to_upper[pl.ds(k, 6, stride=20), :] = v[2:8]
            to_lower[pl.ds(k, 6, stride=20), :] = v[0:6]
        to_upper[120 + f:121 + f] = high[7:8]
        to_lower[120 + f:121 + f] = low[0:1]


def window_kernel(idx, lower, own, upper, edge_low, edge_high, after, win):
    zero = jnp.zeros((2, 128), jnp.float32)
    for f in range(5):
        e = 120 + f
        for xi in range(4):
            k = f * 4 + xi
            win[k, 0:8] = jnp.concatenate([zero, lower[pl.ds(k, 6, stride=20), :]], axis=0)
            win[k, 8:16] = own[k]
            win[k, 16:24] = jnp.concatenate([upper[pl.ds(k, 6, stride=20), :], zero], axis=0)
            if xi == 0:
                win[k, 8:9] = win[k, 8:9] + 1.5 * lower[e:e + 1]
                win[k, 16:17] = win[k, 16:17] + 1.5 * edge_high[e:e + 1]
            if xi == 3:
                win[k, 15:16] = win[k, 15:16] - 1.5 * upper[e:e + 1]
                win[k, 7:8] = win[k, 7:8] - 1.5 * edge_low[e:e + 1]


def first_pass_kernel(idx, quarters, lt, r, m, ar, am, pe, gram, co):
    for f in range(5):
        for xi in range(4):
            for zi in range(4):
                r[f * 16 + xi * 4 + zi] = quarters[zi, f * 4 + xi]
    pass_words(r, m, ar, am, pe, co, gram, lt, gram.shape[0])


def step_sizes(sums, peers):
    s = sums[0]
    for n in range(1, peers):
        s = s + sums[n]
    s = jnp.broadcast_to(jnp.sum(s, axis=1, keepdims=True), (8, 128))
    a1 = s[0:1] / (s[1:2] + EPS)
    up = s[2:3] - a1 * s[3:4] + a1 * a1 * s[4:5]
    low = s[5:6] - 2.0 * a1 * s[6:7] + a1 * a1 * s[7:8]
    return a1, up / (low + EPS)


def next_pass_kernel(first, idx, sums, r, m, ar, am, pe, *rest):
    if first:
        lt, r2, m2, ar2, am2, pe2, acc2, gram, co = rest
    else:
        acc, lt, r2, m2, ar2, am2, pe2, acc2, gram, co = rest
    a1, a2 = step_sizes(sums, gram.shape[0])

    def over_k(k, _):
        q = r[k] - a1 * m[k]
        v = a1 * pe[k, 8:16] + a2 * q[8:16]
        acc2[k] = v if first else acc[k] + v
        r2[k] = q - a2 * (ar[k] - a1 * am[k])
        return 0
    lax.fori_loop(0, 80, over_k, 0, unroll=4)
    pass_words(r2, m2, ar2, am2, pe2, co, gram, lt, gram.shape[0], own=not first)


def third_pass_kernel(idx, sums, r, m, ar, am, pe, acc, lt, ro, mo, po, acc2, gram,
                      r2, m2, ar2, am2, pe2, co):
    next_pass_kernel(False, idx, sums, r, m, ar, am, pe, acc, lt, r2, m2, ar2, am2, pe2, acc2, gram, co)
    ro[...] = r2[:, 8:16]
    mo[...] = m2[:, 8:16]
    po[...] = pe2[:, 8:16]


def last_kernel(idx, sums, r, m, pe, acc, low, h2, select, ec, out, fields, change, stack, rows):
    a1, a2 = step_sizes(sums, sums.shape[0])

    def over_k(k, _):
        q = r[k] - a1 * m[k]
        change[pl.ds(pl.multiple_of(k * 8, 8), 8)] = acc[k] + a1 * pe[k] + a2 * q
        return 0
    lax.fori_loop(0, 80, over_k, 0, unroll=4)
    z = idx[1]
    stack[...] = jnp.zeros_like(stack)
    here = row_of_y()
    for c in range(16):
        for f in range(5):
            k = f * 16 + c
            d = change[pl.ds(k * 8 + z, 1)]
            stack[f:f + 1, 128 * c:128 * c + 128] = d
            n = 8 * (k // 4)
            rows[n:n + 8, 128 * (c % 4):128 * (c % 4) + 128] = (low[5 * c + f:5 * c + f + 1] + d) * here
    fields[...] = project(rows[...], select[...]).reshape(5, 4, 8, 64)
    add = lax.dot_general(stack[...], ec[0], (((0,), (0,)), ((), ())), precision=HI,
                          preferred_element_type=jnp.float32).reshape(16, 8, 16, 128)
    for c in range(16):
        xi, zi = c // 4, c % 4
        v = h2[c] + add[c]
        for y in range(8):
            out[xi, y, pl.ds(zi, 16, stride=4), :] = v[y]


def on_device(distribution, forcing):
    import functools
    tables = {k: jnp.asarray(v) for k, v in constant_tables().items()}
    spaces = lax.axis_size("space")
    blocks = spaces // 8
    idx = jnp.stack([lax.axis_index("vel"), lax.axis_index("space") % 8]).astype(jnp.int32)
    vec, lt = tables["vec"], tables["lanes"]
    wide = (16, 8, 16, 128)
    layer = (4, 8, 16, 128)

    def shifted(x, by):
        return lax.ppermute(x, "space", [(i, (i + by) % spaces) for i in range(spaces)])

    up, down = call(rim_kernel, "rims", idx, [distribution], [vec],
                    [(544, 128)] * 2, [layer, layer, (8, 8, 16, 128), (1024, 8)])
    up, down = shifted(up, 1), shifted(down, -1)
    twice, moma, force = call(local_kernel, "local", idx, [distribution, forcing, tables["select"]],
                              [vec, tables["tab0"], tables["tab1"]],
                              [wide, (16, 16, 128), (4, 20, 128)], [wide, wide, (2048, 48)])
    pay, rest, t2 = call(moment_kernel, "moments", idx, [up, down, twice, moma, tables["mix"], lt],
                         [vec, tables["tab2"], tables["tab1"]], [(4, 30, 128), (280, 128), wide],
                         [layer, layer, layer, (16, 48, 128), (16, 40, 128), (2048, 48), (64, 2048)])
    got = lax.all_to_all(pay, "vel", 0, 0, tiled=True)
    (res,) = call(residual_kernel, "residual", idx, [got, force], [], [(8, 30, 128)])
    near = [[a * 8 + b for b in range(8)] for a in range(blocks)]
    far = [[a * 8 + b for a in range(blocks)] for b in range(8)]
    mine = lax.all_to_all(res, "space", 0, 0, axis_index_groups=near, tiled=True).reshape(240, 128)
    own_r, to_upper, to_lower = call(pack_kernel, "pack", idx, [mine], [],
                                     [(20, 8, 128), (125, 128), (125, 128)])
    lower, upper = shifted(to_upper, 8), shifted(to_lower, -8)
    rest, own_r = lax.optimization_barrier((rest, own_r))
    others = lax.all_gather(rest, "vel")
    h2, low = call(feq_kernel, "feq", idx, [others, t2, lt], [tables["final"]],
                   [wide, (80, 128)], [(16, 8, 128), (4, 8, 128), (4, 8, 128), (56, 2048)])
    (quarter,) = call(window_kernel, "window", idx, [lower, own_r, upper, to_lower, to_upper, low], [],
                      [(20, 24, 128)])
    quarters = lax.all_gather(quarter, "vel")

    def summed(gram):
        return lax.all_to_all(gram, "space", 0, 0, axis_index_groups=far, tiled=True)

    win, own, part = (80, 24, 128), (80, 8, 128), (blocks, 8, 128)
    co = (40, 24, 128)
    r, m, ar, am, pe, gram = call(first_pass_kernel, "pass1", idx, [quarters, lt], [],
                                  [win] * 5 + [part], [co])
    r, m, ar, am, pe, acc, gram = call(functools.partial(next_pass_kernel, True), "pass2", idx,
                                       [summed(gram), r, m, ar, am, pe, lt], [],
                                       [win] * 5 + [own, part], [co])
    r, m, pe, acc, gram = call(third_pass_kernel, "pass3", idx,
                               [summed(gram), r, m, ar, am, pe, acc, lt], [],
                               [own] * 4 + [part], [win, win, own, own, win, co])
    out, fields = call(last_kernel, "last", idx,
                       [summed(gram), r, m, pe, acc, low, h2, tables["select"]], [tables["ec"]],
                       [(4, 8, 64, 128), (5, 4, 8, 64)], [(640, 128), (8, 2048), (160, 512)])
    return out, fields


def solution(mesh):
    return jax.shard_map(
        on_device,
        mesh=mesh,
        in_specs=(P("space", None, None, "vel"), P(None, "space", None, None)),
        out_specs=(P("space", None, None, "vel"), P(None, "space", None, None)),
        check_vma=False,
    )
```

```python
import math

import jax
import jax.numpy as jnp
import numpy as np
from jax import lax
from jax.experimental import pallas as pl
from jax.experimental.pallas import tpu as pltpu
from jax.sharding import PartitionSpec as P

INTERPRET = False
DT = 0.02
RF = 0.4472135954999579
POINTS = [-1.0, -RF, RF, 1.0]
WEIGHTS = [1.0 / 6.0, 5.0 / 6.0, 5.0 / 6.0, 1.0 / 6.0]
EPS = 1e-6
HI = lax.Precision.HIGHEST


def lagrange_table(points):
    n = len(points)
    bary = []
    for i in range(n):
        product = 1.0
        for j in range(n):
            if j != i:
                product *= points[i] - points[j]
        bary.append(1.0 / product)
    rows = [[0.0] * n for _ in range(n)]
    for i in range(n):
        for j in range(n):
            if j != i:
                rows[i][j] = bary[j] / bary[i] / (points[i] - points[j])
        rows[i][i] = -sum(rows[i])
    return rows


D4 = lagrange_table(POINTS)
for _i in (1, 2):
    D4[_i][_i] = 0.0
PR = [[(1.0 - x) / 2.0, (1.0 + x) / 2.0] for x in POINTS]
RT = [[WEIGHTS[i] * PR[i][a] for i in range(4)] for a in range(2)]


def constant_tables():
    k = np.arange(512)
    b, j = k // 128, k % 128
    s = j // 64
    m = ((b * 64 + j % 64) * 5179 + 7) % 16384
    xi = np.stack([16 * s + m // 1024, (m // 32) % 32, m % 32]).astype(np.float64)
    xi = -4.0 + 0.25 * (xi + 0.5)
    sq = (xi * xi).sum(0)
    e = math.pi ** (-1.5) * np.exp(-sq)
    x, y, z = xi
    phi = np.stack(
        [np.ones(512), x, y, z, 2 * sq / 3 - 1, 2 * (x * x - sq / 3), 2 * (y * y - sq / 3),
         2 * x * y, 2 * x * z, 2 * y * z, x * (sq - 2.5), y * (sq - 2.5), z * (sq - 2.5)]
    )
    p = phi[0] + phi[4]
    zero = np.zeros(512)

    def eight(rows):
        return np.stack(list(rows) + [zero] * (8 - len(rows)))

    low = eight(phi[:5])
    along_x = eight([phi[1], p + phi[5], phi[7], phi[8], phi[1] + phi[10]])
    along_y = eight([phi[2], phi[7], p + phi[6], phi[9], phi[2] + phi[11]])
    along_z = eight([phi[3], phi[8], phi[9], p - phi[5] - phi[6], phi[3] + phi[12]])
    rows32 = np.concatenate([low, along_x, along_y, along_z])
    ec = eight([e, 2 * x * e, 2 * y * e, 2 * z * e, e * (sq - 1.5)])
    pos, neg = np.maximum(xi, 0.0), np.minimum(xi, 0.0)

    def per_rank(rows):
        return np.stack([rows[:, r * 128:(r + 1) * 128] for r in range(4)]).astype(np.float32)

    ispos = (x > 0).astype(np.float64)
    ax = np.abs(x)
    d4 = np.array(D4)
    vec = [-DT * 0.5 * x, -DT * 0.5 * y, -DT * 0.5 * z,
           -3 * DT * pos[1], -3 * DT * neg[1], -3 * DT * pos[2], -3 * DT * neg[2],
           -3 * DT * pos[0], 3 * DT * neg[0], 3 * DT * ax]
    for i in range(4):
        kap = -DT * 0.5 * x * np.where(ispos > 0, d4[i][0], d4[i][3])
        if i == 0:
            kap = kap + ispos * (0.8 - 3 * DT * ax)
        if i == 3:
            kap = kap + (1 - ispos) * (0.8 - 3 * DT * ax)
        vec.append(kap)
    vec.append(ispos)
    for jj in range(4):
        vec.append(-DT * 0.5 * x * np.where(ispos > 0, d4[3][jj], d4[0][jj]))
    while len(vec) < 24:
        vec.append(zero)
    vec = per_rank(np.concatenate([np.stack(vec), low]))

    def moment_rows(start, rows, height):
        out = np.zeros((height, 512))
        out[start:start + len(rows)] = rows
        return per_rank(out)

    tab2 = moment_rows(0, rows32, 48)
    tab1 = moment_rows(40, low, 48)
    tab0 = moment_rows(32, low, 48)
    select = np.zeros((64, 512))
    for n in range(4):
        for la in range(128):
            select[4 * (la % 16) + n, 128 * n + la] = 1.0
    g = rows32 @ ec.T
    g5 = g[:8]
    mix = np.zeros((40, 64))
    mix[:32, 0:8] = 0.16 * g + 0.04 * g @ g5
    mix[:32, 8:16] = 0.2 * g
    mix[32:, 0:8] = 0.2 * g5
    mix[32:, 8:16] = np.eye(8)
    final = [ec]
    for d in range(3):
        for i, part in enumerate((pos[d], neg[d])):
            c0 = 16 + 16 * d + 8 * i
            mix[:32, c0:c0 + 8] = -0.2 * DT * (rows32 * part) @ ec.T
            final.append(-0.2 * DT * ec * part)
    final = per_rank(np.concatenate(final))
    lane = np.arange(128)
    yi, ze = (lane // 16) % 4, lane % 16
    rows = []
    shifts = (-3, -2, -1, 1, 2, 3)

    def entry(table, sft):
        return np.array([table(i, i + sft) if 0 <= i + sft < 4 else 0.0 for i in yi])

    for sft in shifts:
        c = entry(lambda i, q: 0.5 * D4[i][q], sft)
        if sft == -1:
            c = c - 1.5 * (yi == 0)
        if sft == 1:
            c = c + 1.5 * (yi == 3)
        rows.append(c)
    for a in range(2):
        for sft in range(-3, 4):
            rows.append(entry(lambda i, q: RT[a][q], sft))
    rows += [np.array([PR[i][0] for i in yi]), np.array([PR[i][1] for i in yi])]
    rows += [np.array([WEIGHTS[i] for i in yi]), (yi == 0) * 1.0, (ze == 0) * 1.0, (ze == 15) * 1.0]
    for sft in shifts:
        rows.append(entry(lambda i, q: 0.5 * D4[i][q], sft))
    rows += [entry(lambda i, q: 0.5 * D4[i][q], 0), 3.0 * (yi == 0), 3.0 * (yi == 3)]
    while len(rows) < 40:
        rows.append(np.zeros(128))
    lanes = np.stack(rows).astype(np.float32)
    return dict(vec=vec, tab2=tab2, tab1=tab1, tab0=tab0, mix=mix.astype(np.float32),
                final=final, lanes=lanes, ec=per_rank(ec), select=select.astype(np.float32))


def call(kernel, name, idx, full, ranked, outs, scratch=(), limit=24):
    n = len(full)

    def body(idx, *refs):
        rank = [r.at[pl.ds(idx[0], 1)] for r in refs[n:n + len(ranked)]]
        kernel(idx, *refs[:n], *rank, *refs[n + len(ranked):])

    vmem = pl.BlockSpec(memory_space=pltpu.VMEM)
    return pl.pallas_call(
        body,
        name=name,
        out_shape=[jax.ShapeDtypeStruct(s, jnp.float32) for s in outs],
        in_specs=[pl.BlockSpec(memory_space=pltpu.SMEM)] + [vmem] * (n + len(ranked)),
        out_specs=[vmem] * len(outs),
        scratch_shapes=[pltpu.VMEM(s, jnp.float32) for s in scratch],
        compiler_params=pltpu.CompilerParams(vmem_limit_bytes=limit << 20),
        interpret=INTERPRET,
    )(idx, *full, *ranked)


def exact_dot(a, b):
    return jnp.dot(a, b, precision=HI, preferred_element_type=jnp.float32)


def project(x, rows):
    return lax.dot_general(x, rows, (((1,), (1,)), ((), ())), precision=HI,
                           preferred_element_type=jnp.float32)


def combine(row, values):
    total = None
    for c, v in zip(row, values):
        if c != 0.0:
            total = c * v if total is None else total + c * v
    return total


def layer_yz(src, dst, vec):
    def over_y(y, _):
        q = [src[zi, y] for zi in range(4)]
        for zi in range(4):
            v = vec[0, 2:3] * combine(D4[zi], q)
            if zi == 0:
                v = v + vec[0, 5:6] * (q[0] - pltpu.roll(q[3], 1, 0))
            if zi == 3:
                v = v + vec[0, 6:7] * (pltpu.roll(q[0], 15, 0) - q[3])
            dst[zi, y] = v
        return 0
    lax.fori_loop(0, 8, over_y, 0, unroll=True)

    def over_z(zi, _):
        q = [src[zi, y] for y in range(8)]
        for y in range(8):
            e, yi = 4 * (y // 4), y % 4
            v = vec[0, 1:2] * combine(D4[yi], q[e:e + 4])
            if yi == 0:
                v = v + vec[0, 3:4] * (q[y] - q[(y + 7) % 8])
            if yi == 3:
                v = v + vec[0, 4:5] * (q[(y + 1) % 8] - q[y])
            dst[zi, y] = dst[zi, y] + v
        return 0
    lax.fori_loop(0, 4, over_z, 0, unroll=True)


def every_fourth(h, xi, y, zi):
    if INTERPRET:
        return h[xi, y][zi::4]
    return h[xi, y, pl.ds(zi, 16, stride=4), :]


def speed_rows(idx, vec):
    j = lax.broadcasted_iota(jnp.int32, (1, 128), 1)
    m = ((idx[0] * 64 + (j & 63)) * 5179 + 7) & 16383
    s = j >> 6
    x, y, z = [-4.0 + 0.25 * (n.astype(jnp.float32) + 0.5)
               for n in (16 * s + (m >> 10), (m >> 5) & 31, m & 31)]
    pos = s > 0
    rows = {0: -DT * 0.5 * x, 1: -DT * 0.5 * y, 2: -DT * 0.5 * z,
            3: -3 * DT * jnp.maximum(y, 0.0), 4: -3 * DT * jnp.minimum(y, 0.0),
            5: -3 * DT * jnp.maximum(z, 0.0), 6: -3 * DT * jnp.minimum(z, 0.0),
            14: pos.astype(jnp.float32)}
    for n in range(4):
        rows[15 + n] = -DT * 0.5 * x * jnp.where(pos, D4[3][n], D4[0][n])
    rows[24], rows[25], rows[26], rows[27] = jnp.ones_like(x), x, y, z
    rows[28] = 2.0 * (x * x + y * y + z * z) / 3.0 - 1.0
    vec[...] = jnp.zeros_like(vec)
    for n, v in rows.items():
        vec[0, n:n + 1] = v


def rim_kernel(idx, h, up, down, q, t, ends, m, vec):
    speed_rows(idx, vec)
    transport_rims(idx, h, vec, up, down, q, t, ends, m)


def transport_rims(idx, h, vec, up, down, q, t, ends, m):
    pos = vec[0, 14:15] > 0.5
    for zi in range(4):
        def over_y(y, _):
            x = [every_fourth(h, xi, y, zi) for xi in range(4)]
            ql = jnp.where(pos, x[3], x[0])
            q[zi, y] = ql
            ends[zi, y] = x[0]
            ends[4 + zi, y] = x[3]
            v = 0.8 * ql
            for j in range(4):
                v = v + vec[0, 15 + j:16 + j] * x[j]
            up[pl.ds(pl.multiple_of((zi * 8 + y) * 16, 16), 16)] = v
            return 0
        lax.fori_loop(0, 8, over_y, 0, unroll=True)
    layer_yz(q, t, vec)
    right = lax.broadcasted_iota(jnp.int32, (16, 128), 1) >= 64

    def pack(n, _):
        zi, y = n // 8, n % 8
        at = pl.ds(pl.multiple_of(n * 16, 16), 16)
        tl = pltpu.roll(t[zi, y] + up[at], 64, 1)
        ql = q[zi, y]
        up[at] = jnp.where(right, ql, tl)
        down[at] = jnp.where(right, tl, ql)
        return 0
    lax.fori_loop(0, 32, pack, 0, unroll=8)
    m[...] = project(ends[...].reshape(1024, 128), vec[0, 24:32])
    for n in range(8):
        zi, out = n % 4, (down, up)[n // 4]
        out[512 + 8 * zi:520 + 8 * zi] = m[128 * n:128 * n + 128].T


def local_update(src, dst, vec):
    def over_y(y, _):
        q = [src[c, y] for c in range(16)]
        for xi in range(4):
            for zi in range(4):
                own = q[xi * 4 + zi]
                v = 0.8 * own + vec[0, 0:1] * combine(D4[xi], [q[j * 4 + zi] for j in range(4)])
                v = v + vec[0, 2:3] * combine(D4[zi], q[xi * 4:xi * 4 + 4])
                if zi == 0:
                    v = v + vec[0, 5:6] * (own - pltpu.roll(q[xi * 4 + 3], 1, 0))
                if zi == 3:
                    v = v + vec[0, 6:7] * (pltpu.roll(q[xi * 4], 15, 0) - own)
                if xi == 0:
                    v = v + vec[0, 7:8] * own
                if xi == 3:
                    v = v + vec[0, 8:9] * own
                dst[xi * 4 + zi, y] = v
        return 0
    lax.fori_loop(0, 8, over_y, 0, unroll=2)

    def over_c(c, _):
        q = [src[c, y] for y in range(8)]
        for y in range(8):
            e, yi = 4 * (y // 4), y % 4
            v = vec[0, 1:2] * combine(D4[yi], q[e:e + 4])
            if yi == 0:
                v = v + vec[0, 3:4] * (q[y] - q[(y + 7) % 8])
            if yi == 3:
                v = v + vec[0, 4:5] * (q[(y + 1) % 8] - q[y])
            dst[c, y] = dst[c, y] + v
        return 0
    lax.fori_loop(0, 16, over_c, 0, unroll=4)


def row_of_y():
    y = lax.broadcasted_iota(jnp.int32, (8, 128), 0)
    return (lax.broadcasted_iota(jnp.int32, (8, 128), 1) // 16 == y).astype(jnp.float32)


def local_kernel(idx, h, forcing, select, vec, tab0, tab1, twice, mom, force, first, once, m):
    spread = exact_dot(forcing[...].reshape(96, 64), select[...])
    here = row_of_y()
    force[...] = jnp.zeros_like(force)
    for f in range(3):
        for c in range(16):
            n = 8 * (f * 4 + c // 4)
            v = spread[n:n + 8, 128 * (c % 4):128 * (c % 4) + 128] * here
            at = 5 * (c // 4) + f + 1
            force[c % 4, at:at + 1] = jnp.sum(v, axis=0, keepdims=True)
    for c in range(16):
        xi, zi = c // 4, c % 4

        def over_y(y, _):
            first[c, y] = every_fourth(h, xi, y, zi)
            return 0
        lax.fori_loop(0, 8, over_y, 0, unroll=True)
    local_update(first, once, vec)
    local_update(once, twice, vec)

    m[...] = project(first[...].reshape(2048, 128), tab0[0])
    m[...] = m[...] + project(once[...].reshape(2048, 128), tab1[0])
    for c in range(16):
        mom[c] = m[128 * c:128 * c + 128].T[32:48]


def z_before(q, lt):
    return jnp.where(lt[24:25] > 0.5, pltpu.roll(q, 113, 1), pltpu.roll(q, 1, 1))


def z_after(q, lt):
    return jnp.where(lt[25:26] > 0.5, pltpu.roll(q, 15, 1), pltpu.roll(q, 127, 1))


SHIFTS = (-3, -2, -1, 1, 2, 3)


def central_y(q, lt):
    total = None
    for n, s in enumerate(SHIFTS):
        term = lt[n:n + 1] * pltpu.roll(q, (-16 * s) % 128, 1)
        total = term if total is None else total + term
    return total


def one_sided(load, low, high, c, lt):
    xi, zi = c // 4, c % 4
    q = load(c)
    cx = combine([0.5 * v for v in D4[xi]], [load(j * 4 + zi) for j in range(4)])
    px = cx + 3.0 * (q - low(zi)) if xi == 0 else cx
    mx = cx + 3.0 * (high(zi) - q) if xi == 3 else cx
    cy = lt[32:33] * q
    for n, s in enumerate(SHIFTS):
        r = pltpu.roll(q, (-16 * s) % 128, 1)
        cy = cy + lt[26 + n:27 + n] * r
        if s == -1:
            py = lt[33:34] * (q - r)
        if s == 1:
            my = lt[34:35] * (r - q)
    cz = combine([0.5 * v for v in D4[zi]], [load(xi * 4 + j) for j in range(4)])
    pz = cz + 3.0 * (q - z_before(load(xi * 4 + 3), lt)) if zi == 0 else cz
    mz = cz + 3.0 * (z_after(load(xi * 4), lt) - q) if zi == 3 else cz
    return [px, mx, cy + py, cy + my, pz, mz]


CENTRAL = [[0.0 if i == j else 0.5 * D4[i][j] for j in range(4)] for i in range(4)]


def moment_kernel(idx, up, down, twice, moma, mix, lt, vec, tab2, tab1, pay, t2,
                  delta, yz, extra, mom, full, m, stack):
    right = lax.broadcasted_iota(jnp.int32, (16, 128), 1) >= 64
    pos = vec[0, 14:15]

    def unpack(n, _):
        at = pl.ds(pl.multiple_of(n * 16, 16), 16)
        u, d = up[at], down[at]
        zi, y = n // 8, n % 8
        delta[zi, y] = vec[0, 9:10] * jnp.where(right, u, d)
        extra[zi, y] = vec[0, 9:10] * pltpu.roll(jnp.where(right, d, u), 64, 1)
        return 0
    lax.fori_loop(0, 32, unpack, 0, unroll=8)
    layer_yz(delta, yz, vec)
    for xi in range(4):
        def over_n(n, _):
            zi, y = n // 8, n % 8
            v = twice[xi * 4 + zi, y] + vec[0, 10 + xi:11 + xi] * delta[zi, y]
            if xi in (0, 3):
                w = pos if xi == 0 else 1.0 - pos
                v = v + w * (yz[zi, y] + extra[zi, y])
            t2[xi * 4 + zi, y] = v
            return 0
        lax.fori_loop(0, 32, over_n, 0, unroll=8)

    m[...] = project(t2[...].reshape(2048, 128), tab2[0])
    d = delta[...].reshape(512, 128)
    m[0:512] = m[0:512] + project(d * pos, tab1[0])
    m[1536:2048] = m[1536:2048] + project(d * (1.0 - pos), tab1[0])
    for c in range(16):
        t = m[128 * c:128 * c + 128].T
        mom[c, 0:32] = t[0:32]
        mom[c, 32:48] = t[32:48] + moma[c]

    def load0(c):
        return mom[c, 32:40]

    for c in range(16):
        six = one_sided(load0, lambda zi: up[512 + 8 * zi:520 + 8 * zi],
                        lambda zi: down[512 + 8 * zi:520 + 8 * zi], c, lt)
        at = slice(128 * c, 128 * c + 128)
        stack[0:16, at] = mom[c, 32:48]
        for n in range(6):
            stack[16 + 8 * n:24 + 8 * n, at] = six[n]
    add = exact_dot(mix[...], stack[...])
    for c in range(16):
        at = slice(128 * c, 128 * c + 128)
        full[c, 0:32] = mom[c, 0:32] + add[0:32, at]
        full[c, 32:40] = add[32:40, at]
    for c in range(16):
        xi, zi = c // 4, c % 4
        r = combine(CENTRAL[xi], [full[j * 4 + zi, 8:16] for j in range(4)])
        r = r + central_y(full[c, 16:24], lt)
        r = r + combine(CENTRAL[zi], [full[xi * 4 + j, 24:32] for j in range(4)])
        if zi == 0:
            r = r - 1.5 * z_before(full[xi * 4 + 3, 24:32], lt)
        if zi == 3:
            r = r + 1.5 * z_after(full[xi * 4, 24:32], lt)
        q = 32 * zi + 5 * xi
        pay[q:q + 5] = -r[0:5]
        pay[128 + 5 * c:133 + 5 * c] = full[c, 0:5]
        pay[208 + 5 * c:213 + 5 * c] = mom[c, 32:37]
        pay[288 + 5 * c:293 + 5 * c] = full[c, 32:37]
    for zi in range(4):
        pay[32 * zi + 20:32 * zi + 25] = full[zi, 8:13]
        pay[32 * zi + 25:32 * zi + 30] = full[12 + zi, 8:13]
        pay[32 * zi + 30:32 * zi + 32] = jnp.zeros((2, 128), jnp.float32)
        pay[368 + 5 * zi:373 + 5 * zi] = up[512 + 8 * zi:517 + 8 * zi]
        pay[388 + 5 * zi:393 + 5 * zi] = down[512 + 8 * zi:517 + 8 * zi]


def residual_kernel(idx, got, force, out):
    at = pl.ds(pl.multiple_of(32 * idx[0], 32), 32)
    t = got[0, at] + got[1, at] + got[2, at] + got[3, at]
    v = t[0:20] + force[idx[0]]
    for n in range(8):
        out[n, 0:20] = v
        out[n, 20:30] = t[20:30]


def feq_kernel(idx, got, t2, lt, final, h2, low, s0, lo, hi, stack):
    def total(a, n):
        return got[0, a:a + n] + got[1, a:a + n] + got[2, a:a + n] + got[3, a:a + n]

    s0[...] = jnp.zeros_like(s0)
    lo[...] = jnp.zeros_like(lo)
    hi[...] = jnp.zeros_like(hi)
    for c in range(16):
        s0[c, 0:5] = total(208 + 5 * c, 5)
    for zi in range(4):
        lo[zi, 0:5] = total(368 + 5 * zi, 5)
        hi[zi, 0:5] = total(388 + 5 * zi, 5)
    low[...] = total(128, 80)
    pad = jnp.zeros((3, 128), jnp.float32)
    for c in range(16):
        z = jnp.concatenate([0.2 * total(288 + 5 * c, 5), pad], axis=0) + 0.16 * s0[c]
        six = one_sided(lambda k: s0[k], lambda zi: lo[zi], lambda zi: hi[zi], c, lt)
        for n, v in enumerate([z] + six):
            stack[8 * n:8 * n + 8, 128 * c:128 * c + 128] = v
    add = lax.dot_general(stack[...], final[0], (((0,), (0,)), ((), ())), precision=HI,
                          preferred_element_type=jnp.float32)
    h2[...] = t2[...] + add.reshape(16, 8, 16, 128)


def apply_operator(src, dst, lt, own=False):
    rows = slice(8, 16) if own else slice(0, 24)

    def before(k, add):
        if own:
            return src[k, 7:15] + src[k + add, 7:15] if add else src[k, 7:15]
        return pltpu.roll(src[k] + src[k + add] if add else src[k], 1, 0)

    def after(k, add):
        if own:
            return src[k, 9:17] + src[k + add, 9:17] if add else src[k, 9:17]
        return pltpu.roll(src[k] + src[k + add] if add else src[k], 23, 0)

    for zi in range(4):
        u = [src[16 + j * 4 + zi, rows] for j in range(4)]
        p = [src[j * 4 + zi, rows] + src[64 + j * 4 + zi, rows] for j in range(4)]
        for xi in range(4):
            du = combine(CENTRAL[xi], u)
            dp = combine(CENTRAL[xi], p)
            if xi == 0:
                du = du - 1.5 * before(28 + zi, 0)
                dp = dp - 1.5 * before(12 + zi, 64)
            if xi == 3:
                du = du + 1.5 * after(16 + zi, 0)
                dp = dp + 1.5 * after(zi, 64)
            dst[xi * 4 + zi] = du
            dst[16 + xi * 4 + zi] = 2.0 * u[xi] + dp
    for xi in range(4):
        u = [src[48 + xi * 4 + j, rows] for j in range(4)]
        p = [src[xi * 4 + j, rows] + src[64 + xi * 4 + j, rows] for j in range(4)]
        for zi in range(4):
            du = combine(CENTRAL[zi], u)
            dp = combine(CENTRAL[zi], p)
            if zi == 0:
                du = du - 1.5 * z_before(u[3], lt)
                dp = dp - 1.5 * z_before(p[3], lt)
            if zi == 3:
                du = du + 1.5 * z_after(u[0], lt)
                dp = dp + 1.5 * z_after(p[0], lt)
            dst[xi * 4 + zi] = dst[xi * 4 + zi] + du
            dst[48 + xi * 4 + zi] = 2.0 * u[zi] + dp

    def along_y(c, _):
        rho, u, t = src[c, rows], src[32 + c, rows], src[64 + c, rows]
        div = dst[c] + central_y(u, lt)
        dst[32 + c] = 2.0 * u + central_y(rho + t, lt)
        dst[c] = 2.0 * rho + div
        dst[64 + c] = 2.0 * t + div
        return 0
    lax.fori_loop(0, 16, along_y, 0, unroll=8)


def two_level(r, pe, co, lt):
    def over_f(f, _):
        tz = [[None, None] for _ in range(4)]
        for xi in range(4):
            q = [r[f * 16 + xi * 4 + zi] for zi in range(4)]
            for za in range(2):
                tz[xi][za] = combine(RT[za], q)
        for za in range(2):
            py = []
            for xa in range(2):
                t = combine(RT[xa], [tz[xi][za] for xi in range(4)])
                e0, e1 = lt[9:10] * t, lt[16:17] * t
                for s in SHIFTS:
                    rolled = pltpu.roll(t, (-16 * s) % 128, 1)
                    e0 = e0 + lt[9 + s:10 + s] * rolled
                    e1 = e1 + lt[16 + s:17 + s] * rolled
                co[f * 8 + xa * 4 + za * 2] = e0
                co[f * 8 + xa * 4 + za * 2 + 1] = e1
                py.append(lt[20:21] * e0 + lt[21:22] * e1)
            for xi in range(4):
                v = combine(PR[xi], py)
                for zi in range(4):
                    if PR[zi][za] == 0.0:
                        continue
                    at = f * 16 + xi * 4 + zi
                    if za == 0 or PR[zi][0] == 0.0:
                        pe[at] = PR[zi][za] * v
                    else:
                        pe[at] = pe[at] + PR[zi][za] * v
        return 0
    lax.fori_loop(0, 5, over_f, 0)


def coarse_products(co, lt):
    def at(f, xa, za, ya):
        return co[f * 8 + xa * 4 + za * 2 + ya]

    def own(q):
        return q[8:16]

    def dx(q, xa, za, ya):
        if xa == 0:
            v = q(1, za, ya)
            return 0.25 * (own(v) - own(pltpu.roll(v, 1, 0)))
        v = q(0, za, ya)
        return 0.25 * (own(pltpu.roll(v, 23, 0)) - own(v))

    def dz(q, xa, za, ya):
        v = own(q(xa, 1 - za, ya))
        if za == 0:
            return 0.25 * (v - z_before(v, lt))
        return 0.25 * (z_after(v, lt) - v)

    def dy(q, xa, za, ya):
        v = own(q(xa, za, 1 - ya))
        w = pltpu.roll(v, 64, 1)
        return 0.25 * (v - w) if ya == 0 else 0.25 * (w - v)

    up = jnp.zeros((8, 128), jnp.float32)
    low = jnp.zeros((8, 128), jnp.float32)
    for xa in range(2):
        for za in range(2):
            for ya in range(2):
                def field(f):
                    return lambda a, b, c: at(f, a, b, c)

                def pressure(a, b, c):
                    return at(0, a, b, c) + at(4, a, b, c)
                e = [own(at(f, xa, za, ya)) for f in range(5)]
                div = (dx(field(1), xa, za, ya) + dy(field(2), xa, za, ya)
                       + dz(field(3), xa, za, ya))
                g = [2.0 * e[0] + div, 2.0 * e[1] + dx(pressure, xa, za, ya),
                     2.0 * e[2] + dy(pressure, xa, za, ya),
                     2.0 * e[3] + dz(pressure, xa, za, ya), 2.0 * e[4] + div]
                for f in range(5):
                    up = up + e[f] * g[f]
                    low = low + g[f] * g[f]
    return up * lt[23:24], low * lt[23:24]


def fine_products(r, m, ar, am, lt, own):
    rows = slice(0, 8) if own else slice(8, 16)
    total = [jnp.zeros((8, 128), jnp.float32) for _ in range(6)]
    for xi in range(4):
        for zi in range(4):
            def over_f(f, acc):
                k = f * 16 + xi * 4 + zi
                a, b, c, d = r[k, 8:16], m[k, 8:16], ar[k, rows], am[k, rows]
                return (acc[0] + a * c, acc[1] + a * d + b * c, acc[2] + b * d,
                        acc[3] + c * c, acc[4] + c * d, acc[5] + d * d)
            zero = jnp.zeros((8, 128), jnp.float32)
            acc = lax.fori_loop(0, 5, over_f, (zero,) * 6, unroll=True)
            w = WEIGHTS[xi] * WEIGHTS[zi]
            total = [t + w * a for t, a in zip(total, acc)]
    return [t * lt[22:23] for t in total]


def pass_words(r, m, ar, am, pe, co, gram, lt, peers, own=False):
    two_level(r, pe, co, lt)
    apply_operator(pe, m, lt)
    apply_operator(r, ar, lt, own)
    apply_operator(m, am, lt, own)
    products = list(coarse_products(co, lt)) + fine_products(r, m, ar, am, lt, own)
    rows = jnp.concatenate([jnp.sum(p, axis=0, keepdims=True) for p in products], axis=0)
    for n in range(peers):
        gram[n] = rows


def pack_kernel(idx, mine, own, to_upper, to_lower):
    first = lax.broadcasted_iota(jnp.int32, (8, 128), 0) == 0
    last = lax.broadcasted_iota(jnp.int32, (8, 128), 0) == 7
    for f in range(5):
        low = mine[pl.ds(20 + f, 8, stride=30), :]
        high = mine[pl.ds(25 + f, 8, stride=30), :]
        for xi in range(4):
            k = f * 4 + xi
            v = mine[pl.ds(5 * xi + f, 8, stride=30), :]
            if xi == 0:
                v = v + 1.5 * jnp.where(first, 0.0, pltpu.roll(high, 1, 0))
            if xi == 3:
                v = v - 1.5 * jnp.where(last, 0.0, pltpu.roll(low, 7, 0))
            own[k] = v
            to_upper[pl.ds(k, 6, stride=20), :] = v[2:8]
            to_lower[pl.ds(k, 6, stride=20), :] = v[0:6]
        to_upper[120 + f:121 + f] = high[7:8]
        to_lower[120 + f:121 + f] = low[0:1]


def window_kernel(idx, lower, own, upper, edge_low, edge_high, after, win):
    for f in range(5):
        e = 120 + f
        for xi in range(4):
            k = f * 4 + xi
            at = 20 * k
            low, mid, high = lower[pl.ds(k, 6, stride=20), :], own[k], upper[pl.ds(k, 6, stride=20), :]
            win[at:at + 6] = low
            win[at + 6:at + 14] = mid
            win[at + 14:at + 20] = high
            if xi == 0:
                win[at + 6:at + 7] = mid[0:1] + 1.5 * lower[e:e + 1]
                win[at + 14:at + 15] = high[0:1] + 1.5 * edge_high[e:e + 1]
            if xi == 3:
                win[at + 13:at + 14] = mid[7:8] - 1.5 * upper[e:e + 1]
                win[at + 5:at + 6] = low[5:6] - 1.5 * edge_low[e:e + 1]


def first_pass_kernel(idx, quarters, lt, r, m, ar, am, pe, gram, co):
    zero = jnp.zeros((2, 128), jnp.float32)
    for f in range(5):
        for xi in range(4):
            for zi in range(4):
                k = f * 16 + xi * 4 + zi
                at = 20 * (f * 4 + xi)
                r[k, 0:2] = zero
                r[k, 2:22] = quarters[zi, at:at + 20]
                r[k, 22:24] = zero
    pass_words(r, m, ar, am, pe, co, gram, lt, gram.shape[0])


def step_sizes(sums, peers):
    s = sums[0]
    for n in range(1, peers):
        s = s + sums[n]
    s = jnp.broadcast_to(jnp.sum(s, axis=1, keepdims=True), (8, 128))
    a1 = s[0:1] / (s[1:2] + EPS)
    up = s[2:3] - a1 * s[3:4] + a1 * a1 * s[4:5]
    low = s[5:6] - 2.0 * a1 * s[6:7] + a1 * a1 * s[7:8]
    return a1, up / (low + EPS)


def next_pass_kernel(first, idx, sums, r, m, ar, am, pe, *rest):
    if first:
        lt, r2, m2, ar2, am2, pe2, acc2, gram, co = rest
    else:
        acc, lt, r2, m2, ar2, am2, pe2, acc2, gram, co = rest
    a1, a2 = step_sizes(sums, gram.shape[0])

    def over_k(k, _):
        q = r[k] - a1 * m[k]
        v = a1 * pe[k, 8:16] + a2 * q[8:16]
        acc2[k] = v if first else acc[k] + v
        r2[k] = q - a2 * (ar[k] - a1 * am[k])
        return 0
    lax.fori_loop(0, 80, over_k, 0, unroll=4)
    pass_words(r2, m2, ar2, am2, pe2, co, gram, lt, gram.shape[0], own=not first)


def third_pass_kernel(idx, sums, r, m, ar, am, pe, acc, lt, ro, mo, po, acc2, gram,
                      r2, m2, ar2, am2, pe2, co):
    next_pass_kernel(False, idx, sums, r, m, ar, am, pe, acc, lt, r2, m2, ar2, am2, pe2, acc2, gram, co)
    ro[...] = r2[:, 8:16]
    mo[...] = m2[:, 8:16]
    po[...] = pe2[:, 8:16]


def last_kernel(idx, sums, r, m, pe, acc, low, h2, select, ec, out, fields, change, stack, rows):
    a1, a2 = step_sizes(sums, sums.shape[0])

    def over_k(k, _):
        q = r[k] - a1 * m[k]
        change[pl.ds(pl.multiple_of(k * 8, 8), 8)] = acc[k] + a1 * pe[k] + a2 * q
        return 0
    lax.fori_loop(0, 80, over_k, 0, unroll=4)
    z = idx[1]
    stack[...] = jnp.zeros_like(stack)
    here = row_of_y()
    for c in range(16):
        for f in range(5):
            k = f * 16 + c
            d = change[pl.ds(k * 8 + z, 1)]
            stack[f:f + 1, 128 * c:128 * c + 128] = d
            n = 8 * (k // 4)
            rows[n:n + 8, 128 * (c % 4):128 * (c % 4) + 128] = (low[5 * c + f:5 * c + f + 1] + d) * here
    fields[...] = project(rows[...], select[...]).reshape(5, 4, 8, 64)
    add = lax.dot_general(stack[...], ec[0], (((0,), (0,)), ((), ())), precision=HI,
                          preferred_element_type=jnp.float32).reshape(16, 8, 16, 128)
    for c in range(16):
        xi, zi = c // 4, c % 4
        v = h2[c] + add[c]
        for y in range(8):
            out[xi, y, pl.ds(zi, 16, stride=4), :] = v[y]


def on_device(distribution, forcing):
    import functools
    tables = {k: jnp.asarray(v) for k, v in constant_tables().items()}
    spaces = lax.axis_size("space")
    blocks = spaces // 8
    idx = jnp.stack([lax.axis_index("vel"), lax.axis_index("space") % 8]).astype(jnp.int32)
    vec, lt = tables["vec"], tables["lanes"]
    wide = (16, 8, 16, 128)
    layer = (4, 8, 16, 128)

    def shifted(x, by):
        return lax.ppermute(x, "space", [(i, (i + by) % spaces) for i in range(spaces)])

    up, down = call(rim_kernel, "rims", idx, [distribution], [],
                    [(544, 128)] * 2, [layer, layer, (8, 8, 16, 128), (1024, 8), (1, 32, 128)])
    up, down = shifted(up, 1), shifted(down, -1)
    twice, moma, force = call(local_kernel, "local", idx, [distribution, forcing, tables["select"]],
                              [vec, tables["tab0"], tables["tab1"]],
                              [wide, (16, 16, 128), (4, 20, 128)], [wide, wide, (2048, 48)])
    pay, t2 = call(moment_kernel, "moments", idx, [up, down, twice, moma, tables["mix"], lt],
                   [vec, tables["tab2"], tables["tab1"]], [(408, 128), wide],
                   [layer, layer, layer, (16, 48, 128), (16, 40, 128), (2048, 48), (64, 2048)])
    got = lax.all_gather(pay, "vel")
    (res,) = call(residual_kernel, "residual", idx, [got, force], [], [(8, 30, 128)])
    near = [[a * 8 + b for b in range(8)] for a in range(blocks)]
    far = [[a * 8 + b for a in range(blocks)] for b in range(8)]
    mine = lax.all_to_all(res, "space", 0, 0, axis_index_groups=near, tiled=True).reshape(240, 128)
    own_r, to_upper, to_lower = call(pack_kernel, "pack", idx, [mine], [],
                                     [(20, 8, 128), (125, 128), (125, 128)])
    lower, upper = shifted(to_upper, 8), shifted(to_lower, -8)
    h2, low = call(feq_kernel, "feq", idx, [got, t2, lt], [tables["final"]],
                   [wide, (80, 128)], [(16, 8, 128), (4, 8, 128), (4, 8, 128), (56, 2048)])
    (quarter,) = call(window_kernel, "window", idx, [lower, own_r, upper, to_lower, to_upper, low], [],
                      [(400, 128)])
    quarters = lax.all_gather(quarter, "vel")

    def summed(gram):
        return lax.all_to_all(gram, "space", 0, 0, axis_index_groups=far, tiled=True)

    win, own, part = (80, 24, 128), (80, 8, 128), (blocks, 8, 128)
    co = (40, 24, 128)
    r, m, ar, am, pe, gram = call(first_pass_kernel, "pass1", idx, [quarters, lt], [],
                                  [win] * 5 + [part], [co])
    r, m, ar, am, pe, acc, gram = call(functools.partial(next_pass_kernel, True), "pass2", idx,
                                       [summed(gram), r, m, ar, am, pe, lt], [],
                                       [win] * 5 + [own, part], [co])
    r, m, pe, acc, gram = call(third_pass_kernel, "pass3", idx,
                               [summed(gram), r, m, ar, am, pe, acc, lt], [],
                               [own] * 4 + [part], [win, win, own, own, win, co])
    out, fields = call(last_kernel, "last", idx,
                       [summed(gram), r, m, pe, acc, low, h2, tables["select"]], [tables["ec"]],
                       [(4, 8, 64, 128), (5, 4, 8, 64)], [(640, 128), (8, 2048), (160, 512)])
    return out, fields


def solution(mesh):
    return jax.shard_map(
        on_device,
        mesh=mesh,
        in_specs=(P("space", None, None, "vel"), P(None, "space", None, None)),
        out_specs=(P("space", None, None, "vel"), P(None, "space", None, None)),
        check_vma=False,
    )
```

```python
import math

import jax
import jax.numpy as jnp
import numpy as np
from jax import lax
from jax.experimental import pallas as pl
from jax.experimental.pallas import tpu as pltpu
from jax.sharding import PartitionSpec as P

INTERPRET = False
DT = 0.02
RF = 0.4472135954999579
POINTS = [-1.0, -RF, RF, 1.0]
WEIGHTS = [1.0 / 6.0, 5.0 / 6.0, 5.0 / 6.0, 1.0 / 6.0]
EPS = 1e-6
HI = lax.Precision.HIGHEST


def lagrange_table(points):
    n = len(points)
    bary = []
    for i in range(n):
        product = 1.0
        for j in range(n):
            if j != i:
                product *= points[i] - points[j]
        bary.append(1.0 / product)
    rows = [[0.0] * n for _ in range(n)]
    for i in range(n):
        for j in range(n):
            if j != i:
                rows[i][j] = bary[j] / bary[i] / (points[i] - points[j])
        rows[i][i] = -sum(rows[i])
    return rows


D4 = lagrange_table(POINTS)
for _i in (1, 2):
    D4[_i][_i] = 0.0
PR = [[(1.0 - x) / 2.0, (1.0 + x) / 2.0] for x in POINTS]
RT = [[WEIGHTS[i] * PR[i][a] for i in range(4)] for a in range(2)]


def constant_tables():
    k = np.arange(512)
    b, j = k // 128, k % 128
    s = j // 64
    m = ((b * 64 + j % 64) * 5179 + 7) % 16384
    xi = np.stack([16 * s + m // 1024, (m // 32) % 32, m % 32]).astype(np.float64)
    xi = -4.0 + 0.25 * (xi + 0.5)
    sq = (xi * xi).sum(0)
    e = math.pi ** (-1.5) * np.exp(-sq)
    x, y, z = xi
    phi = np.stack(
        [np.ones(512), x, y, z, 2 * sq / 3 - 1, 2 * (x * x - sq / 3), 2 * (y * y - sq / 3),
         2 * x * y, 2 * x * z, 2 * y * z, x * (sq - 2.5), y * (sq - 2.5), z * (sq - 2.5)]
    )
    p = phi[0] + phi[4]
    zero = np.zeros(512)

    def eight(rows):
        return np.stack(list(rows) + [zero] * (8 - len(rows)))

    low = eight(phi[:5])
    along_x = eight([phi[1], p + phi[5], phi[7], phi[8], phi[1] + phi[10]])
    along_y = eight([phi[2], phi[7], p + phi[6], phi[9], phi[2] + phi[11]])
    along_z = eight([phi[3], phi[8], phi[9], p - phi[5] - phi[6], phi[3] + phi[12]])
    rows32 = np.concatenate([low, along_x, along_y, along_z])
    ec = eight([e, 2 * x * e, 2 * y * e, 2 * z * e, e * (sq - 1.5)])
    pos, neg = np.maximum(xi, 0.0), np.minimum(xi, 0.0)

    def per_rank(rows):
        return np.stack([rows[:, r * 128:(r + 1) * 128] for r in range(4)]).astype(np.float32)

    ispos = (x > 0).astype(np.float64)
    ax = np.abs(x)
    d4 = np.array(D4)
    vec = [-DT * 0.5 * x, -DT * 0.5 * y, -DT * 0.5 * z,
           -3 * DT * pos[1], -3 * DT * neg[1], -3 * DT * pos[2], -3 * DT * neg[2],
           -3 * DT * pos[0], 3 * DT * neg[0], 3 * DT * ax]
    for i in range(4):
        kap = -DT * 0.5 * x * np.where(ispos > 0, d4[i][0], d4[i][3])
        if i == 0:
            kap = kap + ispos * (0.8 - 3 * DT * ax)
        if i == 3:
            kap = kap + (1 - ispos) * (0.8 - 3 * DT * ax)
        vec.append(kap)
    vec.append(ispos)
    for jj in range(4):
        vec.append(-DT * 0.5 * x * np.where(ispos > 0, d4[3][jj], d4[0][jj]))
    while len(vec) < 24:
        vec.append(zero)
    vec = per_rank(np.concatenate([np.stack(vec), low]))

    def moment_rows(start, rows, height):
        out = np.zeros((height, 512))
        out[start:start + len(rows)] = rows
        return per_rank(out)

    tab2 = moment_rows(0, rows32, 48)
    tab1 = moment_rows(40, low, 48)
    tab0 = moment_rows(32, low, 48)
    select = np.zeros((64, 512))
    for n in range(4):
        for la in range(128):
            select[4 * (la % 16) + n, 128 * n + la] = 1.0
    g = rows32 @ ec.T
    g5 = g[:8]
    mix = np.zeros((40, 64))
    mix[:32, 0:8] = 0.16 * g + 0.04 * g @ g5
    mix[:32, 8:16] = 0.2 * g
    mix[32:, 0:8] = 0.2 * g5
    mix[32:, 8:16] = np.eye(8)
    final = [ec]
    for d in range(3):
        for i, part in enumerate((pos[d], neg[d])):
            c0 = 16 + 16 * d + 8 * i
            mix[:32, c0:c0 + 8] = -0.2 * DT * (rows32 * part) @ ec.T
            final.append(-0.2 * DT * ec * part)
    final = per_rank(np.concatenate(final))
    lane = np.arange(128)
    yi, ze = (lane // 16) % 4, lane % 16
    rows = []
    shifts = (-3, -2, -1, 1, 2, 3)

    def entry(table, sft):
        return np.array([table(i, i + sft) if 0 <= i + sft < 4 else 0.0 for i in yi])

    for sft in shifts:
        c = entry(lambda i, q: 0.5 * D4[i][q], sft)
        if sft == -1:
            c = c - 1.5 * (yi == 0)
        if sft == 1:
            c = c + 1.5 * (yi == 3)
        rows.append(c)
    for a in range(2):
        for sft in range(-3, 4):
            rows.append(entry(lambda i, q: RT[a][q], sft))
    rows += [np.array([PR[i][0] for i in yi]), np.array([PR[i][1] for i in yi])]
    rows += [np.array([WEIGHTS[i] for i in yi]), (yi == 0) * 1.0, (ze == 0) * 1.0, (ze == 15) * 1.0]
    for sft in shifts:
        rows.append(entry(lambda i, q: 0.5 * D4[i][q], sft))
    rows += [entry(lambda i, q: 0.5 * D4[i][q], 0), 3.0 * (yi == 0), 3.0 * (yi == 3)]
    while len(rows) < 40:
        rows.append(np.zeros(128))
    lanes = np.stack(rows).astype(np.float32)
    return dict(vec=vec, tab2=tab2, tab1=tab1, tab0=tab0, mix=mix.astype(np.float32),
                final=final, lanes=lanes, ec=per_rank(ec), select=select.astype(np.float32))


def call(kernel, name, idx, full, ranked, outs, scratch=(), limit=24):
    n = len(full)

    def body(idx, *refs):
        rank = [r.at[pl.ds(idx[0], 1)] for r in refs[n:n + len(ranked)]]
        kernel(idx, *refs[:n], *rank, *refs[n + len(ranked):])

    vmem = pl.BlockSpec(memory_space=pltpu.VMEM)
    return pl.pallas_call(
        body,
        name=name,
        out_shape=[jax.ShapeDtypeStruct(s, jnp.float32) for s in outs],
        in_specs=[pl.BlockSpec(memory_space=pltpu.SMEM)] + [vmem] * (n + len(ranked)),
        out_specs=[vmem] * len(outs),
        scratch_shapes=[pltpu.VMEM(s, jnp.float32) for s in scratch],
        compiler_params=pltpu.CompilerParams(vmem_limit_bytes=limit << 20),
        interpret=INTERPRET,
    )(idx, *full, *ranked)


def exact_dot(a, b):
    return jnp.dot(a, b, precision=HI, preferred_element_type=jnp.float32)


def project(x, rows):
    return lax.dot_general(x, rows, (((1,), (1,)), ((), ())), precision=HI,
                           preferred_element_type=jnp.float32)


def combine(row, values):
    total = None
    for c, v in zip(row, values):
        if c != 0.0:
            total = c * v if total is None else total + c * v
    return total


def layer_yz(src, dst, vec):
    def over_y(y, _):
        q = [src[zi, y] for zi in range(4)]
        for zi in range(4):
            v = vec[0, 2:3] * combine(D4[zi], q)
            if zi == 0:
                v = v + vec[0, 5:6] * (q[0] - pltpu.roll(q[3], 1, 0))
            if zi == 3:
                v = v + vec[0, 6:7] * (pltpu.roll(q[0], 15, 0) - q[3])
            dst[zi, y] = v
        return 0
    lax.fori_loop(0, 8, over_y, 0, unroll=True)

    def over_z(zi, _):
        q = [src[zi, y] for y in range(8)]
        for y in range(8):
            e, yi = 4 * (y // 4), y % 4
            v = vec[0, 1:2] * combine(D4[yi], q[e:e + 4])
            if yi == 0:
                v = v + vec[0, 3:4] * (q[y] - q[(y + 7) % 8])
            if yi == 3:
                v = v + vec[0, 4:5] * (q[(y + 1) % 8] - q[y])
            dst[zi, y] = dst[zi, y] + v
        return 0
    lax.fori_loop(0, 4, over_z, 0, unroll=True)


def every_fourth(h, xi, y, zi):
    if INTERPRET:
        return h[xi, y][zi::4]
    return h[xi, y, pl.ds(zi, 16, stride=4), :]


def speed_rows(idx, vec):
    j = lax.broadcasted_iota(jnp.int32, (1, 128), 1)
    m = ((idx[0] * 64 + (j & 63)) * 5179 + 7) & 16383
    s = j >> 6
    x, y, z = [-4.0 + 0.25 * (n.astype(jnp.float32) + 0.5)
               for n in (16 * s + (m >> 10), (m >> 5) & 31, m & 31)]
    pos = s > 0
    rows = {0: -DT * 0.5 * x, 1: -DT * 0.5 * y, 2: -DT * 0.5 * z,
            3: -3 * DT * jnp.maximum(y, 0.0), 4: -3 * DT * jnp.minimum(y, 0.0),
            5: -3 * DT * jnp.maximum(z, 0.0), 6: -3 * DT * jnp.minimum(z, 0.0),
            14: pos.astype(jnp.float32)}
    for n in range(4):
        rows[15 + n] = -DT * 0.5 * x * jnp.where(pos, D4[3][n], D4[0][n])
    rows[24], rows[25], rows[26], rows[27] = jnp.ones_like(x), x, y, z
    rows[28] = 2.0 * (x * x + y * y + z * z) / 3.0 - 1.0
    vec[...] = jnp.zeros_like(vec)
    for n, v in rows.items():
        vec[0, n:n + 1] = v


def rim_kernel(idx, h, up, down, q, t, ends, m, vec):
    speed_rows(idx, vec)
    transport_rims(idx, h, vec, up, down, q, t, ends, m)


def transport_rims(idx, h, vec, up, down, q, t, ends, m):
    pos = vec[0, 14:15] > 0.5
    for zi in range(4):
        def over_y(y, _):
            x = [every_fourth(h, xi, y, zi) for xi in range(4)]
            ql = jnp.where(pos, x[3], x[0])
            q[zi, y] = ql
            ends[zi, y] = x[0]
            ends[4 + zi, y] = x[3]
            v = 0.8 * ql
            for j in range(4):
                v = v + vec[0, 15 + j:16 + j] * x[j]
            up[pl.ds(pl.multiple_of((zi * 8 + y) * 16, 16), 16)] = v
            return 0
        lax.fori_loop(0, 8, over_y, 0, unroll=True)
    layer_yz(q, t, vec)
    right = lax.broadcasted_iota(jnp.int32, (16, 128), 1) >= 64

    def pack(n, _):
        zi, y = n // 8, n % 8
        at = pl.ds(pl.multiple_of(n * 16, 16), 16)
        tl = pltpu.roll(t[zi, y] + up[at], 64, 1)
        ql = q[zi, y]
        up[at] = jnp.where(right, ql, tl)
        down[at] = jnp.where(right, tl, ql)
        return 0
    lax.fori_loop(0, 32, pack, 0, unroll=8)
    m[...] = project(ends[...].reshape(1024, 128), vec[0, 24:32])
    for n in range(8):
        zi, out = n % 4, (down, up)[n // 4]
        out[512 + 8 * zi:520 + 8 * zi] = m[128 * n:128 * n + 128].T


def local_update(src, dst, vec):
    def over_y(y, _):
        q = [src[c, y] for c in range(16)]
        for xi in range(4):
            for zi in range(4):
                own = q[xi * 4 + zi]
                v = 0.8 * own + vec[0, 0:1] * combine(D4[xi], [q[j * 4 + zi] for j in range(4)])
                v = v + vec[0, 2:3] * combine(D4[zi], q[xi * 4:xi * 4 + 4])
                if zi == 0:
                    v = v + vec[0, 5:6] * (own - pltpu.roll(q[xi * 4 + 3], 1, 0))
                if zi == 3:
                    v = v + vec[0, 6:7] * (pltpu.roll(q[xi * 4], 15, 0) - own)
                if xi == 0:
                    v = v + vec[0, 7:8] * own
                if xi == 3:
                    v = v + vec[0, 8:9] * own
                dst[xi * 4 + zi, y] = v
        return 0
    lax.fori_loop(0, 8, over_y, 0, unroll=2)

    def over_c(c, _):
        q = [src[c, y] for y in range(8)]
        for y in range(8):
            e, yi = 4 * (y // 4), y % 4
            v = vec[0, 1:2] * combine(D4[yi], q[e:e + 4])
            if yi == 0:
                v = v + vec[0, 3:4] * (q[y] - q[(y + 7) % 8])
            if yi == 3:
                v = v + vec[0, 4:5] * (q[(y + 1) % 8] - q[y])
            dst[c, y] = dst[c, y] + v
        return 0
    lax.fori_loop(0, 16, over_c, 0, unroll=4)


def row_of_y():
    y = lax.broadcasted_iota(jnp.int32, (8, 128), 0)
    return (lax.broadcasted_iota(jnp.int32, (8, 128), 1) // 16 == y).astype(jnp.float32)


def local_kernel(idx, h, forcing, select, vec, tab0, tab1, twice, mom, force, first, once, m):
    spread = exact_dot(forcing[...].reshape(96, 64), select[...])
    here = row_of_y()
    force[...] = jnp.zeros_like(force)
    for f in range(3):
        for c in range(16):
            n = 8 * (f * 4 + c // 4)
            v = spread[n:n + 8, 128 * (c % 4):128 * (c % 4) + 128] * here
            at = 5 * (c // 4) + f + 1
            force[c % 4, at:at + 1] = jnp.sum(v, axis=0, keepdims=True)
    for c in range(16):
        xi, zi = c // 4, c % 4

        def over_y(y, _):
            first[c, y] = every_fourth(h, xi, y, zi)
            return 0
        lax.fori_loop(0, 8, over_y, 0, unroll=True)
    local_update(first, once, vec)
    local_update(once, twice, vec)

    m[...] = project(first[...].reshape(2048, 128), tab0[0])
    m[...] = m[...] + project(once[...].reshape(2048, 128), tab1[0])
    for c in range(16):
        mom[c] = m[128 * c:128 * c + 128].T[32:48]


def z_before(q, lt):
    return jnp.where(lt[24:25] > 0.5, pltpu.roll(q, 113, 1), pltpu.roll(q, 1, 1))


def z_after(q, lt):
    return jnp.where(lt[25:26] > 0.5, pltpu.roll(q, 15, 1), pltpu.roll(q, 127, 1))


SHIFTS = (-3, -2, -1, 1, 2, 3)


def central_y(q, lt):
    total = None
    for n, s in enumerate(SHIFTS):
        term = lt[n:n + 1] * pltpu.roll(q, (-16 * s) % 128, 1)
        total = term if total is None else total + term
    return total


def one_sided(load, low, high, c, lt):
    xi, zi = c // 4, c % 4
    q = load(c)
    cx = combine([0.5 * v for v in D4[xi]], [load(j * 4 + zi) for j in range(4)])
    px = cx + 3.0 * (q - low(zi)) if xi == 0 else cx
    mx = cx + 3.0 * (high(zi) - q) if xi == 3 else cx
    cy = lt[32:33] * q
    for n, s in enumerate(SHIFTS):
        r = pltpu.roll(q, (-16 * s) % 128, 1)
        cy = cy + lt[26 + n:27 + n] * r
        if s == -1:
            py = lt[33:34] * (q - r)
        if s == 1:
            my = lt[34:35] * (r - q)
    cz = combine([0.5 * v for v in D4[zi]], [load(xi * 4 + j) for j in range(4)])
    pz = cz + 3.0 * (q - z_before(load(xi * 4 + 3), lt)) if zi == 0 else cz
    mz = cz + 3.0 * (z_after(load(xi * 4), lt) - q) if zi == 3 else cz
    return [px, mx, cy + py, cy + my, pz, mz]


CENTRAL = [[0.0 if i == j else 0.5 * D4[i][j] for j in range(4)] for i in range(4)]


def moment_kernel(idx, up, down, twice, moma, mix, lt, vec, tab2, tab1, pay, t2,
                  delta, yz, extra, mom, full, m, stack):
    right = lax.broadcasted_iota(jnp.int32, (16, 128), 1) >= 64
    pos = vec[0, 14:15]

    def unpack(n, _):
        at = pl.ds(pl.multiple_of(n * 16, 16), 16)
        u, d = up[at], down[at]
        zi, y = n // 8, n % 8
        delta[zi, y] = vec[0, 9:10] * jnp.where(right, u, d)
        extra[zi, y] = vec[0, 9:10] * pltpu.roll(jnp.where(right, d, u), 64, 1)
        return 0
    lax.fori_loop(0, 32, unpack, 0, unroll=8)
    layer_yz(delta, yz, vec)
    for xi in range(4):
        def over_n(n, _):
            zi, y = n // 8, n % 8
            v = twice[xi * 4 + zi, y] + vec[0, 10 + xi:11 + xi] * delta[zi, y]
            if xi in (0, 3):
                w = pos if xi == 0 else 1.0 - pos
                v = v + w * (yz[zi, y] + extra[zi, y])
            t2[xi * 4 + zi, y] = v
            return 0
        lax.fori_loop(0, 32, over_n, 0, unroll=8)

    m[...] = project(t2[...].reshape(2048, 128), tab2[0])
    d = delta[...].reshape(512, 128)
    m[0:512] = m[0:512] + project(d * pos, tab1[0])
    m[1536:2048] = m[1536:2048] + project(d * (1.0 - pos), tab1[0])
    for c in range(16):
        t = m[128 * c:128 * c + 128].T
        mom[c, 0:32] = t[0:32]
        mom[c, 32:48] = t[32:48] + moma[c]

    def load0(c):
        return mom[c, 32:40]

    for c in range(16):
        six = one_sided(load0, lambda zi: up[512 + 8 * zi:520 + 8 * zi],
                        lambda zi: down[512 + 8 * zi:520 + 8 * zi], c, lt)
        at = slice(128 * c, 128 * c + 128)
        stack[0:16, at] = mom[c, 32:48]
        for n in range(6):
            stack[16 + 8 * n:24 + 8 * n, at] = six[n]
    add = exact_dot(mix[...], stack[...])
    for c in range(16):
        at = slice(128 * c, 128 * c + 128)
        full[c, 0:32] = mom[c, 0:32] + add[0:32, at]
        full[c, 32:40] = add[32:40, at]
    for c in range(16):
        xi, zi = c // 4, c % 4
        r = combine(CENTRAL[xi], [full[j * 4 + zi, 8:16] for j in range(4)])
        r = r + central_y(full[c, 16:24], lt)
        r = r + combine(CENTRAL[zi], [full[xi * 4 + j, 24:32] for j in range(4)])
        if zi == 0:
            r = r - 1.5 * z_before(full[xi * 4 + 3, 24:32], lt)
        if zi == 3:
            r = r + 1.5 * z_after(full[xi * 4, 24:32], lt)
        q = 32 * zi + 5 * xi
        pay[q:q + 5] = -r[0:5]
        pay[128 + 5 * c:133 + 5 * c] = full[c, 0:5]
        pay[208 + 5 * c:213 + 5 * c] = mom[c, 32:37]
        pay[288 + 5 * c:293 + 5 * c] = full[c, 32:37]
    for zi in range(4):
        pay[32 * zi + 20:32 * zi + 25] = full[zi, 8:13]
        pay[32 * zi + 25:32 * zi + 30] = full[12 + zi, 8:13]
        pay[32 * zi + 30:32 * zi + 32] = jnp.zeros((2, 128), jnp.float32)
        pay[368 + 5 * zi:373 + 5 * zi] = up[512 + 8 * zi:517 + 8 * zi]
        pay[388 + 5 * zi:393 + 5 * zi] = down[512 + 8 * zi:517 + 8 * zi]


def residual_kernel(idx, got, force, out):
    at = pl.ds(pl.multiple_of(32 * idx[0], 32), 32)
    t = got[0, at] + got[1, at] + got[2, at] + got[3, at]
    v = t[0:20] + force[idx[0]]
    for n in range(8):
        out[n, 0:20] = v
        out[n, 20:30] = t[20:30]


def feq_kernel(idx, got, t2, lt, final, h2, low, s0, lo, hi, stack):
    def total(a, n):
        return got[0, a:a + n] + got[1, a:a + n] + got[2, a:a + n] + got[3, a:a + n]

    s0[...] = jnp.zeros_like(s0)
    lo[...] = jnp.zeros_like(lo)
    hi[...] = jnp.zeros_like(hi)
    for c in range(16):
        s0[c, 0:5] = total(208 + 5 * c, 5)
    for zi in range(4):
        lo[zi, 0:5] = total(368 + 5 * zi, 5)
        hi[zi, 0:5] = total(388 + 5 * zi, 5)
    low[...] = total(128, 80)
    pad = jnp.zeros((3, 128), jnp.float32)
    for c in range(16):
        z = jnp.concatenate([0.2 * total(288 + 5 * c, 5), pad], axis=0) + 0.16 * s0[c]
        six = one_sided(lambda k: s0[k], lambda zi: lo[zi], lambda zi: hi[zi], c, lt)
        for n, v in enumerate([z] + six):
            stack[8 * n:8 * n + 8, 128 * c:128 * c + 128] = v
    add = lax.dot_general(stack[...], final[0], (((0,), (0,)), ((), ())), precision=HI,
                          preferred_element_type=jnp.float32)
    h2[...] = t2[...] + add.reshape(16, 8, 16, 128)


def apply_k(src, dst, lt, own=False):
    rows = slice(8, 16) if own else slice(0, 24)

    def before(k, add):
        if own:
            return src[k, 7:15] + src[k + add, 7:15] if add else src[k, 7:15]
        return pltpu.roll(src[k] + src[k + add] if add else src[k], 1, 0)

    def after(k, add):
        if own:
            return src[k, 9:17] + src[k + add, 9:17] if add else src[k, 9:17]
        return pltpu.roll(src[k] + src[k + add] if add else src[k], 23, 0)

    for zi in range(4):
        u = [src[16 + j * 4 + zi, rows] for j in range(4)]
        p = [src[j * 4 + zi, rows] + src[64 + j * 4 + zi, rows] for j in range(4)]
        for xi in range(4):
            du = combine(CENTRAL[xi], u)
            dp = combine(CENTRAL[xi], p)
            if xi == 0:
                du = du - 1.5 * before(28 + zi, 0)
                dp = dp - 1.5 * before(12 + zi, 64)
            if xi == 3:
                du = du + 1.5 * after(16 + zi, 0)
                dp = dp + 1.5 * after(zi, 64)
            dst[xi * 4 + zi] = du
            dst[16 + xi * 4 + zi] = dp
    for xi in range(4):
        u = [src[48 + xi * 4 + j, rows] for j in range(4)]
        p = [src[xi * 4 + j, rows] + src[64 + xi * 4 + j, rows] for j in range(4)]
        for zi in range(4):
            du = combine(CENTRAL[zi], u)
            dp = combine(CENTRAL[zi], p)
            if zi == 0:
                du = du - 1.5 * z_before(u[3], lt)
                dp = dp - 1.5 * z_before(p[3], lt)
            if zi == 3:
                du = du + 1.5 * z_after(u[0], lt)
                dp = dp + 1.5 * z_after(p[0], lt)
            dst[xi * 4 + zi] = dst[xi * 4 + zi] + du
            dst[48 + xi * 4 + zi] = dp

    def along_y(c, _):
        rho, u, t = src[c, rows], src[32 + c, rows], src[64 + c, rows]
        div = dst[c] + central_y(u, lt)
        dst[32 + c] = central_y(rho + t, lt)
        dst[c] = div
        dst[64 + c] = div
        return 0
    lax.fori_loop(0, 16, along_y, 0, unroll=8)


def two_level(r, pe, co, lt):
    def over_f(f, _):
        tz = [[None, None] for _ in range(4)]
        for xi in range(4):
            q = [r[f * 16 + xi * 4 + zi] for zi in range(4)]
            for za in range(2):
                tz[xi][za] = combine(RT[za], q)
        for za in range(2):
            py = []
            for xa in range(2):
                t = combine(RT[xa], [tz[xi][za] for xi in range(4)])
                e0, e1 = lt[9:10] * t, lt[16:17] * t
                for s in SHIFTS:
                    rolled = pltpu.roll(t, (-16 * s) % 128, 1)
                    e0 = e0 + lt[9 + s:10 + s] * rolled
                    e1 = e1 + lt[16 + s:17 + s] * rolled
                co[f * 8 + xa * 4 + za * 2] = e0
                co[f * 8 + xa * 4 + za * 2 + 1] = e1
                py.append(lt[20:21] * e0 + lt[21:22] * e1)
            for xi in range(4):
                v = combine(PR[xi], py)
                for zi in range(4):
                    if PR[zi][za] == 0.0:
                        continue
                    at = f * 16 + xi * 4 + zi
                    if za == 0 or PR[zi][0] == 0.0:
                        pe[at] = PR[zi][za] * v
                    else:
                        pe[at] = pe[at] + PR[zi][za] * v
        return 0
    lax.fori_loop(0, 5, over_f, 0)


def coarse_products(co, lt):
    def at(f, xa, za, ya):
        return co[f * 8 + xa * 4 + za * 2 + ya]

    def own(q):
        return q[8:16]

    def dx(q, xa, za, ya):
        if xa == 0:
            v = q(1, za, ya)
            return 0.25 * (own(v) - own(pltpu.roll(v, 1, 0)))
        v = q(0, za, ya)
        return 0.25 * (own(pltpu.roll(v, 23, 0)) - own(v))

    def dz(q, xa, za, ya):
        v = own(q(xa, 1 - za, ya))
        if za == 0:
            return 0.25 * (v - z_before(v, lt))
        return 0.25 * (z_after(v, lt) - v)

    def dy(q, xa, za, ya):
        v = own(q(xa, za, 1 - ya))
        w = pltpu.roll(v, 64, 1)
        return 0.25 * (v - w) if ya == 0 else 0.25 * (w - v)

    total = [jnp.zeros((8, 128), jnp.float32)] * 3
    for xa in range(2):
        for za in range(2):
            for ya in range(2):
                def field(f):
                    return lambda a, b, c: at(f, a, b, c)

                def pressure(a, b, c):
                    return at(0, a, b, c) + at(4, a, b, c)
                e = [own(at(f, xa, za, ya)) for f in range(5)]
                div = (dx(field(1), xa, za, ya) + dy(field(2), xa, za, ya)
                       + dz(field(3), xa, za, ya))
                v = [div, dx(pressure, xa, za, ya), dy(pressure, xa, za, ya),
                     dz(pressure, xa, za, ya), div]
                for f in range(5):
                    total = [total[0] + e[f] * e[f], total[1] + e[f] * v[f], total[2] + v[f] * v[f]]
    return [t * lt[23:24] for t in total]


PAIRS = [(i, j) for i in range(3) for j in range(i, 3)]


def fine_products(e, s, t, ke, kt, lt, own):
    rows = slice(0, 8) if own else slice(8, 16)
    zero = jnp.zeros((8, 128), jnp.float32)
    total = [zero] * 18
    for xi in range(4):
        for zi in range(4):
            acc = [zero] * 18
            for f in range(5):
                k = f * 16 + xi * 4 + zi
                x = [e[k, 8:16], s[k, 8:16], t[k, 8:16]]
                y = [ke[k, rows], x[2], kt[k, rows]]
                for n, (i, j) in enumerate(PAIRS):
                    acc[n] = acc[n] + x[i] * x[j]
                    mixed = x[i] * y[j] if i == j else x[i] * y[j] + x[j] * y[i]
                    acc[6 + n] = acc[6 + n] + mixed
                    acc[12 + n] = acc[12 + n] + y[i] * y[j]
            w = WEIGHTS[xi] * WEIGHTS[zi]
            total = [a + w * b for a, b in zip(total, acc)]
    return [a * lt[22:23] for a in total]


def diagonal():
    return (lax.broadcasted_iota(jnp.int32, (24, 128), 0)
            == lax.broadcasted_iota(jnp.int32, (24, 128), 1))


def pass_words(e, s, t, ke, kt, co, gram, lt, own=False):
    two_level(e, s, co, lt)
    apply_k(s, t, lt)

    def over_k(k, _):
        e[k] = e[k] - s[k]
        return 0
    lax.fori_loop(0, 80, over_k, 0, unroll=8)
    apply_k(e, ke, lt, own)
    apply_k(t, kt, lt, own)
    products = coarse_products(co, lt) + fine_products(e, s, t, ke, kt, lt, own)
    rows = [jnp.sum(p, axis=0, keepdims=True) for p in products] + [jnp.zeros((3, 128), jnp.float32)]
    total = jnp.sum(jnp.concatenate(rows, axis=0), axis=1, keepdims=True)
    line = jnp.sum(jnp.where(diagonal(), total, 0.0), axis=0, keepdims=True)
    for n in range(gram.shape[0]):
        gram[n] = jnp.broadcast_to(line, (8, 128))


def pack_kernel(idx, mine, own, to_upper, to_lower):
    first = lax.broadcasted_iota(jnp.int32, (8, 128), 0) == 0
    last = lax.broadcasted_iota(jnp.int32, (8, 128), 0) == 7
    for f in range(5):
        low = mine[pl.ds(20 + f, 8, stride=30), :]
        high = mine[pl.ds(25 + f, 8, stride=30), :]
        for xi in range(4):
            k = f * 4 + xi
            v = mine[pl.ds(5 * xi + f, 8, stride=30), :]
            if xi == 0:
                v = v + 1.5 * jnp.where(first, 0.0, pltpu.roll(high, 1, 0))
            if xi == 3:
                v = v - 1.5 * jnp.where(last, 0.0, pltpu.roll(low, 7, 0))
            own[k] = v
            to_upper[pl.ds(k, 6, stride=20), :] = v[2:8]
            to_lower[pl.ds(k, 6, stride=20), :] = v[0:6]
        to_upper[120 + f:121 + f] = high[7:8]
        to_lower[120 + f:121 + f] = low[0:1]


def window_kernel(idx, lower, own, upper, edge_low, edge_high, after, win):
    for f in range(5):
        e = 120 + f
        for xi in range(4):
            k = f * 4 + xi
            at = 20 * k
            low, mid, high = lower[pl.ds(k, 6, stride=20), :], own[k], upper[pl.ds(k, 6, stride=20), :]
            win[at:at + 6] = low
            win[at + 6:at + 14] = mid
            win[at + 14:at + 20] = high
            if xi == 0:
                win[at + 6:at + 7] = mid[0:1] + 1.5 * lower[e:e + 1]
                win[at + 14:at + 15] = high[0:1] + 1.5 * edge_high[e:e + 1]
            if xi == 3:
                win[at + 13:at + 14] = mid[7:8] - 1.5 * upper[e:e + 1]
                win[at + 5:at + 6] = low[5:6] - 1.5 * edge_low[e:e + 1]


def first_pass_kernel(idx, quarters, lt, r, s, t, ke, kt, gram, co):
    zero = jnp.zeros((2, 128), jnp.float32)
    for f in range(5):
        for xi in range(4):
            for zi in range(4):
                k = f * 16 + xi * 4 + zi
                at = 20 * (f * 4 + xi)
                r[k, 0:2] = zero
                r[k, 2:22] = quarters[zi, at:at + 20]
                r[k, 22:24] = zero
    pass_words(r, s, t, ke, kt, co, gram, lt)


def step_sizes(sums):
    line = sums[0, 0:1]
    for n in range(1, sums.shape[0]):
        line = line + sums[n, 0:1]
    v = jnp.sum(jnp.where(diagonal(), line, 0.0), axis=1, keepdims=True)
    v = jnp.broadcast_to(v, (24, 128))
    c0, c1, c2 = v[0:1], v[1:2], v[2:3]
    den = 4.0 * c0 + 4.0 * c1 + c2 + EPS
    a1, b1 = (2.0 * c0 + c1) / den, (2.0 * c1 + c2 + EPS) / den
    d = [jnp.ones_like(a1), b1, -a1]

    def form(base, twice):
        total = None
        for n, (i, j) in enumerate(PAIRS):
            term = d[i] * d[j] * v[base + n:base + n + 1]
            if twice and i != j:
                term = 2.0 * term
            total = term if total is None else total + term
        return total
    rr, kk = jnp.maximum(form(3, True), 0.0), jnp.maximum(form(15, True), 0.0)
    bound = jnp.sqrt(rr) * jnp.sqrt(kk)
    rk = jnp.clip(form(9, False), -bound, bound)
    den = 4.0 * rr + 4.0 * rk + kk + EPS
    return a1, b1, (2.0 * rr + rk) / den, (2.0 * rk + kk + EPS) / den


def next_pass_kernel(first, idx, sums, e, s, t, ke, kt, *rest):
    if first:
        lt, r2, s2, t2, ke2, kt2, acc2, gram, co = rest
    else:
        acc, lt, r2, s2, t2, ke2, kt2, acc2, gram, co = rest
    a1, b1, a2, b2 = step_sizes(sums)

    def over_k(k, _):
        sk, tk = s[k], t[k]
        r1 = e[k] + b1 * sk - a1 * tk
        v = a1 * sk[8:16] + a2 * r1[8:16]
        acc2[k] = v if first else acc[k] + v
        r2[k] = b2 * r1 - a2 * (ke[k] + b1 * tk - a1 * kt[k])
        return 0
    lax.fori_loop(0, 80, over_k, 0, unroll=4)
    pass_words(r2, s2, t2, ke2, kt2, co, gram, lt, own=not first)


def third_pass_kernel(idx, sums, e, s, t, ke, kt, acc, lt, eo, so, to, acc2, gram,
                      r2, s2, t2, ke2, kt2, co):
    next_pass_kernel(False, idx, sums, e, s, t, ke, kt, acc, lt, r2, s2, t2, ke2, kt2, acc2, gram, co)
    eo[...] = r2[:, 8:16]
    so[...] = s2[:, 8:16]
    to[...] = t2[:, 8:16]


def last_kernel(idx, sums, e, s, t, acc, low, h2, select, ec, out, fields, change, stack, rows):
    a1, b1, a2, _ = step_sizes(sums)

    def over_k(k, _):
        r1 = e[k] + b1 * s[k] - a1 * t[k]
        change[pl.ds(pl.multiple_of(k * 8, 8), 8)] = acc[k] + a1 * s[k] + a2 * r1
        return 0
    lax.fori_loop(0, 80, over_k, 0, unroll=4)
    z = idx[1]
    stack[...] = jnp.zeros_like(stack)
    here = row_of_y()
    for c in range(16):
        for f in range(5):
            k = f * 16 + c
            d = change[pl.ds(k * 8 + z, 1)]
            stack[f:f + 1, 128 * c:128 * c + 128] = d
            n = 8 * (k // 4)
            rows[n:n + 8, 128 * (c % 4):128 * (c % 4) + 128] = (low[5 * c + f:5 * c + f + 1] + d) * here
    fields[...] = project(rows[...], select[...]).reshape(5, 4, 8, 64)
    add = lax.dot_general(stack[...], ec[0], (((0,), (0,)), ((), ())), precision=HI,
                          preferred_element_type=jnp.float32).reshape(16, 8, 16, 128)
    for c in range(16):
        xi, zi = c // 4, c % 4
        v = h2[c] + add[c]
        for y in range(8):
            out[xi, y, pl.ds(zi, 16, stride=4), :] = v[y]


def on_device(distribution, forcing):
    import functools
    tables = {k: jnp.asarray(v) for k, v in constant_tables().items()}
    spaces = lax.axis_size("space")
    blocks = spaces // 8
    idx = jnp.stack([lax.axis_index("vel"), lax.axis_index("space") % 8]).astype(jnp.int32)
    vec, lt = tables["vec"], tables["lanes"]
    wide = (16, 8, 16, 128)
    layer = (4, 8, 16, 128)

    def shifted(x, by):
        return lax.ppermute(x, "space", [(i, (i + by) % spaces) for i in range(spaces)])

    up, down = call(rim_kernel, "rims", idx, [distribution], [],
                    [(544, 128)] * 2, [layer, layer, (8, 8, 16, 128), (1024, 8), (1, 32, 128)])
    up, down = shifted(up, 1), shifted(down, -1)
    twice, moma, force = call(local_kernel, "local", idx, [distribution, forcing, tables["select"]],
                              [vec, tables["tab0"], tables["tab1"]],
                              [wide, (16, 16, 128), (4, 20, 128)], [wide, wide, (2048, 48)])
    pay, t2 = call(moment_kernel, "moments", idx, [up, down, twice, moma, tables["mix"], lt],
                   [vec, tables["tab2"], tables["tab1"]], [(408, 128), wide],
                   [layer, layer, layer, (16, 48, 128), (16, 40, 128), (2048, 48), (64, 2048)])
    got = lax.all_gather(pay, "vel")
    (res,) = call(residual_kernel, "residual", idx, [got, force], [], [(8, 30, 128)])
    near = [[a * 8 + b for b in range(8)] for a in range(blocks)]
    far = [[a * 8 + b for a in range(blocks)] for b in range(8)]
    mine = lax.all_to_all(res, "space", 0, 0, axis_index_groups=near, tiled=True).reshape(240, 128)
    own_r, to_upper, to_lower = call(pack_kernel, "pack", idx, [mine], [],
                                     [(20, 8, 128), (125, 128), (125, 128)])
    lower, upper = shifted(to_upper, 8), shifted(to_lower, -8)
    h2, low = call(feq_kernel, "feq", idx, [got, t2, lt], [tables["final"]],
                   [wide, (80, 128)], [(16, 8, 128), (4, 8, 128), (4, 8, 128), (56, 2048)])
    (quarter,) = call(window_kernel, "window", idx, [lower, own_r, upper, to_lower, to_upper, low], [],
                      [(400, 128)])
    quarters = lax.all_gather(quarter, "vel")

    def summed(gram):
        return lax.all_to_all(gram, "space", 0, 0, axis_index_groups=far, tiled=True)

    win, own, part = (80, 24, 128), (80, 8, 128), (blocks, 8, 128)
    co = (40, 24, 128)
    e, s, t, ke, kt, gram = call(first_pass_kernel, "pass1", idx, [quarters, lt], [],
                                  [win] * 5 + [part], [co])
    e, s, t, ke, kt, acc, gram = call(functools.partial(next_pass_kernel, True), "pass2", idx,
                                       [summed(gram), e, s, t, ke, kt, lt], [],
                                       [win] * 5 + [own, part], [co])
    e, s, t, acc, gram = call(third_pass_kernel, "pass3", idx,
                               [summed(gram), e, s, t, ke, kt, acc, lt], [],
                               [own] * 4 + [part], [win, win, win, own, own, co])
    out, fields = call(last_kernel, "last", idx,
                       [summed(gram), e, s, t, acc, low, h2, tables["select"]], [tables["ec"]],
                       [(4, 8, 64, 128), (5, 4, 8, 64)], [(640, 128), (8, 2048), (160, 512)])
    return out, fields


def solution(mesh):
    return jax.shard_map(
        on_device,
        mesh=mesh,
        in_specs=(P("space", None, None, "vel"), P(None, "space", None, None)),
        out_specs=(P("space", None, None, "vel"), P(None, "space", None, None)),
        check_vma=False,
    )
```

```python
import math

import jax
import jax.numpy as jnp
import numpy as np
from jax import lax
from jax.experimental import pallas as pl
from jax.experimental.pallas import tpu as pltpu
from jax.sharding import PartitionSpec as P

INTERPRET = False
DT = 0.02
RF = 0.4472135954999579
POINTS = [-1.0, -RF, RF, 1.0]
WEIGHTS = [1.0 / 6.0, 5.0 / 6.0, 5.0 / 6.0, 1.0 / 6.0]
EPS = 1e-6
HI = lax.Precision.HIGHEST


def lagrange_table(points):
    n = len(points)
    bary = []
    for i in range(n):
        product = 1.0
        for j in range(n):
            if j != i:
                product *= points[i] - points[j]
        bary.append(1.0 / product)
    rows = [[0.0] * n for _ in range(n)]
    for i in range(n):
        for j in range(n):
            if j != i:
                rows[i][j] = bary[j] / bary[i] / (points[i] - points[j])
        rows[i][i] = -sum(rows[i])
    return rows


D4 = lagrange_table(POINTS)
for _i in (1, 2):
    D4[_i][_i] = 0.0
PR = [[(1.0 - x) / 2.0, (1.0 + x) / 2.0] for x in POINTS]
RT = [[WEIGHTS[i] * PR[i][a] for i in range(4)] for a in range(2)]


def constant_tables():
    k = np.arange(512)
    b, j = k // 128, k % 128
    s = j // 64
    m = ((b * 64 + j % 64) * 5179 + 7) % 16384
    xi = np.stack([16 * s + m // 1024, (m // 32) % 32, m % 32]).astype(np.float64)
    xi = -4.0 + 0.25 * (xi + 0.5)
    sq = (xi * xi).sum(0)
    e = math.pi ** (-1.5) * np.exp(-sq)
    x, y, z = xi
    phi = np.stack(
        [np.ones(512), x, y, z, 2 * sq / 3 - 1, 2 * (x * x - sq / 3), 2 * (y * y - sq / 3),
         2 * x * y, 2 * x * z, 2 * y * z, x * (sq - 2.5), y * (sq - 2.5), z * (sq - 2.5)]
    )
    p = phi[0] + phi[4]
    zero = np.zeros(512)

    def eight(rows):
        return np.stack(list(rows) + [zero] * (8 - len(rows)))

    low = eight(phi[:5])
    along_x = eight([phi[1], p + phi[5], phi[7], phi[8], phi[1] + phi[10]])
    along_y = eight([phi[2], phi[7], p + phi[6], phi[9], phi[2] + phi[11]])
    along_z = eight([phi[3], phi[8], phi[9], p - phi[5] - phi[6], phi[3] + phi[12]])
    rows32 = np.concatenate([low, along_x, along_y, along_z])
    ec = eight([e, 2 * x * e, 2 * y * e, 2 * z * e, e * (sq - 1.5)])
    pos, neg = np.maximum(xi, 0.0), np.minimum(xi, 0.0)

    def per_rank(rows):
        return np.stack([rows[:, r * 128:(r + 1) * 128] for r in range(4)]).astype(np.float32)

    ispos = (x > 0).astype(np.float64)
    ax = np.abs(x)
    d4 = np.array(D4)
    vec = [-DT * 0.5 * x, -DT * 0.5 * y, -DT * 0.5 * z,
           -3 * DT * pos[1], -3 * DT * neg[1], -3 * DT * pos[2], -3 * DT * neg[2],
           -3 * DT * pos[0], 3 * DT * neg[0], 3 * DT * ax]
    for i in range(4):
        kap = -DT * 0.5 * x * np.where(ispos > 0, d4[i][0], d4[i][3])
        if i == 0:
            kap = kap + ispos * (0.8 - 3 * DT * ax)
        if i == 3:
            kap = kap + (1 - ispos) * (0.8 - 3 * DT * ax)
        vec.append(kap)
    kappa = vec[10:14]
    vec.append(ispos)
    for jj in range(4):
        vec.append(-DT * 0.5 * x * np.where(ispos > 0, d4[3][jj], d4[0][jj]))
    while len(vec) < 24:
        vec.append(zero)
    vec = per_rank(np.concatenate([np.stack(vec), low]))

    def moment_rows(start, rows, height):
        out = np.zeros((height, 512))
        out[start:start + len(rows)] = rows
        return per_rank(out)

    tab2 = moment_rows(0, rows32, 48)
    tab1 = moment_rows(40, low, 48)
    tab0 = moment_rows(32, low, 48)
    tabd = per_rank(np.concatenate([v * rows32 for v in kappa] + [ispos * low, (1 - ispos) * low]))
    tabs = per_rank(np.concatenate([ispos * rows32, (1 - ispos) * rows32]))
    select = np.zeros((64, 512))
    for n in range(4):
        for la in range(128):
            select[4 * (la % 16) + n, 128 * n + la] = 1.0
    import ml_dtypes
    pieces, left = [], per_rank(ec)
    for _ in range(3):
        pieces.append(left.astype(ml_dtypes.bfloat16))
        left = left - pieces[-1].astype(np.float32)
    split = np.concatenate([pieces[n].astype(np.float32) for n in (0, 1, 0, 2, 1, 0)], axis=1)
    g = rows32 @ ec.T
    g5 = g[:8]
    mix = np.zeros((40, 64))
    mix[:32, 0:8] = 0.16 * g + 0.04 * g @ g5
    mix[:32, 8:16] = 0.2 * g
    mix[32:, 0:8] = 0.2 * g5
    mix[32:, 8:16] = np.eye(8)
    final = [ec]
    for d in range(3):
        for i, part in enumerate((pos[d], neg[d])):
            c0 = 16 + 16 * d + 8 * i
            mix[:32, c0:c0 + 8] = -0.2 * DT * (rows32 * part) @ ec.T
            final.append(-0.2 * DT * ec * part)
    final = per_rank(np.concatenate(final))
    lane = np.arange(128)
    yi, ze = (lane // 16) % 4, lane % 16
    rows = []
    shifts = (-3, -2, -1, 1, 2, 3)

    def entry(table, sft):
        return np.array([table(i, i + sft) if 0 <= i + sft < 4 else 0.0 for i in yi])

    for sft in shifts:
        c = entry(lambda i, q: 0.5 * D4[i][q], sft)
        if sft == -1:
            c = c - 1.5 * (yi == 0)
        if sft == 1:
            c = c + 1.5 * (yi == 3)
        rows.append(c)
    for a in range(2):
        for sft in range(-3, 4):
            rows.append(entry(lambda i, q: RT[a][q], sft))
    rows += [np.array([PR[i][0] for i in yi]), np.array([PR[i][1] for i in yi])]
    rows += [np.array([WEIGHTS[i] for i in yi]), (yi == 0) * 1.0, (ze == 0) * 1.0, (ze == 15) * 1.0]
    for sft in shifts:
        rows.append(entry(lambda i, q: 0.5 * D4[i][q], sft))
    rows += [entry(lambda i, q: 0.5 * D4[i][q], 0), 3.0 * (yi == 0), 3.0 * (yi == 3)]
    while len(rows) < 40:
        rows.append(np.zeros(128))
    lanes = np.stack(rows).astype(np.float32)
    return dict(vec=vec, tab2=tab2, tab1=tab1, tab0=tab0, mix=mix.astype(np.float32),
                final=final, lanes=lanes, split=split, tabd=tabd, tabs=tabs, select=select.astype(np.float32))


def call(kernel, name, idx, full, ranked, outs, scratch=(), limit=24):
    n = len(full)

    def body(idx, *refs):
        rank = [r.at[pl.ds(idx[0], 1)] for r in refs[n:n + len(ranked)]]
        kernel(idx, *refs[:n], *rank, *refs[n + len(ranked):])

    vmem = pl.BlockSpec(memory_space=pltpu.VMEM)
    return pl.pallas_call(
        body,
        name=name,
        out_shape=[jax.ShapeDtypeStruct(s, jnp.float32) for s in outs],
        in_specs=[pl.BlockSpec(memory_space=pltpu.SMEM)] + [vmem] * (n + len(ranked)),
        out_specs=[vmem] * len(outs),
        scratch_shapes=[pltpu.VMEM(s, jnp.float32) for s in scratch],
        compiler_params=pltpu.CompilerParams(vmem_limit_bytes=limit << 20),
        interpret=INTERPRET,
    )(idx, *full, *ranked)


def exact_dot(a, b):
    return jnp.dot(a, b, precision=HI, preferred_element_type=jnp.float32)


def project(x, rows):
    return lax.dot_general(x, rows, (((1,), (1,)), ((), ())), precision=HI,
                           preferred_element_type=jnp.float32)


def combine(row, values):
    total = None
    for c, v in zip(row, values):
        if c != 0.0:
            total = c * v if total is None else total + c * v
    return total


def layer_yz(src, dst, vec):
    def over_y(y, _):
        q = [src[zi, y] for zi in range(4)]
        for zi in range(4):
            v = vec[0, 2:3] * combine(D4[zi], q)
            if zi == 0:
                v = v + vec[0, 5:6] * (q[0] - pltpu.roll(q[3], 1, 0))
            if zi == 3:
                v = v + vec[0, 6:7] * (pltpu.roll(q[0], 15, 0) - q[3])
            dst[zi, y] = v
        return 0
    lax.fori_loop(0, 8, over_y, 0, unroll=True)

    def over_z(zi, _):
        q = [src[zi, y] for y in range(8)]
        for y in range(8):
            e, yi = 4 * (y // 4), y % 4
            v = vec[0, 1:2] * combine(D4[yi], q[e:e + 4])
            if yi == 0:
                v = v + vec[0, 3:4] * (q[y] - q[(y + 7) % 8])
            if yi == 3:
                v = v + vec[0, 4:5] * (q[(y + 1) % 8] - q[y])
            dst[zi, y] = dst[zi, y] + v
        return 0
    lax.fori_loop(0, 4, over_z, 0, unroll=True)


def every_fourth(h, xi, y, zi):
    if INTERPRET:
        return h[xi, y][zi::4]
    return h[xi, y, pl.ds(zi, 16, stride=4), :]


def speed_rows(idx, vec):
    j = lax.broadcasted_iota(jnp.int32, (1, 128), 1)
    m = ((idx[0] * 64 + (j & 63)) * 5179 + 7) & 16383
    s = j >> 6
    x, y, z = [-4.0 + 0.25 * (n.astype(jnp.float32) + 0.5)
               for n in (16 * s + (m >> 10), (m >> 5) & 31, m & 31)]
    pos = s > 0
    rows = {0: -DT * 0.5 * x, 1: -DT * 0.5 * y, 2: -DT * 0.5 * z,
            3: -3 * DT * jnp.maximum(y, 0.0), 4: -3 * DT * jnp.minimum(y, 0.0),
            5: -3 * DT * jnp.maximum(z, 0.0), 6: -3 * DT * jnp.minimum(z, 0.0),
            14: pos.astype(jnp.float32)}
    for n in range(4):
        rows[15 + n] = -DT * 0.5 * x * jnp.where(pos, D4[3][n], D4[0][n])
    rows[24], rows[25], rows[26], rows[27] = jnp.ones_like(x), x, y, z
    rows[28] = 2.0 * (x * x + y * y + z * z) / 3.0 - 1.0
    vec[...] = jnp.zeros_like(vec)
    for n, v in rows.items():
        vec[0, n:n + 1] = v


def rim_kernel(idx, h, up, down, q, t, ends, m, vec):
    speed_rows(idx, vec)
    transport_rims(idx, h, vec, up, down, q, t, ends, m)


def transport_rims(idx, h, vec, up, down, q, t, ends, m):
    pos = vec[0, 14:15] > 0.5
    for zi in range(4):
        def over_y(y, _):
            x = [every_fourth(h, xi, y, zi) for xi in range(4)]
            ql = jnp.where(pos, x[3], x[0])
            q[zi, y] = ql
            ends[zi, y] = x[0]
            ends[4 + zi, y] = x[3]
            v = 0.8 * ql
            for j in range(4):
                v = v + vec[0, 15 + j:16 + j] * x[j]
            up[pl.ds(pl.multiple_of((zi * 8 + y) * 16, 16), 16)] = v
            return 0
        lax.fori_loop(0, 8, over_y, 0, unroll=True)
    layer_yz(q, t, vec)
    right = lax.broadcasted_iota(jnp.int32, (16, 128), 1) >= 64

    def pack(n, _):
        zi, y = n // 8, n % 8
        at = pl.ds(pl.multiple_of(n * 16, 16), 16)
        tl = pltpu.roll(t[zi, y] + up[at], 64, 1)
        ql = q[zi, y]
        up[at] = jnp.where(right, ql, tl)
        down[at] = jnp.where(right, tl, ql)
        return 0
    lax.fori_loop(0, 32, pack, 0, unroll=8)
    m[...] = project(ends[...].reshape(1024, 128), vec[0, 24:32])
    for n in range(8):
        zi, out = n % 4, (down, up)[n // 4]
        out[512 + 8 * zi:520 + 8 * zi] = m[128 * n:128 * n + 128].T


def local_update(src, dst, vec):
    def over_y(y, _):
        q = [src[c, y] for c in range(16)]
        for xi in range(4):
            for zi in range(4):
                own = q[xi * 4 + zi]
                v = 0.8 * own + vec[0, 0:1] * combine(D4[xi], [q[j * 4 + zi] for j in range(4)])
                v = v + vec[0, 2:3] * combine(D4[zi], q[xi * 4:xi * 4 + 4])
                if zi == 0:
                    v = v + vec[0, 5:6] * (own - pltpu.roll(q[xi * 4 + 3], 1, 0))
                if zi == 3:
                    v = v + vec[0, 6:7] * (pltpu.roll(q[xi * 4], 15, 0) - own)
                if xi == 0:
                    v = v + vec[0, 7:8] * own
                if xi == 3:
                    v = v + vec[0, 8:9] * own
                dst[xi * 4 + zi, y] = v
        return 0
    lax.fori_loop(0, 8, over_y, 0, unroll=2)

    def over_c(c, _):
        q = [src[c, y] for y in range(8)]
        for y in range(8):
            e, yi = 4 * (y // 4), y % 4
            v = vec[0, 1:2] * combine(D4[yi], q[e:e + 4])
            if yi == 0:
                v = v + vec[0, 3:4] * (q[y] - q[(y + 7) % 8])
            if yi == 3:
                v = v + vec[0, 4:5] * (q[(y + 1) % 8] - q[y])
            dst[c, y] = dst[c, y] + v
        return 0
    lax.fori_loop(0, 16, over_c, 0, unroll=4)


def row_of_y():
    y = lax.broadcasted_iota(jnp.int32, (8, 128), 0)
    return (lax.broadcasted_iota(jnp.int32, (8, 128), 1) // 16 == y).astype(jnp.float32)


def local_kernel(idx, h, forcing, select, vec, tab0, tab1, tab2, twice, mom, force, first, once, m):
    spread = exact_dot(forcing[...].reshape(96, 64), select[...])
    here = row_of_y()
    force[...] = jnp.zeros_like(force)
    for f in range(3):
        for c in range(16):
            n = 8 * (f * 4 + c // 4)
            v = spread[n:n + 8, 128 * (c % 4):128 * (c % 4) + 128] * here
            at = 5 * (c // 4) + f + 1
            force[c % 4, at:at + 1] = jnp.sum(v, axis=0, keepdims=True)
    for c in range(16):
        xi, zi = c // 4, c % 4

        def over_y(y, _):
            first[c, y] = every_fourth(h, xi, y, zi)
            return 0
        lax.fori_loop(0, 8, over_y, 0, unroll=True)
    local_update(first, once, vec)
    local_update(once, twice, vec)

    m[...] = project(first[...].reshape(2048, 128), tab0[0])
    m[...] = m[...] + project(once[...].reshape(2048, 128), tab1[0])
    m[...] = m[...] + project(twice[...].reshape(2048, 128), tab2[0])
    for c in range(16):
        mom[c] = m[128 * c:128 * c + 128].T


def z_before(q, lt):
    return jnp.where(lt[24:25] > 0.5, pltpu.roll(q, 113, 1), pltpu.roll(q, 1, 1))


def z_after(q, lt):
    return jnp.where(lt[25:26] > 0.5, pltpu.roll(q, 15, 1), pltpu.roll(q, 127, 1))


SHIFTS = (-3, -2, -1, 1, 2, 3)


def central_y(q, lt):
    total = None
    for n, s in enumerate(SHIFTS):
        term = lt[n:n + 1] * pltpu.roll(q, (-16 * s) % 128, 1)
        total = term if total is None else total + term
    return total


def one_sided(load, low, high, c, lt):
    xi, zi = c // 4, c % 4
    q = load(c)
    cx = combine([0.5 * v for v in D4[xi]], [load(j * 4 + zi) for j in range(4)])
    px = cx + 3.0 * (q - low(zi)) if xi == 0 else cx
    mx = cx + 3.0 * (high(zi) - q) if xi == 3 else cx
    cy = lt[32:33] * q
    for n, s in enumerate(SHIFTS):
        r = pltpu.roll(q, (-16 * s) % 128, 1)
        cy = cy + lt[26 + n:27 + n] * r
        if s == -1:
            py = lt[33:34] * (q - r)
        if s == 1:
            my = lt[34:35] * (r - q)
    cz = combine([0.5 * v for v in D4[zi]], [load(xi * 4 + j) for j in range(4)])
    pz = cz + 3.0 * (q - z_before(load(xi * 4 + 3), lt)) if zi == 0 else cz
    mz = cz + 3.0 * (z_after(load(xi * 4), lt) - q) if zi == 3 else cz
    return [px, mx, cy + py, cy + my, pz, mz]


CENTRAL = [[0.0 if i == j else 0.5 * D4[i][j] for j in range(4)] for i in range(4)]


def moment_kernel(idx, up, down, moma, mix, lt, vec, tabd, tabs, pay, delta, inflow,
                  yz, mom, full, stack):
    right = lax.broadcasted_iota(jnp.int32, (16, 128), 1) >= 64

    def unpack(n, _):
        at = pl.ds(pl.multiple_of(n * 16, 16), 16)
        u, d = up[at], down[at]
        zi, y = n // 8, n % 8
        delta[zi, y] = vec[0, 9:10] * jnp.where(right, u, d)
        inflow[zi, y] = vec[0, 9:10] * pltpu.roll(jnp.where(right, d, u), 64, 1)
        return 0
    lax.fori_loop(0, 32, unpack, 0, unroll=8)
    layer_yz(delta, yz, vec)
    inflow[...] = inflow[...] + yz[...]
    md = project(delta[...].reshape(512, 128), tabd[0])
    ms = project(inflow[...].reshape(512, 128), tabs[0])
    for zi in range(4):
        at = slice(128 * zi, 128 * zi + 128)
        t, u, v = md[at, 0:128].T, md[at, 128:144].T, ms[at].T
        for xi in range(4):
            c = xi * 4 + zi
            q = moma[c, 0:32] + t[32 * xi:32 * xi + 32]
            once = moma[c, 40:48]
            if xi == 0:
                q, once = q + v[0:32], once + u[0:8]
            if xi == 3:
                q, once = q + v[32:64], once + u[8:16]
            mom[c, 0:32] = q
            mom[c, 32:40] = moma[c, 32:40]
            mom[c, 40:48] = once

    def load0(c):
        return mom[c, 32:40]

    for c in range(16):
        six = one_sided(load0, lambda zi: up[512 + 8 * zi:520 + 8 * zi],
                        lambda zi: down[512 + 8 * zi:520 + 8 * zi], c, lt)
        at = slice(128 * c, 128 * c + 128)
        stack[0:16, at] = mom[c, 32:48]
        for n in range(6):
            stack[16 + 8 * n:24 + 8 * n, at] = six[n]
    add = exact_dot(mix[...], stack[...])
    for c in range(16):
        at = slice(128 * c, 128 * c + 128)
        full[c, 0:32] = mom[c, 0:32] + add[0:32, at]
        full[c, 32:40] = add[32:40, at]
    for c in range(16):
        xi, zi = c // 4, c % 4
        r = combine(CENTRAL[xi], [full[j * 4 + zi, 8:16] for j in range(4)])
        r = r + central_y(full[c, 16:24], lt)
        r = r + combine(CENTRAL[zi], [full[xi * 4 + j, 24:32] for j in range(4)])
        if zi == 0:
            r = r - 1.5 * z_before(full[xi * 4 + 3, 24:32], lt)
        if zi == 3:
            r = r + 1.5 * z_after(full[xi * 4, 24:32], lt)
        q = 32 * zi + 5 * xi
        pay[q:q + 5] = -r[0:5]
        pay[128 + 5 * c:133 + 5 * c] = full[c, 0:5]
        pay[208 + 5 * c:213 + 5 * c] = mom[c, 32:37]
        pay[288 + 5 * c:293 + 5 * c] = full[c, 32:37]
    for zi in range(4):
        pay[32 * zi + 20:32 * zi + 25] = full[zi, 8:13]
        pay[32 * zi + 25:32 * zi + 30] = full[12 + zi, 8:13]
        pay[32 * zi + 30:32 * zi + 32] = jnp.zeros((2, 128), jnp.float32)
        pay[368 + 5 * zi:373 + 5 * zi] = up[512 + 8 * zi:517 + 8 * zi]
        pay[388 + 5 * zi:393 + 5 * zi] = down[512 + 8 * zi:517 + 8 * zi]


def residual_kernel(idx, got, force, out):
    at = pl.ds(pl.multiple_of(32 * idx[0], 32), 32)
    t = got[0, at] + got[1, at] + got[2, at] + got[3, at]
    v = t[0:20] + force[idx[0]]
    for n in range(8):
        out[n, 0:20] = v
        out[n, 20:30] = t[20:30]


def feq_kernel(idx, got, twice, delta, inflow, lt, vec, final, h2, low, s0, lo, hi, stack):
    def total(a, n):
        return got[0, a:a + n] + got[1, a:a + n] + got[2, a:a + n] + got[3, a:a + n]

    s0[...] = jnp.zeros_like(s0)
    lo[...] = jnp.zeros_like(lo)
    hi[...] = jnp.zeros_like(hi)
    for c in range(16):
        s0[c, 0:5] = total(208 + 5 * c, 5)
    for zi in range(4):
        lo[zi, 0:5] = total(368 + 5 * zi, 5)
        hi[zi, 0:5] = total(388 + 5 * zi, 5)
    low[...] = total(128, 80)
    pad = jnp.zeros((3, 128), jnp.float32)
    for c in range(16):
        z = jnp.concatenate([0.2 * total(288 + 5 * c, 5), pad], axis=0) + 0.16 * s0[c]
        six = one_sided(lambda k: s0[k], lambda zi: lo[zi], lambda zi: hi[zi], c, lt)
        for n, v in enumerate([z] + six):
            stack[8 * n:8 * n + 8, 128 * c:128 * c + 128] = v
    add = lax.dot_general(stack[...], final[0], (((0,), (0,)), ((), ())), precision=HI,
                          preferred_element_type=jnp.float32)
    add = add.reshape(16, 8, 16, 128)
    pos = vec[0, 14:15]
    for c in range(16):
        xi, zi = c // 4, c % 4
        v = twice[c] + add[c] + vec[0, 10 + xi:11 + xi] * delta[zi]
        if xi in (0, 3):
            v = v + (pos if xi == 0 else 1.0 - pos) * inflow[zi]
        h2[c] = v


def apply_k(src, dst, lt, own=False, four=False):
    rows = slice(8, 16) if own else slice(0, 24)

    def pressure(k, at):
        return 2.0 * src[k, at] if four else src[k, at] + src[64 + k, at]

    def before(load):
        return load(slice(7, 15)) if own else pltpu.roll(load(rows), 1, 0)

    def after(load):
        return load(slice(9, 17)) if own else pltpu.roll(load(rows), 23, 0)

    for zi in range(4):
        u = [src[16 + j * 4 + zi, rows] for j in range(4)]
        p = [pressure(j * 4 + zi, rows) for j in range(4)]
        for xi in range(4):
            du = combine(CENTRAL[xi], u)
            dp = combine(CENTRAL[xi], p)
            if xi == 0:
                du = du - 1.5 * before(lambda at: src[28 + zi, at])
                dp = dp - 1.5 * before(lambda at: pressure(12 + zi, at))
            if xi == 3:
                du = du + 1.5 * after(lambda at: src[16 + zi, at])
                dp = dp + 1.5 * after(lambda at: pressure(zi, at))
            dst[xi * 4 + zi] = du
            dst[16 + xi * 4 + zi] = dp
    for xi in range(4):
        u = [src[48 + xi * 4 + j, rows] for j in range(4)]
        p = [pressure(xi * 4 + j, rows) for j in range(4)]
        for zi in range(4):
            du = combine(CENTRAL[zi], u)
            dp = combine(CENTRAL[zi], p)
            if zi == 0:
                du = du - 1.5 * z_before(u[3], lt)
                dp = dp - 1.5 * z_before(p[3], lt)
            if zi == 3:
                du = du + 1.5 * z_after(u[0], lt)
                dp = dp + 1.5 * z_after(p[0], lt)
            dst[xi * 4 + zi] = dst[xi * 4 + zi] + du
            dst[48 + xi * 4 + zi] = dp

    def along_y(c, _):
        dst[c] = dst[c] + central_y(src[32 + c, rows], lt)
        dst[32 + c] = central_y(pressure(c, rows), lt)
        return 0
    lax.fori_loop(0, 16, along_y, 0, unroll=8)


def two_level(r, pe, co, lt):
    def over_f(f, _):
        tz = [[None, None] for _ in range(4)]
        for xi in range(4):
            q = [r[f * 16 + xi * 4 + zi] for zi in range(4)]
            for za in range(2):
                tz[xi][za] = combine(RT[za], q)
        for za in range(2):
            py = []
            for xa in range(2):
                t = combine(RT[xa], [tz[xi][za] for xi in range(4)])
                e0, e1 = lt[9:10] * t, lt[16:17] * t
                for s in SHIFTS:
                    rolled = pltpu.roll(t, (-16 * s) % 128, 1)
                    e0 = e0 + lt[9 + s:10 + s] * rolled
                    e1 = e1 + lt[16 + s:17 + s] * rolled
                co[f * 8 + xa * 4 + za * 2] = e0
                co[f * 8 + xa * 4 + za * 2 + 1] = e1
                py.append(lt[20:21] * e0 + lt[21:22] * e1)
            for xi in range(4):
                v = combine(PR[xi], py)
                for zi in range(4):
                    if PR[zi][za] == 0.0:
                        continue
                    at = f * 16 + xi * 4 + zi
                    if za == 0 or PR[zi][0] == 0.0:
                        pe[at] = PR[zi][za] * v
                    else:
                        pe[at] = pe[at] + PR[zi][za] * v
        return 0
    lax.fori_loop(0, 5, over_f, 0)


def coarse_products(co, lt):
    def at(f, xa, za, ya):
        return co[f * 8 + xa * 4 + za * 2 + ya]

    def own(q):
        return q[8:16]

    def dx(q, xa, za, ya):
        if xa == 0:
            v = q(1, za, ya)
            return 0.25 * (own(v) - own(pltpu.roll(v, 1, 0)))
        v = q(0, za, ya)
        return 0.25 * (own(pltpu.roll(v, 23, 0)) - own(v))

    def dz(q, xa, za, ya):
        v = own(q(xa, 1 - za, ya))
        if za == 0:
            return 0.25 * (v - z_before(v, lt))
        return 0.25 * (z_after(v, lt) - v)

    def dy(q, xa, za, ya):
        v = own(q(xa, za, 1 - ya))
        w = pltpu.roll(v, 64, 1)
        return 0.25 * (v - w) if ya == 0 else 0.25 * (w - v)

    total = [jnp.zeros((8, 128), jnp.float32)] * 3
    for xa in range(2):
        for za in range(2):
            for ya in range(2):
                def field(f):
                    return lambda a, b, c: at(f, a, b, c)

                def pressure(a, b, c):
                    return at(0, a, b, c) + at(4, a, b, c)
                e = [own(at(f, xa, za, ya)) for f in range(5)]
                div = (dx(field(1), xa, za, ya) + dy(field(2), xa, za, ya)
                       + dz(field(3), xa, za, ya))
                v = [div, dx(pressure, xa, za, ya), dy(pressure, xa, za, ya),
                     dz(pressure, xa, za, ya), div]
                for f in range(5):
                    total = [total[0] + e[f] * e[f], total[1] + e[f] * v[f], total[2] + v[f] * v[f]]
    return [t * lt[23:24] for t in total]


PAIRS = [(i, j) for i in range(3) for j in range(i, 3)]


def fine_products(e, s, t, ke, kt, lt, own):
    rows = slice(0, 8) if own else slice(8, 16)
    zero = jnp.zeros((8, 128), jnp.float32)
    total = [zero] * 18
    for xi in range(4):
        for zi in range(4):
            acc = [zero] * 18
            c = xi * 4 + zi
            for f in range(4):
                k = f * 16 + c
                x = [e[k, 8:16], s[k, 8:16], t[k, 8:16]]
                y = [ke[k, rows], x[2], kt[k, rows]]
                z = x
                if f == 0:
                    last = [e[64 + c, 8:16], s[64 + c, 8:16], x[2]]
                    z = [x[0] + last[0], x[1] + last[1], x[2] + x[2]]
                for n, (i, j) in enumerate(PAIRS):
                    v = x[i] * x[j]
                    if f == 0:
                        v = v + last[i] * last[j]
                    acc[n] = acc[n] + v
                    acc[6 + n] = acc[6 + n] + (z[i] * y[j] if i == j else z[i] * y[j] + z[j] * y[i])
                    v = y[i] * y[j]
                    acc[12 + n] = acc[12 + n] + (2.0 * v if f == 0 else v)
            w = WEIGHTS[xi] * WEIGHTS[zi]
            total = [a + w * b for a, b in zip(total, acc)]
    return [a * lt[22:23] for a in total]


def diagonal():
    return (lax.broadcasted_iota(jnp.int32, (24, 128), 0)
            == lax.broadcasted_iota(jnp.int32, (24, 128), 1))


def pass_words(e, s, t, ke, kt, co, gram, lt, own=False):
    two_level(e, s, co, lt)
    apply_k(s, t, lt)

    def over_k(k, _):
        e[k] = e[k] - s[k]
        return 0
    lax.fori_loop(0, 80, over_k, 0, unroll=8)
    apply_k(e, ke, lt, own)
    apply_k(t, kt, lt, own, four=True)
    products = coarse_products(co, lt) + fine_products(e, s, t, ke, kt, lt, own)
    rows = [jnp.sum(p, axis=0, keepdims=True) for p in products] + [jnp.zeros((3, 128), jnp.float32)]
    total = jnp.sum(jnp.concatenate(rows, axis=0), axis=1, keepdims=True)
    line = jnp.sum(jnp.where(diagonal(), total, 0.0), axis=0, keepdims=True)
    for n in range(gram.shape[0]):
        gram[n] = jnp.broadcast_to(line, (8, 128))


def pack_kernel(idx, mine, own, to_upper, to_lower):
    first = lax.broadcasted_iota(jnp.int32, (8, 128), 0) == 0
    last = lax.broadcasted_iota(jnp.int32, (8, 128), 0) == 7
    for f in range(5):
        low = mine[pl.ds(20 + f, 8, stride=30), :]
        high = mine[pl.ds(25 + f, 8, stride=30), :]
        for xi in range(4):
            k = f * 4 + xi
            v = mine[pl.ds(5 * xi + f, 8, stride=30), :]
            if xi == 0:
                v = v + 1.5 * jnp.where(first, 0.0, pltpu.roll(high, 1, 0))
            if xi == 3:
                v = v - 1.5 * jnp.where(last, 0.0, pltpu.roll(low, 7, 0))
            own[k] = v
            to_upper[pl.ds(k, 6, stride=20), :] = v[2:8]
            to_lower[pl.ds(k, 6, stride=20), :] = v[0:6]
        to_upper[120 + f:121 + f] = high[7:8]
        to_lower[120 + f:121 + f] = low[0:1]


def window_kernel(idx, lower, own, upper, edge_low, edge_high, after, win):
    for f in range(5):
        e = 120 + f
        for xi in range(4):
            k = f * 4 + xi
            at = 20 * k
            low, mid, high = lower[pl.ds(k, 6, stride=20), :], own[k], upper[pl.ds(k, 6, stride=20), :]
            win[at:at + 6] = low
            win[at + 6:at + 14] = mid
            win[at + 14:at + 20] = high
            if xi == 0:
                win[at + 6:at + 7] = mid[0:1] + 1.5 * lower[e:e + 1]
                win[at + 14:at + 15] = high[0:1] + 1.5 * edge_high[e:e + 1]
            if xi == 3:
                win[at + 13:at + 14] = mid[7:8] - 1.5 * upper[e:e + 1]
                win[at + 5:at + 6] = low[5:6] - 1.5 * edge_low[e:e + 1]


def first_pass_kernel(idx, quarters, lt, r, s, t, ke, kt, gram, co):
    zero = jnp.zeros((2, 128), jnp.float32)
    for f in range(5):
        for xi in range(4):
            for zi in range(4):
                k = f * 16 + xi * 4 + zi
                at = 20 * (f * 4 + xi)
                r[k, 0:2] = zero
                r[k, 2:22] = quarters[zi, at:at + 20]
                r[k, 22:24] = zero
    pass_words(r, s, t, ke, kt, co, gram, lt)


def step_sizes(sums):
    line = sums[0, 0:1]
    for n in range(1, sums.shape[0]):
        line = line + sums[n, 0:1]
    v = jnp.sum(jnp.where(diagonal(), line, 0.0), axis=1, keepdims=True)
    v = jnp.broadcast_to(v, (24, 128))
    c0, c1, c2 = v[0:1], v[1:2], v[2:3]
    den = 4.0 * c0 + 4.0 * c1 + c2 + EPS
    a1, b1 = (2.0 * c0 + c1) / den, (2.0 * c1 + c2 + EPS) / den
    d = [jnp.ones_like(a1), b1, -a1]

    def form(base, twice):
        total = None
        for n, (i, j) in enumerate(PAIRS):
            term = d[i] * d[j] * v[base + n:base + n + 1]
            if twice and i != j:
                term = 2.0 * term
            total = term if total is None else total + term
        return total
    rr, kk = jnp.maximum(form(3, True), 0.0), jnp.maximum(form(15, True), 0.0)
    bound = jnp.sqrt(rr) * jnp.sqrt(kk)
    rk = jnp.clip(form(9, False), -bound, bound)
    den = 4.0 * rr + 4.0 * rk + kk + EPS
    return a1, b1, (2.0 * rr + rk) / den, (2.0 * rk + kk + EPS) / den


def next_pass_kernel(first, idx, sums, e, s, t, ke, kt, *rest):
    if first:
        lt, r2, s2, t2, ke2, kt2, acc2, gram, co = rest
    else:
        acc, lt, r2, s2, t2, ke2, kt2, acc2, gram, co = rest
    a1, b1, a2, b2 = step_sizes(sums)

    def put(k, tk, kr):
        sk = s[k]
        r1 = e[k] + b1 * sk - a1 * tk
        v = a1 * sk[8:16] + a2 * r1[8:16]
        acc2[k] = v if first else acc[k] + v
        r2[k] = b2 * r1 - a2 * kr

    def over_k(k, _):
        tk = t[k]
        kr = ke[k] + b1 * tk - a1 * kt[k]
        put(k, tk, kr)
        put(64 + k, tk, kr)
        return 0
    lax.fori_loop(0, 16, over_k, 0, unroll=4)

    def rest_k(k, _):
        tk = t[k]
        put(k, tk, ke[k] + b1 * tk - a1 * kt[k])
        return 0
    lax.fori_loop(16, 64, rest_k, 0, unroll=4)
    pass_words(r2, s2, t2, ke2, kt2, co, gram, lt, own=not first)


def third_pass_kernel(idx, sums, e, s, t, ke, kt, acc, lt, eo, so, to, acc2, gram,
                      r2, s2, t2, ke2, kt2, co):
    next_pass_kernel(False, idx, sums, e, s, t, ke, kt, acc, lt, r2, s2, t2, ke2, kt2, acc2, gram, co)
    eo[...] = r2[:, 8:16]
    so[...] = s2[:, 8:16]
    to[...] = t2[:, 8:16]


def last_kernel(idx, sums, e, s, t, acc, low, h2, select, split, out, fields, change, stack, rows):
    a1, b1, a2, _ = step_sizes(sums)

    def over_k(k, _):
        r1 = e[k] + b1 * s[k] - a1 * t[k % 64]
        change[pl.ds(pl.multiple_of(k * 8, 8), 8)] = acc[k] + a1 * s[k] + a2 * r1
        return 0
    lax.fori_loop(0, 80, over_k, 0, unroll=4)
    z = idx[1]
    stack[...] = jnp.zeros_like(stack)
    here = row_of_y()
    for c in range(16):
        for f in range(5):
            k = f * 16 + c
            d = change[pl.ds(k * 8 + z, 1)]
            stack[f:f + 1, 128 * c:128 * c + 128] = d
            n = 8 * (k // 4)
            rows[n:n + 8, 128 * (c % 4):128 * (c % 4) + 128] = (low[5 * c + f:5 * c + f + 1] + d) * here
    fields[...] = project(rows[...], select[...]).reshape(5, 4, 8, 64)
    whole = stack[...]
    d1 = whole.astype(jnp.bfloat16).astype(jnp.float32)
    d2 = (whole - d1).astype(jnp.bfloat16).astype(jnp.float32)
    d3 = whole - d1 - d2
    parts = jnp.concatenate([d1, d1, d2, d1, d2, d3], axis=0).astype(jnp.bfloat16)
    add = lax.dot_general(parts, split[0].astype(jnp.bfloat16), (((0,), (0,)), ((), ())),
                          preferred_element_type=jnp.float32).reshape(16, 8, 16, 128)
    for c in range(16):
        xi, zi = c // 4, c % 4
        v = h2[c] + add[c]
        for y in range(8):
            out[xi, y, pl.ds(zi, 16, stride=4), :] = v[y]


def on_device(distribution, forcing):
    import functools
    tables = {k: jnp.asarray(v) for k, v in constant_tables().items()}
    spaces = lax.axis_size("space")
    blocks = spaces // 8
    idx = jnp.stack([lax.axis_index("vel"), lax.axis_index("space") % 8]).astype(jnp.int32)
    vec, lt = tables["vec"], tables["lanes"]
    wide = (16, 8, 16, 128)
    layer = (4, 8, 16, 128)

    def shifted(x, by):
        return lax.ppermute(x, "space", [(i, (i + by) % spaces) for i in range(spaces)])

    up, down = call(rim_kernel, "rims", idx, [distribution], [],
                    [(544, 128)] * 2, [layer, layer, (8, 8, 16, 128), (1024, 8), (1, 32, 128)])
    up, down = shifted(up, 1), shifted(down, -1)
    twice, moma, force = call(local_kernel, "local", idx, [distribution, forcing, tables["select"]],
                              [vec, tables["tab0"], tables["tab1"], tables["tab2"]],
                              [wide, (16, 48, 128), (4, 20, 128)], [wide, wide, (2048, 48)])
    pay, delta, inflow = call(moment_kernel, "moments", idx, [up, down, moma, tables["mix"], lt],
                              [vec, tables["tabd"], tables["tabs"]], [(408, 128), layer, layer],
                              [layer, (16, 48, 128), (16, 40, 128), (64, 2048)])
    got = lax.all_gather(pay, "vel")
    (res,) = call(residual_kernel, "residual", idx, [got, force], [], [(8, 30, 128)])
    near = [[a * 8 + b for b in range(8)] for a in range(blocks)]
    far = [[a * 8 + b for a in range(blocks)] for b in range(8)]
    mine = lax.all_to_all(res, "space", 0, 0, axis_index_groups=near, tiled=True).reshape(240, 128)
    own_r, to_upper, to_lower = call(pack_kernel, "pack", idx, [mine], [],
                                     [(20, 8, 128), (125, 128), (125, 128)])
    lower, upper = shifted(to_upper, 8), shifted(to_lower, -8)
    h2, low = call(feq_kernel, "feq", idx, [got, twice, delta, inflow, lt],
                   [vec, tables["final"]],
                   [wide, (80, 128)], [(16, 8, 128), (4, 8, 128), (4, 8, 128), (56, 2048)])
    (quarter,) = call(window_kernel, "window", idx, [lower, own_r, upper, to_lower, to_upper, low], [],
                      [(400, 128)])
    quarters = lax.all_gather(quarter, "vel")

    def summed(gram):
        return lax.all_to_all(gram, "space", 0, 0, axis_index_groups=far, tiled=True)

    win, own, part = (80, 24, 128), (80, 8, 128), (blocks, 8, 128)
    four, own4 = (64, 24, 128), (64, 8, 128)
    co = (40, 24, 128)
    e, s, t, ke, kt, gram = call(first_pass_kernel, "pass1", idx, [quarters, lt], [],
                                  [win, win, four, four, four, part], [co])
    e, s, t, ke, kt, acc, gram = call(functools.partial(next_pass_kernel, True), "pass2", idx,
                                       [summed(gram), e, s, t, ke, kt, lt], [],
                                       [win, win, four, four, four, own, part], [co])
    e, s, t, acc, gram = call(third_pass_kernel, "pass3", idx,
                               [summed(gram), e, s, t, ke, kt, acc, lt], [],
                               [own, own, own4, own, part], [win, win, four, own4, own4, co])
    out, fields = call(last_kernel, "last", idx,
                       [summed(gram), e, s, t, acc, low, h2, tables["select"]], [tables["split"]],
                       [(4, 8, 64, 128), (5, 4, 8, 64)], [(640, 128), (8, 2048), (160, 512)])
    return out, fields


def solution(mesh):
    return jax.shard_map(
        on_device,
        mesh=mesh,
        in_specs=(P("space", None, None, "vel"), P(None, "space", None, None)),
        out_specs=(P("space", None, None, "vel"), P(None, "space", None, None)),
        check_vma=False,
    )
```

```python
import math

import jax
import jax.numpy as jnp
import numpy as np
from jax import lax
from jax.experimental import pallas as pl
from jax.experimental.pallas import tpu as pltpu
from jax.sharding import PartitionSpec as P

INTERPRET = False
DT = 0.02
RF = 0.4472135954999579
POINTS = [-1.0, -RF, RF, 1.0]
WEIGHTS = [1.0 / 6.0, 5.0 / 6.0, 5.0 / 6.0, 1.0 / 6.0]
EPS = 1e-6
HI = lax.Precision.HIGHEST


def lagrange_table(points):
    n = len(points)
    bary = []
    for i in range(n):
        product = 1.0
        for j in range(n):
            if j != i:
                product *= points[i] - points[j]
        bary.append(1.0 / product)
    rows = [[0.0] * n for _ in range(n)]
    for i in range(n):
        for j in range(n):
            if j != i:
                rows[i][j] = bary[j] / bary[i] / (points[i] - points[j])
        rows[i][i] = -sum(rows[i])
    return rows


D4 = lagrange_table(POINTS)
for _i in (1, 2):
    D4[_i][_i] = 0.0
PR = [[(1.0 - x) / 2.0, (1.0 + x) / 2.0] for x in POINTS]
RT = [[WEIGHTS[i] * PR[i][a] for i in range(4)] for a in range(2)]


def constant_tables():
    k = np.arange(512)
    b, j = k // 128, k % 128
    s = j // 64
    m = ((b * 64 + j % 64) * 5179 + 7) % 16384
    xi = np.stack([16 * s + m // 1024, (m // 32) % 32, m % 32]).astype(np.float64)
    xi = -4.0 + 0.25 * (xi + 0.5)
    sq = (xi * xi).sum(0)
    e = math.pi ** (-1.5) * np.exp(-sq)
    x, y, z = xi
    phi = np.stack(
        [np.ones(512), x, y, z, 2 * sq / 3 - 1, 2 * (x * x - sq / 3), 2 * (y * y - sq / 3),
         2 * x * y, 2 * x * z, 2 * y * z, x * (sq - 2.5), y * (sq - 2.5), z * (sq - 2.5)]
    )
    p = phi[0] + phi[4]
    zero = np.zeros(512)

    def eight(rows):
        return np.stack(list(rows) + [zero] * (8 - len(rows)))

    low = eight(phi[:5])
    along_x = eight([phi[1], p + phi[5], phi[7], phi[8], phi[1] + phi[10]])
    along_y = eight([phi[2], phi[7], p + phi[6], phi[9], phi[2] + phi[11]])
    along_z = eight([phi[3], phi[8], phi[9], p - phi[5] - phi[6], phi[3] + phi[12]])
    rows32 = np.concatenate([low, along_x, along_y, along_z])
    ec = eight([e, 2 * x * e, 2 * y * e, 2 * z * e, e * (sq - 1.5)])
    pos, neg = np.maximum(xi, 0.0), np.minimum(xi, 0.0)

    def per_rank(rows):
        return np.stack([rows[:, r * 128:(r + 1) * 128] for r in range(4)]).astype(np.float32)

    ispos = (x > 0).astype(np.float64)
    ax = np.abs(x)
    d4 = np.array(D4)
    vec = [-DT * 0.5 * x, -DT * 0.5 * y, -DT * 0.5 * z,
           -3 * DT * pos[1], -3 * DT * neg[1], -3 * DT * pos[2], -3 * DT * neg[2],
           -3 * DT * pos[0], 3 * DT * neg[0], 3 * DT * ax]
    for i in range(4):
        kap = -DT * 0.5 * x * np.where(ispos > 0, d4[i][0], d4[i][3])
        if i == 0:
            kap = kap + ispos * (0.8 - 3 * DT * ax)
        if i == 3:
            kap = kap + (1 - ispos) * (0.8 - 3 * DT * ax)
        vec.append(kap)
    kappa = vec[10:14]
    vec.append(ispos)
    for jj in range(4):
        vec.append(-DT * 0.5 * x * np.where(ispos > 0, d4[3][jj], d4[0][jj]))
    while len(vec) < 24:
        vec.append(zero)
    vec = per_rank(np.concatenate([np.stack(vec), low]))

    def moment_rows(start, rows, height):
        out = np.zeros((height, 512))
        out[start:start + len(rows)] = rows
        return per_rank(out)

    tab2 = moment_rows(0, rows32, 48)
    tab1 = moment_rows(40, low, 48)
    tab0 = moment_rows(32, low, 48)
    tabd = per_rank(np.concatenate([v * rows32 for v in kappa] + [ispos * low, (1 - ispos) * low]))
    tabs = per_rank(np.concatenate([ispos * rows32, (1 - ispos) * rows32]))
    select = np.zeros((64, 512))
    for n in range(4):
        for la in range(128):
            select[4 * (la % 16) + n, 128 * n + la] = 1.0
    import ml_dtypes
    pieces, left = [], per_rank(ec)
    for _ in range(3):
        pieces.append(left.astype(ml_dtypes.bfloat16))
        left = left - pieces[-1].astype(np.float32)
    split = np.concatenate([pieces[n].astype(np.float32) for n in (0, 1, 0, 2, 1, 0)], axis=1)
    g = rows32 @ ec.T
    g5 = g[:8]
    mix = np.zeros((40, 64))
    mix[:32, 0:8] = 0.16 * g + 0.04 * g @ g5
    mix[:32, 8:16] = 0.2 * g
    mix[32:, 0:8] = 0.2 * g5
    mix[32:, 8:16] = np.eye(8)
    final = [ec]
    for d in range(3):
        for i, part in enumerate((pos[d], neg[d])):
            c0 = 16 + 16 * d + 8 * i
            mix[:32, c0:c0 + 8] = -0.2 * DT * (rows32 * part) @ ec.T
            final.append(-0.2 * DT * ec * part)
    final = per_rank(np.concatenate(final))
    lane = np.arange(128)
    yi, ze = (lane // 16) % 4, lane % 16
    rows = []
    shifts = (-3, -2, -1, 1, 2, 3)

    def entry(table, sft):
        return np.array([table(i, i + sft) if 0 <= i + sft < 4 else 0.0 for i in yi])

    for sft in shifts:
        c = entry(lambda i, q: 0.5 * D4[i][q], sft)
        if sft == -1:
            c = c - 1.5 * (yi == 0)
        if sft == 1:
            c = c + 1.5 * (yi == 3)
        rows.append(c)
    for a in range(2):
        for sft in range(-3, 4):
            rows.append(entry(lambda i, q: RT[a][q], sft))
    rows += [np.array([PR[i][0] for i in yi]), np.array([PR[i][1] for i in yi])]
    rows += [np.array([WEIGHTS[i] for i in yi]), (yi == 0) * 1.0, (ze == 0) * 1.0, (ze == 15) * 1.0]
    for sft in shifts:
        rows.append(entry(lambda i, q: 0.5 * D4[i][q], sft))
    rows += [entry(lambda i, q: 0.5 * D4[i][q], 0), 3.0 * (yi == 0), 3.0 * (yi == 3)]
    while len(rows) < 40:
        rows.append(np.zeros(128))
    mats = np.zeros((3, 128, 128))
    for n, sft in enumerate(shifts):
        mats[0, (lane + 16 * sft) % 128, lane] += rows[n]
    for a in range(2):
        for sft in range(-3, 4):
            mats[1 + a, (lane + 16 * sft) % 128, lane] += rows[6 + 7 * a + sft + 3]
    lanes = np.concatenate([np.stack(rows), mats.reshape(384, 128)]).astype(np.float32)
    return dict(vec=vec, tab2=tab2, tab1=tab1, tab0=tab0, mix=mix.astype(np.float32),
                final=final, lanes=lanes, split=split, tabd=tabd, tabs=tabs, select=select.astype(np.float32))


def call(kernel, name, idx, full, ranked, outs, scratch=(), limit=24):
    n = len(full)

    def body(idx, *refs):
        rank = [r.at[pl.ds(idx[0], 1)] for r in refs[n:n + len(ranked)]]
        kernel(idx, *refs[:n], *rank, *refs[n + len(ranked):])

    vmem = pl.BlockSpec(memory_space=pltpu.VMEM)
    return pl.pallas_call(
        body,
        name=name,
        out_shape=[jax.ShapeDtypeStruct(s, jnp.float32) for s in outs],
        in_specs=[pl.BlockSpec(memory_space=pltpu.SMEM)] + [vmem] * (n + len(ranked)),
        out_specs=[vmem] * len(outs),
        scratch_shapes=[pltpu.VMEM(s, jnp.float32) for s in scratch],
        compiler_params=pltpu.CompilerParams(vmem_limit_bytes=limit << 20),
        interpret=INTERPRET,
    )(idx, *full, *ranked)


def exact_dot(a, b):
    return jnp.dot(a, b, precision=HI, preferred_element_type=jnp.float32)


def project(x, rows):
    return lax.dot_general(x, rows, (((1,), (1,)), ((), ())), precision=HI,
                           preferred_element_type=jnp.float32)


def combine(row, values):
    total = None
    for c, v in zip(row, values):
        if c != 0.0:
            total = c * v if total is None else total + c * v
    return total


def layer_yz(src, dst, vec):
    def over_y(y, _):
        q = [src[zi, y] for zi in range(4)]
        for zi in range(4):
            v = vec[0, 2:3] * combine(D4[zi], q)
            if zi == 0:
                v = v + vec[0, 5:6] * (q[0] - pltpu.roll(q[3], 1, 0))
            if zi == 3:
                v = v + vec[0, 6:7] * (pltpu.roll(q[0], 15, 0) - q[3])
            dst[zi, y] = v
        return 0
    lax.fori_loop(0, 8, over_y, 0, unroll=True)

    def over_z(zi, _):
        q = [src[zi, y] for y in range(8)]
        for y in range(8):
            e, yi = 4 * (y // 4), y % 4
            v = vec[0, 1:2] * combine(D4[yi], q[e:e + 4])
            if yi == 0:
                v = v + vec[0, 3:4] * (q[y] - q[(y + 7) % 8])
            if yi == 3:
                v = v + vec[0, 4:5] * (q[(y + 1) % 8] - q[y])
            dst[zi, y] = dst[zi, y] + v
        return 0
    lax.fori_loop(0, 4, over_z, 0, unroll=True)


def every_fourth(h, xi, y, zi):
    if INTERPRET:
        return h[xi, y][zi::4]
    return h[xi, y, pl.ds(zi, 16, stride=4), :]


def speed_rows(idx, vec):
    j = lax.broadcasted_iota(jnp.int32, (1, 128), 1)
    m = ((idx[0] * 64 + (j & 63)) * 5179 + 7) & 16383
    s = j >> 6
    x, y, z = [-4.0 + 0.25 * (n.astype(jnp.float32) + 0.5)
               for n in (16 * s + (m >> 10), (m >> 5) & 31, m & 31)]
    pos = s > 0
    rows = {0: -DT * 0.5 * x, 1: -DT * 0.5 * y, 2: -DT * 0.5 * z,
            3: -3 * DT * jnp.maximum(y, 0.0), 4: -3 * DT * jnp.minimum(y, 0.0),
            5: -3 * DT * jnp.maximum(z, 0.0), 6: -3 * DT * jnp.minimum(z, 0.0),
            14: pos.astype(jnp.float32)}
    for n in range(4):
        rows[15 + n] = -DT * 0.5 * x * jnp.where(pos, D4[3][n], D4[0][n])
    rows[24], rows[25], rows[26], rows[27] = jnp.ones_like(x), x, y, z
    rows[28] = 2.0 * (x * x + y * y + z * z) / 3.0 - 1.0
    vec[...] = jnp.zeros_like(vec)
    for n, v in rows.items():
        vec[0, n:n + 1] = v


def rim_kernel(idx, h, up, down, q, t, ends, m, vec):
    speed_rows(idx, vec)
    transport_rims(idx, h, vec, up, down, q, t, ends, m)


def transport_rims(idx, h, vec, up, down, q, t, ends, m):
    pos = vec[0, 14:15] > 0.5
    for zi in range(4):
        def over_y(y, _):
            x = [every_fourth(h, xi, y, zi) for xi in range(4)]
            ql = jnp.where(pos, x[3], x[0])
            q[zi, y] = ql
            ends[zi, y] = x[0]
            ends[4 + zi, y] = x[3]
            v = 0.8 * ql
            for j in range(4):
                v = v + vec[0, 15 + j:16 + j] * x[j]
            up[pl.ds(pl.multiple_of((zi * 8 + y) * 16, 16), 16)] = v
            return 0
        lax.fori_loop(0, 8, over_y, 0, unroll=True)
    layer_yz(q, t, vec)
    right = lax.broadcasted_iota(jnp.int32, (16, 128), 1) >= 64

    def pack(n, _):
        zi, y = n // 8, n % 8
        at = pl.ds(pl.multiple_of(n * 16, 16), 16)
        tl = pltpu.roll(t[zi, y] + up[at], 64, 1)
        ql = q[zi, y]
        up[at] = jnp.where(right, ql, tl)
        down[at] = jnp.where(right, tl, ql)
        return 0
    lax.fori_loop(0, 32, pack, 0, unroll=8)
    m[...] = project(ends[...].reshape(1024, 128), vec[0, 24:32])
    for n in range(8):
        zi, out = n % 4, (down, up)[n // 4]
        out[512 + 8 * zi:520 + 8 * zi] = m[128 * n:128 * n + 128].T


def local_update(src, dst, vec):
    def over_y(y, _):
        q = [src[c, y] for c in range(16)]
        for xi in range(4):
            for zi in range(4):
                own = q[xi * 4 + zi]
                v = 0.8 * own + vec[0, 0:1] * combine(D4[xi], [q[j * 4 + zi] for j in range(4)])
                v = v + vec[0, 2:3] * combine(D4[zi], q[xi * 4:xi * 4 + 4])
                if zi == 0:
                    v = v + vec[0, 5:6] * (own - pltpu.roll(q[xi * 4 + 3], 1, 0))
                if zi == 3:
                    v = v + vec[0, 6:7] * (pltpu.roll(q[xi * 4], 15, 0) - own)
                if xi == 0:
                    v = v + vec[0, 7:8] * own
                if xi == 3:
                    v = v + vec[0, 8:9] * own
                dst[xi * 4 + zi, y] = v
        return 0
    lax.fori_loop(0, 8, over_y, 0, unroll=2)

    def over_c(c, _):
        q = [src[c, y] for y in range(8)]
        for y in range(8):
            e, yi = 4 * (y // 4), y % 4
            v = vec[0, 1:2] * combine(D4[yi], q[e:e + 4])
            if yi == 0:
                v = v + vec[0, 3:4] * (q[y] - q[(y + 7) % 8])
            if yi == 3:
                v = v + vec[0, 4:5] * (q[(y + 1) % 8] - q[y])
            dst[c, y] = dst[c, y] + v
        return 0
    lax.fori_loop(0, 16, over_c, 0, unroll=4)


def row_of_y():
    y = lax.broadcasted_iota(jnp.int32, (8, 128), 0)
    return (lax.broadcasted_iota(jnp.int32, (8, 128), 1) // 16 == y).astype(jnp.float32)


def local_kernel(idx, h, forcing, select, vec, tab0, tab1, tab2, twice, mom, force, first, once, m):
    spread = exact_dot(forcing[...].reshape(96, 64), select[...])
    here = row_of_y()
    force[...] = jnp.zeros_like(force)
    for f in range(3):
        for c in range(16):
            n = 8 * (f * 4 + c // 4)
            v = spread[n:n + 8, 128 * (c % 4):128 * (c % 4) + 128] * here
            at = 5 * (c // 4) + f + 1
            force[c % 4, at:at + 1] = jnp.sum(v, axis=0, keepdims=True)
    for c in range(16):
        xi, zi = c // 4, c % 4

        def over_y(y, _):
            first[c, y] = every_fourth(h, xi, y, zi)
            return 0
        lax.fori_loop(0, 8, over_y, 0, unroll=True)
    local_update(first, once, vec)
    local_update(once, twice, vec)

    m[...] = project(first[...].reshape(2048, 128), tab0[0])
    m[...] = m[...] + project(once[...].reshape(2048, 128), tab1[0])
    m[...] = m[...] + project(twice[...].reshape(2048, 128), tab2[0])
    for c in range(16):
        mom[c] = m[128 * c:128 * c + 128].T


def z_before(q, lt):
    return jnp.where(lt[24:25] > 0.5, pltpu.roll(q, 113, 1), pltpu.roll(q, 1, 1))


def z_after(q, lt):
    return jnp.where(lt[25:26] > 0.5, pltpu.roll(q, 15, 1), pltpu.roll(q, 127, 1))


SHIFTS = (-3, -2, -1, 1, 2, 3)


def central_y(q, lt):
    total = None
    for n, s in enumerate(SHIFTS):
        term = lt[n:n + 1] * pltpu.roll(q, (-16 * s) % 128, 1)
        total = term if total is None else total + term
    return total


def one_sided(load, low, high, c, lt):
    xi, zi = c // 4, c % 4
    q = load(c)
    cx = combine([0.5 * v for v in D4[xi]], [load(j * 4 + zi) for j in range(4)])
    px = cx + 3.0 * (q - low(zi)) if xi == 0 else cx
    mx = cx + 3.0 * (high(zi) - q) if xi == 3 else cx
    cy = lt[32:33] * q
    for n, s in enumerate(SHIFTS):
        r = pltpu.roll(q, (-16 * s) % 128, 1)
        cy = cy + lt[26 + n:27 + n] * r
        if s == -1:
            py = lt[33:34] * (q - r)
        if s == 1:
            my = lt[34:35] * (r - q)
    cz = combine([0.5 * v for v in D4[zi]], [load(xi * 4 + j) for j in range(4)])
    pz = cz + 3.0 * (q - z_before(load(xi * 4 + 3), lt)) if zi == 0 else cz
    mz = cz + 3.0 * (z_after(load(xi * 4), lt) - q) if zi == 3 else cz
    return [px, mx, cy + py, cy + my, pz, mz]


CENTRAL = [[0.0 if i == j else 0.5 * D4[i][j] for j in range(4)] for i in range(4)]


def moment_kernel(idx, up, down, moma, mix, lt, vec, tabd, tabs, pay, delta, inflow,
                  yz, mom, full, stack):
    right = lax.broadcasted_iota(jnp.int32, (16, 128), 1) >= 64

    def unpack(n, _):
        at = pl.ds(pl.multiple_of(n * 16, 16), 16)
        u, d = up[at], down[at]
        zi, y = n // 8, n % 8
        delta[zi, y] = vec[0, 9:10] * jnp.where(right, u, d)
        inflow[zi, y] = vec[0, 9:10] * pltpu.roll(jnp.where(right, d, u), 64, 1)
        return 0
    lax.fori_loop(0, 32, unpack, 0, unroll=8)
    layer_yz(delta, yz, vec)
    inflow[...] = inflow[...] + yz[...]
    md = project(delta[...].reshape(512, 128), tabd[0])
    ms = project(inflow[...].reshape(512, 128), tabs[0])
    for zi in range(4):
        at = slice(128 * zi, 128 * zi + 128)
        t, u, v = md[at, 0:128].T, md[at, 128:144].T, ms[at].T
        for xi in range(4):
            c = xi * 4 + zi
            q = moma[c, 0:32] + t[32 * xi:32 * xi + 32]
            once = moma[c, 40:48]
            if xi == 0:
                q, once = q + v[0:32], once + u[0:8]
            if xi == 3:
                q, once = q + v[32:64], once + u[8:16]
            mom[c, 0:32] = q
            mom[c, 32:40] = moma[c, 32:40]
            mom[c, 40:48] = once

    def load0(c):
        return mom[c, 32:40]

    for c in range(16):
        six = one_sided(load0, lambda zi: up[512 + 8 * zi:520 + 8 * zi],
                        lambda zi: down[512 + 8 * zi:520 + 8 * zi], c, lt)
        at = slice(128 * c, 128 * c + 128)
        stack[0:16, at] = mom[c, 32:48]
        for n in range(6):
            stack[16 + 8 * n:24 + 8 * n, at] = six[n]
    add = exact_dot(mix[...], stack[...])
    for c in range(16):
        at = slice(128 * c, 128 * c + 128)
        full[c, 0:32] = mom[c, 0:32] + add[0:32, at]
        full[c, 32:40] = add[32:40, at]
    for c in range(16):
        xi, zi = c // 4, c % 4
        r = combine(CENTRAL[xi], [full[j * 4 + zi, 8:16] for j in range(4)])
        r = r + central_y(full[c, 16:24], lt)
        r = r + combine(CENTRAL[zi], [full[xi * 4 + j, 24:32] for j in range(4)])
        if zi == 0:
            r = r - 1.5 * z_before(full[xi * 4 + 3, 24:32], lt)
        if zi == 3:
            r = r + 1.5 * z_after(full[xi * 4, 24:32], lt)
        q = 32 * zi + 5 * xi
        pay[q:q + 5] = -r[0:5]
        pay[128 + 5 * c:133 + 5 * c] = full[c, 0:5]
        pay[208 + 5 * c:213 + 5 * c] = mom[c, 32:37]
        pay[288 + 5 * c:293 + 5 * c] = full[c, 32:37]
    for zi in range(4):
        pay[32 * zi + 20:32 * zi + 25] = full[zi, 8:13]
        pay[32 * zi + 25:32 * zi + 30] = full[12 + zi, 8:13]
        pay[32 * zi + 30:32 * zi + 32] = jnp.zeros((2, 128), jnp.float32)
        pay[368 + 5 * zi:373 + 5 * zi] = up[512 + 8 * zi:517 + 8 * zi]
        pay[388 + 5 * zi:393 + 5 * zi] = down[512 + 8 * zi:517 + 8 * zi]


def residual_kernel(idx, got, force, out):
    at = pl.ds(pl.multiple_of(32 * idx[0], 32), 32)
    t = got[0, at] + got[1, at] + got[2, at] + got[3, at]
    v = t[0:20] + force[idx[0]]
    for n in range(8):
        out[n, 0:20] = v
        out[n, 20:30] = t[20:30]


def feq_kernel(idx, got, twice, delta, inflow, lt, vec, final, h2, low, s0, lo, hi, stack):
    def total(a, n):
        return got[0, a:a + n] + got[1, a:a + n] + got[2, a:a + n] + got[3, a:a + n]

    s0[...] = jnp.zeros_like(s0)
    lo[...] = jnp.zeros_like(lo)
    hi[...] = jnp.zeros_like(hi)
    for c in range(16):
        s0[c, 0:5] = total(208 + 5 * c, 5)
    for zi in range(4):
        lo[zi, 0:5] = total(368 + 5 * zi, 5)
        hi[zi, 0:5] = total(388 + 5 * zi, 5)
    low[...] = total(128, 80)
    pad = jnp.zeros((3, 128), jnp.float32)
    for c in range(16):
        z = jnp.concatenate([0.2 * total(288 + 5 * c, 5), pad], axis=0) + 0.16 * s0[c]
        six = one_sided(lambda k: s0[k], lambda zi: lo[zi], lambda zi: hi[zi], c, lt)
        for n, v in enumerate([z] + six):
            stack[8 * n:8 * n + 8, 128 * c:128 * c + 128] = v
    add = lax.dot_general(stack[...], final[0], (((0,), (0,)), ((), ())), precision=HI,
                          preferred_element_type=jnp.float32)
    add = add.reshape(16, 8, 16, 128)
    pos = vec[0, 14:15]
    for c in range(16):
        xi, zi = c // 4, c % 4
        v = twice[c] + add[c] + vec[0, 10 + xi:11 + xi] * delta[zi]
        if xi in (0, 3):
            v = v + (pos if xi == 0 else 1.0 - pos) * inflow[zi]
        h2[c] = v


def apply_k(src, dst, lt, own=False, four=False):
    rows = slice(8, 16) if own else slice(0, 24)

    def pressure(k, at):
        return 2.0 * src[k, at] if four else src[k, at] + src[64 + k, at]

    def before(load):
        return load(slice(7, 15)) if own else pltpu.roll(load(rows), 1, 0)

    def after(load):
        return load(slice(9, 17)) if own else pltpu.roll(load(rows), 23, 0)

    for zi in range(4):
        u = [src[16 + j * 4 + zi, rows] for j in range(4)]
        p = [pressure(j * 4 + zi, rows) for j in range(4)]
        for xi in range(4):
            du = combine(CENTRAL[xi], u)
            dp = combine(CENTRAL[xi], p)
            if xi == 0:
                du = du - 1.5 * before(lambda at: src[28 + zi, at])
                dp = dp - 1.5 * before(lambda at: pressure(12 + zi, at))
            if xi == 3:
                du = du + 1.5 * after(lambda at: src[16 + zi, at])
                dp = dp + 1.5 * after(lambda at: pressure(zi, at))
            dst[xi * 4 + zi] = du
            dst[16 + xi * 4 + zi] = dp
    for xi in range(4):
        u = [src[48 + xi * 4 + j, rows] for j in range(4)]
        p = [pressure(xi * 4 + j, rows) for j in range(4)]
        for zi in range(4):
            du = combine(CENTRAL[zi], u)
            dp = combine(CENTRAL[zi], p)
            if zi == 0:
                du = du - 1.5 * z_before(u[3], lt)
                dp = dp - 1.5 * z_before(p[3], lt)
            if zi == 3:
                du = du + 1.5 * z_after(u[0], lt)
                dp = dp + 1.5 * z_after(p[0], lt)
            dst[xi * 4 + zi] = dst[xi * 4 + zi] + du
            dst[48 + xi * 4 + zi] = dp

    n = 8 if own else 24
    u = src[32:48, rows]
    p = 2.0 * src[0:16, rows] if four else src[0:16, rows] + src[64:80, rows]
    x = jnp.concatenate([u, p], axis=0).reshape(32 * n, 128)
    d = exact_dot(x, lt[40:168]).reshape(32, n, 128)
    dst[0:16] = dst[0:16] + d[0:16]
    dst[32:48] = d[16:32]


def two_level(r, pe, co, lt):
    parts = []
    for f in range(5):
        tz = []
        for xi in range(4):
            q = [r[f * 16 + xi * 4 + zi] for zi in range(4)]
            tz.append([combine(RT[za], q) for za in range(2)])
        for xa in range(2):
            for za in range(2):
                parts.append(combine(RT[xa], [tz[xi][za] for xi in range(4)]))
    both = jnp.concatenate([lt[168:296], lt[296:424]], axis=1)
    e = exact_dot(jnp.concatenate(parts, axis=0), both)
    for f in range(5):
        py = [[None, None], [None, None]]
        for xa in range(2):
            for za in range(2):
                n = f * 4 + xa * 2 + za
                e0, e1 = e[24 * n:24 * n + 24, 0:128], e[24 * n:24 * n + 24, 128:256]
                co[2 * n] = e0
                co[2 * n + 1] = e1
                py[za][xa] = lt[20:21] * e0 + lt[21:22] * e1
        for xi in range(4):
            v = [combine(PR[xi], py[za]) for za in range(2)]
            for zi in range(4):
                pe[f * 16 + xi * 4 + zi] = combine(PR[zi], v)


def coarse_products(co, lt):
    def at(f, xa, za, ya):
        return co[f * 8 + xa * 4 + za * 2 + ya]

    def own(q):
        return q[8:16]

    def dx(q, xa, za, ya):
        if xa == 0:
            v = q(1, za, ya)
            return 0.25 * (own(v) - own(pltpu.roll(v, 1, 0)))
        v = q(0, za, ya)
        return 0.25 * (own(pltpu.roll(v, 23, 0)) - own(v))

    def dz(q, xa, za, ya):
        v = own(q(xa, 1 - za, ya))
        if za == 0:
            return 0.25 * (v - z_before(v, lt))
        return 0.25 * (z_after(v, lt) - v)

    def dy(q, xa, za, ya):
        v = own(q(xa, za, 1 - ya))
        w = pltpu.roll(v, 64, 1)
        return 0.25 * (v - w) if ya == 0 else 0.25 * (w - v)

    total = [jnp.zeros((8, 128), jnp.float32)] * 3
    for xa in range(2):
        for za in range(2):
            for ya in range(2):
                def field(f):
                    return lambda a, b, c: at(f, a, b, c)

                def pressure(a, b, c):
                    return at(0, a, b, c) + at(4, a, b, c)
                e = [own(at(f, xa, za, ya)) for f in range(5)]
                div = (dx(field(1), xa, za, ya) + dy(field(2), xa, za, ya)
                       + dz(field(3), xa, za, ya))
                v = [div, dx(pressure, xa, za, ya), dy(pressure, xa, za, ya),
                     dz(pressure, xa, za, ya), div]
                for f in range(5):
                    total = [total[0] + e[f] * e[f], total[1] + e[f] * v[f], total[2] + v[f] * v[f]]
    return [t * lt[23:24] for t in total]


PAIRS = [(i, j) for i in range(3) for j in range(i, 3)]


def fine_products(e, s, t, ke, kt, lt, own):
    rows = slice(0, 8) if own else slice(8, 16)
    zero = jnp.zeros((8, 128), jnp.float32)
    total = [zero] * 18
    for xi in range(4):
        for zi in range(4):
            acc = [zero] * 18
            c = xi * 4 + zi
            for f in range(4):
                k = f * 16 + c
                x = [e[k, 8:16], s[k, 8:16], t[k, 8:16]]
                y = [ke[k, rows], x[2], kt[k, rows]]
                z = x
                if f == 0:
                    last = [e[64 + c, 8:16], s[64 + c, 8:16], x[2]]
                    z = [x[0] + last[0], x[1] + last[1], x[2] + x[2]]
                for n, (i, j) in enumerate(PAIRS):
                    v = x[i] * x[j]
                    if f == 0:
                        v = v + last[i] * last[j]
                    acc[n] = acc[n] + v
                    acc[6 + n] = acc[6 + n] + (z[i] * y[j] if i == j else z[i] * y[j] + z[j] * y[i])
                    v = y[i] * y[j]
                    acc[12 + n] = acc[12 + n] + (2.0 * v if f == 0 else v)
            w = WEIGHTS[xi] * WEIGHTS[zi]
            total = [a + w * b for a, b in zip(total, acc)]
    return [a * lt[22:23] for a in total]


def diagonal():
    return (lax.broadcasted_iota(jnp.int32, (24, 128), 0)
            == lax.broadcasted_iota(jnp.int32, (24, 128), 1))


def pass_words(e, s, t, ke, kt, co, gram, lt, own=False):
    two_level(e, s, co, lt)
    apply_k(s, t, lt)

    def over_k(k, _):
        e[k] = e[k] - s[k]
        return 0
    lax.fori_loop(0, 80, over_k, 0, unroll=8)
    apply_k(e, ke, lt, own)
    apply_k(t, kt, lt, own, four=True)
    products = coarse_products(co, lt) + fine_products(e, s, t, ke, kt, lt, own)
    rows = [jnp.sum(p, axis=0, keepdims=True) for p in products] + [jnp.zeros((3, 128), jnp.float32)]
    total = jnp.sum(jnp.concatenate(rows, axis=0), axis=1, keepdims=True)
    line = jnp.sum(jnp.where(diagonal(), total, 0.0), axis=0, keepdims=True)
    for n in range(gram.shape[0]):
        gram[n] = jnp.broadcast_to(line, (8, 128))


def pack_kernel(idx, mine, own, to_upper, to_lower):
    first = lax.broadcasted_iota(jnp.int32, (8, 128), 0) == 0
    last = lax.broadcasted_iota(jnp.int32, (8, 128), 0) == 7
    for f in range(5):
        low = mine[pl.ds(20 + f, 8, stride=30), :]
        high = mine[pl.ds(25 + f, 8, stride=30), :]
        for xi in range(4):
            k = f * 4 + xi
            v = mine[pl.ds(5 * xi + f, 8, stride=30), :]
            if xi == 0:
                v = v + 1.5 * jnp.where(first, 0.0, pltpu.roll(high, 1, 0))
            if xi == 3:
                v = v - 1.5 * jnp.where(last, 0.0, pltpu.roll(low, 7, 0))
            own[k] = v
            to_upper[pl.ds(k, 6, stride=20), :] = v[2:8]
            to_lower[pl.ds(k, 6, stride=20), :] = v[0:6]
        to_upper[120 + f:121 + f] = high[7:8]
        to_lower[120 + f:121 + f] = low[0:1]


def window_kernel(idx, lower, own, upper, edge_low, edge_high, after, win):
    for f in range(5):
        e = 120 + f
        for xi in range(4):
            k = f * 4 + xi
            at = 20 * k
            low, mid, high = lower[pl.ds(k, 6, stride=20), :], own[k], upper[pl.ds(k, 6, stride=20), :]
            win[at:at + 6] = low
            win[at + 6:at + 14] = mid
            win[at + 14:at + 20] = high
            if xi == 0:
                win[at + 6:at + 7] = mid[0:1] + 1.5 * lower[e:e + 1]
                win[at + 14:at + 15] = high[0:1] + 1.5 * edge_high[e:e + 1]
            if xi == 3:
                win[at + 13:at + 14] = mid[7:8] - 1.5 * upper[e:e + 1]
                win[at + 5:at + 6] = low[5:6] - 1.5 * edge_low[e:e + 1]


def first_pass_kernel(idx, quarters, lt, r, s, t, ke, kt, gram, co):
    zero = jnp.zeros((2, 128), jnp.float32)
    for f in range(5):
        for xi in range(4):
            for zi in range(4):
                k = f * 16 + xi * 4 + zi
                at = 20 * (f * 4 + xi)
                r[k, 0:2] = zero
                r[k, 2:22] = quarters[zi, at:at + 20]
                r[k, 22:24] = zero
    pass_words(r, s, t, ke, kt, co, gram, lt)


def step_sizes(sums):
    line = sums[0, 0:1]
    for n in range(1, sums.shape[0]):
        line = line + sums[n, 0:1]
    v = jnp.sum(jnp.where(diagonal(), line, 0.0), axis=1, keepdims=True)
    v = jnp.broadcast_to(v, (24, 128))
    c0, c1, c2 = v[0:1], v[1:2], v[2:3]
    den = 4.0 * c0 + 4.0 * c1 + c2 + EPS
    a1, b1 = (2.0 * c0 + c1) / den, (2.0 * c1 + c2 + EPS) / den
    d = [jnp.ones_like(a1), b1, -a1]

    def form(base, twice):
        total = None
        for n, (i, j) in enumerate(PAIRS):
            term = d[i] * d[j] * v[base + n:base + n + 1]
            if twice and i != j:
                term = 2.0 * term
            total = term if total is None else total + term
        return total
    rr, kk = jnp.maximum(form(3, True), 0.0), jnp.maximum(form(15, True), 0.0)
    bound = jnp.sqrt(rr) * jnp.sqrt(kk)
    rk = jnp.clip(form(9, False), -bound, bound)
    den = 4.0 * rr + 4.0 * rk + kk + EPS
    return a1, b1, (2.0 * rr + rk) / den, (2.0 * rk + kk + EPS) / den


def next_pass_kernel(first, idx, sums, e, s, t, ke, kt, *rest):
    if first:
        lt, r2, s2, t2, ke2, kt2, acc2, gram, co = rest
    else:
        acc, lt, r2, s2, t2, ke2, kt2, acc2, gram, co = rest
    a1, b1, a2, b2 = step_sizes(sums)

    def put(k, tk, kr):
        sk = s[k]
        r1 = e[k] + b1 * sk - a1 * tk
        v = a1 * sk[8:16] + a2 * r1[8:16]
        acc2[k] = v if first else acc[k] + v
        r2[k] = b2 * r1 - a2 * kr

    def over_k(k, _):
        tk = t[k]
        kr = ke[k] + b1 * tk - a1 * kt[k]
        put(k, tk, kr)
        put(64 + k, tk, kr)
        return 0
    lax.fori_loop(0, 16, over_k, 0, unroll=4)

    def rest_k(k, _):
        tk = t[k]
        put(k, tk, ke[k] + b1 * tk - a1 * kt[k])
        return 0
    lax.fori_loop(16, 64, rest_k, 0, unroll=4)
    pass_words(r2, s2, t2, ke2, kt2, co, gram, lt, own=not first)


def third_pass_kernel(idx, sums, e, s, t, ke, kt, acc, lt, eo, so, to, acc2, gram,
                      r2, s2, t2, ke2, kt2, co):
    next_pass_kernel(False, idx, sums, e, s, t, ke, kt, acc, lt, r2, s2, t2, ke2, kt2, acc2, gram, co)
    eo[...] = r2[:, 8:16]
    so[...] = s2[:, 8:16]
    to[...] = t2[:, 8:16]


def last_kernel(idx, sums, e, s, t, acc, low, h2, select, split, out, fields, change, stack, rows):
    a1, b1, a2, _ = step_sizes(sums)

    def over_k(k, _):
        r1 = e[k] + b1 * s[k] - a1 * t[k % 64]
        change[pl.ds(pl.multiple_of(k * 8, 8), 8)] = acc[k] + a1 * s[k] + a2 * r1
        return 0
    lax.fori_loop(0, 80, over_k, 0, unroll=4)
    z = idx[1]
    stack[...] = jnp.zeros_like(stack)
    here = row_of_y()
    for c in range(16):
        for f in range(5):
            k = f * 16 + c
            d = change[pl.ds(k * 8 + z, 1)]
            stack[f:f + 1, 128 * c:128 * c + 128] = d
            n = 8 * (k // 4)
            rows[n:n + 8, 128 * (c % 4):128 * (c % 4) + 128] = (low[5 * c + f:5 * c + f + 1] + d) * here
    fields[...] = project(rows[...], select[...]).reshape(5, 4, 8, 64)
    whole = stack[...]
    d1 = whole.astype(jnp.bfloat16).astype(jnp.float32)
    d2 = (whole - d1).astype(jnp.bfloat16).astype(jnp.float32)
    d3 = whole - d1 - d2
    parts = jnp.concatenate([d1, d1, d2, d1, d2, d3], axis=0).astype(jnp.bfloat16)
    add = lax.dot_general(parts, split[0].astype(jnp.bfloat16), (((0,), (0,)), ((), ())),
                          preferred_element_type=jnp.float32).reshape(16, 8, 16, 128)
    for c in range(16):
        xi, zi = c // 4, c % 4
        v = h2[c] + add[c]
        for y in range(8):
            out[xi, y, pl.ds(zi, 16, stride=4), :] = v[y]


def on_device(distribution, forcing):
    import functools
    tables = {k: jnp.asarray(v) for k, v in constant_tables().items()}
    spaces = lax.axis_size("space")
    blocks = spaces // 8
    idx = jnp.stack([lax.axis_index("vel"), lax.axis_index("space") % 8]).astype(jnp.int32)
    vec, lt = tables["vec"], tables["lanes"]
    wide = (16, 8, 16, 128)
    layer = (4, 8, 16, 128)

    def shifted(x, by):
        return lax.ppermute(x, "space", [(i, (i + by) % spaces) for i in range(spaces)])

    up, down = call(rim_kernel, "rims", idx, [distribution], [],
                    [(544, 128)] * 2, [layer, layer, (8, 8, 16, 128), (1024, 8), (1, 32, 128)])
    up, down = shifted(up, 1), shifted(down, -1)
    twice, moma, force = call(local_kernel, "local", idx, [distribution, forcing, tables["select"]],
                              [vec, tables["tab0"], tables["tab1"], tables["tab2"]],
                              [wide, (16, 48, 128), (4, 20, 128)], [wide, wide, (2048, 48)])
    pay, delta, inflow = call(moment_kernel, "moments", idx, [up, down, moma, tables["mix"], lt],
                              [vec, tables["tabd"], tables["tabs"]], [(408, 128), layer, layer],
                              [layer, (16, 48, 128), (16, 40, 128), (64, 2048)])
    got = lax.all_gather(pay, "vel")
    (res,) = call(residual_kernel, "residual", idx, [got, force], [], [(8, 30, 128)])
    near = [[a * 8 + b for b in range(8)] for a in range(blocks)]
    far = [[a * 8 + b for a in range(blocks)] for b in range(8)]
    mine = lax.all_to_all(res, "space", 0, 0, axis_index_groups=near, tiled=True).reshape(240, 128)
    own_r, to_upper, to_lower = call(pack_kernel, "pack", idx, [mine], [],
                                     [(20, 8, 128), (125, 128), (125, 128)])
    lower, upper = shifted(to_upper, 8), shifted(to_lower, -8)
    h2, low = call(feq_kernel, "feq", idx, [got, twice, delta, inflow, lt],
                   [vec, tables["final"]],
                   [wide, (80, 128)], [(16, 8, 128), (4, 8, 128), (4, 8, 128), (56, 2048)])
    (quarter,) = call(window_kernel, "window", idx, [lower, own_r, upper, to_lower, to_upper, low], [],
                      [(400, 128)])
    quarters = lax.all_gather(quarter, "vel")

    def summed(gram):
        return lax.all_to_all(gram, "space", 0, 0, axis_index_groups=far, tiled=True)

    win, own, part = (80, 24, 128), (80, 8, 128), (blocks, 8, 128)
    four, own4 = (64, 24, 128), (64, 8, 128)
    co = (40, 24, 128)
    e, s, t, ke, kt, gram = call(first_pass_kernel, "pass1", idx, [quarters, lt], [],
                                  [win, win, four, four, four, part], [co])
    e, s, t, ke, kt, acc, gram = call(functools.partial(next_pass_kernel, True), "pass2", idx,
                                       [summed(gram), e, s, t, ke, kt, lt], [],
                                       [win, win, four, four, four, own, part], [co])
    e, s, t, acc, gram = call(third_pass_kernel, "pass3", idx,
                               [summed(gram), e, s, t, ke, kt, acc, lt], [],
                               [own, own, own4, own, part], [win, win, four, own4, own4, co])
    out, fields = call(last_kernel, "last", idx,
                       [summed(gram), e, s, t, acc, low, h2, tables["select"]], [tables["split"]],
                       [(4, 8, 64, 128), (5, 4, 8, 64)], [(640, 128), (8, 2048), (160, 512)])
    return out, fields


def solution(mesh):
    return jax.shard_map(
        on_device,
        mesh=mesh,
        in_specs=(P("space", None, None, "vel"), P(None, "space", None, None)),
        out_specs=(P("space", None, None, "vel"), P(None, "space", None, None)),
        check_vma=False,
    )
```

```python
import math

import jax
import jax.numpy as jnp
import numpy as np
from jax import lax
from jax.experimental import pallas as pl
from jax.experimental.pallas import tpu as pltpu
from jax.sharding import PartitionSpec as P

INTERPRET = False
DT = 0.02
RF = 0.4472135954999579
POINTS = [-1.0, -RF, RF, 1.0]
WEIGHTS = [1.0 / 6.0, 5.0 / 6.0, 5.0 / 6.0, 1.0 / 6.0]
EPS = 1e-6
HI = lax.Precision.HIGHEST


def lagrange_table(points):
    n = len(points)
    bary = []
    for i in range(n):
        product = 1.0
        for j in range(n):
            if j != i:
                product *= points[i] - points[j]
        bary.append(1.0 / product)
    rows = [[0.0] * n for _ in range(n)]
    for i in range(n):
        for j in range(n):
            if j != i:
                rows[i][j] = bary[j] / bary[i] / (points[i] - points[j])
        rows[i][i] = -sum(rows[i])
    return rows


D4 = lagrange_table(POINTS)
for _i in (1, 2):
    D4[_i][_i] = 0.0
PR = [[(1.0 - x) / 2.0, (1.0 + x) / 2.0] for x in POINTS]
RT = [[WEIGHTS[i] * PR[i][a] for i in range(4)] for a in range(2)]


def constant_tables():
    k = np.arange(512)
    b, j = k // 128, k % 128
    s = j // 64
    m = ((b * 64 + j % 64) * 5179 + 7) % 16384
    xi = np.stack([16 * s + m // 1024, (m // 32) % 32, m % 32]).astype(np.float64)
    xi = -4.0 + 0.25 * (xi + 0.5)
    sq = (xi * xi).sum(0)
    e = math.pi ** (-1.5) * np.exp(-sq)
    x, y, z = xi
    phi = np.stack(
        [np.ones(512), x, y, z, 2 * sq / 3 - 1, 2 * (x * x - sq / 3), 2 * (y * y - sq / 3),
         2 * x * y, 2 * x * z, 2 * y * z, x * (sq - 2.5), y * (sq - 2.5), z * (sq - 2.5)]
    )
    p = phi[0] + phi[4]
    zero = np.zeros(512)

    def eight(rows):
        return np.stack(list(rows) + [zero] * (8 - len(rows)))

    low = eight(phi[:5])
    along_x = eight([phi[1], p + phi[5], phi[7], phi[8], phi[1] + phi[10]])
    along_y = eight([phi[2], phi[7], p + phi[6], phi[9], phi[2] + phi[11]])
    along_z = eight([phi[3], phi[8], phi[9], p - phi[5] - phi[6], phi[3] + phi[12]])
    rows32 = np.concatenate([low, along_x, along_y, along_z])
    ec = eight([e, 2 * x * e, 2 * y * e, 2 * z * e, e * (sq - 1.5)])
    pos, neg = np.maximum(xi, 0.0), np.minimum(xi, 0.0)

    def per_rank(rows):
        return np.stack([rows[:, r * 128:(r + 1) * 128] for r in range(4)]).astype(np.float32)

    ispos = (x > 0).astype(np.float64)
    ax = np.abs(x)
    d4 = np.array(D4)
    vec = [-DT * 0.5 * x, -DT * 0.5 * y, -DT * 0.5 * z,
           -3 * DT * pos[1], -3 * DT * neg[1], -3 * DT * pos[2], -3 * DT * neg[2],
           -3 * DT * pos[0], 3 * DT * neg[0], 3 * DT * ax]
    for i in range(4):
        kap = -DT * 0.5 * x * np.where(ispos > 0, d4[i][0], d4[i][3])
        if i == 0:
            kap = kap + ispos * (0.8 - 3 * DT * ax)
        if i == 3:
            kap = kap + (1 - ispos) * (0.8 - 3 * DT * ax)
        vec.append(kap)
    kappa = vec[10:14]
    vec.append(ispos)
    for jj in range(4):
        vec.append(-DT * 0.5 * x * np.where(ispos > 0, d4[3][jj], d4[0][jj]))
    while len(vec) < 24:
        vec.append(zero)
    vec = per_rank(np.concatenate([np.stack(vec), low]))

    def moment_rows(start, rows, height):
        out = np.zeros((height, 512))
        out[start:start + len(rows)] = rows
        return per_rank(out)

    tab2 = moment_rows(0, rows32, 48)
    tab1 = moment_rows(40, low, 48)
    tab0 = moment_rows(32, low, 48)
    tabd = per_rank(np.concatenate([v * rows32 for v in kappa] + [ispos * low, (1 - ispos) * low]))
    tabs = per_rank(np.concatenate([ispos * rows32, (1 - ispos) * rows32]))
    select = np.zeros((64, 512))
    for n in range(4):
        for la in range(128):
            select[4 * (la % 16) + n, 128 * n + la] = 1.0
    import ml_dtypes
    pieces, left = [], per_rank(ec)
    for _ in range(3):
        pieces.append(left.astype(ml_dtypes.bfloat16))
        left = left - pieces[-1].astype(np.float32)
    split = np.concatenate([pieces[n].astype(np.float32) for n in (0, 1, 0, 2, 1, 0)], axis=1)
    g = rows32 @ ec.T
    g5 = g[:8]
    mix = np.zeros((40, 64))
    mix[:32, 0:8] = 0.16 * g + 0.04 * g @ g5
    mix[:32, 8:16] = 0.2 * g
    mix[32:, 0:8] = 0.2 * g5
    mix[32:, 8:16] = np.eye(8)
    final = [ec]
    for d in range(3):
        for i, part in enumerate((pos[d], neg[d])):
            c0 = 16 + 16 * d + 8 * i
            mix[:32, c0:c0 + 8] = -0.2 * DT * (rows32 * part) @ ec.T
            final.append(-0.2 * DT * ec * part)
    final = per_rank(np.concatenate(final))
    lane = np.arange(128)
    yi, ze = (lane // 16) % 4, lane % 16
    rows = []
    shifts = (-3, -2, -1, 1, 2, 3)

    def entry(table, sft):
        return np.array([table(i, i + sft) if 0 <= i + sft < 4 else 0.0 for i in yi])

    for sft in shifts:
        c = entry(lambda i, q: 0.5 * D4[i][q], sft)
        if sft == -1:
            c = c - 1.5 * (yi == 0)
        if sft == 1:
            c = c + 1.5 * (yi == 3)
        rows.append(c)
    for a in range(2):
        for sft in range(-3, 4):
            rows.append(entry(lambda i, q: RT[a][q], sft))
    rows += [np.array([PR[i][0] for i in yi]), np.array([PR[i][1] for i in yi])]
    rows += [np.array([WEIGHTS[i] for i in yi]), (yi == 0) * 1.0, (ze == 0) * 1.0, (ze == 15) * 1.0]
    for sft in shifts:
        rows.append(entry(lambda i, q: 0.5 * D4[i][q], sft))
    rows += [entry(lambda i, q: 0.5 * D4[i][q], 0), 3.0 * (yi == 0), 3.0 * (yi == 3)]
    while len(rows) < 40:
        rows.append(np.zeros(128))
    mats = np.zeros((3, 128, 128))
    for n, sft in enumerate(shifts):
        mats[0, (lane + 16 * sft) % 128, lane] += rows[n]
    for a in range(2):
        for sft in range(-3, 4):
            mats[1 + a, (lane + 16 * sft) % 128, lane] += rows[6 + 7 * a + sft + 3]
    lanes = np.concatenate([np.stack(rows), mats.reshape(384, 128)]).astype(np.float32)
    return dict(vec=vec, tab2=tab2, tab1=tab1, tab0=tab0, mix=mix.astype(np.float32),
                final=final, lanes=lanes, split=split, tabd=tabd, tabs=tabs, select=select.astype(np.float32))


def call(kernel, name, idx, full, ranked, outs, scratch=(), limit=24):
    n = len(full)

    def body(idx, *refs):
        rank = [r.at[pl.ds(idx[0], 1)] for r in refs[n:n + len(ranked)]]
        kernel(idx, *refs[:n], *rank, *refs[n + len(ranked):])

    vmem = pl.BlockSpec(memory_space=pltpu.VMEM)
    return pl.pallas_call(
        body,
        name=name,
        out_shape=[jax.ShapeDtypeStruct(s, jnp.float32) for s in outs],
        in_specs=[pl.BlockSpec(memory_space=pltpu.SMEM)] + [vmem] * (n + len(ranked)),
        out_specs=[vmem] * len(outs),
        scratch_shapes=[pltpu.VMEM(s, jnp.float32) for s in scratch],
        compiler_params=pltpu.CompilerParams(vmem_limit_bytes=limit << 20),
        interpret=INTERPRET,
    )(idx, *full, *ranked)


def exact_dot(a, b):
    return jnp.dot(a, b, precision=HI, preferred_element_type=jnp.float32)


def project(x, rows):
    return lax.dot_general(x, rows, (((1,), (1,)), ((), ())), precision=HI,
                           preferred_element_type=jnp.float32)


def combine(row, values):
    total = None
    for c, v in zip(row, values):
        if c != 0.0:
            total = c * v if total is None else total + c * v
    return total


def layer_yz(src, dst, vec):
    def over_y(y, _):
        q = [src[zi, y] for zi in range(4)]
        for zi in range(4):
            v = vec[0, 2:3] * combine(D4[zi], q)
            if zi == 0:
                v = v + vec[0, 5:6] * (q[0] - pltpu.roll(q[3], 1, 0))
            if zi == 3:
                v = v + vec[0, 6:7] * (pltpu.roll(q[0], 15, 0) - q[3])
            dst[zi, y] = v
        return 0
    lax.fori_loop(0, 8, over_y, 0, unroll=True)

    def over_z(zi, _):
        q = [src[zi, y] for y in range(8)]
        for y in range(8):
            e, yi = 4 * (y // 4), y % 4
            v = vec[0, 1:2] * combine(D4[yi], q[e:e + 4])
            if yi == 0:
                v = v + vec[0, 3:4] * (q[y] - q[(y + 7) % 8])
            if yi == 3:
                v = v + vec[0, 4:5] * (q[(y + 1) % 8] - q[y])
            dst[zi, y] = dst[zi, y] + v
        return 0
    lax.fori_loop(0, 4, over_z, 0, unroll=True)


def every_fourth(h, xi, y, zi):
    if INTERPRET:
        return h[xi, y][zi::4]
    return h[xi, y, pl.ds(zi, 16, stride=4), :]


def speed_rows(idx, vec):
    j = lax.broadcasted_iota(jnp.int32, (1, 128), 1)
    m = ((idx[0] * 64 + (j & 63)) * 5179 + 7) & 16383
    s = j >> 6
    x, y, z = [-4.0 + 0.25 * (n.astype(jnp.float32) + 0.5)
               for n in (16 * s + (m >> 10), (m >> 5) & 31, m & 31)]
    pos = s > 0
    rows = {0: -DT * 0.5 * x, 1: -DT * 0.5 * y, 2: -DT * 0.5 * z,
            3: -3 * DT * jnp.maximum(y, 0.0), 4: -3 * DT * jnp.minimum(y, 0.0),
            5: -3 * DT * jnp.maximum(z, 0.0), 6: -3 * DT * jnp.minimum(z, 0.0),
            14: pos.astype(jnp.float32)}
    for n in range(4):
        rows[15 + n] = -DT * 0.5 * x * jnp.where(pos, D4[3][n], D4[0][n])
    rows[24], rows[25], rows[26], rows[27] = jnp.ones_like(x), x, y, z
    rows[28] = 2.0 * (x * x + y * y + z * z) / 3.0 - 1.0
    vec[...] = jnp.zeros_like(vec)
    for n, v in rows.items():
        vec[0, n:n + 1] = v


def rim_kernel(idx, h, up, down, q, t, ends, m, vec):
    speed_rows(idx, vec)
    transport_rims(idx, h, vec, up, down, q, t, ends, m)


def transport_rims(idx, h, vec, up, down, q, t, ends, m):
    pos = vec[0, 14:15] > 0.5
    for zi in range(4):
        def over_y(y, _):
            x = [every_fourth(h, xi, y, zi) for xi in range(4)]
            ql = jnp.where(pos, x[3], x[0])
            q[zi, y] = ql
            ends[zi, y] = x[0]
            ends[4 + zi, y] = x[3]
            v = 0.8 * ql
            for j in range(4):
                v = v + vec[0, 15 + j:16 + j] * x[j]
            up[pl.ds(pl.multiple_of((zi * 8 + y) * 16, 16), 16)] = v
            return 0
        lax.fori_loop(0, 8, over_y, 0, unroll=True)
    layer_yz(q, t, vec)
    right = lax.broadcasted_iota(jnp.int32, (16, 128), 1) >= 64

    def pack(n, _):
        zi, y = n // 8, n % 8
        at = pl.ds(pl.multiple_of(n * 16, 16), 16)
        tl = pltpu.roll(t[zi, y] + up[at], 64, 1)
        ql = q[zi, y]
        up[at] = jnp.where(right, ql, tl)
        down[at] = jnp.where(right, tl, ql)
        return 0
    lax.fori_loop(0, 32, pack, 0, unroll=8)
    m[...] = project(ends[...].reshape(1024, 128), vec[0, 24:32])
    for n in range(8):
        zi, out = n % 4, (down, up)[n // 4]
        out[512 + 8 * zi:520 + 8 * zi] = m[128 * n:128 * n + 128].T


def local_update(src, dst, vec):
    def over_y(y, _):
        q = [src[c, y] for c in range(16)]
        for xi in range(4):
            for zi in range(4):
                own = q[xi * 4 + zi]
                v = 0.8 * own + vec[0, 0:1] * combine(D4[xi], [q[j * 4 + zi] for j in range(4)])
                v = v + vec[0, 2:3] * combine(D4[zi], q[xi * 4:xi * 4 + 4])
                if zi == 0:
                    v = v + vec[0, 5:6] * (own - pltpu.roll(q[xi * 4 + 3], 1, 0))
                if zi == 3:
                    v = v + vec[0, 6:7] * (pltpu.roll(q[xi * 4], 15, 0) - own)
                if xi == 0:
                    v = v + vec[0, 7:8] * own
                if xi == 3:
                    v = v + vec[0, 8:9] * own
                dst[xi * 4 + zi, y] = v
        return 0
    lax.fori_loop(0, 8, over_y, 0, unroll=2)

    def over_c(c, _):
        q = [src[c, y] for y in range(8)]
        for y in range(8):
            e, yi = 4 * (y // 4), y % 4
            v = vec[0, 1:2] * combine(D4[yi], q[e:e + 4])
            if yi == 0:
                v = v + vec[0, 3:4] * (q[y] - q[(y + 7) % 8])
            if yi == 3:
                v = v + vec[0, 4:5] * (q[(y + 1) % 8] - q[y])
            dst[c, y] = dst[c, y] + v
        return 0
    lax.fori_loop(0, 16, over_c, 0, unroll=4)


def row_of_y():
    y = lax.broadcasted_iota(jnp.int32, (8, 128), 0)
    return (lax.broadcasted_iota(jnp.int32, (8, 128), 1) // 16 == y).astype(jnp.float32)


def local_kernel(idx, h, forcing, select, vec, tab0, tab1, tab2, twice, mom, force, first, once, m):
    spread = exact_dot(forcing[...].reshape(96, 64), select[...])
    here = row_of_y()
    force[...] = jnp.zeros_like(force)
    for f in range(3):
        for c in range(16):
            n = 8 * (f * 4 + c // 4)
            v = spread[n:n + 8, 128 * (c % 4):128 * (c % 4) + 128] * here
            at = 5 * (c // 4) + f + 1
            force[c % 4, at:at + 1] = jnp.sum(v, axis=0, keepdims=True)
    for c in range(16):
        xi, zi = c // 4, c % 4

        def over_y(y, _):
            first[c, y] = every_fourth(h, xi, y, zi)
            return 0
        lax.fori_loop(0, 8, over_y, 0, unroll=True)
    local_update(first, once, vec)
    local_update(once, twice, vec)

    m[...] = project(first[...].reshape(2048, 128), tab0[0])
    m[...] = m[...] + project(once[...].reshape(2048, 128), tab1[0])
    m[...] = m[...] + project(twice[...].reshape(2048, 128), tab2[0])
    for c in range(16):
        mom[c] = m[128 * c:128 * c + 128].T


def z_before(q, lt):
    return jnp.where(lt[24:25] > 0.5, pltpu.roll(q, 113, 1), pltpu.roll(q, 1, 1))


def z_after(q, lt):
    return jnp.where(lt[25:26] > 0.5, pltpu.roll(q, 15, 1), pltpu.roll(q, 127, 1))


SHIFTS = (-3, -2, -1, 1, 2, 3)


def central_y(q, lt):
    total = None
    for n, s in enumerate(SHIFTS):
        term = lt[n:n + 1] * pltpu.roll(q, (-16 * s) % 128, 1)
        total = term if total is None else total + term
    return total


def one_sided(load, low, high, c, cy, lt):
    xi, zi = c // 4, c % 4
    q = load(c)
    cx = combine([0.5 * v for v in D4[xi]], [load(j * 4 + zi) for j in range(4)])
    px = cx + 3.0 * (q - low(zi)) if xi == 0 else cx
    mx = cx + 3.0 * (high(zi) - q) if xi == 3 else cx
    w = 0.5 * (lt[33:34] * (q - pltpu.roll(q, 16, 1)) - lt[34:35] * (pltpu.roll(q, 112, 1) - q))
    cz = combine([0.5 * v for v in D4[zi]], [load(xi * 4 + j) for j in range(4)])
    pz = cz + 3.0 * (q - z_before(load(xi * 4 + 3), lt)) if zi == 0 else cz
    mz = cz + 3.0 * (z_after(load(xi * 4), lt) - q) if zi == 3 else cz
    return [px, mx, cy + w, cy - w, pz, mz]


CENTRAL = [[0.0 if i == j else 0.5 * D4[i][j] for j in range(4)] for i in range(4)]


def moment_kernel(idx, up, down, moma, mix, lt, vec, tabd, tabs, pay, delta, inflow,
                  yz, mom, full, stack):
    right = lax.broadcasted_iota(jnp.int32, (16, 128), 1) >= 64

    def unpack(n, _):
        at = pl.ds(pl.multiple_of(n * 16, 16), 16)
        u, d = up[at], down[at]
        zi, y = n // 8, n % 8
        delta[zi, y] = vec[0, 9:10] * jnp.where(right, u, d)
        inflow[zi, y] = vec[0, 9:10] * pltpu.roll(jnp.where(right, d, u), 64, 1)
        return 0
    lax.fori_loop(0, 32, unpack, 0, unroll=8)
    layer_yz(delta, yz, vec)
    inflow[...] = inflow[...] + yz[...]
    md = project(delta[...].reshape(512, 128), tabd[0])
    ms = project(inflow[...].reshape(512, 128), tabs[0])
    for zi in range(4):
        at = slice(128 * zi, 128 * zi + 128)
        t, u, v = md[at, 0:128].T, md[at, 128:144].T, ms[at].T
        for xi in range(4):
            c = xi * 4 + zi
            q = moma[c, 0:32] + t[32 * xi:32 * xi + 32]
            once = moma[c, 40:48]
            if xi == 0:
                q, once = q + v[0:32], once + u[0:8]
            if xi == 3:
                q, once = q + v[32:64], once + u[8:16]
            mom[c, 0:32] = q
            mom[c, 32:40] = moma[c, 32:40]
            mom[c, 40:48] = once

    def load0(c):
        return mom[c, 32:40]

    cy = exact_dot(mom[:, 32:40].reshape(128, 128), lt[40:168])
    for c in range(16):
        six = one_sided(load0, lambda zi: up[512 + 8 * zi:520 + 8 * zi],
                        lambda zi: down[512 + 8 * zi:520 + 8 * zi], c, cy[8 * c:8 * c + 8], lt)
        at = slice(128 * c, 128 * c + 128)
        stack[0:16, at] = mom[c, 32:48]
        for n in range(6):
            stack[16 + 8 * n:24 + 8 * n, at] = six[n]
    add = exact_dot(mix[...], stack[...])
    for c in range(16):
        at = slice(128 * c, 128 * c + 128)
        full[c, 0:32] = mom[c, 0:32] + add[0:32, at]
        full[c, 32:40] = add[32:40, at]
    cy = exact_dot(full[:, 16:24].reshape(128, 128), lt[40:168])
    for c in range(16):
        xi, zi = c // 4, c % 4
        r = combine(CENTRAL[xi], [full[j * 4 + zi, 8:16] for j in range(4)])
        r = r + cy[8 * c:8 * c + 8]
        r = r + combine(CENTRAL[zi], [full[xi * 4 + j, 24:32] for j in range(4)])
        if zi == 0:
            r = r - 1.5 * z_before(full[xi * 4 + 3, 24:32], lt)
        if zi == 3:
            r = r + 1.5 * z_after(full[xi * 4, 24:32], lt)
        q = 32 * zi + 5 * xi
        pay[q:q + 5] = -r[0:5]
        pay[128 + 5 * c:133 + 5 * c] = full[c, 0:5]
        pay[208 + 5 * c:213 + 5 * c] = mom[c, 32:37]
        pay[288 + 5 * c:293 + 5 * c] = full[c, 32:37]
    for zi in range(4):
        pay[32 * zi + 20:32 * zi + 25] = full[zi, 8:13]
        pay[32 * zi + 25:32 * zi + 30] = full[12 + zi, 8:13]
        pay[32 * zi + 30:32 * zi + 32] = jnp.zeros((2, 128), jnp.float32)
        pay[368 + 5 * zi:373 + 5 * zi] = up[512 + 8 * zi:517 + 8 * zi]
        pay[388 + 5 * zi:393 + 5 * zi] = down[512 + 8 * zi:517 + 8 * zi]


def residual_kernel(idx, got, force, out):
    at = pl.ds(pl.multiple_of(32 * idx[0], 32), 32)
    t = got[0, at] + got[1, at] + got[2, at] + got[3, at]
    v = t[0:20] + force[idx[0]]
    for n in range(8):
        out[n, 0:20] = v
        out[n, 20:30] = t[20:30]


def feq_kernel(idx, got, twice, delta, inflow, lt, vec, final, h2, low, s0, lo, hi, stack):
    def total(a, n):
        return got[0, a:a + n] + got[1, a:a + n] + got[2, a:a + n] + got[3, a:a + n]

    s0[...] = jnp.zeros_like(s0)
    lo[...] = jnp.zeros_like(lo)
    hi[...] = jnp.zeros_like(hi)
    for c in range(16):
        s0[c, 0:5] = total(208 + 5 * c, 5)
    for zi in range(4):
        lo[zi, 0:5] = total(368 + 5 * zi, 5)
        hi[zi, 0:5] = total(388 + 5 * zi, 5)
    low[...] = total(128, 80)
    pad = jnp.zeros((3, 128), jnp.float32)
    cy = exact_dot(s0[...].reshape(128, 128), lt[40:168])
    for c in range(16):
        z = jnp.concatenate([0.2 * total(288 + 5 * c, 5), pad], axis=0) + 0.16 * s0[c]
        six = one_sided(lambda k: s0[k], lambda zi: lo[zi], lambda zi: hi[zi], c,
                        cy[8 * c:8 * c + 8], lt)
        for n, v in enumerate([z] + six):
            stack[8 * n:8 * n + 8, 128 * c:128 * c + 128] = v
    add = lax.dot_general(stack[...], final[0], (((0,), (0,)), ((), ())), precision=HI,
                          preferred_element_type=jnp.float32)
    add = add.reshape(16, 8, 16, 128)
    pos = vec[0, 14:15]
    for c in range(16):
        xi, zi = c // 4, c % 4
        v = twice[c] + add[c] + vec[0, 10 + xi:11 + xi] * delta[zi]
        if xi in (0, 3):
            v = v + (pos if xi == 0 else 1.0 - pos) * inflow[zi]
        h2[c] = v


def apply_k(src, dst, lt, own=False, four=False):
    rows = slice(8, 16) if own else slice(0, 24)

    def pressure(k, at):
        return 2.0 * src[k, at] if four else src[k, at] + src[64 + k, at]

    def before(load):
        return load(slice(7, 15)) if own else pltpu.roll(load(rows), 1, 0)

    def after(load):
        return load(slice(9, 17)) if own else pltpu.roll(load(rows), 23, 0)

    for zi in range(4):
        u = [src[16 + j * 4 + zi, rows] for j in range(4)]
        p = [pressure(j * 4 + zi, rows) for j in range(4)]
        for xi in range(4):
            du = combine(CENTRAL[xi], u)
            dp = combine(CENTRAL[xi], p)
            if xi == 0:
                du = du - 1.5 * before(lambda at: src[28 + zi, at])
                dp = dp - 1.5 * before(lambda at: pressure(12 + zi, at))
            if xi == 3:
                du = du + 1.5 * after(lambda at: src[16 + zi, at])
                dp = dp + 1.5 * after(lambda at: pressure(zi, at))
            dst[xi * 4 + zi] = du
            dst[16 + xi * 4 + zi] = dp
    for xi in range(4):
        u = [src[48 + xi * 4 + j, rows] for j in range(4)]
        p = [pressure(xi * 4 + j, rows) for j in range(4)]
        for zi in range(4):
            du = combine(CENTRAL[zi], u)
            dp = combine(CENTRAL[zi], p)
            if zi == 0:
                du = du - 1.5 * z_before(u[3], lt)
                dp = dp - 1.5 * z_before(p[3], lt)
            if zi == 3:
                du = du + 1.5 * z_after(u[0], lt)
                dp = dp + 1.5 * z_after(p[0], lt)
            dst[xi * 4 + zi] = dst[xi * 4 + zi] + du
            dst[48 + xi * 4 + zi] = dp

    n = 8 if own else 24
    u = src[32:48, rows]
    p = 2.0 * src[0:16, rows] if four else src[0:16, rows] + src[64:80, rows]
    x = jnp.concatenate([u, p], axis=0).reshape(32 * n, 128)
    d = exact_dot(x, lt[40:168]).reshape(32, n, 128)
    dst[0:16] = dst[0:16] + d[0:16]
    dst[32:48] = d[16:32]


def two_level(r, pe, co, lt):
    parts = []
    for f in range(5):
        tz = []
        for xi in range(4):
            q = [r[f * 16 + xi * 4 + zi] for zi in range(4)]
            tz.append([combine(RT[za], q) for za in range(2)])
        for xa in range(2):
            for za in range(2):
                parts.append(combine(RT[xa], [tz[xi][za] for xi in range(4)]))
    both = jnp.concatenate([lt[168:296], lt[296:424]], axis=1)
    e = exact_dot(jnp.concatenate(parts, axis=0), both)
    for f in range(5):
        py = [[None, None], [None, None]]
        for xa in range(2):
            for za in range(2):
                n = f * 4 + xa * 2 + za
                e0, e1 = e[24 * n:24 * n + 24, 0:128], e[24 * n:24 * n + 24, 128:256]
                co[2 * n] = e0
                co[2 * n + 1] = e1
                py[za][xa] = lt[20:21] * e0 + lt[21:22] * e1
        for xi in range(4):
            v = [combine(PR[xi], py[za]) for za in range(2)]
            for zi in range(4):
                pe[f * 16 + xi * 4 + zi] = combine(PR[zi], v)


def coarse_products(co, lt):
    def at(f, xa, za, ya):
        return co[f * 8 + xa * 4 + za * 2 + ya]

    def own(q):
        return q[8:16]

    def dx(q, xa, za, ya):
        if xa == 0:
            v = q(1, za, ya)
            return 0.25 * (own(v) - own(pltpu.roll(v, 1, 0)))
        v = q(0, za, ya)
        return 0.25 * (own(pltpu.roll(v, 23, 0)) - own(v))

    def dz(q, xa, za, ya):
        v = own(q(xa, 1 - za, ya))
        if za == 0:
            return 0.25 * (v - z_before(v, lt))
        return 0.25 * (z_after(v, lt) - v)

    def dy(q, xa, za, ya):
        v = own(q(xa, za, 1 - ya))
        w = pltpu.roll(v, 64, 1)
        return 0.25 * (v - w) if ya == 0 else 0.25 * (w - v)

    total = [jnp.zeros((8, 128), jnp.float32)] * 3
    for xa in range(2):
        for za in range(2):
            for ya in range(2):
                def field(f):
                    return lambda a, b, c: at(f, a, b, c)

                def pressure(a, b, c):
                    return at(0, a, b, c) + at(4, a, b, c)
                e = [own(at(f, xa, za, ya)) for f in range(5)]
                div = (dx(field(1), xa, za, ya) + dy(field(2), xa, za, ya)
                       + dz(field(3), xa, za, ya))
                v = [div, dx(pressure, xa, za, ya), dy(pressure, xa, za, ya),
                     dz(pressure, xa, za, ya), div]
                for f in range(5):
                    total = [total[0] + e[f] * e[f], total[1] + e[f] * v[f], total[2] + v[f] * v[f]]
    return [t * lt[23:24] for t in total]


PAIRS = [(i, j) for i in range(3) for j in range(i, 3)]


def fine_products(e, s, t, ke, kt, lt, own):
    rows = slice(0, 8) if own else slice(8, 16)
    zero = jnp.zeros((8, 128), jnp.float32)
    total = [zero] * 18
    for xi in range(4):
        for zi in range(4):
            acc = [zero] * 18
            c = xi * 4 + zi
            for f in range(4):
                k = f * 16 + c
                x = [e[k, 8:16], s[k, 8:16], t[k, 8:16]]
                y = [ke[k, rows], x[2], kt[k, rows]]
                z = x
                if f == 0:
                    last = [e[64 + c, 8:16], s[64 + c, 8:16], x[2]]
                    z = [x[0] + last[0], x[1] + last[1], x[2] + x[2]]
                for n, (i, j) in enumerate(PAIRS):
                    v = x[i] * x[j]
                    if f == 0:
                        v = v + last[i] * last[j]
                    acc[n] = acc[n] + v
                    acc[6 + n] = acc[6 + n] + (z[i] * y[j] if i == j else z[i] * y[j] + z[j] * y[i])
                    v = y[i] * y[j]
                    acc[12 + n] = acc[12 + n] + (2.0 * v if f == 0 else v)
            w = WEIGHTS[xi] * WEIGHTS[zi]
            total = [a + w * b for a, b in zip(total, acc)]
    return [a * lt[22:23] for a in total]


def diagonal():
    return (lax.broadcasted_iota(jnp.int32, (24, 128), 0)
            == lax.broadcasted_iota(jnp.int32, (24, 128), 1))


def pass_words(e, s, t, ke, kt, co, gram, lt, own=False):
    two_level(e, s, co, lt)
    apply_k(s, t, lt)

    def over_k(k, _):
        e[k] = e[k] - s[k]
        return 0
    lax.fori_loop(0, 80, over_k, 0, unroll=8)
    apply_k(e, ke, lt, own)
    apply_k(t, kt, lt, own, four=True)
    products = coarse_products(co, lt) + fine_products(e, s, t, ke, kt, lt, own)
    rows = [jnp.sum(p, axis=0, keepdims=True) for p in products] + [jnp.zeros((3, 128), jnp.float32)]
    total = jnp.sum(jnp.concatenate(rows, axis=0), axis=1, keepdims=True)
    line = jnp.sum(jnp.where(diagonal(), total, 0.0), axis=0, keepdims=True)
    for n in range(gram.shape[0]):
        gram[n] = jnp.broadcast_to(line, (8, 128))


def pack_kernel(idx, mine, own, to_upper, to_lower):
    first = lax.broadcasted_iota(jnp.int32, (8, 128), 0) == 0
    last = lax.broadcasted_iota(jnp.int32, (8, 128), 0) == 7
    for f in range(5):
        low = mine[pl.ds(20 + f, 8, stride=30), :]
        high = mine[pl.ds(25 + f, 8, stride=30), :]
        for xi in range(4):
            k = f * 4 + xi
            v = mine[pl.ds(5 * xi + f, 8, stride=30), :]
            if xi == 0:
                v = v + 1.5 * jnp.where(first, 0.0, pltpu.roll(high, 1, 0))
            if xi == 3:
                v = v - 1.5 * jnp.where(last, 0.0, pltpu.roll(low, 7, 0))
            own[k] = v
            to_upper[pl.ds(k, 6, stride=20), :] = v[2:8]
            to_lower[pl.ds(k, 6, stride=20), :] = v[0:6]
        to_upper[120 + f:121 + f] = high[7:8]
        to_lower[120 + f:121 + f] = low[0:1]


def window_kernel(idx, lower, own, upper, edge_low, edge_high, after, win):
    for f in range(5):
        e = 120 + f
        for xi in range(4):
            k = f * 4 + xi
            at = 20 * k
            low, mid, high = lower[pl.ds(k, 6, stride=20), :], own[k], upper[pl.ds(k, 6, stride=20), :]
            win[at:at + 6] = low
            win[at + 6:at + 14] = mid
            win[at + 14:at + 20] = high
            if xi == 0:
                win[at + 6:at + 7] = mid[0:1] + 1.5 * lower[e:e + 1]
                win[at + 14:at + 15] = high[0:1] + 1.5 * edge_high[e:e + 1]
            if xi == 3:
                win[at + 13:at + 14] = mid[7:8] - 1.5 * upper[e:e + 1]
                win[at + 5:at + 6] = low[5:6] - 1.5 * edge_low[e:e + 1]


def first_pass_kernel(idx, quarters, lt, r, s, t, ke, kt, gram, co):
    zero = jnp.zeros((2, 128), jnp.float32)
    for f in range(5):
        for xi in range(4):
            for zi in range(4):
                k = f * 16 + xi * 4 + zi
                at = 20 * (f * 4 + xi)
                r[k, 0:2] = zero
                r[k, 2:22] = quarters[zi, at:at + 20]
                r[k, 22:24] = zero
    pass_words(r, s, t, ke, kt, co, gram, lt)


def step_sizes(sums):
    line = sums[0, 0:1]
    for n in range(1, sums.shape[0]):
        line = line + sums[n, 0:1]
    v = jnp.sum(jnp.where(diagonal(), line, 0.0), axis=1, keepdims=True)
    v = jnp.broadcast_to(v, (24, 128))
    c0, c1, c2 = v[0:1], v[1:2], v[2:3]
    den = 4.0 * c0 + 4.0 * c1 + c2 + EPS
    a1, b1 = (2.0 * c0 + c1) / den, (2.0 * c1 + c2 + EPS) / den
    d = [jnp.ones_like(a1), b1, -a1]

    def form(base, twice):
        total = None
        for n, (i, j) in enumerate(PAIRS):
            term = d[i] * d[j] * v[base + n:base + n + 1]
            if twice and i != j:
                term = 2.0 * term
            total = term if total is None else total + term
        return total
    rr, kk = jnp.maximum(form(3, True), 0.0), jnp.maximum(form(15, True), 0.0)
    bound = jnp.sqrt(rr) * jnp.sqrt(kk)
    rk = jnp.clip(form(9, False), -bound, bound)
    den = 4.0 * rr + 4.0 * rk + kk + EPS
    return a1, b1, (2.0 * rr + rk) / den, (2.0 * rk + kk + EPS) / den


def next_pass_kernel(first, idx, sums, e, s, t, ke, kt, *rest):
    if first:
        lt, r2, s2, t2, ke2, kt2, acc2, gram, co = rest
    else:
        acc, lt, r2, s2, t2, ke2, kt2, acc2, gram, co = rest
    a1, b1, a2, b2 = step_sizes(sums)

    def put(k, tk, kr):
        sk = s[k]
        r1 = e[k] + b1 * sk - a1 * tk
        v = a1 * sk[8:16] + a2 * r1[8:16]
        acc2[k] = v if first else acc[k] + v
        r2[k] = b2 * r1 - a2 * kr

    def over_k(k, _):
        tk = t[k]
        kr = ke[k] + b1 * tk - a1 * kt[k]
        put(k, tk, kr)
        put(64 + k, tk, kr)
        return 0
    lax.fori_loop(0, 16, over_k, 0, unroll=4)

    def rest_k(k, _):
        tk = t[k]
        put(k, tk, ke[k] + b1 * tk - a1 * kt[k])
        return 0
    lax.fori_loop(16, 64, rest_k, 0, unroll=8)
    pass_words(r2, s2, t2, ke2, kt2, co, gram, lt, own=not first)


def third_pass_kernel(idx, sums, e, s, t, ke, kt, acc, lt, eo, so, to, acc2, gram,
                      r2, s2, t2, ke2, kt2, co):
    next_pass_kernel(False, idx, sums, e, s, t, ke, kt, acc, lt, r2, s2, t2, ke2, kt2, acc2, gram, co)
    eo[...] = r2[:, 8:16]
    so[...] = s2[:, 8:16]
    to[...] = t2[:, 8:16]


def last_kernel(idx, sums, e, s, t, acc, low, h2, select, split, out, fields, change, stack, rows):
    a1, b1, a2, _ = step_sizes(sums)

    def over_k(k, _):
        r1 = e[k] + b1 * s[k] - a1 * t[k % 64]
        change[pl.ds(pl.multiple_of(k * 8, 8), 8)] = acc[k] + a1 * s[k] + a2 * r1
        return 0
    lax.fori_loop(0, 80, over_k, 0, unroll=16)
    z = idx[1]
    stack[...] = jnp.zeros_like(stack)
    here = row_of_y()
    for c in range(16):
        for f in range(5):
            k = f * 16 + c
            d = change[pl.ds(k * 8 + z, 1)]
            stack[f:f + 1, 128 * c:128 * c + 128] = d
            n = 8 * (k // 4)
            rows[n:n + 8, 128 * (c % 4):128 * (c % 4) + 128] = (low[5 * c + f:5 * c + f + 1] + d) * here
    fields[...] = project(rows[...], select[...]).reshape(5, 4, 8, 64)
    whole = stack[...]
    d1 = whole.astype(jnp.bfloat16).astype(jnp.float32)
    d2 = (whole - d1).astype(jnp.bfloat16).astype(jnp.float32)
    d3 = whole - d1 - d2
    parts = jnp.concatenate([d1, d1, d2, d1, d2, d3], axis=0).astype(jnp.bfloat16)
    add = lax.dot_general(parts, split[0].astype(jnp.bfloat16), (((0,), (0,)), ((), ())),
                          preferred_element_type=jnp.float32).reshape(16, 8, 16, 128)
    for c in range(16):
        xi, zi = c // 4, c % 4
        v = h2[c] + add[c]
        for y in range(8):
            out[xi, y, pl.ds(zi, 16, stride=4), :] = v[y]


def on_device(distribution, forcing):
    import functools
    tables = {k: jnp.asarray(v) for k, v in constant_tables().items()}
    spaces = lax.axis_size("space")
    blocks = spaces // 8
    idx = jnp.stack([lax.axis_index("vel"), lax.axis_index("space") % 8]).astype(jnp.int32)
    vec, lt = tables["vec"], tables["lanes"]
    wide = (16, 8, 16, 128)
    layer = (4, 8, 16, 128)

    def shifted(x, by):
        return lax.ppermute(x, "space", [(i, (i + by) % spaces) for i in range(spaces)])

    up, down = call(rim_kernel, "rims", idx, [distribution], [],
                    [(544, 128)] * 2, [layer, layer, (8, 8, 16, 128), (1024, 8), (1, 32, 128)])
    up, down = shifted(up, 1), shifted(down, -1)
    twice, moma, force = call(local_kernel, "local", idx, [distribution, forcing, tables["select"]],
                              [vec, tables["tab0"], tables["tab1"], tables["tab2"]],
                              [wide, (16, 48, 128), (4, 20, 128)], [wide, wide, (2048, 48)])
    pay, delta, inflow = call(moment_kernel, "moments", idx, [up, down, moma, tables["mix"], lt],
                              [vec, tables["tabd"], tables["tabs"]], [(408, 128), layer, layer],
                              [layer, (16, 48, 128), (16, 40, 128), (64, 2048)])
    got = lax.all_gather(pay, "vel")
    (res,) = call(residual_kernel, "residual", idx, [got, force], [], [(8, 30, 128)])
    near = [[a * 8 + b for b in range(8)] for a in range(blocks)]
    far = [[a * 8 + b for a in range(blocks)] for b in range(8)]
    mine = lax.all_to_all(res, "space", 0, 0, axis_index_groups=near, tiled=True).reshape(240, 128)
    own_r, to_upper, to_lower = call(pack_kernel, "pack", idx, [mine], [],
                                     [(20, 8, 128), (125, 128), (125, 128)])
    lower, upper = shifted(to_upper, 8), shifted(to_lower, -8)
    h2, low = call(feq_kernel, "feq", idx, [got, twice, delta, inflow, lt],
                   [vec, tables["final"]],
                   [wide, (80, 128)], [(16, 8, 128), (4, 8, 128), (4, 8, 128), (56, 2048)])
    (quarter,) = call(window_kernel, "window", idx, [lower, own_r, upper, to_lower, to_upper, low], [],
                      [(400, 128)])
    quarters = lax.all_gather(quarter, "vel")

    def summed(gram):
        return lax.all_to_all(gram, "space", 0, 0, axis_index_groups=far, tiled=True)

    win, own, part = (80, 24, 128), (80, 8, 128), (blocks, 8, 128)
    four, own4 = (64, 24, 128), (64, 8, 128)
    co = (40, 24, 128)
    e, s, t, ke, kt, gram = call(first_pass_kernel, "pass1", idx, [quarters, lt], [],
                                  [win, win, four, four, four, part], [co])
    e, s, t, ke, kt, acc, gram = call(functools.partial(next_pass_kernel, True), "pass2", idx,
                                       [summed(gram), e, s, t, ke, kt, lt], [],
                                       [win, win, four, four, four, own, part], [co])
    e, s, t, acc, gram = call(third_pass_kernel, "pass3", idx,
                               [summed(gram), e, s, t, ke, kt, acc, lt], [],
                               [own, own, own4, own, part], [win, win, four, own4, own4, co])
    out, fields = call(last_kernel, "last", idx,
                       [summed(gram), e, s, t, acc, low, h2, tables["select"]], [tables["split"]],
                       [(4, 8, 64, 128), (5, 4, 8, 64)], [(640, 128), (8, 2048), (160, 512)])
    return out, fields


def solution(mesh):
    return jax.shard_map(
        on_device,
        mesh=mesh,
        in_specs=(P("space", None, None, "vel"), P(None, "space", None, None)),
        out_specs=(P("space", None, None, "vel"), P(None, "space", None, None)),
        check_vma=False,
    )
```

```python
import math

import jax
import jax.numpy as jnp
import numpy as np
from jax import lax
from jax.experimental import pallas as pl
from jax.experimental.pallas import tpu as pltpu
from jax.sharding import PartitionSpec as P

INTERPRET = False
DT = 0.02
RF = 0.4472135954999579
POINTS = [-1.0, -RF, RF, 1.0]
WEIGHTS = [1.0 / 6.0, 5.0 / 6.0, 5.0 / 6.0, 1.0 / 6.0]
EPS = 1e-6
HI = lax.Precision.HIGHEST


def lagrange_table(points):
    n = len(points)
    bary = []
    for i in range(n):
        product = 1.0
        for j in range(n):
            if j != i:
                product *= points[i] - points[j]
        bary.append(1.0 / product)
    rows = [[0.0] * n for _ in range(n)]
    for i in range(n):
        for j in range(n):
            if j != i:
                rows[i][j] = bary[j] / bary[i] / (points[i] - points[j])
        rows[i][i] = -sum(rows[i])
    return rows


D4 = lagrange_table(POINTS)
for _i in (1, 2):
    D4[_i][_i] = 0.0
PR = [[(1.0 - x) / 2.0, (1.0 + x) / 2.0] for x in POINTS]
RT = [[WEIGHTS[i] * PR[i][a] for i in range(4)] for a in range(2)]


def constant_tables():
    k = np.arange(512)
    b, j = k // 128, k % 128
    s = j // 64
    m = ((b * 64 + j % 64) * 5179 + 7) % 16384
    xi = np.stack([16 * s + m // 1024, (m // 32) % 32, m % 32]).astype(np.float64)
    xi = -4.0 + 0.25 * (xi + 0.5)
    sq = (xi * xi).sum(0)
    e = math.pi ** (-1.5) * np.exp(-sq)
    x, y, z = xi
    phi = np.stack(
        [np.ones(512), x, y, z, 2 * sq / 3 - 1, 2 * (x * x - sq / 3), 2 * (y * y - sq / 3),
         2 * x * y, 2 * x * z, 2 * y * z, x * (sq - 2.5), y * (sq - 2.5), z * (sq - 2.5)]
    )
    p = phi[0] + phi[4]
    zero = np.zeros(512)

    def eight(rows):
        return np.stack(list(rows) + [zero] * (8 - len(rows)))

    low = eight(phi[:5])
    along_x = eight([phi[1], p + phi[5], phi[7], phi[8], phi[1] + phi[10]])
    along_y = eight([phi[2], phi[7], p + phi[6], phi[9], phi[2] + phi[11]])
    along_z = eight([phi[3], phi[8], phi[9], p - phi[5] - phi[6], phi[3] + phi[12]])
    rows32 = np.concatenate([low, along_x, along_y, along_z])
    ec = eight([e, 2 * x * e, 2 * y * e, 2 * z * e, e * (sq - 1.5)])
    pos, neg = np.maximum(xi, 0.0), np.minimum(xi, 0.0)

    def per_rank(rows):
        return np.stack([rows[:, r * 128:(r + 1) * 128] for r in range(4)]).astype(np.float32)

    ispos = (x > 0).astype(np.float64)
    ax = np.abs(x)
    d4 = np.array(D4)
    vec = [-DT * 0.5 * x, -DT * 0.5 * y, -DT * 0.5 * z,
           -3 * DT * pos[1], -3 * DT * neg[1], -3 * DT * pos[2], -3 * DT * neg[2],
           -3 * DT * pos[0], 3 * DT * neg[0], 3 * DT * ax]
    for i in range(4):
        kap = -DT * 0.5 * x * np.where(ispos > 0, d4[i][0], d4[i][3])
        if i == 0:
            kap = kap + ispos * (0.8 - 3 * DT * ax)
        if i == 3:
            kap = kap + (1 - ispos) * (0.8 - 3 * DT * ax)
        vec.append(kap)
    kappa = vec[10:14]
    vec.append(ispos)
    for jj in range(4):
        vec.append(-DT * 0.5 * x * np.where(ispos > 0, d4[3][jj], d4[0][jj]))
    while len(vec) < 24:
        vec.append(zero)
    vec = per_rank(np.concatenate([np.stack(vec), low]))

    def moment_rows(start, rows, height):
        out = np.zeros((height, 512))
        out[start:start + len(rows)] = rows
        return per_rank(out)

    tab2 = moment_rows(0, rows32, 48)
    tab1 = moment_rows(40, low, 48)
    tab0 = moment_rows(32, low, 48)
    tabd = per_rank(np.concatenate([v * rows32 for v in kappa] + [ispos * low, (1 - ispos) * low]))
    tabs = per_rank(np.concatenate([ispos * rows32, (1 - ispos) * rows32]))
    select = np.zeros((64, 512))
    for n in range(4):
        for la in range(128):
            select[4 * (la % 16) + n, 128 * n + la] = 1.0
    import ml_dtypes
    pieces, left = [], per_rank(ec)
    for _ in range(3):
        pieces.append(left.astype(ml_dtypes.bfloat16))
        left = left - pieces[-1].astype(np.float32)
    split = np.concatenate([pieces[n].astype(np.float32) for n in (0, 1, 0, 2, 1, 0)], axis=1)
    g = rows32 @ ec.T
    g5 = g[:8]
    mix = np.zeros((40, 64))
    mix[:32, 0:8] = 0.16 * g + 0.04 * g @ g5
    mix[:32, 8:16] = 0.2 * g
    mix[32:, 0:8] = 0.2 * g5
    mix[32:, 8:16] = np.eye(8)
    final = [ec]
    for d in range(3):
        for i, part in enumerate((pos[d], neg[d])):
            c0 = 16 + 16 * d + 8 * i
            mix[:32, c0:c0 + 8] = -0.2 * DT * (rows32 * part) @ ec.T
            final.append(-0.2 * DT * ec * part)
    final = per_rank(np.concatenate(final))
    lane = np.arange(128)
    yi, ze = (lane // 16) % 4, lane % 16
    rows = []
    shifts = (-3, -2, -1, 1, 2, 3)

    def entry(table, sft):
        return np.array([table(i, i + sft) if 0 <= i + sft < 4 else 0.0 for i in yi])

    for sft in shifts:
        c = entry(lambda i, q: 0.5 * D4[i][q], sft)
        if sft == -1:
            c = c - 1.5 * (yi == 0)
        if sft == 1:
            c = c + 1.5 * (yi == 3)
        rows.append(c)
    for a in range(2):
        for sft in range(-3, 4):
            rows.append(entry(lambda i, q: RT[a][q], sft))
    rows += [np.array([PR[i][0] for i in yi]), np.array([PR[i][1] for i in yi])]
    rows += [np.array([WEIGHTS[i] for i in yi]), (yi == 0) * 1.0, (ze == 0) * 1.0, (ze == 15) * 1.0]
    for sft in shifts:
        rows.append(entry(lambda i, q: 0.5 * D4[i][q], sft))
    rows += [entry(lambda i, q: 0.5 * D4[i][q], 0), 3.0 * (yi == 0), 3.0 * (yi == 3)]
    while len(rows) < 40:
        rows.append(np.zeros(128))
    mats = np.zeros((3, 128, 128))
    for n, sft in enumerate(shifts):
        mats[0, (lane + 16 * sft) % 128, lane] += rows[n]
    for a in range(2):
        for sft in range(-3, 4):
            mats[1 + a, (lane + 16 * sft) % 128, lane] += rows[6 + 7 * a + sft + 3]
    lanes = np.concatenate([np.stack(rows), mats.reshape(384, 128)]).astype(np.float32)
    return dict(vec=vec, tab2=tab2, tab1=tab1, tab0=tab0, mix=mix.astype(np.float32),
                final=final, lanes=lanes, split=split, tabd=tabd, tabs=tabs, select=select.astype(np.float32))


def call(kernel, name, idx, full, ranked, outs, scratch=(), limit=24):
    n = len(full)

    def body(idx, *refs):
        rank = [r.at[pl.ds(idx[0], 1)] for r in refs[n:n + len(ranked)]]
        kernel(idx, *refs[:n], *rank, *refs[n + len(ranked):])

    vmem = pl.BlockSpec(memory_space=pltpu.VMEM)
    return pl.pallas_call(
        body,
        name=name,
        out_shape=[jax.ShapeDtypeStruct(s, jnp.float32) for s in outs],
        in_specs=[pl.BlockSpec(memory_space=pltpu.SMEM)] + [vmem] * (n + len(ranked)),
        out_specs=[vmem] * len(outs),
        scratch_shapes=[pltpu.VMEM(s, jnp.float32) for s in scratch],
        compiler_params=pltpu.CompilerParams(vmem_limit_bytes=limit << 20),
        interpret=INTERPRET,
    )(idx, *full, *ranked)


def exact_dot(a, b):
    return jnp.dot(a, b, precision=HI, preferred_element_type=jnp.float32)


def project(x, rows):
    return lax.dot_general(x, rows, (((1,), (1,)), ((), ())), precision=HI,
                           preferred_element_type=jnp.float32)


def combine(row, values):
    total = None
    for c, v in zip(row, values):
        if c != 0.0:
            total = c * v if total is None else total + c * v
    return total


def layer_yz(src, dst, vec):
    def over_y(y, _):
        q = [src[zi, y] for zi in range(4)]
        for zi in range(4):
            v = vec[0, 2:3] * combine(D4[zi], q)
            if zi == 0:
                v = v + vec[0, 5:6] * (q[0] - pltpu.roll(q[3], 1, 0))
            if zi == 3:
                v = v + vec[0, 6:7] * (pltpu.roll(q[0], 15, 0) - q[3])
            dst[zi, y] = v
        return 0
    lax.fori_loop(0, 8, over_y, 0, unroll=True)

    def over_z(zi, _):
        q = [src[zi, y] for y in range(8)]
        for y in range(8):
            e, yi = 4 * (y // 4), y % 4
            v = vec[0, 1:2] * combine(D4[yi], q[e:e + 4])
            if yi == 0:
                v = v + vec[0, 3:4] * (q[y] - q[(y + 7) % 8])
            if yi == 3:
                v = v + vec[0, 4:5] * (q[(y + 1) % 8] - q[y])
            dst[zi, y] = dst[zi, y] + v
        return 0
    lax.fori_loop(0, 4, over_z, 0, unroll=True)


def every_fourth(h, xi, y, zi):
    if INTERPRET:
        return h[xi, y][zi::4]
    return h[xi, y, pl.ds(zi, 16, stride=4), :]


def speed_rows(idx, vec):
    j = lax.broadcasted_iota(jnp.int32, (1, 128), 1)
    m = ((idx[0] * 64 + (j & 63)) * 5179 + 7) & 16383
    s = j >> 6
    x, y, z = [-4.0 + 0.25 * (n.astype(jnp.float32) + 0.5)
               for n in (16 * s + (m >> 10), (m >> 5) & 31, m & 31)]
    pos = s > 0
    rows = {0: -DT * 0.5 * x, 1: -DT * 0.5 * y, 2: -DT * 0.5 * z,
            3: -3 * DT * jnp.maximum(y, 0.0), 4: -3 * DT * jnp.minimum(y, 0.0),
            5: -3 * DT * jnp.maximum(z, 0.0), 6: -3 * DT * jnp.minimum(z, 0.0),
            14: pos.astype(jnp.float32)}
    for n in range(4):
        rows[15 + n] = -DT * 0.5 * x * jnp.where(pos, D4[3][n], D4[0][n])
    rows[24], rows[25], rows[26], rows[27] = jnp.ones_like(x), x, y, z
    rows[28] = 2.0 * (x * x + y * y + z * z) / 3.0 - 1.0
    vec[...] = jnp.zeros_like(vec)
    for n, v in rows.items():
        vec[0, n:n + 1] = v


def rim_kernel(idx, h, up, down, q, t, ends, m, vec):
    speed_rows(idx, vec)
    transport_rims(idx, h, vec, up, down, q, t, ends, m)


def transport_rims(idx, h, vec, up, down, q, t, ends, m):
    pos = vec[0, 14:15] > 0.5
    for zi in range(4):
        def over_y(y, _):
            x = [every_fourth(h, xi, y, zi) for xi in range(4)]
            ql = jnp.where(pos, x[3], x[0])
            q[zi, y] = ql
            ends[zi, y] = x[0]
            ends[4 + zi, y] = x[3]
            v = 0.8 * ql
            for j in range(4):
                v = v + vec[0, 15 + j:16 + j] * x[j]
            up[pl.ds(pl.multiple_of((zi * 8 + y) * 16, 16), 16)] = v
            return 0
        lax.fori_loop(0, 8, over_y, 0, unroll=True)
    layer_yz(q, t, vec)
    right = lax.broadcasted_iota(jnp.int32, (16, 128), 1) >= 64

    def pack(n, _):
        zi, y = n // 8, n % 8
        at = pl.ds(pl.multiple_of(n * 16, 16), 16)
        tl = pltpu.roll(t[zi, y] + up[at], 64, 1)
        ql = q[zi, y]
        up[at] = jnp.where(right, ql, tl)
        down[at] = jnp.where(right, tl, ql)
        return 0
    lax.fori_loop(0, 32, pack, 0, unroll=8)
    m[...] = project(ends[...].reshape(1024, 128), vec[0, 24:32])
    for n in range(8):
        zi, out = n % 4, (down, up)[n // 4]
        out[512 + 8 * zi:520 + 8 * zi] = m[128 * n:128 * n + 128].T


def local_update(src, dst, vec):
    def over_y(y, _):
        q = [src[c, y] for c in range(16)]
        for xi in range(4):
            for zi in range(4):
                own = q[xi * 4 + zi]
                v = 0.8 * own + vec[0, 0:1] * combine(D4[xi], [q[j * 4 + zi] for j in range(4)])
                v = v + vec[0, 2:3] * combine(D4[zi], q[xi * 4:xi * 4 + 4])
                if zi == 0:
                    v = v + vec[0, 5:6] * (own - pltpu.roll(q[xi * 4 + 3], 1, 0))
                if zi == 3:
                    v = v + vec[0, 6:7] * (pltpu.roll(q[xi * 4], 15, 0) - own)
                if xi == 0:
                    v = v + vec[0, 7:8] * own
                if xi == 3:
                    v = v + vec[0, 8:9] * own
                dst[xi * 4 + zi, y] = v
        return 0
    lax.fori_loop(0, 8, over_y, 0, unroll=2)

    def over_c(c, _):
        q = [src[c, y] for y in range(8)]
        for y in range(8):
            e, yi = 4 * (y // 4), y % 4
            v = vec[0, 1:2] * combine(D4[yi], q[e:e + 4])
            if yi == 0:
                v = v + vec[0, 3:4] * (q[y] - q[(y + 7) % 8])
            if yi == 3:
                v = v + vec[0, 4:5] * (q[(y + 1) % 8] - q[y])
            dst[c, y] = dst[c, y] + v
        return 0
    lax.fori_loop(0, 16, over_c, 0, unroll=4)


def row_of_y():
    y = lax.broadcasted_iota(jnp.int32, (8, 128), 0)
    return (lax.broadcasted_iota(jnp.int32, (8, 128), 1) // 16 == y).astype(jnp.float32)


def local_kernel(idx, h, forcing, select, vec, tab0, tab1, tab2, twice, mom, force, first, once, m):
    spread = exact_dot(forcing[...].reshape(96, 64), select[...])
    here = row_of_y()
    force[...] = jnp.zeros_like(force)
    for f in range(3):
        for c in range(16):
            n = 8 * (f * 4 + c // 4)
            v = spread[n:n + 8, 128 * (c % 4):128 * (c % 4) + 128] * here
            at = 5 * (c // 4) + f + 1
            force[c % 4, at:at + 1] = jnp.sum(v, axis=0, keepdims=True)
    for c in range(16):
        xi, zi = c // 4, c % 4

        def over_y(y, _):
            first[c, y] = every_fourth(h, xi, y, zi)
            return 0
        lax.fori_loop(0, 8, over_y, 0, unroll=True)
    local_update(first, once, vec)
    local_update(once, twice, vec)

    m[...] = project(first[...].reshape(2048, 128), tab0[0])
    m[...] = m[...] + project(once[...].reshape(2048, 128), tab1[0])
    m[...] = m[...] + project(twice[...].reshape(2048, 128), tab2[0])
    for c in range(16):
        mom[c] = m[128 * c:128 * c + 128].T


def z_before(q, lt):
    return jnp.where(lt[24:25] > 0.5, pltpu.roll(q, 113, 1), pltpu.roll(q, 1, 1))


def z_after(q, lt):
    return jnp.where(lt[25:26] > 0.5, pltpu.roll(q, 15, 1), pltpu.roll(q, 127, 1))


SHIFTS = (-3, -2, -1, 1, 2, 3)


def central_y(q, lt):
    total = None
    for n, s in enumerate(SHIFTS):
        term = lt[n:n + 1] * pltpu.roll(q, (-16 * s) % 128, 1)
        total = term if total is None else total + term
    return total


def one_sided(load, low, high, c, cy, lt):
    xi, zi = c // 4, c % 4
    q = load(c)
    cx = combine([0.5 * v for v in D4[xi]], [load(j * 4 + zi) for j in range(4)])
    px = cx + 3.0 * (q - low(zi)) if xi == 0 else cx
    mx = cx + 3.0 * (high(zi) - q) if xi == 3 else cx
    w = 0.5 * (lt[33:34] * (q - pltpu.roll(q, 16, 1)) - lt[34:35] * (pltpu.roll(q, 112, 1) - q))
    cz = combine([0.5 * v for v in D4[zi]], [load(xi * 4 + j) for j in range(4)])
    pz = cz + 3.0 * (q - z_before(load(xi * 4 + 3), lt)) if zi == 0 else cz
    mz = cz + 3.0 * (z_after(load(xi * 4), lt) - q) if zi == 3 else cz
    return [px, mx, cy + w, cy - w, pz, mz]


CENTRAL = [[0.0 if i == j else 0.5 * D4[i][j] for j in range(4)] for i in range(4)]


def moment_kernel(idx, up, down, moma, mix, lt, vec, tabd, tabs, pay, delta, inflow,
                  yz, mom, full, stack):
    right = lax.broadcasted_iota(jnp.int32, (16, 128), 1) >= 64

    def unpack(n, _):
        at = pl.ds(pl.multiple_of(n * 16, 16), 16)
        u, d = up[at], down[at]
        zi, y = n // 8, n % 8
        delta[zi, y] = vec[0, 9:10] * jnp.where(right, u, d)
        inflow[zi, y] = vec[0, 9:10] * pltpu.roll(jnp.where(right, d, u), 64, 1)
        return 0
    lax.fori_loop(0, 32, unpack, 0, unroll=8)
    layer_yz(delta, yz, vec)
    inflow[...] = inflow[...] + yz[...]
    md = project(delta[...].reshape(512, 128), tabd[0])
    ms = project(inflow[...].reshape(512, 128), tabs[0])
    for zi in range(4):
        at = slice(128 * zi, 128 * zi + 128)
        t, u, v = md[at, 0:128].T, md[at, 128:144].T, ms[at].T
        for xi in range(4):
            c = xi * 4 + zi
            q = moma[c, 0:32] + t[32 * xi:32 * xi + 32]
            once = moma[c, 40:48]
            if xi == 0:
                q, once = q + v[0:32], once + u[0:8]
            if xi == 3:
                q, once = q + v[32:64], once + u[8:16]
            mom[c, 0:32] = q
            mom[c, 32:40] = moma[c, 32:40]
            mom[c, 40:48] = once

    def load0(c):
        return mom[c, 32:40]

    for c in range(16):
        six = one_sided(load0, lambda zi: up[512 + 8 * zi:520 + 8 * zi],
                        lambda zi: down[512 + 8 * zi:520 + 8 * zi], c,
                        central_y(mom[c, 32:40], lt), lt)
        at = slice(128 * c, 128 * c + 128)
        stack[0:16, at] = mom[c, 32:48]
        for n in range(6):
            stack[16 + 8 * n:24 + 8 * n, at] = six[n]
    add = exact_dot(mix[...], stack[...])
    for c in range(16):
        at = slice(128 * c, 128 * c + 128)
        full[c, 0:32] = mom[c, 0:32] + add[0:32, at]
        full[c, 32:40] = add[32:40, at]
    for c in range(16):
        xi, zi = c // 4, c % 4
        r = combine(CENTRAL[xi], [full[j * 4 + zi, 8:16] for j in range(4)])
        r = r + central_y(full[c, 16:24], lt)
        r = r + combine(CENTRAL[zi], [full[xi * 4 + j, 24:32] for j in range(4)])
        if zi == 0:
            r = r - 1.5 * z_before(full[xi * 4 + 3, 24:32], lt)
        if zi == 3:
            r = r + 1.5 * z_after(full[xi * 4, 24:32], lt)
        q = 32 * zi + 5 * xi
        pay[q:q + 5] = -r[0:5]
        pay[128 + 5 * c:133 + 5 * c] = full[c, 0:5]
        pay[208 + 5 * c:213 + 5 * c] = mom[c, 32:37]
        pay[288 + 5 * c:293 + 5 * c] = full[c, 32:37]
    for zi in range(4):
        pay[32 * zi + 20:32 * zi + 25] = full[zi, 8:13]
        pay[32 * zi + 25:32 * zi + 30] = full[12 + zi, 8:13]
        pay[32 * zi + 30:32 * zi + 32] = jnp.zeros((2, 128), jnp.float32)
        pay[368 + 5 * zi:373 + 5 * zi] = up[512 + 8 * zi:517 + 8 * zi]
        pay[388 + 5 * zi:393 + 5 * zi] = down[512 + 8 * zi:517 + 8 * zi]


def residual_kernel(idx, got, force, out):
    at = pl.ds(pl.multiple_of(32 * idx[0], 32), 32)
    t = got[0, at] + got[1, at] + got[2, at] + got[3, at]
    v = t[0:20] + force[idx[0]]
    for n in range(8):
        out[n, 0:20] = v
        out[n, 20:30] = t[20:30]


def feq_kernel(idx, got, twice, delta, inflow, lt, vec, final, h2, low, s0, lo, hi, stack):
    def total(a, n):
        return got[0, a:a + n] + got[1, a:a + n] + got[2, a:a + n] + got[3, a:a + n]

    s0[...] = jnp.zeros_like(s0)
    lo[...] = jnp.zeros_like(lo)
    hi[...] = jnp.zeros_like(hi)
    for c in range(16):
        s0[c, 0:5] = total(208 + 5 * c, 5)
    for zi in range(4):
        lo[zi, 0:5] = total(368 + 5 * zi, 5)
        hi[zi, 0:5] = total(388 + 5 * zi, 5)
    low[...] = total(128, 80)
    pad = jnp.zeros((3, 128), jnp.float32)
    cy = exact_dot(s0[...].reshape(128, 128), lt[40:168])
    for c in range(16):
        z = jnp.concatenate([0.2 * total(288 + 5 * c, 5), pad], axis=0) + 0.16 * s0[c]
        six = one_sided(lambda k: s0[k], lambda zi: lo[zi], lambda zi: hi[zi], c,
                        cy[8 * c:8 * c + 8], lt)
        for n, v in enumerate([z] + six):
            stack[8 * n:8 * n + 8, 128 * c:128 * c + 128] = v
    add = lax.dot_general(stack[...], final[0], (((0,), (0,)), ((), ())), precision=HI,
                          preferred_element_type=jnp.float32)
    add = add.reshape(16, 8, 16, 128)
    pos = vec[0, 14:15]
    for c in range(16):
        xi, zi = c // 4, c % 4
        v = twice[c] + add[c] + vec[0, 10 + xi:11 + xi] * delta[zi]
        if xi in (0, 3):
            v = v + (pos if xi == 0 else 1.0 - pos) * inflow[zi]
        h2[c] = v


def apply_k(src, dst, lt, own=False, four=False):
    rows = slice(8, 16) if own else slice(0, 24)

    def pressure(k, at):
        return 2.0 * src[k, at] if four else src[k, at] + src[64 + k, at]

    def before(load):
        return load(slice(7, 15)) if own else pltpu.roll(load(rows), 1, 0)

    def after(load):
        return load(slice(9, 17)) if own else pltpu.roll(load(rows), 23, 0)

    for zi in range(4):
        u = [src[16 + j * 4 + zi, rows] for j in range(4)]
        p = [pressure(j * 4 + zi, rows) for j in range(4)]
        for xi in range(4):
            du = combine(CENTRAL[xi], u)
            dp = combine(CENTRAL[xi], p)
            if xi == 0:
                du = du - 1.5 * before(lambda at: src[28 + zi, at])
                dp = dp - 1.5 * before(lambda at: pressure(12 + zi, at))
            if xi == 3:
                du = du + 1.5 * after(lambda at: src[16 + zi, at])
                dp = dp + 1.5 * after(lambda at: pressure(zi, at))
            dst[xi * 4 + zi] = du
            dst[16 + xi * 4 + zi] = dp
    for xi in range(4):
        u = [src[48 + xi * 4 + j, rows] for j in range(4)]
        p = [pressure(xi * 4 + j, rows) for j in range(4)]
        for zi in range(4):
            du = combine(CENTRAL[zi], u)
            dp = combine(CENTRAL[zi], p)
            if zi == 0:
                du = du - 1.5 * z_before(u[3], lt)
                dp = dp - 1.5 * z_before(p[3], lt)
            if zi == 3:
                du = du + 1.5 * z_after(u[0], lt)
                dp = dp + 1.5 * z_after(p[0], lt)
            dst[xi * 4 + zi] = dst[xi * 4 + zi] + du
            dst[48 + xi * 4 + zi] = dp

    n = 8 if own else 24
    u = src[32:48, rows]
    p = 2.0 * src[0:16, rows] if four else src[0:16, rows] + src[64:80, rows]
    x = jnp.concatenate([u, p], axis=0).reshape(32 * n, 128)
    d = exact_dot(x, lt[40:168]).reshape(32, n, 128)
    dst[0:16] = dst[0:16] + d[0:16]
    dst[32:48] = d[16:32]


def two_level(r, pe, co, lt):
    parts = []
    for f in range(5):
        tz = []
        for xi in range(4):
            q = [r[f * 16 + xi * 4 + zi] for zi in range(4)]
            tz.append([combine(RT[za], q) for za in range(2)])
        for xa in range(2):
            for za in range(2):
                parts.append(combine(RT[xa], [tz[xi][za] for xi in range(4)]))
    both = jnp.concatenate([lt[168:296], lt[296:424]], axis=1)
    e = exact_dot(jnp.concatenate(parts, axis=0), both)
    for f in range(5):
        py = [[None, None], [None, None]]
        for xa in range(2):
            for za in range(2):
                n = f * 4 + xa * 2 + za
                e0, e1 = e[24 * n:24 * n + 24, 0:128], e[24 * n:24 * n + 24, 128:256]
                co[2 * n] = e0
                co[2 * n + 1] = e1
                py[za][xa] = lt[20:21] * e0 + lt[21:22] * e1
        for xi in range(4):
            v = [combine(PR[xi], py[za]) for za in range(2)]
            for zi in range(4):
                pe[f * 16 + xi * 4 + zi] = combine(PR[zi], v)


def coarse_products(co, lt):
    def at(f, xa, za, ya):
        return co[f * 8 + xa * 4 + za * 2 + ya]

    def own(q):
        return q[8:16]

    def dx(q, xa, za, ya):
        if xa == 0:
            v = q(1, za, ya)
            return 0.25 * (own(v) - own(pltpu.roll(v, 1, 0)))
        v = q(0, za, ya)
        return 0.25 * (own(pltpu.roll(v, 23, 0)) - own(v))

    def dz(q, xa, za, ya):
        v = own(q(xa, 1 - za, ya))
        if za == 0:
            return 0.25 * (v - z_before(v, lt))
        return 0.25 * (z_after(v, lt) - v)

    def dy(q, xa, za, ya):
        v = own(q(xa, za, 1 - ya))
        w = pltpu.roll(v, 64, 1)
        return 0.25 * (v - w) if ya == 0 else 0.25 * (w - v)

    total = [jnp.zeros((8, 128), jnp.float32)] * 3
    for xa in range(2):
        for za in range(2):
            for ya in range(2):
                def field(f):
                    return lambda a, b, c: at(f, a, b, c)

                def pressure(a, b, c):
                    return at(0, a, b, c) + at(4, a, b, c)
                e = [own(at(f, xa, za, ya)) for f in range(5)]
                div = (dx(field(1), xa, za, ya) + dy(field(2), xa, za, ya)
                       + dz(field(3), xa, za, ya))
                v = [div, dx(pressure, xa, za, ya), dy(pressure, xa, za, ya),
                     dz(pressure, xa, za, ya), div]
                for f in range(5):
                    total = [total[0] + e[f] * e[f], total[1] + e[f] * v[f], total[2] + v[f] * v[f]]
    return [t * lt[23:24] for t in total]


PAIRS = [(i, j) for i in range(3) for j in range(i, 3)]


def fine_products(e, s, t, ke, kt, lt, own):
    rows = slice(0, 8) if own else slice(8, 16)
    zero = jnp.zeros((8, 128), jnp.float32)
    total = [zero] * 18
    for xi in range(4):
        for zi in range(4):
            acc = [zero] * 18
            c = xi * 4 + zi
            for f in range(4):
                k = f * 16 + c
                x = [e[k, 8:16], s[k, 8:16], t[k, 8:16]]
                y = [ke[k, rows], x[2], kt[k, rows]]
                z = x
                if f == 0:
                    last = [e[64 + c, 8:16], s[64 + c, 8:16], x[2]]
                    z = [x[0] + last[0], x[1] + last[1], x[2] + x[2]]
                for n, (i, j) in enumerate(PAIRS):
                    v = x[i] * x[j]
                    if f == 0:
                        v = v + last[i] * last[j]
                    acc[n] = acc[n] + v
                    acc[6 + n] = acc[6 + n] + (z[i] * y[j] if i == j else z[i] * y[j] + z[j] * y[i])
                    v = y[i] * y[j]
                    acc[12 + n] = acc[12 + n] + (2.0 * v if f == 0 else v)
            w = WEIGHTS[xi] * WEIGHTS[zi]
            total = [a + w * b for a, b in zip(total, acc)]
    return [a * lt[22:23] for a in total]


def diagonal():
    return (lax.broadcasted_iota(jnp.int32, (24, 128), 0)
            == lax.broadcasted_iota(jnp.int32, (24, 128), 1))


def pass_words(e, s, t, ke, kt, co, gram, lt, own=False):
    two_level(e, s, co, lt)
    apply_k(s, t, lt)

    def over_k(k, _):
        e[k] = e[k] - s[k]
        return 0
    lax.fori_loop(0, 80, over_k, 0, unroll=8)
    apply_k(e, ke, lt, own)
    apply_k(t, kt, lt, own, four=True)
    products = coarse_products(co, lt) + fine_products(e, s, t, ke, kt, lt, own)
    rows = [jnp.sum(p, axis=0, keepdims=True) for p in products] + [jnp.zeros((3, 128), jnp.float32)]
    total = jnp.sum(jnp.concatenate(rows, axis=0), axis=1, keepdims=True)
    line = jnp.sum(jnp.where(diagonal(), total, 0.0), axis=0, keepdims=True)
    for n in range(gram.shape[0]):
        gram[n] = line


def pack_kernel(idx, mine, own, to_upper, to_lower):
    first = lax.broadcasted_iota(jnp.int32, (8, 128), 0) == 0
    last = lax.broadcasted_iota(jnp.int32, (8, 128), 0) == 7
    for f in range(5):
        low = mine[pl.ds(20 + f, 8, stride=30), :]
        high = mine[pl.ds(25 + f, 8, stride=30), :]
        for xi in range(4):
            k = f * 4 + xi
            v = mine[pl.ds(5 * xi + f, 8, stride=30), :]
            if xi == 0:
                v = v + 1.5 * jnp.where(first, 0.0, pltpu.roll(high, 1, 0))
            if xi == 3:
                v = v - 1.5 * jnp.where(last, 0.0, pltpu.roll(low, 7, 0))
            own[k] = v
            to_upper[pl.ds(k, 6, stride=20), :] = v[2:8]
            to_lower[pl.ds(k, 6, stride=20), :] = v[0:6]
        to_upper[120 + f:121 + f] = high[7:8]
        to_lower[120 + f:121 + f] = low[0:1]


def window_kernel(idx, lower, own, upper, edge_low, edge_high, after, win):
    for f in range(5):
        e = 120 + f
        for xi in range(4):
            k = f * 4 + xi
            at = 20 * k
            low, mid, high = lower[pl.ds(k, 6, stride=20), :], own[k], upper[pl.ds(k, 6, stride=20), :]
            win[at:at + 6] = low
            win[at + 6:at + 14] = mid
            win[at + 14:at + 20] = high
            if xi == 0:
                win[at + 6:at + 7] = mid[0:1] + 1.5 * lower[e:e + 1]
                win[at + 14:at + 15] = high[0:1] + 1.5 * edge_high[e:e + 1]
            if xi == 3:
                win[at + 13:at + 14] = mid[7:8] - 1.5 * upper[e:e + 1]
                win[at + 5:at + 6] = low[5:6] - 1.5 * edge_low[e:e + 1]


def first_pass_kernel(idx, quarters, lt, r, s, t, ke, kt, gram, co):
    zero = jnp.zeros((2, 128), jnp.float32)
    for f in range(5):
        for xi in range(4):
            for zi in range(4):
                k = f * 16 + xi * 4 + zi
                at = 20 * (f * 4 + xi)
                r[k, 0:2] = zero
                r[k, 2:22] = quarters[zi, at:at + 20]
                r[k, 22:24] = zero
    pass_words(r, s, t, ke, kt, co, gram, lt)


def step_sizes(sums):
    line = sums[0, 0:1]
    for n in range(1, sums.shape[0]):
        line = line + sums[n, 0:1]
    v = jnp.sum(jnp.where(diagonal(), line, 0.0), axis=1, keepdims=True)
    v = jnp.broadcast_to(v, (24, 128))
    c0, c1, c2 = v[0:1], v[1:2], v[2:3]
    den = 4.0 * c0 + 4.0 * c1 + c2 + EPS
    a1, b1 = (2.0 * c0 + c1) / den, (2.0 * c1 + c2 + EPS) / den
    d = [jnp.ones_like(a1), b1, -a1]

    def form(base, twice):
        total = None
        for n, (i, j) in enumerate(PAIRS):
            term = d[i] * d[j] * v[base + n:base + n + 1]
            if twice and i != j:
                term = 2.0 * term
            total = term if total is None else total + term
        return total
    rr, kk = jnp.maximum(form(3, True), 0.0), jnp.maximum(form(15, True), 0.0)
    bound = jnp.sqrt(rr) * jnp.sqrt(kk)
    rk = jnp.clip(form(9, False), -bound, bound)
    den = 4.0 * rr + 4.0 * rk + kk + EPS
    return a1, b1, (2.0 * rr + rk) / den, (2.0 * rk + kk + EPS) / den


def next_pass_kernel(first, idx, sums, e, s, t, ke, kt, *rest):
    if first:
        lt, r2, s2, t2, ke2, kt2, acc2, gram, co = rest
    else:
        acc, lt, r2, s2, t2, ke2, kt2, acc2, gram, co = rest
    a1, b1, a2, b2 = step_sizes(sums)

    def put(k, tk, kr):
        sk = s[k]
        r1 = e[k] + b1 * sk - a1 * tk
        v = a1 * sk[8:16] + a2 * r1[8:16]
        acc2[k] = v if first else acc[k] + v
        r2[k] = b2 * r1 - a2 * kr

    def over_k(k, _):
        tk = t[k]
        kr = ke[k] + b1 * tk - a1 * kt[k]
        put(k, tk, kr)
        put(64 + k, tk, kr)
        return 0
    lax.fori_loop(0, 16, over_k, 0, unroll=4)

    def rest_k(k, _):
        tk = t[k]
        put(k, tk, ke[k] + b1 * tk - a1 * kt[k])
        return 0
    lax.fori_loop(16, 64, rest_k, 0, unroll=8)
    pass_words(r2, s2, t2, ke2, kt2, co, gram, lt, own=not first)


def third_pass_kernel(idx, sums, e, s, t, ke, kt, acc, lt, eo, so, to, acc2, gram,
                      r2, s2, t2, ke2, kt2, co):
    next_pass_kernel(False, idx, sums, e, s, t, ke, kt, acc, lt, r2, s2, t2, ke2, kt2, acc2, gram, co)
    eo[...] = r2[:, 8:16]
    so[...] = s2[:, 8:16]
    to[...] = t2[:, 8:16]


def last_kernel(idx, sums, e, s, t, acc, low, h2, select, split, out, fields, change, stack, rows):
    a1, b1, a2, _ = step_sizes(sums)

    def over_k(k, _):
        r1 = e[k] + b1 * s[k] - a1 * t[k % 64]
        change[pl.ds(pl.multiple_of(k * 8, 8), 8)] = acc[k] + a1 * s[k] + a2 * r1
        return 0
    lax.fori_loop(0, 80, over_k, 0, unroll=16)
    z = idx[1]
    stack[...] = jnp.zeros_like(stack)
    here = row_of_y()
    for c in range(16):
        for f in range(5):
            k = f * 16 + c
            d = change[pl.ds(k * 8 + z, 1)]
            stack[f:f + 1, 128 * c:128 * c + 128] = d
            n = 8 * (k // 4)
            rows[n:n + 8, 128 * (c % 4):128 * (c % 4) + 128] = (low[5 * c + f:5 * c + f + 1] + d) * here
    fields[...] = project(rows[...], select[...]).reshape(5, 4, 8, 64)
    whole = stack[...]
    d1 = whole.astype(jnp.bfloat16).astype(jnp.float32)
    d2 = (whole - d1).astype(jnp.bfloat16).astype(jnp.float32)
    d3 = whole - d1 - d2
    parts = jnp.concatenate([d1, d1, d2, d1, d2, d3], axis=0).astype(jnp.bfloat16)
    add = lax.dot_general(parts, split[0].astype(jnp.bfloat16), (((0,), (0,)), ((), ())),
                          preferred_element_type=jnp.float32).reshape(16, 8, 16, 128)
    for c in range(16):
        xi, zi = c // 4, c % 4
        v = h2[c] + add[c]
        for y in range(8):
            out[xi, y, pl.ds(zi, 16, stride=4), :] = v[y]


def on_device(distribution, forcing):
    import functools
    tables = {k: jnp.asarray(v) for k, v in constant_tables().items()}
    spaces = lax.axis_size("space")
    blocks = spaces // 8
    idx = jnp.stack([lax.axis_index("vel"), lax.axis_index("space") % 8]).astype(jnp.int32)
    vec, lt = tables["vec"], tables["lanes"]
    wide = (16, 8, 16, 128)
    layer = (4, 8, 16, 128)

    def shifted(x, by):
        return lax.ppermute(x, "space", [(i, (i + by) % spaces) for i in range(spaces)])

    up, down = call(rim_kernel, "rims", idx, [distribution], [],
                    [(544, 128)] * 2, [layer, layer, (8, 8, 16, 128), (1024, 8), (1, 32, 128)])
    up, down = shifted(up, 1), shifted(down, -1)
    twice, moma, force = call(local_kernel, "local", idx, [distribution, forcing, tables["select"]],
                              [vec, tables["tab0"], tables["tab1"], tables["tab2"]],
                              [wide, (16, 48, 128), (4, 20, 128)], [wide, wide, (2048, 48)])
    pay, delta, inflow = call(moment_kernel, "moments", idx, [up, down, moma, tables["mix"], lt],
                              [vec, tables["tabd"], tables["tabs"]], [(408, 128), layer, layer],
                              [layer, (16, 48, 128), (16, 40, 128), (64, 2048)])
    got = lax.all_gather(pay, "vel")
    (res,) = call(residual_kernel, "residual", idx, [got, force], [], [(8, 30, 128)])
    near = [[a * 8 + b for b in range(8)] for a in range(blocks)]
    far = [[a * 8 + b for a in range(blocks)] for b in range(8)]
    mine = lax.all_to_all(res, "space", 0, 0, axis_index_groups=near, tiled=True).reshape(240, 128)
    own_r, to_upper, to_lower = call(pack_kernel, "pack", idx, [mine], [],
                                     [(20, 8, 128), (125, 128), (125, 128)])
    lower, upper = shifted(to_upper, 8), shifted(to_lower, -8)
    h2, low = call(feq_kernel, "feq", idx, [got, twice, delta, inflow, lt],
                   [vec, tables["final"]],
                   [wide, (80, 128)], [(16, 8, 128), (4, 8, 128), (4, 8, 128), (56, 2048)])
    (quarter,) = call(window_kernel, "window", idx, [lower, own_r, upper, to_lower, to_upper, low], [],
                      [(400, 128)])
    quarters = lax.all_gather(quarter, "vel")

    def summed(gram):
        return lax.all_to_all(gram, "space", 0, 0, axis_index_groups=far, tiled=True)

    win, own, part = (80, 24, 128), (80, 8, 128), (blocks, 1, 128)
    four, own4 = (64, 24, 128), (64, 8, 128)
    co = (40, 24, 128)
    e, s, t, ke, kt, gram = call(first_pass_kernel, "pass1", idx, [quarters, lt], [],
                                  [win, win, four, four, four, part], [co])
    e, s, t, ke, kt, acc, gram = call(functools.partial(next_pass_kernel, True), "pass2", idx,
                                       [summed(gram), e, s, t, ke, kt, lt], [],
                                       [win, win, four, four, four, own, part], [co])
    e, s, t, acc, gram = call(third_pass_kernel, "pass3", idx,
                               [summed(gram), e, s, t, ke, kt, acc, lt], [],
                               [own, own, own4, own, part], [win, win, four, own4, own4, co])
    out, fields = call(last_kernel, "last", idx,
                       [summed(gram), e, s, t, acc, low, h2, tables["select"]], [tables["split"]],
                       [(4, 8, 64, 128), (5, 4, 8, 64)], [(640, 128), (8, 2048), (160, 512)])
    return out, fields


def solution(mesh):
    return jax.shard_map(
        on_device,
        mesh=mesh,
        in_specs=(P("space", None, None, "vel"), P(None, "space", None, None)),
        out_specs=(P("space", None, None, "vel"), P(None, "space", None, None)),
        check_vma=False,
    )
```
